32 devices in a mesh: ctx: 8 (over y, x, core), fsdp: 4 (over z).
Axes of the slice: x: 2, y: 2, z: 4, core: 2. Of those that a mesh axis runs over, the one named last changes fastest.
Arguments:
- hidden_in: bfloat16 [4, 1024, 768], P('fsdp', 'ctx'), may hold values from -6 to 6
- out_grad: bfloat16 [4, 1024, 768], P('fsdp', 'ctx'), may hold values from -6 to 6
- block_ids: int32 [4, 1024], P('fsdp'), may hold values from 0 to 7, never falling along the last dimension, each value on 1 to 256 neighbouring positions
- clusters: int32 [4, 12, 1024], P('fsdp'), may hold values from 0 to 1023, as said below
- w_query: bfloat16 [768, 768], P('fsdp'), may hold values from -0.21875 to 0.21875
- w_key: bfloat16 [768, 768], P('fsdp'), may hold values from -0.21875 to 0.21875
- w_value: bfloat16 [768, 768], P('fsdp'), may hold values from -0.21875 to 0.21875
- w_out: bfloat16 [768, 768], P('fsdp'), may hold values from -1.25 to 1.25
- b_query: bfloat16 [768], P('fsdp'), may hold values from -3 to 3
- b_value: bfloat16 [768], P('fsdp'), may hold values from -3 to 3
- b_out: bfloat16 [768], P('fsdp'), may hold values from -3 to 3
- ln1_gain: bfloat16 [768], P('fsdp'), may hold values from 0.5 to 1.5
- ln1_bias: bfloat16 [768], P('fsdp'), may hold values from -3 to 3
- w_in: bfloat16 [768, 3072], P('fsdp'), may hold values from -0.21875 to 0.21875
- b_in: bfloat16 [3072], P('fsdp'), may hold values from -3 to 3
- w_down: bfloat16 [3072, 768], P('fsdp'), may hold values from -0.109375 to 0.109375
- b_down: bfloat16 [768], P('fsdp'), may hold values from -3 to 3
- ln2_gain: bfloat16 [768], P('fsdp'), may hold values from 0.5 to 1.5
- ln2_bias: bfloat16 [768], P('fsdp'), may hold values from -3 to 3
Outputs:
- layer_out: bfloat16 [4, 1024, 768], P('fsdp', 'ctx')
- input_grad: bfloat16 [4, 1024, 768], P('fsdp', 'ctx')
- grad_w_query: float32 [768, 768], P('fsdp')
- grad_w_key: float32 [768, 768], P('fsdp')
- grad_w_value: float32 [768, 768], P('fsdp')
- grad_w_out: float32 [768, 768], P('fsdp')
- grad_b_query: float32 [768], P('fsdp')
- grad_b_value: float32 [768], P('fsdp')
- grad_b_out: float32 [768], P('fsdp')
- grad_ln1_gain: float32 [768], P('fsdp')
- grad_ln1_bias: float32 [768], P('fsdp')
- grad_w_in: float32 [768, 3072], P('fsdp')
- grad_b_in: float32 [3072], P('fsdp')
- grad_w_down: float32 [3072, 768], P('fsdp')
- grad_b_down: float32 [768], P('fsdp')
- grad_ln2_gain: float32 [768], P('fsdp')
- grad_ln2_bias: float32 [768], P('fsdp')
The draws below stay inside these ranges and needn't reach their ends.
Inputs may be any that keep to these rules, and one draw needn't show every extreme that they name: `clusters`: each head's row is an order of all 1024 stored rows of its sequence; every cluster (128 consecutive entries) holds exactly 16 stored rows of each aligned range of 128 stored rows. `block_ids`: never falls along the positions; each block holds 1 to 256 positions.
All inputs are finite; a program needn't handle non-finite values.
Results may differ from the reference program's by a relative error of at most 0.022.
Values may be sent and summed in bfloat16 or wider, within the bound.
No kernel may reach another device: no remote copies, remote signals or barrier semaphores. Data moves between devices by JAX's collectives and lax.ppermute only.
A program may use at most 192 MiB of HBM per device.

```python
import math
import jax
import jax.numpy as jnp
import numpy as np
from jax import lax

D = 768
H = 12
DH = 64
FF = 3072
TOK_DEV = 128
CLUSTER = 128
BLOCK = 256
SEQ = 1024
BATCH = 4
N_CTX = 8


def draw_clusters(key, part):
    parts = SEQ // TOK_DEV
    members = CLUSTER // parts
    groups = TOK_DEV // members
    count = BATCH * H
    first_keys = jax.random.split(jax.random.fold_in(key, 11), count * parts)
    base = jnp.arange(TOK_DEV, dtype=jnp.int32)
    shuffled = jax.vmap(lambda item: jax.random.permutation(item, base))(first_keys)
    offsets = (jnp.arange(parts, dtype=jnp.int32) * TOK_DEV)[None, :, None, None]
    shuffled = shuffled.reshape(count, parts, groups, members) + offsets
    grouped = jnp.transpose(shuffled, (0, 2, 1, 3)).reshape(count * groups, CLUSTER)
    second_keys = jax.random.split(jax.random.fold_in(key, 23), count * groups)
    mixed = jax.vmap(lambda item, entries: jax.random.permutation(item, entries))(second_keys, grouped)
    return mixed.reshape(BATCH, H, SEQ).astype(jnp.int32)


def block_levels(rng, extent, pieces, low, top_value):
    level, own = 1.0, jax.random.fold_in(rng, 6)
    for axis_at, blocks in pieces:
        heights = jnp.exp(jax.random.uniform(jax.random.fold_in(own, axis_at), (blocks,), jnp.float32, low / len(pieces), top_value / len(pieces)))
        level = level * jnp.repeat(heights, extent[axis_at] // blocks).reshape([-1 if axis == axis_at else 1 for axis in range(len(extent))])
    return level


def length_profile(count, total, limit, skew):
    weights = [(1 << 20) // math.isqrt(standing ** skew) + 1 for standing in range(2, count + 1)]
    rest, given = total - limit - (count - 1), [1] * (count - 1)
    while rest > 0:
        candidates = [i for i in range(count - 1) if given[i] < limit]
        whole, budget = sum([weights[i] for i in candidates]), rest
        for i in candidates:
            addition = min(limit - given[i], max(1, budget * weights[i] // whole), rest)
            given[i] = given[i] + addition
            rest = rest - addition
    return np.array([limit] + given)


def uneven(rng, count, total, limit, skew):
    if count == 2:
        one = jax.random.randint(rng, (), max(1, total - limit), min(limit, total - 1) + 1)
        return jnp.stack([one, total - one])
    sizes = jnp.asarray(length_profile(count, total, limit, skew), jnp.int32)
    couples = (count - 1) // 2
    source_of, receiver = sizes[1:1 + 2 * couples:2], sizes[2:2 + 2 * couples:2]
    slack = jnp.minimum(source_of - 1, limit - receiver)
    moved = jax.random.randint(jax.random.fold_in(rng, 1), (couples,), 0, 1 << 20) % (slack + 1)
    sizes = sizes.at[1:1 + 2 * couples:2].set(source_of - moved).at[2:2 + 2 * couples:2].set(receiver + moved)
    return sizes[jax.random.permutation(jax.random.fold_in(rng, 2), count)]


def normal_values(own_key, extent, width, most, shards=(), kind=jnp.bfloat16):
    values = jax.random.normal(own_key, extent, jnp.float32) * width
    if len(shards) > 0:
        values = block_levels(own_key, extent, shards, -0.22, 0.18) * values
    return jnp.clip(values, min=-most, max=most).astype(kind)


def setup_inputs(seed: int = 0) -> dict:
    key_list = jax.random.split(jax.random.key(seed), 20)
    return {
        "hidden_in": normal_values(key_list[0], (BATCH, SEQ, D), 1.0, 6.0, ((0, 4), (1, 8))),
        "out_grad": normal_values(key_list[1], (BATCH, SEQ, D), 1.0, 6.0, ((0, 4), (1, 8))),
        "block_ids": jax.vmap(lambda own: jnp.searchsorted(jnp.cumsum(uneven(own, 2 * SEQ // BLOCK, SEQ, BLOCK, 1)), jnp.arange(SEQ), side="right"))(jax.random.split(key_list[2], BATCH)).reshape((BATCH, SEQ)).astype(jnp.int32),
        "clusters": draw_clusters(jax.random.fold_in(key_list[19], 71), 0),
        "w_query": normal_values(key_list[4], (D, D), D ** -0.5, 0.21875, ((0, 4),)),
        "w_key": normal_values(key_list[5], (D, D), D ** -0.5, 0.21875, ((0, 4),)),
        "w_value": normal_values(key_list[6], (D, D), D ** -0.5, 0.21875, ((0, 4),)),
        "w_out": normal_values(key_list[7], (D, D), (D // 32) ** -0.5, 1.25, ((0, 4),)),
        "b_query": normal_values(key_list[8], (D,), 0.5, 3.0, ((0, 4),)),
        "b_value": normal_values(key_list[9], (D,), 0.5, 3.0, ((0, 4),)),
        "b_out": normal_values(key_list[10], (D,), 0.5, 3.0, ((0, 4),)),
        "ln1_gain": jnp.clip(1.0 + 0.1 * jax.random.normal(key_list[11], (D,), jnp.float32), 0.5, 1.5).astype(jnp.bfloat16),
        "ln1_bias": normal_values(key_list[12], (D,), 0.5, 3.0, ((0, 4),)),
        "w_in": normal_values(key_list[13], (D, FF), D ** -0.5, 0.21875, ((0, 4),)),
        "b_in": normal_values(key_list[14], (FF,), 0.5, 3.0, ((0, 4),)),
        "w_down": normal_values(key_list[15], (FF, D), FF ** -0.5, 0.109375, ((0, 4),)),
        "b_down": normal_values(key_list[16], (D,), 0.5, 3.0, ((0, 4),)),
        "ln2_gain": jnp.clip(1.0 + 0.1 * jax.random.normal(key_list[17], (D,), jnp.float32), 0.5, 1.5).astype(jnp.bfloat16),
        "ln2_bias": normal_values(key_list[18], (D,), 0.5, 3.0, ((0, 4),)),
    }


EPSILON = 1e-12
FLOOR = -1e+30
HIGHEST = lax.Precision.HIGHEST

@jax.custom_vjp
def low(v):
    return lax.optimization_barrier(v.astype(jnp.bfloat16)).astype(jnp.float32)

@jax.custom_vjp
def low_back(v):
    return v

def low_keep(v):
    return (low(v), None)

def low_pass(kept, grad):
    return (grad,)

def back_keep(v):
    return (v, None)

def back_low(kept, grad):
    return (low(grad),)
low.defvjp(low_keep, low_pass)
low_back.defvjp(back_keep, back_low)

def layer_norm(values, gain, shift):
    centre = values - lax.optimization_barrier(jnp.mean(values, axis=-1, keepdims=True))
    spread = lax.optimization_barrier(jnp.mean(centre * centre, axis=-1, keepdims=True))
    return centre * lax.rsqrt(spread + EPSILON) * gain + shift

def positions(length, per_device, parts):
    stored = jnp.arange(length, dtype=jnp.int32)
    device = stored // per_device
    within = stored % per_device
    half = per_device // 2
    return jnp.where(within < half, device * half + within, (2 * parts - 1 - device) * half + within - half).astype(jnp.int32)

def head_attention(query, key_rows, value_rows, order, stored):
    length = order.shape[0]
    groups = length // CLUSTER
    q_part = query[order].reshape(groups, CLUSTER, DH)
    k_part = key_rows[order].reshape(groups, CLUSTER, DH)
    v_part = value_rows[order].reshape(groups, CLUSTER, DH)
    blocks = stored[order].reshape(groups, CLUSTER)
    scores = low_back(jnp.einsum('cqd,ckd->cqk', q_part, k_part, precision=HIGHEST) * DH ** (-0.5))
    allowed = blocks[:, None, :] <= blocks[:, :, None]
    masked = jnp.where(allowed, scores, FLOOR)
    top = lax.optimization_barrier(jnp.max(masked, axis=-1, keepdims=True))
    weights = jnp.where(allowed, jnp.exp(masked - top), 0.0)
    probs = weights / lax.optimization_barrier(jnp.sum(weights, axis=-1, keepdims=True))
    mixed = jnp.einsum('cqk,ckd->cqd', low(probs), v_part, precision=HIGHEST).reshape(length, DH)
    inverse = jnp.zeros(length, jnp.int32).at[order].set(jnp.arange(length, dtype=jnp.int32))
    return mixed[inverse]

def forward(params, hidden, stored, order):
    w_query, w_key, w_value, w_out, b_query, b_value, b_out, gain_one, shift_one, w_in, b_in, w_down, b_down, gain_two, shift_two = params
    length = hidden.shape[0]
    query = low(low_back(jnp.dot(hidden, w_query, precision=HIGHEST) + b_query))
    key_rows = low(low_back(jnp.dot(hidden, w_key, precision=HIGHEST)))
    value_rows = low(low_back(jnp.dot(hidden, w_value, precision=HIGHEST) + b_value))

    def split_heads(values):
        return jnp.transpose(values.reshape(length, H, DH), (1, 0, 2))

    def one_head(item):
        return head_attention(item[0], item[1], item[2], item[3], stored)
    mixed = lax.map(jax.checkpoint(one_head), (split_heads(query), split_heads(key_rows), split_heads(value_rows), order))
    context = low(low_back(jnp.transpose(mixed, (1, 0, 2)).reshape(length, H * DH)))
    attended = low_back(jnp.dot(context, w_out, precision=HIGHEST) + b_out)
    first = layer_norm(hidden + attended, gain_one, shift_one)
    inner = low_back(jnp.dot(low(first), w_in, precision=HIGHEST) + b_in)
    active = low(jax.nn.gelu(inner, approximate=False))
    branch = low_back(jnp.dot(active, w_down, precision=HIGHEST) + b_down)
    return layer_norm(first + branch, gain_two, shift_two)

def reference(hidden_in, out_grad, block_ids, clusters, w_query, w_key, w_value, w_out, b_query, b_value, b_out, ln1_gain, ln1_bias, w_in, b_in, w_down, b_down, ln2_gain, ln2_bias):
    params = tuple((entry.astype(jnp.float32) for entry in (w_query, w_key, w_value, w_out, b_query, b_value, b_out, ln1_gain, ln1_bias, w_in, b_in, w_down, b_down, ln2_gain, ln2_bias)))
    place = positions(SEQ, TOK_DEV, N_CTX)

    def one_sequence(totals, item):
        hidden, cotangent, blocks, order = item
        stored = blocks[place]

        def forward_of(weights, rows):
            return forward(weights, rows, stored, order)
        output, pullback = jax.vjp(forward_of, params, hidden.astype(jnp.float32))
        grads, hidden_grad = pullback(cotangent.astype(jnp.float32))
        totals = jax.tree.map(jnp.add, totals, grads)
        return (totals, (output.astype(jnp.bfloat16), hidden_grad.astype(jnp.bfloat16)))
    start = jax.tree.map(jnp.zeros_like, params)
    totals, results = lax.scan(one_sequence, start, (hidden_in, out_grad, block_ids, clusters))
    return (results[0], results[1], totals[0], totals[1], totals[2], totals[3], totals[4], totals[5], totals[6], totals[7], totals[8], totals[9], totals[10], totals[11], totals[12], totals[13], totals[14])
```

```python
import functools

import jax
import jax.numpy as jnp
from jax import lax
from jax.experimental import pallas as pl
from jax.experimental.pallas import tpu as pltpu
from jax.sharding import PartitionSpec as P

H = 12
DH = 64
CLUSTER = 128


EPSILON = 1e-12
FLOOR = -1e30


def layer_norm(values, gain, shift):
    centre = values - jnp.mean(values, axis=-1, keepdims=True)
    spread = jnp.mean(centre * centre, axis=-1, keepdims=True)
    return centre * lax.rsqrt(spread + EPSILON) * gain + shift


def exact_gelu(values):
    return jax.nn.gelu(values, approximate=False)


def positions(length, per_device, parts):
    stored = jnp.arange(length, dtype=jnp.int32)
    device = stored // per_device
    within = stored % per_device
    half = per_device // 2
    return jnp.where(
        within < half, device * half + within, (2 * parts - 1 - device) * half + within - half
    )


def contract(left, right):
    return lax.dot_general(
        left, right, (((0,), (0,)), ((), ())), preferred_element_type=jnp.float32
    )


def back_product(grad, weight):
    return lax.dot_general(
        grad, weight, (((1,), (1,)), ((), ())), preferred_element_type=jnp.float32
    )


def column_sum(values):
    return jnp.sum(values.astype(jnp.float32), axis=0)


def per_head_rows(rows, index):
    split = rows.reshape(rows.shape[0], H, DH)
    return jnp.take_along_axis(split, index.T[:, :, None], axis=0)


def cluster_tables(order, device, per_device, parts):
    heads, length = order.shape
    groups = length // CLUSTER
    members = CLUSTER // parts
    mine = (order // per_device == device).astype(jnp.int32)
    rank = jnp.cumsum(mine.reshape(heads, groups, CLUSTER), axis=-1).reshape(heads, length) - 1
    entry = jnp.arange(length, dtype=jnp.int32)[None, :]
    slot = jnp.where(mine == 1, entry // CLUSTER * members + rank, per_device)
    head_index = jnp.arange(heads, dtype=jnp.int32)[:, None]
    picked = (
        jnp.zeros((heads, per_device), jnp.int32)
        .at[head_index, slot]
        .set(order - device * per_device, mode="drop")
    )
    counter = jnp.broadcast_to(
        jnp.arange(per_device, dtype=jnp.int32)[None, :], (heads, per_device)
    )
    placed = jnp.zeros((heads, per_device), jnp.int32).at[head_index, picked].set(counter)
    inverse = (
        jnp.zeros((heads, length), jnp.int32)
        .at[head_index, order]
        .set(jnp.broadcast_to(jnp.arange(length, dtype=jnp.int32)[None, :], (heads, length)))
    )
    return (picked, placed, inverse)


def score_blocks(query, key_rows, query_blocks, key_blocks, scale):
    scores = (
        jnp.einsum("cqhd,ckhd->hcqk", query, key_rows, preferred_element_type=jnp.float32) * scale
    )
    allowed = key_blocks[:, :, None, :] <= query_blocks[:, :, :, None]
    return (scores, allowed)


def attend(query, key_rows, value_rows, query_blocks, key_blocks, scale):
    scores, allowed = score_blocks(query, key_rows, query_blocks, key_blocks, scale)
    masked = jnp.where(allowed, scores, FLOOR)
    top = jnp.max(masked, axis=-1, keepdims=True)
    weights = jnp.where(allowed, jnp.exp(masked - top), 0.0)
    total = jnp.sum(weights, axis=-1, keepdims=True)
    probs = (weights / total).astype(jnp.bfloat16)
    mixed = jnp.einsum("hcqk,ckhd->cqhd", probs, value_rows, preferred_element_type=jnp.float32)
    return (mixed.astype(jnp.bfloat16), top + jnp.log(total))


def attend_back(query, key_rows, value_rows, query_blocks, key_blocks, logsum, d_mixed, scale):
    scores, allowed = score_blocks(query, key_rows, query_blocks, key_blocks, scale)
    probs = jnp.where(allowed, jnp.exp(jnp.where(allowed, scores, FLOOR) - logsum), 0.0)
    rounded = probs.astype(jnp.bfloat16)
    d_probs = jnp.einsum("cqhd,ckhd->hcqk", d_mixed, value_rows, preferred_element_type=jnp.float32)
    centred = jnp.sum(probs * d_probs, axis=-1, keepdims=True)
    d_scores = (probs * (d_probs - centred)).astype(jnp.bfloat16)
    d_query = (
        jnp.einsum("hcqk,ckhd->cqhd", d_scores, key_rows, preferred_element_type=jnp.float32)
        * scale
    )
    d_key = (
        jnp.einsum("hcqk,cqhd->ckhd", d_scores, query, preferred_element_type=jnp.float32) * scale
    )
    d_value = jnp.einsum("hcqk,cqhd->ckhd", rounded, d_mixed, preferred_element_type=jnp.float32)
    return (d_query, d_key, d_value)


def general_body(
    hidden_in,
    out_grad,
    block_ids,
    clusters,
    w_query,
    w_key,
    w_value,
    w_out,
    b_query,
    b_value,
    b_out,
    ln1_gain,
    ln1_bias,
    w_in,
    b_in,
    w_down,
    b_down,
    ln2_gain,
    ln2_bias,
):
    parts = lax.axis_size("ctx")
    device = lax.axis_index("ctx")
    sequences, per_device, width = hidden_in.shape
    length = per_device * parts
    members = CLUSTER // parts
    groups = length // CLUSTER
    scale = DH ** (-0.5)
    (
        full_query,
        full_key,
        full_value,
        full_out,
        bias_query,
        bias_value,
        bias_out,
        gain_one,
        shift_one,
    ) = (
        lax.all_gather(w_query, "fsdp", axis=0, tiled=True),
        lax.all_gather(w_key, "fsdp", axis=0, tiled=True),
        lax.all_gather(w_value, "fsdp", axis=0, tiled=True),
        lax.all_gather(w_out, "fsdp", axis=0, tiled=True),
        lax.all_gather(b_query, "fsdp", axis=0, tiled=True),
        lax.all_gather(b_value, "fsdp", axis=0, tiled=True),
        lax.all_gather(b_out, "fsdp", axis=0, tiled=True),
        lax.all_gather(ln1_gain, "fsdp", axis=0, tiled=True),
        lax.all_gather(ln1_bias, "fsdp", axis=0, tiled=True),
    )
    full_in, full_down, bias_in, bias_down, gain_two, shift_two = (
        lax.all_gather(w_in, "fsdp", axis=0, tiled=True),
        lax.all_gather(w_down, "fsdp", axis=0, tiled=True),
        lax.all_gather(b_in, "fsdp", axis=0, tiled=True),
        lax.all_gather(b_down, "fsdp", axis=0, tiled=True),
        lax.all_gather(ln2_gain, "fsdp", axis=0, tiled=True),
        lax.all_gather(ln2_bias, "fsdp", axis=0, tiled=True),
    )
    hidden = hidden_in.reshape(sequences * per_device, width)
    query_rows = (
        jnp.dot(hidden, full_query, preferred_element_type=jnp.float32) + bias_query
    ).astype(jnp.bfloat16)
    key_rows = jnp.dot(hidden, full_key, preferred_element_type=jnp.float32).astype(jnp.bfloat16)
    value_rows = (
        jnp.dot(hidden, full_value, preferred_element_type=jnp.float32) + bias_value
    ).astype(jnp.bfloat16)
    place = positions(length, per_device, parts)
    index = 0
    order = clusters[index]
    stored_blocks = block_ids[index][place]
    picked, placed, inverse = cluster_tables(order, device, per_device, parts)
    q_local = per_head_rows(query_rows, picked).reshape(groups, members, H, DH)
    query_blocks = stored_blocks[device * per_device + picked].reshape(H, groups, members)
    key_all = lax.all_gather(key_rows, "ctx", axis=0, tiled=True)
    value_all = lax.all_gather(value_rows, "ctx", axis=0, tiled=True)
    key_cluster = per_head_rows(key_all, order).reshape(groups, CLUSTER, H, DH)
    value_cluster = per_head_rows(value_all, order).reshape(groups, CLUSTER, H, DH)
    key_blocks = stored_blocks[order].reshape(H, groups, CLUSTER)
    mixed, logsum = attend(q_local, key_cluster, value_cluster, query_blocks, key_blocks, scale)
    contexts = per_head_rows(mixed.reshape(per_device, width), placed).reshape(per_device, width)
    kept = [
        (
            q_local,
            key_cluster,
            value_cluster,
            query_blocks,
            key_blocks,
            logsum,
            picked,
            placed,
            inverse,
        )
    ]
    attended = jnp.dot(contexts, full_out, preferred_element_type=jnp.float32) + bias_out
    first_sum = hidden.astype(jnp.float32) + attended
    first, first_pull = jax.vjp(
        layer_norm, first_sum, gain_one.astype(jnp.float32), shift_one.astype(jnp.float32)
    )
    first_low = first.astype(jnp.bfloat16)
    inner = jnp.dot(first_low, full_in, preferred_element_type=jnp.float32) + bias_in
    active_full, gelu_pull = jax.vjp(exact_gelu, inner)
    active = active_full.astype(jnp.bfloat16)
    second_sum = first + jnp.dot(active, full_down, preferred_element_type=jnp.float32) + bias_down
    second, second_pull = jax.vjp(
        layer_norm, second_sum, gain_two.astype(jnp.float32), shift_two.astype(jnp.float32)
    )
    layer_out = second.astype(jnp.bfloat16).reshape(sequences, per_device, width)
    d_out = out_grad.reshape(sequences * per_device, width).astype(jnp.float32)
    d_second, g_gain_two, g_shift_two = second_pull(d_out)
    d_branch = d_second.astype(jnp.bfloat16)
    g_w_down = contract(active, d_branch)
    g_b_down = column_sum(d_branch)
    d_active = back_product(d_branch, full_down)
    d_inner = gelu_pull(d_active)[0].astype(jnp.bfloat16)
    g_w_in = contract(first_low, d_inner)
    g_b_in = column_sum(d_inner)
    d_first = d_second + back_product(d_inner, full_in)
    d_sum, g_gain_one, g_shift_one = first_pull(d_first)
    d_attended = d_sum.astype(jnp.bfloat16)
    g_w_out = contract(contexts, d_attended)
    g_b_out = column_sum(d_attended)
    d_context = back_product(d_attended, full_out).astype(jnp.bfloat16)
    index = 0
    q_kept, k_kept, v_kept, blocks_q, blocks_k, logsum, picked, placed, inverse = kept[index]
    d_cluster = per_head_rows(d_context, picked).reshape(groups, members, H, DH)
    d_query, d_key, d_value = attend_back(
        q_kept, k_kept, v_kept, blocks_q, blocks_k, logsum, d_cluster, scale
    )
    key_full = per_head_rows(d_key.reshape(length, width), inverse).reshape(length, width)
    value_full = per_head_rows(d_value.reshape(length, width), inverse).reshape(length, width)
    key_part = lax.psum_scatter(
        key_full.astype(jnp.bfloat16), "ctx", scatter_dimension=0, tiled=True
    )
    value_part = lax.psum_scatter(
        value_full.astype(jnp.bfloat16), "ctx", scatter_dimension=0, tiled=True
    )
    query_local = d_query.astype(jnp.bfloat16).reshape(per_device, width)
    query_grads = per_head_rows(query_local, placed).reshape(per_device, width)
    g_w_query = contract(hidden, query_grads)
    g_b_query = column_sum(query_grads)
    g_w_key = contract(hidden, key_part)
    g_w_value = contract(hidden, value_part)
    g_b_value = column_sum(value_part)
    input_total = (
        d_sum
        + back_product(query_grads, full_query)
        + back_product(key_part, full_key)
        + back_product(value_part, full_value)
    )
    input_grad = input_total.astype(jnp.bfloat16).reshape(sequences, per_device, width)
    shares = (
        lax.psum_scatter(
            g_w_query.astype(jnp.bfloat16), "fsdp", scatter_dimension=0, tiled=True
        ).astype(jnp.float32),
        lax.psum_scatter(
            g_w_key.astype(jnp.bfloat16), "fsdp", scatter_dimension=0, tiled=True
        ).astype(jnp.float32),
        lax.psum_scatter(
            g_w_value.astype(jnp.bfloat16), "fsdp", scatter_dimension=0, tiled=True
        ).astype(jnp.float32),
        lax.psum_scatter(
            g_w_out.astype(jnp.bfloat16), "fsdp", scatter_dimension=0, tiled=True
        ).astype(jnp.float32),
        lax.psum_scatter(
            g_b_query.astype(jnp.bfloat16), "fsdp", scatter_dimension=0, tiled=True
        ).astype(jnp.float32),
        lax.psum_scatter(
            g_b_value.astype(jnp.bfloat16), "fsdp", scatter_dimension=0, tiled=True
        ).astype(jnp.float32),
        lax.psum_scatter(
            g_b_out.astype(jnp.bfloat16), "fsdp", scatter_dimension=0, tiled=True
        ).astype(jnp.float32),
        lax.psum_scatter(
            g_gain_one.astype(jnp.bfloat16), "fsdp", scatter_dimension=0, tiled=True
        ).astype(jnp.float32),
        lax.psum_scatter(
            g_shift_one.astype(jnp.bfloat16), "fsdp", scatter_dimension=0, tiled=True
        ).astype(jnp.float32),
        lax.psum_scatter(
            g_w_in.astype(jnp.bfloat16), "fsdp", scatter_dimension=0, tiled=True
        ).astype(jnp.float32),
        lax.psum_scatter(
            g_b_in.astype(jnp.bfloat16), "fsdp", scatter_dimension=0, tiled=True
        ).astype(jnp.float32),
        lax.psum_scatter(
            g_w_down.astype(jnp.bfloat16), "fsdp", scatter_dimension=0, tiled=True
        ).astype(jnp.float32),
        lax.psum_scatter(
            g_b_down.astype(jnp.bfloat16), "fsdp", scatter_dimension=0, tiled=True
        ).astype(jnp.float32),
        lax.psum_scatter(
            g_gain_two.astype(jnp.bfloat16), "fsdp", scatter_dimension=0, tiled=True
        ).astype(jnp.float32),
        lax.psum_scatter(
            g_shift_two.astype(jnp.bfloat16), "fsdp", scatter_dimension=0, tiled=True
        ).astype(jnp.float32),
    )
    totals = (
        lax.psum(shares[0].astype(jnp.bfloat16), "ctx").astype(jnp.float32),
        lax.psum(shares[1].astype(jnp.bfloat16), "ctx").astype(jnp.float32),
        lax.psum(shares[2].astype(jnp.bfloat16), "ctx").astype(jnp.float32),
        lax.psum(shares[3].astype(jnp.bfloat16), "ctx").astype(jnp.float32),
        lax.psum(shares[4].astype(jnp.bfloat16), "ctx").astype(jnp.float32),
        lax.psum(shares[5].astype(jnp.bfloat16), "ctx").astype(jnp.float32),
        lax.psum(shares[6].astype(jnp.bfloat16), "ctx").astype(jnp.float32),
        lax.psum(shares[7].astype(jnp.bfloat16), "ctx").astype(jnp.float32),
        lax.psum(shares[8].astype(jnp.bfloat16), "ctx").astype(jnp.float32),
        lax.psum(shares[9].astype(jnp.bfloat16), "ctx").astype(jnp.float32),
        lax.psum(shares[10].astype(jnp.bfloat16), "ctx").astype(jnp.float32),
        lax.psum(shares[11].astype(jnp.bfloat16), "ctx").astype(jnp.float32),
        lax.psum(shares[12].astype(jnp.bfloat16), "ctx").astype(jnp.float32),
        lax.psum(shares[13].astype(jnp.bfloat16), "ctx").astype(jnp.float32),
        lax.psum(shares[14].astype(jnp.bfloat16), "ctx").astype(jnp.float32),
    )
    return (
        layer_out,
        input_grad,
        totals[0],
        totals[1],
        totals[2],
        totals[3],
        totals[4],
        totals[5],
        totals[6],
        totals[7],
        totals[8],
        totals[9],
        totals[10],
        totals[11],
        totals[12],
        totals[13],
        totals[14],
    )


BF = jnp.bfloat16
F32 = jnp.float32
LANES = 256
VMEM = pl.BlockSpec(memory_space=pltpu.VMEM)
HBM = pl.BlockSpec(memory_space=pl.ANY)
SMEM = pl.BlockSpec(memory_space=pltpu.SMEM)
VEC = 16


def shaped(shape, dtype):
    return jax.ShapeDtypeStruct(shape, dtype)


def call(kernel, outs, ins, args, scratch=(), flops=0, name=None):
    moved = sum(a.size * a.dtype.itemsize for a in args)
    moved += sum(o.size * o.dtype.itemsize for o in outs)
    return pl.pallas_call(
        kernel,
        out_shape=outs,
        in_specs=ins,
        out_specs=[VMEM] * len(outs),
        scratch_shapes=list(scratch),
        name=name,
        cost_estimate=pl.CostEstimate(flops=flops, transcendentals=0, bytes_accessed=moved),
        compiler_params=pltpu.CompilerParams(vmem_limit_bytes=60000 * 1024),
    )(*args)


def dot(left, right):
    return jnp.dot(left, right, preferred_element_type=F32)


def dot_nt(left, right):
    return lax.dot_general(left, right, (((1,), (1,)), ((), ())), preferred_element_type=F32)


def dot_tn(left, right):
    return lax.dot_general(left, right, (((0,), (0,)), ((), ())), preferred_element_type=F32)


def turned(ring, f, s):
    return lax.rem(f - s + ring, ring)


class Plan:
    def __init__(self, chips, ring, width, hidden, per_device):
        self.chips, self.ring, self.width, self.hidden = chips, ring, width, hidden
        self.rows = per_device
        self.tokens = chips * per_device
        self.shard = width // ring
        self.half = self.shard // 2
        self.share = hidden // chips
        self.hshard = hidden // ring
        self.block = self.hshard // chips
        self.bhalf = self.block // 2
        self.heads = H // chips
        self.cols = self.heads * DH
        self.qkv = 3 * self.cols
        self.padded = self.heads * LANES
        self.clusters = chips
        self.entries = chips * CLUSTER


def prep_kernel(g, sc, wq, wk, wv, wi, wd, wo, vec, qall, qsend, iall, msend, osend, sem):
    p, k = sc[0], sc[1]
    at = pl.multiple_of(g.block * p + g.bhalf * k, 16)
    one = pltpu.make_async_copy(wd.at[pl.ds(at, g.bhalf)], msend.at[pl.ds(g.half, g.bhalf)], sem.at[0])
    one.start()
    two = pltpu.make_async_copy(
        wo.at[pl.ds(pl.multiple_of(g.half * k, 16), g.half)], osend, sem.at[1]
    )
    two.start()
    for q in range(g.chips):

        @pl.when(p == q)
        def _(q=q):
            for h in range(g.heads):
                for i, w in enumerate((wq, wk, wv)):
                    src = g.cols * q + DH * h
                    qall[:, 3 * DH * h + DH * i : 3 * DH * h + DH * (i + 1)] = w[:, src : src + DH]
            for r in range(g.ring):
                src = g.hshard * r + g.block * q
                iall[:, g.block * r : g.block * (r + 1)] = wi[:, src : src + g.block]

    mine = pl.ds(pl.multiple_of(g.half * k, 16), g.half)
    qsend[0 : g.half] = qall[mine]
    qsend[g.half : g.half + VEC, 0:LANES] = vec[...]
    qsend[g.half : g.half + VEC, LANES:] = jnp.zeros((VEC, g.qkv - LANES), BF)
    msend[0 : g.half] = iall[mine]
    one.wait()
    two.wait()


def gathers(g, sc, own, own_at, mine, theirs, at, piece, dst, sem):
    k, f = sc[1], sc[2]
    size = piece
    out = [
        pltpu.make_async_copy(
            own.at[pl.ds(own_at, 2 * size)],
            dst.at[pl.ds(pl.multiple_of(2 * size * f, 16), 2 * size)],
            sem.at[0],
        )
    ]
    for s in range(1, g.ring):
        base = 2 * size * turned(g.ring, f, s)
        for i, (src, core) in enumerate(((mine[s - 1], k), (theirs[s - 1], 1 - k))):
            out.append(
                pltpu.make_async_copy(
                    src.at[pl.ds(at, size)],
                    dst.at[pl.ds(pl.multiple_of(base + size * core, 16), size)],
                    sem.at[2 * s - 1 + i],
                )
            )
    return out


def start(copies):
    for copy in copies:
        copy.start()


def finish(copies):
    for copy in copies:
        copy.wait()


def qkv_kernel(g, sc, *refs):
    n = g.ring - 1
    xs = refs[: g.chips]
    vec, own = refs[g.chips : g.chips + 2]
    mine = refs[g.chips + 2 : g.chips + 2 + n]
    theirs = refs[g.chips + 2 + n : g.chips + 2 + 2 * n]
    out, wpad, full, w, vs, sem, vsem = refs[g.chips + 2 + 2 * n :]
    p, f = sc[0], sc[2]
    copies = gathers(g, sc, own, 0, mine, theirs, 0, g.half, w, sem)
    start(copies)
    vcopies = [
        pltpu.make_async_copy(
            mine[s].at[pl.ds(g.half, VEC), pl.ds(0, LANES)], vs.at[s], vsem.at[s]
        )
        for s in range(n)
    ]
    start(vcopies)
    finish(vcopies)
    rest = jnp.zeros((VEC, g.width - LANES), F32)
    total = jnp.zeros((VEC, g.width), F32)
    for s in range(g.ring):
        piece = (vec[...] if s == 0 else vs[s - 1]).astype(F32)
        wide = jnp.concatenate([piece, rest], axis=1)
        total = total + pltpu.roll(wide, g.shard * turned(g.ring, f, s), 1)
    full[...] = total
    back = pltpu.roll(total, lax.rem(g.width - g.cols * p, g.width), 1)
    gap = jnp.zeros((1, DH), F32)
    parts = []
    for h in range(g.heads):
        parts += [back[0:1, DH * h : DH * (h + 1)], gap, back[1:2, DH * h : DH * (h + 1)], gap]
    bias = jnp.concatenate(parts, axis=1)
    finish(copies)
    for h in range(g.heads):
        wpad[:, LANES * h : LANES * h + 3 * DH] = w[:, 3 * DH * h : 3 * DH * (h + 1)]
        wpad[:, LANES * h + 3 * DH : LANES * (h + 1)] = jnp.zeros((g.width, DH), BF)
    rows = jnp.concatenate([x[...] for x in xs], axis=0)
    out[...] = (dot(rows, wpad[...]) + bias).astype(BF)


def select(index, size, axis_size, lanes):
    if lanes:
        ids = lax.broadcasted_iota(jnp.int32, (size, axis_size), 1)
    else:
        ids = lax.broadcasted_iota(jnp.int32, (axis_size, size), 0)
    return jnp.where(ids == index, 1.0, 0.0).astype(BF)


def attend_kernel(g, own, other, posr, posc, blocks, ctx_own, ctx_other, kept, probs):
    both = 2 * g.tokens
    for h in range(g.heads):
        pick = select(posc[:, h : h + 1], g.entries, both, True)
        place = select(posr[h : h + 1, :], g.entries, both, False)
        lanes = slice(LANES * h, LANES * (h + 1))
        rows = jnp.concatenate([own[:, lanes], other[:, lanes]], axis=0)
        picked = dot(pick, rows).astype(BF)
        kept[h] = picked
        ids = dot(blocks[...], place)
        mixed = []
        for c in range(g.clusters):
            at = slice(CLUSTER * c, CLUSTER * (c + 1))
            q, key, v = picked[at, 0:DH], picked[at, DH : 2 * DH], picked[at, 2 * DH : 3 * DH]
            scores = dot_nt(q, key) * (DH ** (-0.5))
            row_ids = ids[:, at]
            col_ids = jnp.transpose(row_ids)[:, 0:1]
            allowed = row_ids[0:1, :] <= col_ids
            masked = jnp.where(allowed, scores, FLOOR)
            top = jnp.max(masked, axis=-1, keepdims=True)
            weights = jnp.where(allowed, jnp.exp(masked - top), 0.0)
            share = weights / jnp.sum(weights, axis=-1, keepdims=True)
            probs[h * g.clusters + c] = share
            mixed.append(dot(share.astype(BF), v).astype(BF))
        back = dot(place, jnp.concatenate(mixed, axis=0)).astype(BF)
        ctx_own[:, DH * h : DH * (h + 1)] = back[: g.tokens]
        ctx_other[:, DH * h : DH * (h + 1)] = back[g.tokens :]


def attend_back_kernel(g, own, other, posr, posc, kept, probs, grad_own, grad_other):
    both = 2 * g.tokens
    rows = jnp.concatenate([own[...], other[...]], axis=0)
    for h in range(g.heads):
        pick = select(posc[:, h : h + 1], g.entries, both, True)
        place = select(posr[h : h + 1, :], g.entries, both, False)
        d_mixed = dot(pick, rows[:, DH * h : DH * (h + 1)]).astype(BF)
        picked = kept[h]
        found = []
        for c in range(g.clusters):
            at = slice(CLUSTER * c, CLUSTER * (c + 1))
            q, key, v = picked[at, 0:DH], picked[at, DH : 2 * DH], picked[at, 2 * DH : 3 * DH]
            d_m = d_mixed[at]
            share = probs[h * g.clusters + c]
            d_share = dot_nt(d_m, v)
            delta = jnp.sum(share * d_share, axis=-1, keepdims=True)
            d_s = (share * (d_share - delta)).astype(BF)
            scale = DH ** (-0.5)
            d_q = dot(d_s, key) * scale
            d_k = dot_tn(d_s, q) * scale
            d_v = dot_tn(share.astype(BF), d_m)
            zero = jnp.zeros((CLUSTER, DH), F32)
            found.append(jnp.concatenate([d_q, d_k, d_v, zero], axis=1).astype(BF))
        back = dot(place, jnp.concatenate(found, axis=0)).astype(BF)
        grad_own[:, LANES * h : LANES * (h + 1)] = back[: g.tokens]
        grad_other[:, LANES * h : LANES * (h + 1)] = back[g.tokens :]


def norm_parts(values):
    centre = values - jnp.mean(values, axis=-1, keepdims=True)
    spread = jnp.mean(centre * centre, axis=-1, keepdims=True)
    scale = lax.rsqrt(spread + EPSILON)
    return centre * scale, scale


def norm_back(grad, z, scale):
    return scale * (
        grad
        - jnp.mean(grad, axis=-1, keepdims=True)
        - z * jnp.mean(grad * z, axis=-1, keepdims=True)
    )


def seen(g, ref, j):
    return jnp.concatenate(
        [ref[g.rows * (i ^ j) : g.rows * ((i ^ j) + 1)] for i in range(g.chips)], axis=0
    )


def up_kernel(g, sc, *refs):
    n, c = g.ring - 1, g.chips
    ctxs, xs, full = refs[:c], refs[c : 2 * c], refs[2 * c]
    refs = refs[2 * c + 1 :]
    wo_own, wi_own = refs[:2]
    wo_mine, wo_theirs = refs[2 : 2 + n], refs[2 + n : 2 + 2 * n]
    m_mine, m_theirs = refs[2 + 2 * n : 2 + 3 * n], refs[2 + 3 * n : 2 + 4 * n]
    inner, low, first_own, z_own, s_own, wo, wi, sem_o, sem_i = refs[2 + 4 * n :]
    p = sc[0]
    copies_o = gathers(g, sc, wo_own, 0, wo_mine, wo_theirs, 0, g.half, wo, sem_o)
    copies_i = gathers(g, sc, wi_own, 0, m_mine, m_theirs, 0, g.half, wi, sem_i)
    start(copies_o)
    start(copies_i)
    rows = jnp.concatenate([x[...] for x in xs], axis=0).astype(F32)
    total = rows + full[2:3, :]
    finish(copies_o)
    for j in range(c):
        q = jnp.bitwise_xor(p, j)
        total = total + dot(seen(g, ctxs[j], j), wo[pl.ds(pl.multiple_of(g.cols * q, 64), g.cols), :])
    z, scale = norm_parts(total)
    first = z * full[3:4, :] + full[4:5, :]
    first_own[...] = first[: g.rows]
    z_own[...] = z[: g.rows]
    s_own[...] = jnp.broadcast_to(scale[: g.rows], (g.rows, 128))
    low[...] = first.astype(BF)
    finish(copies_i)
    bias = full[pl.ds(8 + p, 1), :]
    inner[...] = dot(low[...], wi[...]) + bias


def down_kernel(g, sc, *refs):
    n, c = g.ring - 1, g.chips
    inner, first_own, full, wd_own = refs[:4]
    mine, theirs = refs[4 : 4 + n], refs[4 + n : 4 + 2 * n]
    refs = refs[4 + 2 * n :]
    parts, active = refs[:c], refs[c]
    wd, sem = refs[c + 1 :]
    p = sc[0]
    at = pl.multiple_of(g.block * p, 16)
    copies = gathers(g, sc, wd_own, at, mine, theirs, g.half, g.bhalf, wd, sem)
    start(copies)
    u = inner[...]
    active[...] = (u * (1.0 + lax.erf(u * (0.5**0.5))) * 0.5).astype(BF)
    finish(copies)
    second = dot(active[...], wd[...])
    parts[0][...] = second[: g.rows] + first_own[...] + full[5:6, :]
    for j in range(1, c):
        parts[j][...] = second[g.rows * j : g.rows * (j + 1)].astype(BF)


def turn_kernel(g, *refs):
    c = g.chips
    parts, full, cotangent = refs[:c], refs[c], refs[c + 1]
    out, d_second, branch = refs[c + 2 :]
    second = parts[0][...]
    for j in range(1, c):
        second = second + parts[j][...].astype(F32)
    z, scale = norm_parts(second)
    gain = full[6:7, :]
    out[...] = (z * gain + full[7:8, :]).astype(BF)
    dy = cotangent[...].astype(F32)
    grad = norm_back(dy * gain, z, scale)
    d_second[...] = grad
    branch[0 : g.rows] = grad.astype(BF)
    one = jnp.sum(dy * z, axis=0, keepdims=True)
    two = jnp.sum(dy, axis=0, keepdims=True)
    rest = jnp.zeros((VEC - 2, g.width), F32)
    branch[g.rows : g.rows + VEC] = jnp.concatenate([one, two, rest], axis=0).astype(BF)


def back_kernel(g, sc, *refs):
    n, c = g.ring - 1, g.chips
    branches, slope, wd_own, wi_own = refs[:c], refs[c], refs[c + 1], refs[c + 2]
    mine, theirs = refs[c + 3 : c + 3 + n], refs[c + 3 + n : c + 3 + 2 * n]
    refs = refs[c + 3 + 2 * n :]
    parts, d_inner, wd, wi, sem_d, sem_i = refs[:c], *refs[c:]
    p = sc[0]
    at = pl.multiple_of(g.block * p, 16)
    copies_d = gathers(g, sc, wd_own, at, mine, theirs, g.half, g.bhalf, wd, sem_d)
    copies_i = gathers(g, sc, wi_own, 0, mine, theirs, 0, g.half, wi, sem_i)
    start(copies_d)
    start(copies_i)
    rows = jnp.concatenate([b[0 : g.rows] for b in branches], axis=0)
    finish(copies_d)
    d_active = dot_nt(rows, wd[...])
    d_inner[...] = (d_active * slope[...]).astype(BF)
    finish(copies_i)
    total = dot_nt(d_inner[...], wi[...])
    parts[0][...] = total[: g.rows]
    for j in range(1, c):
        parts[j][...] = total[g.rows * j : g.rows * (j + 1)].astype(BF)


def split_rows(g, sc, total, size, own, other, at):
    k, f = sc[1], sc[2]
    for s in range(g.ring):
        base = 2 * size * lax.rem(f + s, g.ring)
        own[s, at : at + size] = total[pl.ds(pl.multiple_of(base + size * k, 8), size), :]
        other[s, at : at + size] = total[
            pl.ds(pl.multiple_of(base + size * (1 - k), 8), size), :
        ].astype(BF)


def mlp_grads_kernel(g, sc, *refs):
    c = g.chips
    branches, active, low, d_inner = refs[:c], refs[c], refs[c + 1], refs[c + 2]
    own, other, sums, total = refs[c + 3 :]
    rows = jnp.concatenate([b[0 : g.rows] for b in branches], axis=0)
    total[...] = dot_tn(active[...], rows)
    split_rows(g, sc, total, g.bhalf, own, other, g.half)
    total[...] = dot_tn(low[...], d_inner[...])
    split_rows(g, sc, total, g.half, own, other, 0)
    stats = branches[0][g.rows : g.rows + VEC].astype(F32)
    for j in range(1, c):
        stats = stats + branches[j][g.rows : g.rows + VEC].astype(F32)
    down = jnp.sum(rows.astype(F32), axis=0, keepdims=True)
    up = jnp.sum(d_inner[...].astype(F32), axis=0, keepdims=True)
    sums[...] = jnp.concatenate([stats[0:2], down, up, jnp.zeros((4, g.width), F32)], axis=0)


def first_kernel(g, *refs):
    c = g.chips
    parts, d_second, z_own, s_own, full = refs[:c], *refs[c : c + 4]
    d_sum, attended = refs[c + 4 :]
    d_first = d_second[...] + parts[0][...]
    for j in range(1, c):
        d_first = d_first + parts[j][...].astype(F32)
    z = z_own[...]
    grad = norm_back(d_first * full[3:4, :], z, s_own[:, 0:1])
    d_sum[...] = grad
    attended[0 : g.rows] = grad.astype(BF)
    one = jnp.sum(d_first * z, axis=0, keepdims=True)
    two = jnp.sum(d_first, axis=0, keepdims=True)
    rest = jnp.zeros((VEC - 2, g.width), F32)
    attended[g.rows : g.rows + VEC] = jnp.concatenate([one, two, rest], axis=0).astype(BF)


def context_kernel(g, sc, *refs):
    n, c = g.ring - 1, g.chips
    grads, own = refs[:c], refs[c]
    mine, theirs = refs[c + 1 : c + 1 + n], refs[c + 1 + n : c + 1 + 2 * n]
    out, wo, sem = refs[c + 1 + 2 * n :]
    p = sc[0]
    copies = gathers(g, sc, own, 0, mine, theirs, 0, g.half, wo, sem)
    start(copies)
    rows = jnp.concatenate([b[0 : g.rows] for b in grads], axis=0)
    finish(copies)
    out[...] = dot_nt(rows, wo[pl.ds(pl.multiple_of(g.cols * p, 64), g.cols), :]).astype(BF)


def out_grads_kernel(g, sc, *refs):
    c = g.chips
    grads, ctxs, sums = refs[:c], refs[c : 2 * c], refs[2 * c]
    own, other, total = refs[2 * c + 1 :]
    p, k, f = sc[0], sc[1], sc[2]
    rows = jnp.concatenate([b[0 : g.rows] for b in grads], axis=0)
    for j in range(c):
        q = jnp.bitwise_xor(p, j)
        total[pl.ds(pl.multiple_of(g.cols * q, 64), g.cols), :] = dot_tn(seen(g, ctxs[j], j), rows)
    size = g.half // c
    for s in range(g.ring):
        base = g.shard * lax.rem(f + s, g.ring) + 2 * size * p
        own[s, 0:size] = total[pl.ds(pl.multiple_of(base + size * k, 8), size), :]
        other[s, 0:size] = total[
            pl.ds(pl.multiple_of(base + size * (1 - k), 8), size), :
        ].astype(BF)
    stats = grads[0][g.rows : g.rows + VEC].astype(F32)
    for j in range(1, c):
        stats = stats + grads[j][g.rows : g.rows + VEC].astype(F32)
    out = jnp.sum(rows.astype(F32), axis=0, keepdims=True)
    rest = jnp.zeros((VEC - 7, g.width), F32)
    block = jnp.concatenate([sums[0:4], stats[0:2], out, rest], axis=0)
    spare = own.shape[1] - size - VEC
    if spare:
        block = jnp.concatenate([block, jnp.zeros((spare, g.width), F32)], axis=0)
    for s in range(g.ring):
        own[s, size:] = block
        other[s, size:] = block.astype(BF)


def input_kernel(g, *refs):
    c = g.chips
    own, other, wpad = refs[:3]
    parts, d_qkv = refs[3 : 3 + c], refs[3 + c]
    d_qkv[...] = (own[...].astype(F32) + other[...].astype(F32)).astype(BF)
    total = dot_nt(d_qkv[...], wpad[...])
    parts[0][...] = total[: g.rows]
    for j in range(1, c):
        parts[j][...] = total[g.rows * j : g.rows * (j + 1)].astype(BF)


def qkv_grads_kernel(g, sc, *refs):
    c = g.chips
    xs, d_qkv = refs[:c], refs[c]
    own, other, wide, total = refs[c + 1 :]
    rows = jnp.concatenate([x[...] for x in xs], axis=0)
    wide[...] = dot_tn(rows, d_qkv[...])
    sums = jnp.sum(d_qkv[...].astype(F32), axis=0, keepdims=True)
    for h in range(g.heads):
        total[:, 3 * DH * h : 3 * DH * (h + 1)] = wide[:, LANES * h : LANES * h + 3 * DH]
    split_rows(g, sc, total, g.half, own, other, 0)
    row = jnp.concatenate(
        [sums[:, LANES * h : LANES * h + 3 * DH] for h in range(g.heads)], axis=1
    )
    block = jnp.concatenate([row, jnp.zeros((VEC - 1, g.qkv), F32)], axis=0)
    for s in range(g.ring):
        own[s, g.half :] = block
        other[s, g.half :] = block.astype(BF)


def sources(g, sc, refs):
    p, k = sc[0], sc[1]
    out = []
    for j in range(g.chips):
        q = jnp.bitwise_xor(p, j)
        out.append((q, k, refs[j]))
        out.append((q, 1 - k, refs[g.chips + j]))
    return out


def mlp_final_kernel(g, sc, *refs):
    found, (g_in, g_down) = refs[: 2 * g.chips], refs[2 * g.chips :]
    for q, core, ref in sources(g, sc, found):
        at = pl.multiple_of(g.block * q + g.bhalf * core, 8)
        g_down[pl.ds(at, g.bhalf), :] = ref[g.half :, :].astype(F32)
        mine = pl.ds(pl.multiple_of(g.half * core, 8), g.half)
        for chip in range(g.chips):

            @pl.when(q == chip)
            def _(chip=chip, ref=ref, mine=mine):
                for r in range(g.ring):
                    lane = g.hshard * r + g.block * chip
                    g_in[mine, lane : lane + g.block] = ref[
                        0 : g.half, g.block * r : g.block * (r + 1)
                    ].astype(F32)


def out_final_kernel(g, sc, *refs):
    found, (g_out, vec, wide) = refs[: 2 * g.chips], refs[2 * g.chips :]
    f = sc[2]
    size = g.half // g.chips
    for q, core, ref in sources(g, sc, found):
        at = pl.multiple_of(2 * size * q + size * core, 8)
        g_out[pl.ds(at, size), :] = ref[0:size, :].astype(F32)

        @pl.when(core == 0)
        def _(q=q, ref=ref):
            for chip in range(g.chips):

                @pl.when(q == chip)
                def _(chip=chip):
                    block = ref[size : size + VEC, :].astype(F32)
                    back = pltpu.roll(block, lax.rem(g.width - g.shard * f, g.width), 1)
                    if chip == 0:
                        wide[:, :] = back[:, : g.shard]
                    vec[3 + chip : 4 + chip, :] = back[3:4, : g.shard]

    vec[0:3, :] = wide[0:3, :]
    vec[3 + g.chips : 6 + g.chips, :] = wide[4:7, :]


def qkv_final_kernel(g, sc, *refs):
    found, (gq, gk, gv, vec) = refs[: 2 * g.chips], refs[2 * g.chips :]
    f = sc[2]
    for q, core, ref in sources(g, sc, found):
        mine = pl.ds(pl.multiple_of(g.half * core, 8), g.half)

        @pl.when((q == f) & (core == 0))
        def _(ref=ref):
            row = ref[g.half : g.half + VEC, :].astype(F32)[0:1]
            for i, at in ((0, 0), (1, 2)):
                vec[i : i + 1, :] = jnp.concatenate(
                    [
                        row[:, 3 * DH * h + DH * at : 3 * DH * h + DH * (at + 1)]
                        for h in range(g.heads)
                    ],
                    axis=1,
                )

        for chip in range(g.chips):

            @pl.when(q == chip)
            def _(chip=chip, ref=ref, mine=mine):
                for i, dst in enumerate((gq, gk, gv)):
                    for h in range(g.heads):
                        lane, src = g.cols * chip + DH * h, 3 * DH * h + DH * i
                        dst[mine, lane : lane + DH] = ref[0 : g.half, src : src + DH].astype(F32)


def to_core(x):
    n = lax.axis_size("ctx")
    return lax.ppermute(x, "ctx", [(i, i ^ 1) for i in range(n)])


def to_chip(x, j):
    n = lax.axis_size("ctx")
    return lax.ppermute(x, "ctx", [(i, i ^ (2 * j)) for i in range(n)])


def along(x, s):
    n = lax.axis_size("fsdp")
    return lax.ppermute(x, "fsdp", [(i, (i + s) % n) for i in range(n)])


def spread(x, chips):
    far = {j: to_chip(x, j) for j in sorted(range(1, chips), key=lambda j: -bin(j).count("1"))}
    return [x] + [far[j] for j in range(1, chips)]


def swap(parts):
    far = {j: to_chip(parts[j], j) for j in sorted(range(1, len(parts)), key=lambda j: -bin(j).count("1"))}
    return [parts[0]] + [far[j] for j in range(1, len(parts))]


def ring_sum(own, other, ring):
    got = to_core(other)
    mine = [own[s] + got[s].astype(F32) for s in range(ring)]
    far = [along(mine[s].astype(BF), s) for s in range(1, ring)]
    total = mine[0]
    for part in far:
        total = total + part.astype(F32)
    return total.astype(BF)


def plane_pieces(piece, chips):
    near = spread(piece, chips)
    return near + [to_core(part) for part in near]


def chip_body(
    hidden_in,
    out_grad,
    block_ids,
    clusters,
    w_query,
    w_key,
    w_value,
    w_out,
    b_query,
    b_value,
    b_out,
    ln1_gain,
    ln1_bias,
    w_in,
    b_in,
    w_down,
    b_down,
    ln2_gain,
    ln2_bias,
):
    n, ring = lax.axis_size("ctx"), lax.axis_size("fsdp")
    chips = n // 2
    rows, width = hidden_in.shape[1:]
    hidden = w_in.shape[1]
    g = Plan(chips, ring, width, hidden, rows)
    c, f = lax.axis_index("ctx"), lax.axis_index("fsdp")
    p, k = c // 2, c % 2
    sc = jnp.stack([p, k, f]).astype(jnp.int32)
    bind = functools.partial

    x_own = hidden_in.reshape(rows, width)
    xs = spread(x_own, chips)

    small = jnp.concatenate(
        [
            v.reshape(-1, g.shard)
            for v in (b_query, b_value, b_out, ln1_gain, ln1_bias, b_down, ln2_gain, ln2_bias)
        ]
        + [b_in.reshape(chips, g.block)],
        axis=0,
    )
    vec = jnp.pad(small, ((0, VEC - small.shape[0]), (0, LANES - g.shard)))
    qall, qsend, iall, msend, osend = call(
        bind(prep_kernel, g),
        [
            shaped((g.shard, g.qkv), BF),
            shaped((g.half + VEC, g.qkv), BF),
            shaped((g.shard, g.share), BF),
            shaped((g.half + g.bhalf, width), BF),
            shaped((g.half, width), BF),
        ],
        [SMEM] + [VMEM] * 4 + [HBM] * 2 + [VMEM],
        [sc, w_query, w_key, w_value, w_in, w_down, w_out, vec],
        [pltpu.SemaphoreType.DMA((2,))],
        name="pick_weights",
    )
    q_mine = [along(qsend, s) for s in range(1, ring)]
    q_theirs = [to_core(part) for part in q_mine]
    o_mine = [along(osend, s) for s in range(1, ring)]
    o_theirs = [to_core(part) for part in o_mine]
    m_mine = [along(msend, s) for s in range(1, ring)]
    m_theirs = [to_core(part) for part in m_mine]

    order = lax.dynamic_slice(
        clusters[0], (g.heads * p, g.entries * k), (g.heads, g.entries)
    )
    chip, core, within = order // (2 * rows), (order // rows) % 2, order % rows
    pos = (core ^ k) * g.tokens + (chip ^ p) * rows + within
    posr = jnp.pad(pos, ((0, 8 - g.heads), (0, 0)))
    posc = posr.T
    half_rows = rows // 2
    devices = 2 * (p ^ jnp.arange(chips)[None, :]) + (k ^ jnp.arange(2)[:, None])
    pieces = jnp.stack([devices, 2 * n - 1 - devices], axis=-1).reshape(-1)
    hot = (pieces[:, None] == jnp.arange(2 * n)[None, :]).astype(BF)
    blk = dot(hot, block_ids[0].reshape(2 * n, half_rows).astype(BF)).astype(BF)
    blk = jnp.broadcast_to(blk.reshape(1, 2 * g.tokens), (8, 2 * g.tokens))

    gate = pltpu.SemaphoreType.DMA((2 * ring - 1,))
    qkv, wpad, full = call(
        bind(qkv_kernel, g),
        [
            shaped((g.tokens, g.padded), BF),
            shaped((width, g.padded), BF),
            shaped((VEC, width), F32),
        ],
        [SMEM] + [VMEM] * (chips + 1) + [HBM] * (2 * ring - 1),
        [sc, *xs, vec, qall, *q_mine, *q_theirs],
        [
            pltpu.VMEM((width, g.qkv), BF),
            pltpu.VMEM((ring - 1, VEC, LANES), BF),
            gate,
            pltpu.SemaphoreType.DMA((ring - 1,)),
        ],
        flops=2 * g.tokens * width * g.padded,
        name="project",
    )
    qkv_other = to_core(qkv)
    ctx_own, ctx_other, kept, probs = call(
        bind(attend_kernel, g),
        [
            shaped((g.tokens, g.cols), BF),
            shaped((g.tokens, g.cols), BF),
            shaped((g.heads, g.entries, LANES), BF),
            shaped((g.heads * g.clusters, CLUSTER, CLUSTER), F32),
        ],
        [VMEM] * 5,
        [qkv, qkv_other, posr, posc, blk],
        flops=8 * g.entries * g.tokens * LANES * g.heads,
        name="attend",
    )
    ctx = ctx_own + to_core(ctx_other)
    ctxs = spread(ctx, chips)

    inner, low, first_own, z_own, s_own = call(
        bind(up_kernel, g),
        [
            shaped((g.tokens, g.share), F32),
            shaped((g.tokens, width), BF),
            shaped((rows, width), F32),
            shaped((rows, width), F32),
            shaped((rows, 128), F32),
        ],
        [SMEM] + [VMEM] * (2 * chips + 1) + [HBM] * (4 * ring - 2),
        [sc, *ctxs, *xs, full, w_out, iall, *o_mine, *o_theirs, *m_mine, *m_theirs],
        [pltpu.VMEM((width, width), BF), pltpu.VMEM((width, g.share), BF), gate, gate],
        flops=4 * g.tokens * width * g.share,
        name="mlp_up",
    )
    *second, active = call(
        bind(down_kernel, g),
        [shaped((rows, width), F32)]
        + [shaped((rows, width), BF)] * (chips - 1)
        + [shaped((g.tokens, g.share), BF)],
        [SMEM] + [VMEM] * 3 + [HBM] * (2 * ring - 1),
        [sc, inner, first_own, full, w_down, *m_mine, *m_theirs],
        [pltpu.VMEM((g.share, width), BF), gate],
        flops=2 * g.tokens * width * g.share,
        name="mlp_down",
    )
    slope = 0.5 * (1.0 + lax.erf(inner * (0.5**0.5))) + inner * jnp.exp(
        -0.5 * inner * inner
    ) * (1.0 / (2.0 * jnp.pi) ** 0.5)
    second = swap(second)
    layer_out, d_second, branch = call(
        bind(turn_kernel, g),
        [
            shaped((rows, width), BF),
            shaped((rows, width), F32),
            shaped((rows + VEC, width), BF),
        ],
        [VMEM] * (chips + 2),
        [*second, full, out_grad.reshape(rows, width)],
        name="norm_two",
    )
    branches = spread(branch, chips)
    *d_first, d_inner = call(
        bind(back_kernel, g),
        [shaped((rows, width), F32)]
        + [shaped((rows, width), BF)] * (chips - 1)
        + [shaped((g.tokens, g.share), BF)],
        [SMEM] + [VMEM] * (chips + 1) + [HBM] * (2 * ring),
        [sc, *branches, slope, w_down, iall, *m_mine, *m_theirs],
        [pltpu.VMEM((g.share, width), BF), pltpu.VMEM((width, g.share), BF), gate, gate],
        flops=4 * g.tokens * width * g.share,
        name="mlp_back",
    )
    d_first = swap(d_first)
    m_own, m_other, sums = call(
        bind(mlp_grads_kernel, g),
        [
            shaped((ring, g.half + g.bhalf, width), F32),
            shaped((ring, g.half + g.bhalf, width), BF),
            shaped((8, width), F32),
        ],
        [SMEM] + [VMEM] * (chips + 3),
        [sc, *branches, active, low, d_inner],
        [pltpu.VMEM((width, g.share), F32)],
        flops=4 * g.tokens * width * g.share,
        name="mlp_grads",
    )
    m_piece = ring_sum(m_own, m_other, ring)
    d_sum, attended = call(
        bind(first_kernel, g),
        [shaped((rows, width), F32), shaped((rows + VEC, width), BF)],
        [VMEM] * (chips + 4),
        [*d_first, d_second, z_own, s_own, full],
        name="norm_one",
    )
    grads = spread(attended, chips)
    (d_ctx,) = call(
        bind(context_kernel, g),
        [shaped((g.tokens, g.cols), BF)],
        [SMEM] + [VMEM] * chips + [HBM] * (2 * ring - 1),
        [sc, *grads, w_out, *o_mine, *o_theirs],
        [pltpu.VMEM((width, width), BF), gate],
        flops=2 * g.tokens * width * g.cols,
        name="context_back",
    )
    d_ctx_other = to_core(d_ctx)
    size = g.half // chips
    o_rows = -(-(size + VEC) // 16) * 16
    o_own, o_other = call(
        bind(out_grads_kernel, g),
        [shaped((ring, o_rows, width), F32), shaped((ring, o_rows, width), BF)],
        [SMEM] + [VMEM] * (2 * chips + 1),
        [sc, *grads, *ctxs, sums],
        [pltpu.VMEM((width, width), F32)],
        flops=2 * g.tokens * width * width,
        name="out_grads",
    )
    o_piece = ring_sum(o_own, o_other, ring)
    dq_own, dq_other = call(
        bind(attend_back_kernel, g),
        [shaped((g.tokens, g.padded), BF)] * 2,
        [VMEM] * 6,
        [d_ctx, d_ctx_other, posr, posc, kept, probs],
        flops=8 * g.entries * g.tokens * LANES * g.heads,
        name="attend_back",
    )
    *d_in, d_qkv = call(
        bind(input_kernel, g),
        [shaped((rows, width), F32)]
        + [shaped((rows, width), BF)] * (chips - 1)
        + [shaped((g.tokens, g.padded), BF)],
        [VMEM] * 3,
        [dq_own, to_core(dq_other), wpad],
        flops=2 * g.tokens * width * g.padded,
        name="project_back",
    )
    q_own, q_other = call(
        bind(qkv_grads_kernel, g),
        [shaped((ring, g.half + VEC, g.qkv), F32), shaped((ring, g.half + VEC, g.qkv), BF)],
        [SMEM] + [VMEM] * (chips + 1),
        [sc, *xs, d_qkv],
        [pltpu.VMEM((width, g.padded), F32), pltpu.VMEM((width, g.qkv), F32)],
        flops=2 * g.tokens * width * g.padded,
        name="project_grads",
    )
    d_in = swap(d_in)
    q_piece = ring_sum(q_own, q_other, ring)
    total = d_sum
    for part in d_in:
        total = total + part.astype(F32)
    input_grad = total.astype(BF)

    g_in, g_down = call(
        bind(mlp_final_kernel, g),
        [shaped((g.shard, hidden), F32), shaped((g.hshard, width), F32)],
        [SMEM] + [VMEM] * (2 * chips),
        [sc, *plane_pieces(m_piece, chips)],
        name="mlp_lay",
    )
    g_out, vec_two = call(
        bind(out_final_kernel, g),
        [shaped((g.shard, width), F32), shaped((VEC, g.shard), F32)],
        [SMEM] + [VMEM] * (2 * chips),
        [sc, *plane_pieces(o_piece, chips)],
        [pltpu.VMEM((VEC, g.shard), F32)],
        name="out_lay",
    )
    gq, gk, gv, vec_one = call(
        bind(qkv_final_kernel, g),
        [shaped((g.shard, width), F32)] * 3 + [shaped((8, g.shard), F32)],
        [SMEM] + [VMEM] * (2 * chips),
        [sc, *plane_pieces(q_piece, chips)],
        name="project_lay",
    )
    last = 3 + chips
    return (
        layer_out.reshape(1, rows, width),
        input_grad.reshape(1, rows, width),
        gq,
        gk,
        gv,
        g_out,
        vec_one[0],
        vec_one[1],
        vec_two[last + 2],
        vec_two[last],
        vec_two[last + 1],
        g_in,
        vec_two[3:last].reshape(-1),
        g_down,
        vec_two[2],
        vec_two[0],
        vec_two[1],
    )


def fits(mesh):
    n, ring = mesh.shape["ctx"], mesh.shape["fsdp"]
    chips = n // 2
    return n % 2 == 0 and chips & (chips - 1) == 0 and H % chips == 0 and ring * chips <= 16


def solution(mesh):
    in_specs = (
        P("fsdp", "ctx", None),
        P("fsdp", "ctx", None),
        P("fsdp", None),
        P("fsdp", None, None),
        P("fsdp", None),
        P("fsdp", None),
        P("fsdp", None),
        P("fsdp", None),
        P("fsdp"),
        P("fsdp"),
        P("fsdp"),
        P("fsdp"),
        P("fsdp"),
        P("fsdp", None),
        P("fsdp"),
        P("fsdp", None),
        P("fsdp"),
        P("fsdp"),
        P("fsdp"),
    )
    out_specs = (
        P("fsdp", "ctx", None),
        P("fsdp", "ctx", None),
        P("fsdp", None),
        P("fsdp", None),
        P("fsdp", None),
        P("fsdp", None),
        P("fsdp"),
        P("fsdp"),
        P("fsdp"),
        P("fsdp"),
        P("fsdp"),
        P("fsdp", None),
        P("fsdp"),
        P("fsdp", None),
        P("fsdp"),
        P("fsdp"),
        P("fsdp"),
    )
    body = chip_body if fits(mesh) else general_body
    return jax.shard_map(body, mesh=mesh, in_specs=in_specs, out_specs=out_specs, check_vma=False)
```

```python
import functools
import math

import jax
import jax.numpy as jnp
from jax import lax
from jax.experimental import pallas as pl
from jax.experimental.pallas import tpu as pltpu
from jax.sharding import PartitionSpec as P

H = 12
DH = 64
CLUSTER = 128


EPSILON = 1e-12
FLOOR = -1e30


def layer_norm(values, gain, shift):
    centre = values - jnp.mean(values, axis=-1, keepdims=True)
    spread = jnp.mean(centre * centre, axis=-1, keepdims=True)
    return centre * lax.rsqrt(spread + EPSILON) * gain + shift


def exact_gelu(values):
    return jax.nn.gelu(values, approximate=False)


def positions(length, per_device, parts):
    stored = jnp.arange(length, dtype=jnp.int32)
    device = stored // per_device
    within = stored % per_device
    half = per_device // 2
    return jnp.where(
        within < half, device * half + within, (2 * parts - 1 - device) * half + within - half
    )


def contract(left, right):
    return lax.dot_general(
        left, right, (((0,), (0,)), ((), ())), preferred_element_type=jnp.float32
    )


def back_product(grad, weight):
    return lax.dot_general(
        grad, weight, (((1,), (1,)), ((), ())), preferred_element_type=jnp.float32
    )


def column_sum(values):
    return jnp.sum(values.astype(jnp.float32), axis=0)


def per_head_rows(rows, index):
    split = rows.reshape(rows.shape[0], H, DH)
    return jnp.take_along_axis(split, index.T[:, :, None], axis=0)


def cluster_tables(order, device, per_device, parts):
    heads, length = order.shape
    groups = length // CLUSTER
    members = CLUSTER // parts
    mine = (order // per_device == device).astype(jnp.int32)
    rank = jnp.cumsum(mine.reshape(heads, groups, CLUSTER), axis=-1).reshape(heads, length) - 1
    entry = jnp.arange(length, dtype=jnp.int32)[None, :]
    slot = jnp.where(mine == 1, entry // CLUSTER * members + rank, per_device)
    head_index = jnp.arange(heads, dtype=jnp.int32)[:, None]
    picked = (
        jnp.zeros((heads, per_device), jnp.int32)
        .at[head_index, slot]
        .set(order - device * per_device, mode="drop")
    )
    counter = jnp.broadcast_to(
        jnp.arange(per_device, dtype=jnp.int32)[None, :], (heads, per_device)
    )
    placed = jnp.zeros((heads, per_device), jnp.int32).at[head_index, picked].set(counter)
    inverse = (
        jnp.zeros((heads, length), jnp.int32)
        .at[head_index, order]
        .set(jnp.broadcast_to(jnp.arange(length, dtype=jnp.int32)[None, :], (heads, length)))
    )
    return (picked, placed, inverse)


def score_blocks(query, key_rows, query_blocks, key_blocks, scale):
    scores = (
        jnp.einsum("cqhd,ckhd->hcqk", query, key_rows, preferred_element_type=jnp.float32) * scale
    )
    allowed = key_blocks[:, :, None, :] <= query_blocks[:, :, :, None]
    return (scores, allowed)


def attend(query, key_rows, value_rows, query_blocks, key_blocks, scale):
    scores, allowed = score_blocks(query, key_rows, query_blocks, key_blocks, scale)
    masked = jnp.where(allowed, scores, FLOOR)
    top = jnp.max(masked, axis=-1, keepdims=True)
    weights = jnp.where(allowed, jnp.exp(masked - top), 0.0)
    total = jnp.sum(weights, axis=-1, keepdims=True)
    probs = (weights / total).astype(jnp.bfloat16)
    mixed = jnp.einsum("hcqk,ckhd->cqhd", probs, value_rows, preferred_element_type=jnp.float32)
    return (mixed.astype(jnp.bfloat16), top + jnp.log(total))


def attend_back(query, key_rows, value_rows, query_blocks, key_blocks, logsum, d_mixed, scale):
    scores, allowed = score_blocks(query, key_rows, query_blocks, key_blocks, scale)
    probs = jnp.where(allowed, jnp.exp(jnp.where(allowed, scores, FLOOR) - logsum), 0.0)
    rounded = probs.astype(jnp.bfloat16)
    d_probs = jnp.einsum("cqhd,ckhd->hcqk", d_mixed, value_rows, preferred_element_type=jnp.float32)
    centred = jnp.sum(probs * d_probs, axis=-1, keepdims=True)
    d_scores = (probs * (d_probs - centred)).astype(jnp.bfloat16)
    d_query = (
        jnp.einsum("hcqk,ckhd->cqhd", d_scores, key_rows, preferred_element_type=jnp.float32)
        * scale
    )
    d_key = (
        jnp.einsum("hcqk,cqhd->ckhd", d_scores, query, preferred_element_type=jnp.float32) * scale
    )
    d_value = jnp.einsum("hcqk,cqhd->ckhd", rounded, d_mixed, preferred_element_type=jnp.float32)
    return (d_query, d_key, d_value)


def general_body(
    hidden_in,
    out_grad,
    block_ids,
    clusters,
    w_query,
    w_key,
    w_value,
    w_out,
    b_query,
    b_value,
    b_out,
    ln1_gain,
    ln1_bias,
    w_in,
    b_in,
    w_down,
    b_down,
    ln2_gain,
    ln2_bias,
):
    parts = lax.axis_size("ctx")
    device = lax.axis_index("ctx")
    sequences, per_device, width = hidden_in.shape
    length = per_device * parts
    members = CLUSTER // parts
    groups = length // CLUSTER
    scale = DH ** (-0.5)
    (
        full_query,
        full_key,
        full_value,
        full_out,
        bias_query,
        bias_value,
        bias_out,
        gain_one,
        shift_one,
    ) = (
        lax.all_gather(w_query, "fsdp", axis=0, tiled=True),
        lax.all_gather(w_key, "fsdp", axis=0, tiled=True),
        lax.all_gather(w_value, "fsdp", axis=0, tiled=True),
        lax.all_gather(w_out, "fsdp", axis=0, tiled=True),
        lax.all_gather(b_query, "fsdp", axis=0, tiled=True),
        lax.all_gather(b_value, "fsdp", axis=0, tiled=True),
        lax.all_gather(b_out, "fsdp", axis=0, tiled=True),
        lax.all_gather(ln1_gain, "fsdp", axis=0, tiled=True),
        lax.all_gather(ln1_bias, "fsdp", axis=0, tiled=True),
    )
    full_in, full_down, bias_in, bias_down, gain_two, shift_two = (
        lax.all_gather(w_in, "fsdp", axis=0, tiled=True),
        lax.all_gather(w_down, "fsdp", axis=0, tiled=True),
        lax.all_gather(b_in, "fsdp", axis=0, tiled=True),
        lax.all_gather(b_down, "fsdp", axis=0, tiled=True),
        lax.all_gather(ln2_gain, "fsdp", axis=0, tiled=True),
        lax.all_gather(ln2_bias, "fsdp", axis=0, tiled=True),
    )
    hidden = hidden_in.reshape(sequences * per_device, width)
    query_rows = (
        jnp.dot(hidden, full_query, preferred_element_type=jnp.float32) + bias_query
    ).astype(jnp.bfloat16)
    key_rows = jnp.dot(hidden, full_key, preferred_element_type=jnp.float32).astype(jnp.bfloat16)
    value_rows = (
        jnp.dot(hidden, full_value, preferred_element_type=jnp.float32) + bias_value
    ).astype(jnp.bfloat16)
    place = positions(length, per_device, parts)
    index = 0
    order = clusters[index]
    stored_blocks = block_ids[index][place]
    picked, placed, inverse = cluster_tables(order, device, per_device, parts)
    q_local = per_head_rows(query_rows, picked).reshape(groups, members, H, DH)
    query_blocks = stored_blocks[device * per_device + picked].reshape(H, groups, members)
    key_all = lax.all_gather(key_rows, "ctx", axis=0, tiled=True)
    value_all = lax.all_gather(value_rows, "ctx", axis=0, tiled=True)
    key_cluster = per_head_rows(key_all, order).reshape(groups, CLUSTER, H, DH)
    value_cluster = per_head_rows(value_all, order).reshape(groups, CLUSTER, H, DH)
    key_blocks = stored_blocks[order].reshape(H, groups, CLUSTER)
    mixed, logsum = attend(q_local, key_cluster, value_cluster, query_blocks, key_blocks, scale)
    contexts = per_head_rows(mixed.reshape(per_device, width), placed).reshape(per_device, width)
    kept = [
        (
            q_local,
            key_cluster,
            value_cluster,
            query_blocks,
            key_blocks,
            logsum,
            picked,
            placed,
            inverse,
        )
    ]
    attended = jnp.dot(contexts, full_out, preferred_element_type=jnp.float32) + bias_out
    first_sum = hidden.astype(jnp.float32) + attended
    first, first_pull = jax.vjp(
        layer_norm, first_sum, gain_one.astype(jnp.float32), shift_one.astype(jnp.float32)
    )
    first_low = first.astype(jnp.bfloat16)
    inner = jnp.dot(first_low, full_in, preferred_element_type=jnp.float32) + bias_in
    active_full, gelu_pull = jax.vjp(exact_gelu, inner)
    active = active_full.astype(jnp.bfloat16)
    second_sum = first + jnp.dot(active, full_down, preferred_element_type=jnp.float32) + bias_down
    second, second_pull = jax.vjp(
        layer_norm, second_sum, gain_two.astype(jnp.float32), shift_two.astype(jnp.float32)
    )
    layer_out = second.astype(jnp.bfloat16).reshape(sequences, per_device, width)
    d_out = out_grad.reshape(sequences * per_device, width).astype(jnp.float32)
    d_second, g_gain_two, g_shift_two = second_pull(d_out)
    d_branch = d_second.astype(jnp.bfloat16)
    g_w_down = contract(active, d_branch)
    g_b_down = column_sum(d_branch)
    d_active = back_product(d_branch, full_down)
    d_inner = gelu_pull(d_active)[0].astype(jnp.bfloat16)
    g_w_in = contract(first_low, d_inner)
    g_b_in = column_sum(d_inner)
    d_first = d_second + back_product(d_inner, full_in)
    d_sum, g_gain_one, g_shift_one = first_pull(d_first)
    d_attended = d_sum.astype(jnp.bfloat16)
    g_w_out = contract(contexts, d_attended)
    g_b_out = column_sum(d_attended)
    d_context = back_product(d_attended, full_out).astype(jnp.bfloat16)
    index = 0
    q_kept, k_kept, v_kept, blocks_q, blocks_k, logsum, picked, placed, inverse = kept[index]
    d_cluster = per_head_rows(d_context, picked).reshape(groups, members, H, DH)
    d_query, d_key, d_value = attend_back(
        q_kept, k_kept, v_kept, blocks_q, blocks_k, logsum, d_cluster, scale
    )
    key_full = per_head_rows(d_key.reshape(length, width), inverse).reshape(length, width)
    value_full = per_head_rows(d_value.reshape(length, width), inverse).reshape(length, width)
    key_part = lax.psum_scatter(
        key_full.astype(jnp.bfloat16), "ctx", scatter_dimension=0, tiled=True
    )
    value_part = lax.psum_scatter(
        value_full.astype(jnp.bfloat16), "ctx", scatter_dimension=0, tiled=True
    )
    query_local = d_query.astype(jnp.bfloat16).reshape(per_device, width)
    query_grads = per_head_rows(query_local, placed).reshape(per_device, width)
    g_w_query = contract(hidden, query_grads)
    g_b_query = column_sum(query_grads)
    g_w_key = contract(hidden, key_part)
    g_w_value = contract(hidden, value_part)
    g_b_value = column_sum(value_part)
    input_total = (
        d_sum
        + back_product(query_grads, full_query)
        + back_product(key_part, full_key)
        + back_product(value_part, full_value)
    )
    input_grad = input_total.astype(jnp.bfloat16).reshape(sequences, per_device, width)
    shares = (
        lax.psum_scatter(
            g_w_query.astype(jnp.bfloat16), "fsdp", scatter_dimension=0, tiled=True
        ).astype(jnp.float32),
        lax.psum_scatter(
            g_w_key.astype(jnp.bfloat16), "fsdp", scatter_dimension=0, tiled=True
        ).astype(jnp.float32),
        lax.psum_scatter(
            g_w_value.astype(jnp.bfloat16), "fsdp", scatter_dimension=0, tiled=True
        ).astype(jnp.float32),
        lax.psum_scatter(
            g_w_out.astype(jnp.bfloat16), "fsdp", scatter_dimension=0, tiled=True
        ).astype(jnp.float32),
        lax.psum_scatter(
            g_b_query.astype(jnp.bfloat16), "fsdp", scatter_dimension=0, tiled=True
        ).astype(jnp.float32),
        lax.psum_scatter(
            g_b_value.astype(jnp.bfloat16), "fsdp", scatter_dimension=0, tiled=True
        ).astype(jnp.float32),
        lax.psum_scatter(
            g_b_out.astype(jnp.bfloat16), "fsdp", scatter_dimension=0, tiled=True
        ).astype(jnp.float32),
        lax.psum_scatter(
            g_gain_one.astype(jnp.bfloat16), "fsdp", scatter_dimension=0, tiled=True
        ).astype(jnp.float32),
        lax.psum_scatter(
            g_shift_one.astype(jnp.bfloat16), "fsdp", scatter_dimension=0, tiled=True
        ).astype(jnp.float32),
        lax.psum_scatter(
            g_w_in.astype(jnp.bfloat16), "fsdp", scatter_dimension=0, tiled=True
        ).astype(jnp.float32),
        lax.psum_scatter(
            g_b_in.astype(jnp.bfloat16), "fsdp", scatter_dimension=0, tiled=True
        ).astype(jnp.float32),
        lax.psum_scatter(
            g_w_down.astype(jnp.bfloat16), "fsdp", scatter_dimension=0, tiled=True
        ).astype(jnp.float32),
        lax.psum_scatter(
            g_b_down.astype(jnp.bfloat16), "fsdp", scatter_dimension=0, tiled=True
        ).astype(jnp.float32),
        lax.psum_scatter(
            g_gain_two.astype(jnp.bfloat16), "fsdp", scatter_dimension=0, tiled=True
        ).astype(jnp.float32),
        lax.psum_scatter(
            g_shift_two.astype(jnp.bfloat16), "fsdp", scatter_dimension=0, tiled=True
        ).astype(jnp.float32),
    )
    totals = (
        lax.psum(shares[0].astype(jnp.bfloat16), "ctx").astype(jnp.float32),
        lax.psum(shares[1].astype(jnp.bfloat16), "ctx").astype(jnp.float32),
        lax.psum(shares[2].astype(jnp.bfloat16), "ctx").astype(jnp.float32),
        lax.psum(shares[3].astype(jnp.bfloat16), "ctx").astype(jnp.float32),
        lax.psum(shares[4].astype(jnp.bfloat16), "ctx").astype(jnp.float32),
        lax.psum(shares[5].astype(jnp.bfloat16), "ctx").astype(jnp.float32),
        lax.psum(shares[6].astype(jnp.bfloat16), "ctx").astype(jnp.float32),
        lax.psum(shares[7].astype(jnp.bfloat16), "ctx").astype(jnp.float32),
        lax.psum(shares[8].astype(jnp.bfloat16), "ctx").astype(jnp.float32),
        lax.psum(shares[9].astype(jnp.bfloat16), "ctx").astype(jnp.float32),
        lax.psum(shares[10].astype(jnp.bfloat16), "ctx").astype(jnp.float32),
        lax.psum(shares[11].astype(jnp.bfloat16), "ctx").astype(jnp.float32),
        lax.psum(shares[12].astype(jnp.bfloat16), "ctx").astype(jnp.float32),
        lax.psum(shares[13].astype(jnp.bfloat16), "ctx").astype(jnp.float32),
        lax.psum(shares[14].astype(jnp.bfloat16), "ctx").astype(jnp.float32),
    )
    return (
        layer_out,
        input_grad,
        totals[0],
        totals[1],
        totals[2],
        totals[3],
        totals[4],
        totals[5],
        totals[6],
        totals[7],
        totals[8],
        totals[9],
        totals[10],
        totals[11],
        totals[12],
        totals[13],
        totals[14],
    )


BF = jnp.bfloat16
F32 = jnp.float32
LANES = 256
VMEM = pl.BlockSpec(memory_space=pltpu.VMEM)
HBM = pl.BlockSpec(memory_space=pl.ANY)
FAR = pl.BlockSpec(memory_space=pltpu.HBM)
SMEM = pl.BlockSpec(memory_space=pltpu.SMEM)
VEC = 16


def shaped(shape, dtype):
    return jax.ShapeDtypeStruct(shape, dtype)


def call(kernel, outs, ins, args, scratch=(), flops=0, name=None):
    moved = sum(a.size * a.dtype.itemsize for a in args)
    moved += sum(o.size * o.dtype.itemsize for o in outs)
    held = sum(
        math.prod(r.shape) * jnp.dtype(r.dtype).itemsize
        for r in scratch
        if jnp.issubdtype(r.dtype, jnp.number)
    )
    return pl.pallas_call(
        kernel,
        out_shape=outs,
        in_specs=ins,
        out_specs=[VMEM] * len(outs),
        scratch_shapes=list(scratch),
        name=name,
        cost_estimate=pl.CostEstimate(flops=1, transcendentals=0, bytes_accessed=1),
        compiler_params=pltpu.CompilerParams(vmem_limit_bytes=moved + held + (4 << 20)),
    )(*args)


def dot(left, right):
    return jnp.dot(left, right, preferred_element_type=F32)


def dot_nt(left, right):
    return lax.dot_general(left, right, (((1,), (1,)), ((), ())), preferred_element_type=F32)


def dot_tn(left, right):
    return lax.dot_general(left, right, (((0,), (0,)), ((), ())), preferred_element_type=F32)


def turned(ring, f, s):
    return lax.rem(f - s + ring, ring)


class Plan:
    def __init__(self, chips, ring, width, hidden, per_device):
        self.chips, self.ring, self.width, self.hidden = chips, ring, width, hidden
        self.rows = per_device
        self.tokens = chips * per_device
        self.shard = width // ring
        self.half = self.shard // 2
        self.share = hidden // chips
        self.hshard = hidden // ring
        self.block = self.hshard // chips
        self.bhalf = self.block // 2
        self.heads = H // chips
        self.cols = self.heads * DH
        self.qkv = 3 * self.cols
        self.padded = self.heads * LANES
        self.wide = -(-self.qkv // 128) * 128
        self.packed = self.half * self.qkv // width
        self.clusters = chips
        self.entries = chips * CLUSTER


def pick_kernel(g, sc, *refs):
    weights, small = refs[:3], refs[3:12]
    qall, qsend, vec, here, *lines, sem = refs[12:]
    p, k = sc[0], sc[1]
    copies = [
        pltpu.make_async_copy(w, here.at[i], sem.at[i]) for i, w in enumerate(weights)
    ]
    copies += [
        pltpu.make_async_copy(ref, lines[i], sem.at[3 + i])
        for i, ref in enumerate(small)
    ]
    start(copies)
    finish(copies)
    for q in range(g.chips):

        @pl.when(p == q)
        def _(q=q):
            for h in range(g.heads):
                for i in range(3):
                    src = g.cols * q + DH * h
                    qall[:, 3 * DH * h + DH * i : 3 * DH * h + DH * (i + 1)] = here[
                        i, :, src : src + DH
                    ]

    vec[...] = jnp.zeros((VEC, LANES), BF)
    for i in range(8):
        vec[i : i + 1, 0 : g.shard] = lines[i][...].reshape(1, g.shard)
    for q in range(g.chips):
        vec[8 + q : 9 + q, 0 : g.block] = lines[8][g.block * q : g.block * (q + 1)].reshape(
            1, g.block
        )
    mine = pl.ds(pl.multiple_of(g.half * k, 16), g.half)
    qsend[0 : g.half] = qall[mine]
    qsend[g.half : g.half + VEC, 0:LANES] = vec[...]
    qsend[g.half : g.half + VEC, LANES:] = jnp.zeros((VEC, g.qkv - LANES), BF)


def prep_kernel(g, sc, _, wi, wd, wo, iall, send, here, sem):
    p, k = sc[0], sc[1]
    at = pl.multiple_of(g.block * p + g.bhalf * k, 16)
    mine = pl.ds(pl.multiple_of(g.half * k, 16), g.half)
    copies = [
        pltpu.make_async_copy(wi, here, sem.at[0]),
        pltpu.make_async_copy(wo.at[mine], send.at[pl.ds(g.half, g.half)], sem.at[1]),
        pltpu.make_async_copy(
            wd.at[pl.ds(at, g.bhalf)], send.at[pl.ds(2 * g.half, g.bhalf)], sem.at[2]
        ),
    ]
    start(copies)
    finish(copies[:1])
    for q in range(g.chips):

        @pl.when(p == q)
        def _(q=q):
            for r in range(g.ring):
                src = g.hshard * r + g.block * q
                iall[:, g.block * r : g.block * (r + 1)] = here[:, src : src + g.block]

    send[0 : g.half] = iall[mine]
    finish(copies[1:])


def gathers(g, sc, own, own_at, mine, theirs, at, piece, dst, sem):
    k, f = sc[1], sc[2]
    size = piece
    out = [
        pltpu.make_async_copy(
            own.at[pl.ds(own_at, 2 * size)],
            dst.at[pl.ds(pl.multiple_of(2 * size * f, 16), 2 * size)],
            sem.at[0],
        )
    ]
    for s in range(1, g.ring):
        base = 2 * size * turned(g.ring, f, s)
        for i, (src, core) in enumerate(((mine[s - 1], k), (theirs[s - 1], 1 - k))):
            out.append(
                pltpu.make_async_copy(
                    src.at[pl.ds(at, size)],
                    dst.at[pl.ds(pl.multiple_of(base + size * core, 16), size)],
                    sem.at[2 * s - 1 + i],
                )
            )
    return out


def start(copies):
    for copy in copies:
        copy.start()


def finish(copies):
    for copy in copies:
        copy.wait()


def qkv_kernel(g, sc, *refs):
    n = g.ring - 1
    xs = refs[: g.chips]
    vec, own = refs[g.chips : g.chips + 2]
    mine = refs[g.chips + 2 : g.chips + 2 + n]
    theirs = refs[g.chips + 2 + n : g.chips + 2 + 2 * n]
    out, w, full, vs, sem, vsem = refs[g.chips + 2 + 2 * n :]
    p, f = sc[0], sc[2]
    copies = gathers(g, sc, own, 0, mine, theirs, 0, g.half, w, sem)
    start(copies)
    vcopies = [
        pltpu.make_async_copy(
            mine[s].at[pl.ds(g.half, VEC), pl.ds(0, LANES)], vs.at[s], vsem.at[s]
        )
        for s in range(n)
    ]
    start(vcopies)
    finish(vcopies)
    rest = jnp.zeros((VEC, g.width - LANES), F32)
    total = jnp.zeros((VEC, g.width), F32)
    for s in range(g.ring):
        piece = (vec[...] if s == 0 else vs[s - 1]).astype(F32)
        wide = jnp.concatenate([piece, rest], axis=1)
        total = total + pltpu.roll(wide, g.shard * turned(g.ring, f, s), 1)
    full[...] = total
    back = pltpu.roll(total, lax.rem(g.width - g.cols * p, g.width), 1)
    gap = jnp.zeros((1, DH), F32)
    parts = []
    for h in range(g.heads):
        parts += [back[0:1, DH * h : DH * (h + 1)], gap, back[1:2, DH * h : DH * (h + 1)]]
    bias = jnp.concatenate(parts, axis=1)
    finish(copies)
    rows = jnp.concatenate([x[...] for x in xs], axis=0)
    found = (dot(rows, w[...]) + bias).astype(BF)
    for h in range(g.heads):
        out[:, LANES * h : LANES * h + 3 * DH] = found[:, 3 * DH * h : 3 * DH * (h + 1)]
        out[:, LANES * h + 3 * DH : LANES * (h + 1)] = jnp.zeros((g.tokens, DH), BF)


def select(index, size, axis_size, lanes):
    if lanes:
        ids = lax.broadcasted_iota(jnp.int32, (size, axis_size), 1)
    else:
        ids = lax.broadcasted_iota(jnp.int32, (axis_size, size), 0)
    return jnp.where(ids == index, 1.0, 0.0).astype(BF)


def attend_kernel(g, own, other, posr, posc, blocks, ctx_own, ctx_other, kept, probs):
    both = 2 * g.tokens
    for h in range(g.heads):
        pick = select(posc[:, h : h + 1], g.entries, both, True)
        place = select(posr[h : h + 1, :], g.entries, both, False)
        lanes = slice(LANES * h, LANES * (h + 1))
        rows = jnp.concatenate([own[:, lanes], other[:, lanes]], axis=0)
        picked = dot(pick, rows).astype(BF)
        kept[h] = picked
        ids = dot(blocks[...], place)
        mixed = []
        for c in range(g.clusters):
            at = slice(CLUSTER * c, CLUSTER * (c + 1))
            q, key, v = picked[at, 0:DH], picked[at, DH : 2 * DH], picked[at, 2 * DH : 3 * DH]
            scores = dot_nt(q, key) * (DH ** (-0.5))
            row_ids = ids[:, at]
            col_ids = jnp.transpose(row_ids)[:, 0:1]
            allowed = row_ids[0:1, :] <= col_ids
            masked = jnp.where(allowed, scores, FLOOR)
            top = jnp.max(masked, axis=-1, keepdims=True)
            weights = jnp.where(allowed, jnp.exp(masked - top), 0.0)
            share = weights / jnp.sum(weights, axis=-1, keepdims=True)
            probs[h * g.clusters + c] = share
            mixed.append(dot(share.astype(BF), v).astype(BF))
        back = dot(place, jnp.concatenate(mixed, axis=0)).astype(BF)
        ctx_own[:, DH * h : DH * (h + 1)] = back[: g.tokens]
        ctx_other[:, DH * h : DH * (h + 1)] = back[g.tokens :]


def attend_back_kernel(g, own, other, posr, posc, kept, probs, grads):
    both = 2 * g.tokens
    rows = jnp.concatenate([own[...], other[...]], axis=0)
    for h in range(g.heads):
        pick = select(posc[:, h : h + 1], g.entries, both, True)
        place = select(posr[h : h + 1, :], g.entries, both, False)
        d_mixed = dot(pick, rows[:, DH * h : DH * (h + 1)]).astype(BF)
        picked = kept[h]
        found = []
        for c in range(g.clusters):
            at = slice(CLUSTER * c, CLUSTER * (c + 1))
            q, key, v = picked[at, 0:DH], picked[at, DH : 2 * DH], picked[at, 2 * DH : 3 * DH]
            d_m = d_mixed[at]
            share = probs[h * g.clusters + c]
            d_share = dot_nt(d_m, v)
            delta = jnp.sum(share * d_share, axis=-1, keepdims=True)
            d_s = (share * (d_share - delta)).astype(BF)
            scale = DH ** (-0.5)
            d_q = dot(d_s, key) * scale
            d_k = dot_tn(d_s, q) * scale
            d_v = dot_tn(share.astype(BF), d_m)
            found.append(jnp.concatenate([d_q, d_k, d_v], axis=1).astype(BF))
        back = dot(place, jnp.concatenate(found, axis=0)).astype(BF)
        grads[:, 3 * DH * h : 3 * DH * (h + 1)] = back
    grads[:, g.qkv :] = jnp.zeros((both, g.wide - g.qkv), BF)


def norm_parts(values):
    centre = values - jnp.mean(values, axis=-1, keepdims=True)
    spread = jnp.mean(centre * centre, axis=-1, keepdims=True)
    scale = lax.rsqrt(spread + EPSILON)
    return centre * scale, scale


def norm_back(grad, z, scale):
    return scale * (
        grad
        - jnp.mean(grad, axis=-1, keepdims=True)
        - z * jnp.mean(grad * z, axis=-1, keepdims=True)
    )


def seen(g, ref, j):
    return jnp.concatenate(
        [ref[g.rows * (i ^ j) : g.rows * ((i ^ j) + 1)] for i in range(g.chips)], axis=0
    )


def lay_kernel(g, sc, *refs):
    n = g.ring - 1
    wo_own, wi_own, wd_own = refs[:3]
    mine, theirs = refs[3 : 3 + n], refs[3 + n : 3 + 2 * n]
    wo, wi, wd, *sems = refs[3 + 2 * n :]
    at = pl.multiple_of(g.block * sc[0], 16)
    copies = gathers(g, sc, wo_own, 0, mine, theirs, g.half, g.half, wo, sems[0])
    copies += gathers(g, sc, wi_own, 0, mine, theirs, 0, g.half, wi, sems[1])
    copies += gathers(g, sc, wd_own, at, mine, theirs, 2 * g.half, g.bhalf, wd, sems[2])
    start(copies)
    finish(copies)


def first_norm_kernel(g, sc, *refs):
    c = g.chips
    ctxs, xs, full, wo = refs[:c], refs[c : 2 * c], refs[2 * c], refs[2 * c + 1]
    low, first_own, z_own, s_own, wo_rows = refs[2 * c + 2 :]
    p = sc[0]
    rows = jnp.concatenate([x[...] for x in xs], axis=0).astype(F32)
    total = rows + full[2:3, :]
    for j in range(c):
        q = jnp.bitwise_xor(p, j)
        part = wo[pl.ds(pl.multiple_of(g.cols * q, 64), g.cols), :]
        total = total + dot(seen(g, ctxs[j], j), part)
        if j == 0:
            wo_rows[...] = part
    z, scale = norm_parts(total)
    first = z * full[3:4, :] + full[4:5, :]
    first_own[...] = first[: g.rows]
    z_own[...] = z[: g.rows]
    s_own[...] = jnp.broadcast_to(scale[: g.rows], (g.rows, 128))
    low[...] = first.astype(BF)


def up_kernel(g, sc, low, wi, full, inner):
    inner[...] = dot(low[...], wi[...]) + full[pl.ds(8 + sc[0], 1), :]


def down_kernel(g, inner, first_own, full, wd, *refs):
    parts, active = refs[: g.chips], refs[g.chips]
    u = inner[...]
    active[...] = (u * (1.0 + lax.erf(u * (0.5**0.5))) * 0.5).astype(BF)
    second = dot(active[...], wd[...])
    parts[0][...] = second[: g.rows] + first_own[...] + full[5:6, :]
    for j in range(1, g.chips):
        parts[j][...] = second[g.rows * j : g.rows * (j + 1)].astype(BF)


def turn_kernel(g, *refs):
    c = g.chips
    parts, full, cotangent = refs[:c], refs[c], refs[c + 1]
    out, d_second, branch = refs[c + 2 :]
    second = parts[0][...]
    for j in range(1, c):
        second = second + parts[j][...].astype(F32)
    z, scale = norm_parts(second)
    gain = full[6:7, :]
    out[...] = (z * gain + full[7:8, :]).astype(BF)
    dy = cotangent[...].astype(F32)
    grad = norm_back(dy * gain, z, scale)
    d_second[...] = grad
    branch[0 : g.rows] = grad.astype(BF)
    one = jnp.sum(dy * z, axis=0, keepdims=True)
    two = jnp.sum(dy, axis=0, keepdims=True)
    rest = jnp.zeros((VEC - 2, g.width), F32)
    branch[g.rows : g.rows + VEC] = jnp.concatenate([one, two, rest], axis=0).astype(BF)


def back_kernel(g, *refs):
    c = g.chips
    branches, slope, wd, wi = refs[:c], refs[c], refs[c + 1], refs[c + 2]
    parts, d_inner = refs[c + 3 : 2 * c + 3], refs[2 * c + 3]
    rows = jnp.concatenate([b[0 : g.rows] for b in branches], axis=0)
    d_active = dot_nt(rows, wd[...])
    d_inner[...] = (d_active * slope[...]).astype(BF)
    total = dot_nt(d_inner[...], wi[...])
    parts[0][...] = total[: g.rows]
    for j in range(1, c):
        parts[j][...] = total[g.rows * j : g.rows * (j + 1)].astype(BF)


def split_rows(g, sc, total, size, own, other, at):
    k, f = sc[1], sc[2]
    for s in range(g.ring):
        base = 2 * size * lax.rem(f + s, g.ring)
        own[s, at : at + size] = total[pl.ds(pl.multiple_of(base + size * k, 8), size), :]
        other[s, at : at + size] = total[
            pl.ds(pl.multiple_of(base + size * (1 - k), 8), size), :
        ].astype(BF)


def mlp_grads_kernel(g, sc, *refs):
    c = g.chips
    branches, active, low, d_inner = refs[:c], refs[c], refs[c + 1], refs[c + 2]
    own, other, sums, total = refs[c + 3 :]
    rows = jnp.concatenate([b[0 : g.rows] for b in branches], axis=0)
    total[...] = dot_tn(active[...], rows)
    split_rows(g, sc, total, g.bhalf, own, other, g.half)
    total[...] = dot_tn(low[...], d_inner[...])
    split_rows(g, sc, total, g.half, own, other, 0)
    stats = branches[0][g.rows : g.rows + VEC].astype(F32)
    for j in range(1, c):
        stats = stats + branches[j][g.rows : g.rows + VEC].astype(F32)
    down = jnp.sum(rows.astype(F32), axis=0, keepdims=True)
    up = jnp.sum(d_inner[...].astype(F32), axis=0, keepdims=True)
    sums[...] = jnp.concatenate([stats[0:2], down, up, jnp.zeros((4, g.width), F32)], axis=0)


def first_kernel(g, *refs):
    c = g.chips
    parts, d_second, z_own, s_own, full = refs[:c], *refs[c : c + 4]
    d_sum, attended = refs[c + 4 :]
    d_first = d_second[...] + parts[0][...]
    for j in range(1, c):
        d_first = d_first + parts[j][...].astype(F32)
    z = z_own[...]
    grad = norm_back(d_first * full[3:4, :], z, s_own[:, 0:1])
    d_sum[...] = grad
    attended[0 : g.rows] = grad.astype(BF)
    one = jnp.sum(d_first * z, axis=0, keepdims=True)
    two = jnp.sum(d_first, axis=0, keepdims=True)
    rest = jnp.zeros((VEC - 2, g.width), F32)
    attended[g.rows : g.rows + VEC] = jnp.concatenate([one, two, rest], axis=0).astype(BF)


def context_kernel(g, *refs):
    grads, wo_rows, out = refs[: g.chips], refs[g.chips], refs[g.chips + 1]
    rows = jnp.concatenate([b[0 : g.rows] for b in grads], axis=0)
    out[...] = dot_nt(rows, wo_rows[...]).astype(BF)


def out_grads_kernel(g, sc, *refs):
    c = g.chips
    grads, ctxs, sums = refs[:c], refs[c : 2 * c], refs[2 * c]
    own, total = refs[2 * c + 1], refs[-1]
    away = refs[2 * c + 2 : -1]
    p, f = sc[0], sc[2]
    rows = jnp.concatenate([b[0 : g.rows] for b in grads], axis=0)
    for j in range(c):
        q = jnp.bitwise_xor(p, j)
        total[pl.ds(pl.multiple_of(g.cols * q, 64), g.cols), :] = dot_tn(seen(g, ctxs[j], j), rows)
    stats = grads[0][g.rows : g.rows + VEC].astype(F32)
    for j in range(1, c):
        stats = stats + grads[j][g.rows : g.rows + VEC].astype(F32)
    out = jnp.sum(rows.astype(F32), axis=0, keepdims=True)
    rest = jnp.zeros((VEC - 7, g.width), F32)
    block = jnp.concatenate([sums[0:4], stats[0:2], out, rest], axis=0)
    size = g.shard // c
    for s in range(g.ring):
        base = g.shard * lax.rem(f + s, g.ring) + size * p
        part = total[pl.ds(pl.multiple_of(base, 8), size), :]
        if s == 0:
            own[0:size] = part
            own[size:] = block
        else:
            away[s - 1][0:size] = part.astype(BF)
            away[s - 1][size:] = block.astype(BF)


def summed(g, mine, theirs, at):
    one = mine[g.tokens * at : g.tokens * (at + 1), : g.qkv].astype(F32)
    two = theirs[g.tokens * (1 - at) : g.tokens * (2 - at), : g.qkv].astype(F32)
    return (one + two).astype(BF)


def input_kernel(g, mine, theirs, w, *parts):
    total = dot_nt(summed(g, mine, theirs, 0), w[...])
    parts[0][...] = total[: g.rows]
    for j in range(1, g.chips):
        parts[j][...] = total[g.rows * j : g.rows * (j + 1)].astype(BF)


def turn_rows_kernel(g, sc, *refs):
    xs, out = refs[: 2 * g.chips], refs[2 * g.chips]
    rows = jnp.concatenate([x[...] for x in xs], axis=0)
    for core in range(2):

        @pl.when(sc[1] == core)
        def _(core=core):
            for r in range(g.ring):
                lane = g.shard * r + g.half * core
                out[g.half * r : g.half * (r + 1), :] = jnp.transpose(rows[:, lane : lane + g.half])


def qkv_grads_kernel(g, sc, mine, theirs, turned_x, own, *refs):
    away, total = refs[:-1], refs[-1]
    f = sc[2]
    rows = jnp.concatenate([summed(g, mine, theirs, 0), summed(g, mine, theirs, 1)], axis=0)
    total[...] = dot(turned_x[...], rows)
    sums = jnp.sum(rows.astype(F32), axis=0, keepdims=True)
    gap = jnp.zeros((8, g.width - g.qkv), F32)
    block = jnp.concatenate(
        [jnp.concatenate([sums, jnp.zeros((7, g.qkv), F32)], axis=0), gap], axis=1
    )
    for s in range(g.ring):
        part = total[pl.ds(pl.multiple_of(g.half * lax.rem(f + s, g.ring), 8), g.half), :]
        dst = own if s == 0 else away[s - 1]
        packed = pack(g, part)
        dst[0 : g.packed] = packed if s == 0 else packed.astype(BF)
        dst[g.packed :] = block if s == 0 else block.astype(BF)


def pack(g, part):
    step = g.half - g.packed
    beside = [
        part[g.packed :, step_lanes : step_lanes + g.width - g.qkv]
        for step_lanes in range(0, g.qkv, g.width - g.qkv)
    ]
    return jnp.concatenate(
        [part[0 : g.packed], jnp.concatenate(beside, axis=0)], axis=1
    )


def sources(g, sc, refs):
    p, k = sc[0], sc[1]
    out = []
    for j in range(g.chips):
        q = jnp.bitwise_xor(p, j)
        out.append((q, k, refs[j]))
        out.append((q, 1 - k, refs[g.chips + j]))
    return out


def mlp_final_kernel(g, sc, *refs):
    found = refs[: 2 * g.chips]
    g_in, g_down = refs[2 * g.chips :]
    for q, core, ref in sources(g, sc, found):
        at = pl.multiple_of(g.block * q + g.bhalf * core, 8)
        g_down[pl.ds(at, g.bhalf), :] = ref[g.half :, :].astype(F32)
        mine = pl.ds(pl.multiple_of(g.half * core, 8), g.half)
        for chip in range(g.chips):

            @pl.when(q == chip)
            def _(chip=chip, ref=ref, mine=mine):
                for r in range(g.ring):
                    lane = g.hshard * r + g.block * chip
                    g_in[mine, lane : lane + g.block] = ref[
                        0 : g.half, g.block * r : g.block * (r + 1)
                    ].astype(F32)


def last_kernel(g, sc, *refs):
    found = refs[: 2 * g.chips]
    gq, gk, gv, g_bq, g_bv, g_out, g_bin, *small = refs[2 * g.chips :]
    p, f = sc[0], sc[2]
    size, side, step = g.shard // g.chips, g.width - g.qkv, g.half - g.packed
    top = g.packed + 8
    for q, core, ref in sources(g, sc, found):

        @pl.when((q == f) & (core == 0))
        def _(ref=ref):
            row = ref[g.packed : top, :].astype(F32)[0:1]
            for dst, at in zip((g_bq, g_bv), (0, 2)):
                dst[...] = jnp.concatenate(
                    [
                        row[:, 3 * DH * h + DH * at : 3 * DH * h + DH * (at + 1)]
                        for h in range(g.heads)
                    ],
                    axis=1,
                ).reshape(g.shard)

        base = pl.multiple_of(g.half * core, 8)
        for chip in range(g.chips):

            @pl.when(q == chip)
            def _(chip=chip, ref=ref, base=base):
                part = ref[0 : g.packed, :].astype(F32)
                for i, dst in enumerate((gq, gk, gv)):
                    for h in range(g.heads):
                        lane, src = g.cols * chip + DH * h, 3 * DH * h + DH * i
                        dst[pl.ds(base, g.packed), lane : lane + DH] = part[:, src : src + DH]
                        third, at = src // side, g.qkv + src % side
                        dst[pl.ds(base + g.packed, step), lane : lane + DH] = part[
                            step * third : step * (third + 1), at : at + DH
                        ]

    for j in range(g.chips):
        q = jnp.bitwise_xor(p, j)
        one, two = found[j], found[g.chips + j]
        both = one[top:, :].astype(F32) + two[top:, :].astype(F32)
        g_out[pl.ds(pl.multiple_of(size * q, 8), size), :] = both[0:size]
        back = pltpu.roll(both[size : size + VEC], lax.rem(g.width - g.shard * f, g.width), 1)
        for chip in range(g.chips):

            @pl.when(q == chip)
            def _(chip=chip, back=back):
                g_bin[g.block * chip : g.block * (chip + 1)] = back[3:4, : g.shard].reshape(g.shard)
                if chip == 0:
                    for i, dst in zip((0, 1, 2, 4, 5, 6), small):
                        dst[...] = back[i : i + 1, : g.shard].reshape(g.shard)


def to_core(x):
    n = lax.axis_size("ctx")
    return lax.ppermute(x, "ctx", [(i, i ^ 1) for i in range(n)])


def to_chip(x, j):
    n = lax.axis_size("ctx")
    return lax.ppermute(x, "ctx", [(i, i ^ (2 * j)) for i in range(n)])


def along(x, s):
    n = lax.axis_size("fsdp")
    return lax.ppermute(x, "fsdp", [(i, (i + s) % n) for i in range(n)])


def spread(x, chips):
    far = {j: to_chip(x, j) for j in sorted(range(1, chips), key=lambda j: -bin(j).count("1"))}
    return [x] + [far[j] for j in range(1, chips)]


def swap(parts):
    far = {j: to_chip(parts[j], j) for j in sorted(range(1, len(parts)), key=lambda j: -bin(j).count("1"))}
    return [parts[0]] + [far[j] for j in range(1, len(parts))]


def ring_sum(own, far):
    total = own
    for part in far:
        total = total + part.astype(F32)
    return total.astype(BF)


def kept_far(x):
    return pltpu.with_memory_space_constraint(x, pltpu.HBM)


def after(x, *first):
    return lax.optimization_barrier((x, *first))[0]


def plane_pieces(piece, chips):
    near = spread(piece, chips)
    return near + [to_core(part) for part in near]


def chip_body(
    hidden_in,
    out_grad,
    block_ids,
    clusters,
    w_query,
    w_key,
    w_value,
    w_out,
    b_query,
    b_value,
    b_out,
    ln1_gain,
    ln1_bias,
    w_in,
    b_in,
    w_down,
    b_down,
    ln2_gain,
    ln2_bias,
):
    n, ring = lax.axis_size("ctx"), lax.axis_size("fsdp")
    chips = n // 2
    rows, width = hidden_in.shape[1:]
    hidden = w_in.shape[1]
    g = Plan(chips, ring, width, hidden, rows)
    c, f = lax.axis_index("ctx"), lax.axis_index("fsdp")
    p, k = c // 2, c % 2
    sc = jnp.stack([p, k, f]).astype(jnp.int32)
    bind = functools.partial

    gate = pltpu.SemaphoreType.DMA((2 * ring - 1,))

    qall, qsend, vec = call(
        bind(pick_kernel, g),
        [
            shaped((g.shard, g.qkv), BF),
            shaped((g.half + VEC, g.qkv), BF),
            shaped((VEC, LANES), BF),
        ],
        [SMEM] + [FAR] * 12,
        [
            sc,
            *map(
                kept_far,
                (
                    w_query,
                    w_key,
                    w_value,
                    b_query,
                    b_value,
                    b_out,
                    ln1_gain,
                    ln1_bias,
                    b_down,
                    ln2_gain,
                    ln2_bias,
                    b_in,
                ),
            ),
        ],
        [
            pltpu.VMEM((3, g.shard, width), BF),
        ]
        + [pltpu.VMEM((g.shard,), BF)] * 8
        + [pltpu.VMEM((g.hshard,), BF), pltpu.SemaphoreType.DMA((12,))],
        name="pick_weights",
    )
    q_mine = [along(qsend, s) for s in range(1, ring)]
    x_own = after(hidden_in.reshape(rows, width), qsend)
    xs = spread(x_own, chips)
    iall, send = call(
        bind(prep_kernel, g),
        [
            shaped((g.shard, g.share), BF),
            shaped((2 * g.half + g.bhalf, width), BF),
        ],
        [SMEM, HBM, FAR, FAR, FAR],
        [sc, qsend, kept_far(w_in), kept_far(w_down), kept_far(w_out)],
        [pltpu.VMEM((g.shard, hidden), BF), pltpu.SemaphoreType.DMA((3,))],
        name="prepare_weights",
    )
    w_mine = [along(send, s) for s in range(1, ring)]
    q_theirs = [to_core(part) for part in q_mine]

    order = lax.dynamic_slice(
        clusters[0], (g.heads * p, g.entries * k), (g.heads, g.entries)
    )
    chip, core, within = order // (2 * rows), (order // rows) % 2, order % rows
    pos = (core ^ k) * g.tokens + (chip ^ p) * rows + within
    posr = jnp.pad(pos, ((0, 8 - g.heads), (0, 0)))
    posc = posr.T
    half_rows = rows // 2
    devices = 2 * (p ^ jnp.arange(chips)[None, :]) + (k ^ jnp.arange(2)[:, None])
    pieces = jnp.stack([devices, 2 * n - 1 - devices], axis=-1).reshape(-1)
    hot = (pieces[:, None] == jnp.arange(2 * n)[None, :]).astype(BF)
    blk = dot(hot, block_ids[0].reshape(2 * n, half_rows).astype(BF)).astype(BF)
    blk = jnp.broadcast_to(blk.reshape(1, 2 * g.tokens), (8, 2 * g.tokens))

    qkv, w_qkv, full = call(
        bind(qkv_kernel, g),
        [
            shaped((g.tokens, g.padded), BF),
            shaped((width, g.qkv), BF),
            shaped((VEC, width), F32),
        ],
        [SMEM] + [VMEM] * (chips + 1) + [HBM] * (2 * ring - 1),
        [sc, *xs, vec, qall, *q_mine, *q_theirs],
        [
            pltpu.VMEM((ring - 1, VEC, LANES), BF),
            gate,
            pltpu.SemaphoreType.DMA((ring - 1,)),
        ],
        flops=2 * g.tokens * width * g.qkv,
        name="project",
    )
    ctx_own, ctx_other, kept, probs = call(
        bind(attend_kernel, g),
        [
            shaped((g.tokens, g.cols), BF),
            shaped((g.tokens, g.cols), BF),
            shaped((g.heads, g.entries, LANES), BF),
            shaped((g.heads * g.clusters, CLUSTER, CLUSTER), F32),
        ],
        [VMEM] * 5,
        [qkv, to_core(qkv), posr, posc, blk],
        flops=8 * g.entries * g.tokens * LANES * g.heads,
        name="attend",
    )
    ctx = ctx_own + to_core(ctx_other)
    ctxs = spread(ctx, chips)

    w_theirs = [to_core(after(part, *ctxs[1:])) for part in w_mine]
    wo, wi, wd = call(
        bind(lay_kernel, g),
        [shaped((width, width), BF), shaped((width, g.share), BF), shaped((g.share, width), BF)],
        [SMEM] + [FAR, HBM, FAR] + [HBM] * (2 * ring - 2),
        [sc, kept_far(w_out), iall, kept_far(w_down), *w_mine, *w_theirs],
        [gate, gate, gate],
        name="lay_weights",
    )
    low, first_own, z_own, s_own, wo_rows = call(
        bind(first_norm_kernel, g),
        [
            shaped((g.tokens, width), BF),
            shaped((rows, width), F32),
            shaped((rows, width), F32),
            shaped((rows, 128), F32),
            shaped((g.cols, width), BF),
        ],
        [SMEM] + [VMEM] * (2 * chips + 2),
        [sc, *ctxs, *xs, full, wo],
        flops=2 * g.tokens * width * width,
        name="out_project",
    )
    (inner,) = call(
        bind(up_kernel, g),
        [shaped((g.tokens, g.share), F32)],
        [SMEM] + [VMEM] * 3,
        [sc, low, wi, full],
        flops=2 * g.tokens * width * g.share,
        name="mlp_up",
    )
    *second, active = call(
        bind(down_kernel, g),
        [shaped((rows, width), F32)]
        + [shaped((rows, width), BF)] * (chips - 1)
        + [shaped((g.tokens, g.share), BF)],
        [VMEM] * 4,
        [inner, first_own, full, wd],
        flops=2 * g.tokens * width * g.share,
        name="mlp_down",
    )
    inner = after(inner, active)
    slope = 0.5 * (1.0 + lax.erf(inner * (0.5**0.5))) + inner * jnp.exp(
        -0.5 * inner * inner
    ) * (1.0 / (2.0 * jnp.pi) ** 0.5)
    x_other = [to_core(after(x, inner)) for x in xs]
    (turned_x,) = call(
        bind(turn_rows_kernel, g),
        [shaped((ring * g.half, 2 * g.tokens), BF)],
        [SMEM] + [VMEM] * (2 * chips),
        [sc, *xs, *x_other],
        name="turn_rows",
    )
    second = swap(second)
    layer_out, d_second, branch = call(
        bind(turn_kernel, g),
        [
            shaped((rows, width), BF),
            shaped((rows, width), F32),
            shaped((rows + VEC, width), BF),
        ],
        [VMEM] * (chips + 2),
        [*second, after(full, turned_x), out_grad.reshape(rows, width)],
        name="norm_two",
    )
    branches = spread(branch, chips)
    *d_first, d_inner = call(
        bind(back_kernel, g),
        [shaped((rows, width), F32)]
        + [shaped((rows, width), BF)] * (chips - 1)
        + [shaped((g.tokens, g.share), BF)],
        [VMEM] * (chips + 3),
        [*branches, slope, wd, wi],
        flops=4 * g.tokens * width * g.share,
        name="mlp_back",
    )
    d_first = swap(d_first)
    m_own, m_other, sums = call(
        bind(mlp_grads_kernel, g),
        [
            shaped((ring, g.half + g.bhalf, width), F32),
            shaped((ring, g.half + g.bhalf, width), BF),
            shaped((8, width), F32),
        ],
        [SMEM] + [VMEM] * (chips + 3),
        [sc, *branches, active, low, d_inner],
        [pltpu.VMEM((width, g.share), F32)],
        flops=4 * g.tokens * width * g.share,
        name="mlp_grads",
    )
    m_got = to_core(m_other)
    m_mine = [m_own[s] + m_got[s].astype(F32) for s in range(ring)]
    m_away = [m_mine[s].astype(BF) for s in range(1, ring)]
    m_far = [along(part, s) for s, part in enumerate(m_away, 1)]
    m_piece = ring_sum(m_mine[0], m_far)
    d_sum, attended = call(
        bind(first_kernel, g),
        [shaped((rows, width), F32), shaped((rows + VEC, width), BF)],
        [VMEM] * (chips + 4),
        [*d_first, after(d_second, *m_away), z_own, s_own, full],
        name="norm_one",
    )
    grads = spread(attended, chips)
    (d_ctx,) = call(
        bind(context_kernel, g),
        [shaped((g.tokens, g.cols), BF)],
        [VMEM] * (chips + 1),
        [*grads, after(wo_rows, m_piece)],
        flops=2 * g.tokens * width * g.cols,
        name="context_back",
    )
    d_ctx_other = to_core(d_ctx)
    o_rows = g.shard // chips + VEC
    o_own, *o_away = call(
        bind(out_grads_kernel, g),
        [shaped((o_rows, width), F32)] + [shaped((o_rows, width), BF)] * (ring - 1),
        [SMEM] + [VMEM] * (2 * chips + 1),
        [sc, *grads, *ctxs, sums],
        [pltpu.VMEM((width, width), F32)],
        flops=2 * g.tokens * width * width,
        name="out_grads",
    )
    (dq_mine,) = call(
        bind(attend_back_kernel, g),
        [shaped((2 * g.tokens, g.wide), BF)],
        [VMEM] * 6,
        [d_ctx, d_ctx_other, posr, posc, after(kept, o_own), probs],
        flops=8 * g.entries * g.tokens * LANES * g.heads,
        name="attend_back",
    )
    o_far = [along(after(part, dq_mine), s) for s, part in enumerate(o_away, 1)]
    dq_theirs = to_core(dq_mine)
    q_rows = g.packed + 8
    q_own, *q_away = call(
        bind(qkv_grads_kernel, g),
        [shaped((q_rows, width), F32)] + [shaped((q_rows, width), BF)] * (ring - 1),
        [SMEM] + [VMEM] * 3,
        [sc, dq_mine, dq_theirs, turned_x],
        [pltpu.VMEM((ring * g.half, g.qkv), F32)],
        flops=2 * g.tokens * width * g.qkv,
        name="project_grads",
    )
    q_far = [along(part, s) for s, part in enumerate(q_away, 1)]
    d_in = call(
        bind(input_kernel, g),
        [shaped((rows, width), F32)] + [shaped((rows, width), BF)] * (chips - 1),
        [VMEM] * 3,
        [after(dq_mine, *q_away), dq_theirs, w_qkv],
        flops=2 * g.tokens * width * g.qkv,
        name="project_back",
    )
    d_in = swap(d_in)
    m_pieces = plane_pieces(m_piece, chips)
    g_in, g_down = call(
        bind(mlp_final_kernel, g),
        [shaped((g.shard, hidden), F32), shaped((g.hshard, width), F32)],
        [SMEM] + [VMEM] * (2 * chips),
        [sc, *m_pieces],
        name="mlp_lay",
    )
    total = d_sum
    for part in d_in:
        total = total + part.astype(F32)
    input_grad = total.astype(BF)
    vector = shaped((g.shard,), F32)
    piece = jnp.concatenate([ring_sum(q_own, q_far), ring_sum(o_own, o_far)], axis=0)
    found = call(
        bind(last_kernel, g),
        [shaped((g.shard, width), F32)] * 3
        + [vector] * 2
        + [shaped((g.shard, width), F32), shaped((g.hshard,), F32)]
        + [vector] * 6,
        [SMEM] + [VMEM] * (2 * chips),
        [after(sc, g_down), *plane_pieces(piece, chips)],
        name="last_lay",
    )
    gq, gk, gv, g_bq, g_bv, g_out, g_bin, g_gain2, g_bias2, g_bdown, g_gain1, g_bias1, g_bout = found
    return (
        layer_out.reshape(1, rows, width),
        input_grad.reshape(1, rows, width),
        gq,
        gk,
        gv,
        g_out,
        g_bq,
        g_bv,
        g_bout,
        g_gain1,
        g_bias1,
        g_in,
        g_bin,
        g_down,
        g_bdown,
        g_gain2,
        g_bias2,
    )


def fits(mesh):
    n, ring = mesh.shape["ctx"], mesh.shape["fsdp"]
    chips = n // 2
    return n % 2 == 0 and chips & (chips - 1) == 0 and H % chips == 0 and ring * chips <= 16


def solution(mesh):
    in_specs = (
        P("fsdp", "ctx", None),
        P("fsdp", "ctx", None),
        P("fsdp", None),
        P("fsdp", None, None),
        P("fsdp", None),
        P("fsdp", None),
        P("fsdp", None),
        P("fsdp", None),
        P("fsdp"),
        P("fsdp"),
        P("fsdp"),
        P("fsdp"),
        P("fsdp"),
        P("fsdp", None),
        P("fsdp"),
        P("fsdp", None),
        P("fsdp"),
        P("fsdp"),
        P("fsdp"),
    )
    out_specs = (
        P("fsdp", "ctx", None),
        P("fsdp", "ctx", None),
        P("fsdp", None),
        P("fsdp", None),
        P("fsdp", None),
        P("fsdp", None),
        P("fsdp"),
        P("fsdp"),
        P("fsdp"),
        P("fsdp"),
        P("fsdp"),
        P("fsdp", None),
        P("fsdp"),
        P("fsdp", None),
        P("fsdp"),
        P("fsdp"),
        P("fsdp"),
    )
    body = chip_body if fits(mesh) else general_body
    return jax.shard_map(body, mesh=mesh, in_specs=in_specs, out_specs=out_specs, check_vma=False)
```

```python
import functools
import math

import jax
import jax.numpy as jnp
from jax import lax
from jax.experimental import pallas as pl
from jax.experimental.pallas import tpu as pltpu
from jax.sharding import PartitionSpec as P

H = 12
DH = 64
CLUSTER = 128


EPSILON = 1e-12
FLOOR = -1e30


def layer_norm(values, gain, shift):
    centre = values - jnp.mean(values, axis=-1, keepdims=True)
    spread = jnp.mean(centre * centre, axis=-1, keepdims=True)
    return centre * lax.rsqrt(spread + EPSILON) * gain + shift


def exact_gelu(values):
    return jax.nn.gelu(values, approximate=False)


def positions(length, per_device, parts):
    stored = jnp.arange(length, dtype=jnp.int32)
    device = stored // per_device
    within = stored % per_device
    half = per_device // 2
    return jnp.where(
        within < half, device * half + within, (2 * parts - 1 - device) * half + within - half
    )


def contract(left, right):
    return lax.dot_general(
        left, right, (((0,), (0,)), ((), ())), preferred_element_type=jnp.float32
    )


def back_product(grad, weight):
    return lax.dot_general(
        grad, weight, (((1,), (1,)), ((), ())), preferred_element_type=jnp.float32
    )


def column_sum(values):
    return jnp.sum(values.astype(jnp.float32), axis=0)


def per_head_rows(rows, index):
    split = rows.reshape(rows.shape[0], H, DH)
    return jnp.take_along_axis(split, index.T[:, :, None], axis=0)


def cluster_tables(order, device, per_device, parts):
    heads, length = order.shape
    groups = length // CLUSTER
    members = CLUSTER // parts
    mine = (order // per_device == device).astype(jnp.int32)
    rank = jnp.cumsum(mine.reshape(heads, groups, CLUSTER), axis=-1).reshape(heads, length) - 1
    entry = jnp.arange(length, dtype=jnp.int32)[None, :]
    slot = jnp.where(mine == 1, entry // CLUSTER * members + rank, per_device)
    head_index = jnp.arange(heads, dtype=jnp.int32)[:, None]
    picked = (
        jnp.zeros((heads, per_device), jnp.int32)
        .at[head_index, slot]
        .set(order - device * per_device, mode="drop")
    )
    counter = jnp.broadcast_to(
        jnp.arange(per_device, dtype=jnp.int32)[None, :], (heads, per_device)
    )
    placed = jnp.zeros((heads, per_device), jnp.int32).at[head_index, picked].set(counter)
    inverse = (
        jnp.zeros((heads, length), jnp.int32)
        .at[head_index, order]
        .set(jnp.broadcast_to(jnp.arange(length, dtype=jnp.int32)[None, :], (heads, length)))
    )
    return (picked, placed, inverse)


def score_blocks(query, key_rows, query_blocks, key_blocks, scale):
    scores = (
        jnp.einsum("cqhd,ckhd->hcqk", query, key_rows, preferred_element_type=jnp.float32) * scale
    )
    allowed = key_blocks[:, :, None, :] <= query_blocks[:, :, :, None]
    return (scores, allowed)


def attend(query, key_rows, value_rows, query_blocks, key_blocks, scale):
    scores, allowed = score_blocks(query, key_rows, query_blocks, key_blocks, scale)
    masked = jnp.where(allowed, scores, FLOOR)
    top = jnp.max(masked, axis=-1, keepdims=True)
    weights = jnp.where(allowed, jnp.exp(masked - top), 0.0)
    total = jnp.sum(weights, axis=-1, keepdims=True)
    probs = (weights / total).astype(jnp.bfloat16)
    mixed = jnp.einsum("hcqk,ckhd->cqhd", probs, value_rows, preferred_element_type=jnp.float32)
    return (mixed.astype(jnp.bfloat16), top + jnp.log(total))


def attend_back(query, key_rows, value_rows, query_blocks, key_blocks, logsum, d_mixed, scale):
    scores, allowed = score_blocks(query, key_rows, query_blocks, key_blocks, scale)
    probs = jnp.where(allowed, jnp.exp(jnp.where(allowed, scores, FLOOR) - logsum), 0.0)
    rounded = probs.astype(jnp.bfloat16)
    d_probs = jnp.einsum("cqhd,ckhd->hcqk", d_mixed, value_rows, preferred_element_type=jnp.float32)
    centred = jnp.sum(probs * d_probs, axis=-1, keepdims=True)
    d_scores = (probs * (d_probs - centred)).astype(jnp.bfloat16)
    d_query = (
        jnp.einsum("hcqk,ckhd->cqhd", d_scores, key_rows, preferred_element_type=jnp.float32)
        * scale
    )
    d_key = (
        jnp.einsum("hcqk,cqhd->ckhd", d_scores, query, preferred_element_type=jnp.float32) * scale
    )
    d_value = jnp.einsum("hcqk,cqhd->ckhd", rounded, d_mixed, preferred_element_type=jnp.float32)
    return (d_query, d_key, d_value)


def general_body(
    hidden_in,
    out_grad,
    block_ids,
    clusters,
    w_query,
    w_key,
    w_value,
    w_out,
    b_query,
    b_value,
    b_out,
    ln1_gain,
    ln1_bias,
    w_in,
    b_in,
    w_down,
    b_down,
    ln2_gain,
    ln2_bias,
):
    parts = lax.axis_size("ctx")
    device = lax.axis_index("ctx")
    sequences, per_device, width = hidden_in.shape
    length = per_device * parts
    members = CLUSTER // parts
    groups = length // CLUSTER
    scale = DH ** (-0.5)
    (
        full_query,
        full_key,
        full_value,
        full_out,
        bias_query,
        bias_value,
        bias_out,
        gain_one,
        shift_one,
    ) = (
        lax.all_gather(w_query, "fsdp", axis=0, tiled=True),
        lax.all_gather(w_key, "fsdp", axis=0, tiled=True),
        lax.all_gather(w_value, "fsdp", axis=0, tiled=True),
        lax.all_gather(w_out, "fsdp", axis=0, tiled=True),
        lax.all_gather(b_query, "fsdp", axis=0, tiled=True),
        lax.all_gather(b_value, "fsdp", axis=0, tiled=True),
        lax.all_gather(b_out, "fsdp", axis=0, tiled=True),
        lax.all_gather(ln1_gain, "fsdp", axis=0, tiled=True),
        lax.all_gather(ln1_bias, "fsdp", axis=0, tiled=True),
    )
    full_in, full_down, bias_in, bias_down, gain_two, shift_two = (
        lax.all_gather(w_in, "fsdp", axis=0, tiled=True),
        lax.all_gather(w_down, "fsdp", axis=0, tiled=True),
        lax.all_gather(b_in, "fsdp", axis=0, tiled=True),
        lax.all_gather(b_down, "fsdp", axis=0, tiled=True),
        lax.all_gather(ln2_gain, "fsdp", axis=0, tiled=True),
        lax.all_gather(ln2_bias, "fsdp", axis=0, tiled=True),
    )
    hidden = hidden_in.reshape(sequences * per_device, width)
    query_rows = (
        jnp.dot(hidden, full_query, preferred_element_type=jnp.float32) + bias_query
    ).astype(jnp.bfloat16)
    key_rows = jnp.dot(hidden, full_key, preferred_element_type=jnp.float32).astype(jnp.bfloat16)
    value_rows = (
        jnp.dot(hidden, full_value, preferred_element_type=jnp.float32) + bias_value
    ).astype(jnp.bfloat16)
    place = positions(length, per_device, parts)
    index = 0
    order = clusters[index]
    stored_blocks = block_ids[index][place]
    picked, placed, inverse = cluster_tables(order, device, per_device, parts)
    q_local = per_head_rows(query_rows, picked).reshape(groups, members, H, DH)
    query_blocks = stored_blocks[device * per_device + picked].reshape(H, groups, members)
    key_all = lax.all_gather(key_rows, "ctx", axis=0, tiled=True)
    value_all = lax.all_gather(value_rows, "ctx", axis=0, tiled=True)
    key_cluster = per_head_rows(key_all, order).reshape(groups, CLUSTER, H, DH)
    value_cluster = per_head_rows(value_all, order).reshape(groups, CLUSTER, H, DH)
    key_blocks = stored_blocks[order].reshape(H, groups, CLUSTER)
    mixed, logsum = attend(q_local, key_cluster, value_cluster, query_blocks, key_blocks, scale)
    contexts = per_head_rows(mixed.reshape(per_device, width), placed).reshape(per_device, width)
    kept = [
        (
            q_local,
            key_cluster,
            value_cluster,
            query_blocks,
            key_blocks,
            logsum,
            picked,
            placed,
            inverse,
        )
    ]
    attended = jnp.dot(contexts, full_out, preferred_element_type=jnp.float32) + bias_out
    first_sum = hidden.astype(jnp.float32) + attended
    first, first_pull = jax.vjp(
        layer_norm, first_sum, gain_one.astype(jnp.float32), shift_one.astype(jnp.float32)
    )
    first_low = first.astype(jnp.bfloat16)
    inner = jnp.dot(first_low, full_in, preferred_element_type=jnp.float32) + bias_in
    active_full, gelu_pull = jax.vjp(exact_gelu, inner)
    active = active_full.astype(jnp.bfloat16)
    second_sum = first + jnp.dot(active, full_down, preferred_element_type=jnp.float32) + bias_down
    second, second_pull = jax.vjp(
        layer_norm, second_sum, gain_two.astype(jnp.float32), shift_two.astype(jnp.float32)
    )
    layer_out = second.astype(jnp.bfloat16).reshape(sequences, per_device, width)
    d_out = out_grad.reshape(sequences * per_device, width).astype(jnp.float32)
    d_second, g_gain_two, g_shift_two = second_pull(d_out)
    d_branch = d_second.astype(jnp.bfloat16)
    g_w_down = contract(active, d_branch)
    g_b_down = column_sum(d_branch)
    d_active = back_product(d_branch, full_down)
    d_inner = gelu_pull(d_active)[0].astype(jnp.bfloat16)
    g_w_in = contract(first_low, d_inner)
    g_b_in = column_sum(d_inner)
    d_first = d_second + back_product(d_inner, full_in)
    d_sum, g_gain_one, g_shift_one = first_pull(d_first)
    d_attended = d_sum.astype(jnp.bfloat16)
    g_w_out = contract(contexts, d_attended)
    g_b_out = column_sum(d_attended)
    d_context = back_product(d_attended, full_out).astype(jnp.bfloat16)
    index = 0
    q_kept, k_kept, v_kept, blocks_q, blocks_k, logsum, picked, placed, inverse = kept[index]
    d_cluster = per_head_rows(d_context, picked).reshape(groups, members, H, DH)
    d_query, d_key, d_value = attend_back(
        q_kept, k_kept, v_kept, blocks_q, blocks_k, logsum, d_cluster, scale
    )
    key_full = per_head_rows(d_key.reshape(length, width), inverse).reshape(length, width)
    value_full = per_head_rows(d_value.reshape(length, width), inverse).reshape(length, width)
    key_part = lax.psum_scatter(
        key_full.astype(jnp.bfloat16), "ctx", scatter_dimension=0, tiled=True
    )
    value_part = lax.psum_scatter(
        value_full.astype(jnp.bfloat16), "ctx", scatter_dimension=0, tiled=True
    )
    query_local = d_query.astype(jnp.bfloat16).reshape(per_device, width)
    query_grads = per_head_rows(query_local, placed).reshape(per_device, width)
    g_w_query = contract(hidden, query_grads)
    g_b_query = column_sum(query_grads)
    g_w_key = contract(hidden, key_part)
    g_w_value = contract(hidden, value_part)
    g_b_value = column_sum(value_part)
    input_total = (
        d_sum
        + back_product(query_grads, full_query)
        + back_product(key_part, full_key)
        + back_product(value_part, full_value)
    )
    input_grad = input_total.astype(jnp.bfloat16).reshape(sequences, per_device, width)
    shares = (
        lax.psum_scatter(
            g_w_query.astype(jnp.bfloat16), "fsdp", scatter_dimension=0, tiled=True
        ).astype(jnp.float32),
        lax.psum_scatter(
            g_w_key.astype(jnp.bfloat16), "fsdp", scatter_dimension=0, tiled=True
        ).astype(jnp.float32),
        lax.psum_scatter(
            g_w_value.astype(jnp.bfloat16), "fsdp", scatter_dimension=0, tiled=True
        ).astype(jnp.float32),
        lax.psum_scatter(
            g_w_out.astype(jnp.bfloat16), "fsdp", scatter_dimension=0, tiled=True
        ).astype(jnp.float32),
        lax.psum_scatter(
            g_b_query.astype(jnp.bfloat16), "fsdp", scatter_dimension=0, tiled=True
        ).astype(jnp.float32),
        lax.psum_scatter(
            g_b_value.astype(jnp.bfloat16), "fsdp", scatter_dimension=0, tiled=True
        ).astype(jnp.float32),
        lax.psum_scatter(
            g_b_out.astype(jnp.bfloat16), "fsdp", scatter_dimension=0, tiled=True
        ).astype(jnp.float32),
        lax.psum_scatter(
            g_gain_one.astype(jnp.bfloat16), "fsdp", scatter_dimension=0, tiled=True
        ).astype(jnp.float32),
        lax.psum_scatter(
            g_shift_one.astype(jnp.bfloat16), "fsdp", scatter_dimension=0, tiled=True
        ).astype(jnp.float32),
        lax.psum_scatter(
            g_w_in.astype(jnp.bfloat16), "fsdp", scatter_dimension=0, tiled=True
        ).astype(jnp.float32),
        lax.psum_scatter(
            g_b_in.astype(jnp.bfloat16), "fsdp", scatter_dimension=0, tiled=True
        ).astype(jnp.float32),
        lax.psum_scatter(
            g_w_down.astype(jnp.bfloat16), "fsdp", scatter_dimension=0, tiled=True
        ).astype(jnp.float32),
        lax.psum_scatter(
            g_b_down.astype(jnp.bfloat16), "fsdp", scatter_dimension=0, tiled=True
        ).astype(jnp.float32),
        lax.psum_scatter(
            g_gain_two.astype(jnp.bfloat16), "fsdp", scatter_dimension=0, tiled=True
        ).astype(jnp.float32),
        lax.psum_scatter(
            g_shift_two.astype(jnp.bfloat16), "fsdp", scatter_dimension=0, tiled=True
        ).astype(jnp.float32),
    )
    totals = (
        lax.psum(shares[0].astype(jnp.bfloat16), "ctx").astype(jnp.float32),
        lax.psum(shares[1].astype(jnp.bfloat16), "ctx").astype(jnp.float32),
        lax.psum(shares[2].astype(jnp.bfloat16), "ctx").astype(jnp.float32),
        lax.psum(shares[3].astype(jnp.bfloat16), "ctx").astype(jnp.float32),
        lax.psum(shares[4].astype(jnp.bfloat16), "ctx").astype(jnp.float32),
        lax.psum(shares[5].astype(jnp.bfloat16), "ctx").astype(jnp.float32),
        lax.psum(shares[6].astype(jnp.bfloat16), "ctx").astype(jnp.float32),
        lax.psum(shares[7].astype(jnp.bfloat16), "ctx").astype(jnp.float32),
        lax.psum(shares[8].astype(jnp.bfloat16), "ctx").astype(jnp.float32),
        lax.psum(shares[9].astype(jnp.bfloat16), "ctx").astype(jnp.float32),
        lax.psum(shares[10].astype(jnp.bfloat16), "ctx").astype(jnp.float32),
        lax.psum(shares[11].astype(jnp.bfloat16), "ctx").astype(jnp.float32),
        lax.psum(shares[12].astype(jnp.bfloat16), "ctx").astype(jnp.float32),
        lax.psum(shares[13].astype(jnp.bfloat16), "ctx").astype(jnp.float32),
        lax.psum(shares[14].astype(jnp.bfloat16), "ctx").astype(jnp.float32),
    )
    return (
        layer_out,
        input_grad,
        totals[0],
        totals[1],
        totals[2],
        totals[3],
        totals[4],
        totals[5],
        totals[6],
        totals[7],
        totals[8],
        totals[9],
        totals[10],
        totals[11],
        totals[12],
        totals[13],
        totals[14],
    )


BF = jnp.bfloat16
F32 = jnp.float32
LANES = 256
VMEM = pl.BlockSpec(memory_space=pltpu.VMEM)
HBM = pl.BlockSpec(memory_space=pl.ANY)
FAR = pl.BlockSpec(memory_space=pltpu.HBM)
SMEM = pl.BlockSpec(memory_space=pltpu.SMEM)
VEC = 16
SLAB = 64


def shaped(shape, dtype):
    return jax.ShapeDtypeStruct(shape, dtype)


def call(kernel, outs, ins, args, scratch=(), name=None, weight=1):
    moved = sum(a.size * a.dtype.itemsize for a in args)
    moved += sum(o.size * o.dtype.itemsize for o in outs)
    held = sum(
        math.prod(r.shape) * jnp.dtype(r.dtype).itemsize
        for r in scratch
        if jnp.issubdtype(r.dtype, jnp.number)
    )
    return pl.pallas_call(
        kernel,
        out_shape=outs,
        in_specs=ins,
        out_specs=[VMEM] * len(outs),
        scratch_shapes=list(scratch),
        name=name,
        cost_estimate=pl.CostEstimate(flops=weight, transcendentals=0, bytes_accessed=weight),
        compiler_params=pltpu.CompilerParams(vmem_limit_bytes=moved + held + (4 << 20)),
    )(*args)


def mix(function, outs, *args, name=None):
    def kernel(*refs):
        found = function(*(ref[...] for ref in refs[: len(args)]))
        for ref, value in zip(refs[len(args) :], found):
            ref[...] = value

    return call(kernel, outs, [VMEM] * len(args), args, name=name)


def dot(left, right):
    return jnp.dot(left, right, preferred_element_type=F32)


def dot_nt(left, right):
    return lax.dot_general(left, right, (((1,), (1,)), ((), ())), preferred_element_type=F32)


def dot_tn(left, right):
    return lax.dot_general(left, right, (((0,), (0,)), ((), ())), preferred_element_type=F32)


class Plan:
    def __init__(self, chips, ring, width, hidden, per_device):
        self.chips, self.ring, self.width, self.hidden = chips, ring, width, hidden
        self.rows = per_device
        self.tokens = chips * per_device
        self.shard = width // ring
        self.half = self.shard // 2
        self.share = hidden // chips
        self.hshard = hidden // ring
        self.block = self.hshard // chips
        self.bhalf = self.block // 2
        self.heads = H // chips
        self.cols = self.heads * DH
        self.qkv = 3 * self.cols
        self.padded = self.heads * LANES
        self.wide = -(-self.qkv // 128) * 128
        self.packed = self.half * self.qkv // width
        self.clusters = chips
        self.members = CLUSTER // (2 * chips)
        self.entries = chips * CLUSTER


def pick_kernel(g, sc, *refs):
    weights, small = refs[:3], refs[3:12]
    qall, qsend, vec, here, *lines, sem = refs[12:]
    p, k = sc[0], sc[1]
    copies = [
        pltpu.make_async_copy(w, here.at[i], sem.at[i]) for i, w in enumerate(weights)
    ]
    copies += [
        pltpu.make_async_copy(ref, lines[i], sem.at[3 + i])
        for i, ref in enumerate(small)
    ]
    start(copies)
    finish(copies)
    for q in range(g.chips):

        @pl.when(p == q)
        def _(q=q):
            for i in range(3):
                qall[:, g.cols * i : g.cols * (i + 1)] = here[
                    i, :, g.cols * q : g.cols * (q + 1)
                ]

    vec[...] = jnp.zeros((VEC, LANES), BF)
    for i in range(8):
        vec[i : i + 1, 0 : g.shard] = lines[i][...].reshape(1, g.shard)
    for q in range(g.chips):
        vec[8 + q : 9 + q, 0 : g.block] = lines[8][g.block * q : g.block * (q + 1)].reshape(
            1, g.block
        )
    mine = pl.ds(pl.multiple_of(g.half * k, 16), g.half)
    qsend[0 : g.half] = qall[mine]
    qsend[g.half : g.half + VEC, 0:LANES] = vec[...]
    qsend[g.half : g.half + VEC, LANES:] = jnp.zeros((VEC, g.qkv - LANES), BF)


def prep_kernel(g, sc, _, wi, wd, wo, iall, send, here, sem):
    p, k = sc[0], sc[1]
    at = pl.multiple_of(g.block * p + g.bhalf * k, 16)
    mine = pl.ds(pl.multiple_of(g.half * k, 16), g.half)
    copies = [
        pltpu.make_async_copy(wi, here, sem.at[0]),
        pltpu.make_async_copy(wo.at[mine], send.at[pl.ds(g.half, g.half)], sem.at[1]),
        pltpu.make_async_copy(
            wd.at[pl.ds(at, g.bhalf)], send.at[pl.ds(2 * g.half, g.bhalf)], sem.at[2]
        ),
    ]
    start(copies)
    finish(copies[:1])
    for q in range(g.chips):

        @pl.when(p == q)
        def _(q=q):
            for r in range(g.ring):
                src = g.hshard * r + g.block * q
                iall[:, g.block * r : g.block * (r + 1)] = here[:, src : src + g.block]

    send[0 : g.half] = iall[mine]
    finish(copies[1:])


def gathers(g, sc, own, own_at, mine, theirs, at, piece, dst, sem, turn=0):
    k, f = sc[1], jnp.bitwise_xor(sc[2], turn)
    size = piece
    out = [
        pltpu.make_async_copy(
            own.at[pl.ds(own_at, 2 * size)],
            dst.at[pl.ds(pl.multiple_of(2 * size * f, 16), 2 * size)],
            sem.at[0],
        )
    ]
    for s in range(1, g.ring):
        base = 2 * size * jnp.bitwise_xor(f, s)
        for i, (src, core) in enumerate(((mine[s - 1], k), (theirs[s - 1], 1 - k))):
            out.append(
                pltpu.make_async_copy(
                    src.at[pl.ds(at, size)],
                    dst.at[pl.ds(pl.multiple_of(base + size * core, 16), size)],
                    sem.at[2 * s - 1 + i],
                )
            )
    return out


def start(copies):
    for copy in copies:
        copy.start()


def finish(copies):
    for copy in copies:
        copy.wait()


def qkv_kernel(g, sc, *refs):
    n, c = g.ring - 1, 2 * g.chips
    xs = refs[:c]
    vec, own = refs[c : c + 2]
    mine = refs[c + 2 : c + 2 + n]
    theirs = refs[c + 2 + n : c + 2 + 2 * n]
    out, w, full, vs, sem, vsem = refs[c + 2 + 2 * n :]
    p, f = sc[0], sc[2]
    copies = gathers(g, sc, own, 0, mine, theirs, 0, g.half, w, sem)
    start(copies)
    vcopies = [
        pltpu.make_async_copy(
            mine[s].at[pl.ds(g.half, VEC), pl.ds(0, LANES)], vs.at[s], vsem.at[s]
        )
        for s in range(n)
    ]
    start(vcopies)
    finish(vcopies)
    rest = jnp.zeros((VEC, g.width - LANES), F32)
    total = jnp.zeros((VEC, g.width), F32)
    for s in range(g.ring):
        piece = (vec[...] if s == 0 else vs[s - 1]).astype(F32)
        wide = jnp.concatenate([piece, rest], axis=1)
        total = total + pltpu.roll(wide, g.shard * jnp.bitwise_xor(f, s), 1)
    full[...] = total
    back = pltpu.roll(total, lax.rem(g.width - g.cols * p, g.width), 1)
    bias = jnp.concatenate(
        [back[0:1, : g.cols], jnp.zeros((1, g.cols), F32), back[1:2, : g.cols]], axis=1
    )
    finish(copies)
    rows = jnp.concatenate([x[...] for x in xs], axis=0)
    found = (dot(rows, w[...]) + bias).astype(BF)
    for h in range(g.heads):
        for i in range(3):
            out[:, LANES * h + DH * i : LANES * h + DH * (i + 1)] = found[
                :, g.cols * i + DH * h : g.cols * i + DH * (h + 1)
            ]
        out[:, LANES * h + 3 * DH : LANES * (h + 1)] = jnp.zeros((2 * g.tokens, DH), BF)


def select(index, size, axis_size, lanes):
    if lanes:
        ids = lax.broadcasted_iota(jnp.int32, (size, axis_size), 1)
    else:
        ids = lax.broadcasted_iota(jnp.int32, (axis_size, size), 0)
    return jnp.where(ids == index, 1.0, 0.0).astype(BF)


def over(x, size):
    return lax.shift_right_logical(x, jnp.int32(size.bit_length() - 1))


def tables_kernel(g, sc, _, clusters, block_ids, pick, place, blocks):
    p, k = sc[0], sc[1]
    ranges, step = 2 * g.chips, g.clusters * g.members
    shape = (2 * ranges, 2 * ranges)
    piece, source = (lax.broadcasted_iota(jnp.int32, shape, axis) for axis in (0, 1))
    device = 2 * jnp.bitwise_xor(p, over(piece, 2) & (g.chips - 1)) + jnp.bitwise_xor(
        k, over(piece, 2 * g.chips)
    )
    found = jnp.where(piece & 1 == 0, device, 2 * ranges - 1 - device)
    hot = jnp.where(found == source, 1.0, 0.0).astype(BF)
    half = g.rows // 2
    line = block_ids[...].astype(F32)
    lines = [line[:, half * i : half * (i + 1)] for i in range(2 * ranges)]
    ids = dot(hot, jnp.concatenate(lines, axis=0).astype(BF))
    for d in range(ranges):
        line = jnp.concatenate([ids[2 * d : 2 * d + 1], ids[2 * d + 1 : 2 * d + 2]], axis=1)
        blocks[:, g.rows * d : g.rows * (d + 1)] = jnp.broadcast_to(line, (8, g.rows)).astype(BF)
    before = lax.broadcasted_iota(jnp.int32, (CLUSTER, CLUSTER), 1) < lax.broadcasted_iota(
        jnp.int32, (CLUSTER, CLUSTER), 0
    )
    rows, cols, tokens = [], [], []
    for h in range(g.heads):
        order = clusters[
            pl.ds(g.heads * p + h, 1), pl.ds(pl.multiple_of(g.entries * k, 128), g.entries)
        ]
        chip, core = over(order, 2 * g.rows), over(order, g.rows) & 1
        within = order & (g.rows - 1)
        rows.append(
            jnp.bitwise_xor(core, k) * g.tokens + jnp.bitwise_xor(chip, p) * g.rows + within
        )
    units = [(h, c) for h in range(g.heads) for c in range(g.clusters)]
    for h, c in units:
        row = rows[h][:, CLUSTER * c : CLUSTER * (c + 1)]
        tall = jnp.broadcast_to(row.astype(F32), (CLUSTER, CLUSTER))
        cols.append(over(jnp.transpose(tall)[:, 0:1].astype(jnp.int32), g.rows))
    spots = []
    for (h, c), col in zip(units, cols):
        row = rows[h][:, CLUSTER * c : CLUSTER * (c + 1)]
        same = (col == over(row, g.rows)) & before
        rank = jnp.sum(jnp.where(same, 1.0, 0.0), axis=1, keepdims=True).astype(jnp.int32)
        spots.append(select(col * g.members + rank, CLUSTER, CLUSTER, True))
    for (h, c), spot in zip(units, spots):
        row = rows[h][:, CLUSTER * c : CLUSTER * (c + 1)]
        within = jnp.broadcast_to((row & (g.rows - 1)).astype(F32), (8, CLUSTER)).astype(BF)
        tokens.append(dot(within, spot))
    for h in range(g.heads):
        for d in range(ranges):
            lanes = slice(g.members * d, g.members * (d + 1))
            mine = jnp.concatenate(
                [tokens[h * g.clusters + c][:, lanes] for c in range(g.clusters)], axis=1
            ).astype(jnp.int32)
            place[h, g.rows * d : g.rows * (d + 1)] = select(mine[0:1, :], step, g.rows, False)
            pick[h, step * d : step * (d + 1)] = select(
                jnp.transpose(mine)[:, 0:1], step, g.rows, True
            )


def mask_kernel(g, blocks, place, mask):
    ids = [
        [
            dot(blocks[:, g.rows * d : g.rows * (d + 1)], place[h, g.rows * d : g.rows * (d + 1)])
            for d in range(2 * g.chips)
        ]
        for h in range(g.heads)
    ]
    for h in range(g.heads):
        for c in range(g.clusters):
            lanes = slice(g.members * c, g.members * (c + 1))
            keys = jnp.concatenate([part[:, lanes] for part in ids[h]], axis=1)
            allowed = keys[0:1, :] <= jnp.transpose(keys)[:, 0:1]
            mask[h * g.clusters + c] = jnp.where(allowed, 0.0, FLOOR)


def cluster_rows(g, ref, c):
    step = g.clusters * g.members
    return jnp.concatenate(
        [
            ref[step * d + g.members * c : step * d + g.members * (c + 1)]
            for d in range(2 * g.chips)
        ],
        axis=0,
    )


def put_cluster(g, ref, c, values):
    step = g.clusters * g.members
    for d in range(2 * g.chips):
        ref[step * d + g.members * c : step * d + g.members * (c + 1)] = values[
            g.members * d : g.members * (d + 1)
        ]


def attend_kernel(g, qkv, pick, place, mask, ctx_own, ctx_other, kept, probs, mixed):
    step, ranges = g.clusters * g.members, 2 * g.chips
    units = [(h, c) for h in range(g.heads) for c in range(g.clusters)]
    for h in range(g.heads):
        for d in range(ranges):
            rows = qkv[g.rows * d : g.rows * (d + 1), LANES * h : LANES * (h + 1)]
            slots = slice(step * d, step * (d + 1))
            kept[h, slots] = dot(pick[h, slots], rows).astype(BF)
    for h, c in units:
        rows = cluster_rows(g, kept.at[h], c)
        q, key = rows[:, 0:DH], rows[:, DH : 2 * DH]
        at = h * g.clusters + c
        probs[at] = dot_nt(q, key) * (DH ** (-0.5)) + mask[at]
    for h, c in units:
        at = h * g.clusters + c
        masked = probs[at]
        weights = jnp.exp(masked - jnp.max(masked, axis=-1, keepdims=True))
        probs[at] = weights * (1.0 / jnp.sum(weights, axis=-1, keepdims=True))
    for h, c in units:
        v = cluster_rows(g, kept.at[h], c)[:, 2 * DH : 3 * DH]
        put_cluster(
            g, mixed.at[h], c, dot(probs[h * g.clusters + c].astype(BF), v).astype(BF)
        )
    for h in range(g.heads):
        for d in range(ranges):
            side, at = (ctx_own, d) if d < g.chips else (ctx_other, d - g.chips)
            rows = dot(
                place[h, g.rows * d : g.rows * (d + 1)], mixed[h, step * d : step * (d + 1)]
            )
            side[g.rows * at : g.rows * (at + 1), DH * h : DH * (h + 1)] = rows.astype(BF)


def attend_back_kernel(g, own, other, pick, place, kept, probs, grads, d_mixed, found, d_scores):
    step, ranges = g.clusters * g.members, 2 * g.chips
    scale = DH ** (-0.5)
    units = [(h, c) for h in range(g.heads) for c in range(g.clusters)]
    for h in range(g.heads):
        for d in range(ranges):
            side, at = (own, d) if d < g.chips else (other, d - g.chips)
            rows = side[g.rows * at : g.rows * (at + 1), DH * h : DH * (h + 1)]
            slots = slice(step * d, step * (d + 1))
            d_mixed[h, slots] = dot(pick[h, slots], rows).astype(BF)
    for h, c in units:
        v = cluster_rows(g, kept.at[h], c)[:, 2 * DH : 3 * DH]
        share = probs[h * g.clusters + c]
        d_share = dot_nt(cluster_rows(g, d_mixed.at[h], c), v)
        delta = jnp.sum(share * d_share, axis=-1, keepdims=True)
        d_scores[h * g.clusters + c] = (share * (d_share - delta)).astype(BF)
    for h, c in units:
        rows = cluster_rows(g, kept.at[h], c)
        d_s, share = d_scores[h * g.clusters + c], probs[h * g.clusters + c].astype(BF)
        d_q = dot(d_s, rows[:, DH : 2 * DH]) * scale
        d_k = dot_tn(d_s, rows[:, 0:DH]) * scale
        d_v = dot_tn(share, cluster_rows(g, d_mixed.at[h], c))
        put_cluster(g, found.at[h], c, jnp.concatenate([d_q, d_k, d_v], axis=1).astype(BF))
    for h in range(g.heads):
        for d in range(ranges):
            at = slice(g.rows * d, g.rows * (d + 1))
            rows = dot(place[h, at], found[h, step * d : step * (d + 1)]).astype(BF)
            for i in range(3):
                grads[at, g.cols * i + DH * h : g.cols * i + DH * (h + 1)] = rows[
                    :, DH * i : DH * (i + 1)
                ]
    grads[:, g.qkv :] = jnp.zeros((2 * g.tokens, g.wide - g.qkv), BF)


def norm_parts(values):
    centre = values - jnp.mean(values, axis=-1, keepdims=True)
    spread = jnp.mean(centre * centre, axis=-1, keepdims=True)
    scale = lax.rsqrt(spread + EPSILON)
    return centre * scale, scale


def norm_back(grad, z, scale):
    return scale * (
        grad
        - jnp.mean(grad, axis=-1, keepdims=True)
        - z * jnp.mean(grad * z, axis=-1, keepdims=True)
    )


def seen(g, ref, j):
    return jnp.concatenate(
        [ref[g.rows * (i ^ j) : g.rows * ((i ^ j) + 1)] for i in range(g.chips)], axis=0
    )


def forward_kernel(g, sc, *refs):
    c, n = g.chips, g.ring - 1
    ctxs, xs, full = refs[:c], refs[c : 2 * c], refs[2 * c]
    wo_own, wi_own, wd_own = refs[2 * c + 1 : 2 * c + 4]
    refs = refs[2 * c + 4 :]
    mine, theirs = refs[:n], refs[n : 2 * n]
    refs = refs[2 * n :]
    parts, (active, inner, low, z_own, s_own, wo_rows, wi, wd) = refs[:c], refs[c : c + 8]
    wo, work, sem_o, sem_i, sem_d = refs[c + 8 :]
    p = sc[0]
    at = pl.multiple_of(g.block * p, 16)
    copies_o = gathers(g, sc, wo_own, 0, mine, theirs, g.half, g.half, wo, sem_o, p)
    copies_i = gathers(g, sc, wi_own, 0, mine, theirs, 0, g.half, wi, sem_i)
    copies_d = gathers(g, sc, wd_own, at, mine, theirs, 2 * g.half, g.bhalf, wd, sem_d)
    start(copies_o)
    rows = jnp.concatenate([seen(g, ctxs[j], j) for j in range(c)], axis=1)
    finish(copies_o)
    start(copies_i)
    start(copies_d)
    wo_rows[...] = wo[0 : g.cols]
    halves = [slice(i, i + g.tokens // 2) for i in range(0, g.tokens, g.tokens // 2)]
    bias = full[pl.ds(8 + p, 1), :]

    def first_norm(half):
        for i in range(half.start, half.stop, SLAB):
            at = slice(i, i + SLAB)
            x = xs[i // g.rows][i % g.rows : i % g.rows + SLAB].astype(F32)
            z, scale = norm_parts(work[at] + x + full[2:3, :])
            first = z * full[3:4, :] + full[4:5, :]
            low[at] = first.astype(BF)
            if i < g.rows:
                z_own[at] = z
                s_own[at] = jnp.broadcast_to(scale, (SLAB, 128))
                parts[0][at] = first + full[5:6, :]

    def activate(half):
        for i in range(half.start, half.stop, SLAB):
            at = slice(i, i + SLAB)
            u = inner[at] + bias
            inner[at] = u
            active[at] = (u * (1.0 + lax.erf(u * (0.5**0.5))) * 0.5).astype(BF)

    def descend(half):
        second = dot(active[half], wd[...])
        for i in range(half.start, half.stop, g.rows):
            block = second[i - half.start : i - half.start + g.rows]
            if i == 0:
                parts[0][...] += block
            else:
                parts[i // g.rows][...] = block.astype(BF)

    one, two = halves
    work[one] = dot(rows[one], wo[...])
    work[two] = dot(rows[two], wo[...])
    first_norm(one)
    finish(copies_i)
    inner[one] = dot(low[one], wi[...])
    first_norm(two)
    inner[two] = dot(low[two], wi[...])
    activate(one)
    finish(copies_d)
    descend(one)
    activate(two)
    descend(two)


def turn_kernel(g, *refs):
    c = g.chips
    parts, full, cotangent = refs[:c], refs[c], refs[c + 1]
    out, d_second, branch = refs[c + 2 :]
    second = parts[0][...]
    for j in range(1, c):
        second = second + parts[j][...].astype(F32)
    z, scale = norm_parts(second)
    gain = full[6:7, :]
    out[...] = (z * gain + full[7:8, :]).astype(BF)
    dy = cotangent[...].astype(F32)
    grad = norm_back(dy * gain, z, scale)
    d_second[...] = grad
    branch[0 : g.rows] = grad.astype(BF)
    one = jnp.sum(dy * z, axis=0, keepdims=True)
    two = jnp.sum(dy, axis=0, keepdims=True)
    rest = jnp.zeros((VEC - 2, g.width), F32)
    branch[g.rows : g.rows + VEC] = jnp.concatenate([one, two, rest], axis=0).astype(BF)


def back_kernel(g, *refs):
    c = g.chips
    branches, slope, wd, wi = refs[:c], refs[c], refs[c + 1], refs[c + 2]
    parts, d_inner = refs[c + 3 : 2 * c + 3], refs[2 * c + 3]
    rows = jnp.concatenate([b[0 : g.rows] for b in branches], axis=0)
    d_active = dot_nt(rows, wd[...])
    d_inner[...] = (d_active * slope[...]).astype(BF)
    total = dot_nt(d_inner[...], wi[...])
    parts[0][...] = total[: g.rows]
    for j in range(1, c):
        parts[j][...] = total[g.rows * j : g.rows * (j + 1)].astype(BF)


def split_rows(g, sc, total, size, own, other, at):
    k, f = sc[1], sc[2]
    for s in range(g.ring):
        base = 2 * size * jnp.bitwise_xor(f, s)
        own[s, at : at + size] = total[pl.ds(pl.multiple_of(base + size * k, 8), size), :]
        other[s, at : at + size] = total[
            pl.ds(pl.multiple_of(base + size * (1 - k), 8), size), :
        ].astype(BF)


def mlp_grads_kernel(g, sc, *refs):
    c = g.chips
    branches, active, low, d_inner = refs[:c], refs[c], refs[c + 1], refs[c + 2]
    own, other, sums, total = refs[c + 3 :]
    rows = jnp.concatenate([b[0 : g.rows] for b in branches], axis=0)
    total[...] = dot_tn(active[...], rows)
    split_rows(g, sc, total, g.bhalf, own, other, g.half)
    total[...] = dot_tn(low[...], d_inner[...])
    split_rows(g, sc, total, g.half, own, other, 0)
    stats = branches[0][g.rows : g.rows + VEC].astype(F32)
    for j in range(1, c):
        stats = stats + branches[j][g.rows : g.rows + VEC].astype(F32)
    down = jnp.sum(rows.astype(F32), axis=0, keepdims=True)
    up = jnp.sum(d_inner[...].astype(F32), axis=0, keepdims=True)
    sums[...] = jnp.concatenate([stats[0:2], down, up, jnp.zeros((4, g.width), F32)], axis=0)


def first_kernel(g, *refs):
    c = g.chips
    parts, d_second, z_own, s_own, full = refs[:c], *refs[c : c + 4]
    d_sum, attended = refs[c + 4 :]
    d_first = d_second[...] + parts[0][...]
    for j in range(1, c):
        d_first = d_first + parts[j][...].astype(F32)
    z = z_own[...]
    grad = norm_back(d_first * full[3:4, :], z, s_own[:, 0:1])
    d_sum[...] = grad
    attended[0 : g.rows] = grad.astype(BF)
    one = jnp.sum(d_first * z, axis=0, keepdims=True)
    two = jnp.sum(d_first, axis=0, keepdims=True)
    rest = jnp.zeros((VEC - 2, g.width), F32)
    attended[g.rows : g.rows + VEC] = jnp.concatenate([one, two, rest], axis=0).astype(BF)


def context_kernel(g, *refs):
    grads, wo_rows, out = refs[: g.chips], refs[g.chips], refs[g.chips + 1]
    rows = jnp.concatenate([b[0 : g.rows] for b in grads], axis=0)
    out[...] = dot_nt(rows, wo_rows[...]).astype(BF)


def out_grads_kernel(g, sc, *refs):
    c = g.chips
    grads, ctxs, sums = refs[:c], refs[c : 2 * c], refs[2 * c]
    own, away, total = refs[2 * c + 1 :]
    p, f = sc[0], sc[2]
    rows = jnp.concatenate([b[0 : g.rows] for b in grads], axis=0)
    for j in range(c):
        q = jnp.bitwise_xor(p, j)
        total[pl.ds(pl.multiple_of(g.cols * q, 64), g.cols), :] = dot_tn(seen(g, ctxs[j], j), rows)
    stats = grads[0][g.rows : g.rows + VEC].astype(F32)
    for j in range(1, c):
        stats = stats + grads[j][g.rows : g.rows + VEC].astype(F32)
    out = jnp.sum(rows.astype(F32), axis=0, keepdims=True)
    rest = jnp.zeros((VEC - 7, g.width), F32)
    block = jnp.concatenate([sums[0:4], stats[0:2], out, rest], axis=0)
    size = g.shard // c
    for s in range(g.ring):
        base = g.shard * jnp.bitwise_xor(f, s) + size * p
        part = total[pl.ds(pl.multiple_of(base, 8), size), :]
        if s % 2:
            away[s // 2, 0:size] = part.astype(BF)
            away[s // 2, size:] = block.astype(BF)
        else:
            own[s // 2, 0:size] = part
            own[s // 2, size:] = block


def summed(g, mine, theirs, at):
    one = mine[g.tokens * at : g.tokens * (at + 1), : g.qkv].astype(F32)
    two = theirs[g.tokens * (1 - at) : g.tokens * (2 - at), : g.qkv].astype(F32)
    return (one + two).astype(BF)


def input_kernel(g, mine, theirs, w, *parts):
    total = dot_nt(summed(g, mine, theirs, 0), w[...])
    parts[0][...] = total[: g.rows]
    for j in range(1, g.chips):
        parts[j][...] = total[g.rows * j : g.rows * (j + 1)].astype(BF)


def turn_rows_kernel(g, sc, *refs):
    xs, out = refs[: 2 * g.chips], refs[2 * g.chips]
    rows = jnp.concatenate([x[...] for x in xs], axis=0)
    for core in range(2):

        @pl.when(sc[1] == core)
        def _(core=core):
            for r in range(g.ring):
                lane = g.shard * r + g.half * core
                out[g.half * r : g.half * (r + 1), :] = jnp.transpose(rows[:, lane : lane + g.half])


def qkv_grads_kernel(g, sc, mine, theirs, turned_x, own, away, total):
    f = sc[2]
    rows = jnp.concatenate([summed(g, mine, theirs, 0), summed(g, mine, theirs, 1)], axis=0)
    total[...] = dot(turned_x[...], rows)
    sums = jnp.sum(rows.astype(F32), axis=0, keepdims=True)
    gap = jnp.zeros((8, g.width - g.qkv), F32)
    block = jnp.concatenate(
        [jnp.concatenate([sums, jnp.zeros((7, g.qkv), F32)], axis=0), gap], axis=1
    )
    for s in range(g.ring):
        part = total[pl.ds(pl.multiple_of(g.half * jnp.bitwise_xor(f, s), 8), g.half), :]
        packed = pack(g, part)
        if s % 2:
            away[s // 2, 0 : g.packed] = packed.astype(BF)
            away[s // 2, g.packed :] = block.astype(BF)
        else:
            own[s // 2, 0 : g.packed] = packed
            own[s // 2, g.packed :] = block


def pack(g, part):
    step = g.half - g.packed
    beside = [
        part[g.packed :, step_lanes : step_lanes + g.width - g.qkv]
        for step_lanes in range(0, g.qkv, g.width - g.qkv)
    ]
    return jnp.concatenate(
        [part[0 : g.packed], jnp.concatenate(beside, axis=0)], axis=1
    )


def sources(g, sc, refs):
    p, k = sc[0], sc[1]
    out = []
    for j, (mine, theirs) in enumerate(zip(refs, others(g, refs))):
        q = jnp.bitwise_xor(p, j)
        out.append((q, k, mine))
        out.append((q, 1 - k, theirs))
    return out


def others(g, refs):
    far = refs[g.chips :]
    return far if len(far) > 1 else [far[0].at[j] for j in range(g.chips)]


def mlp_final_kernel(g, sc, *refs):
    found, (g_in, g_down) = refs[:-2], refs[-2:]
    for q, core, ref in sources(g, sc, found):
        at = pl.multiple_of(g.block * q + g.bhalf * core, 8)
        g_down[pl.ds(at, g.bhalf), :] = ref[g.half :, :].astype(F32)
        mine = pl.ds(pl.multiple_of(g.half * core, 8), g.half)
        for chip in range(g.chips):

            @pl.when(q == chip)
            def _(chip=chip, ref=ref, mine=mine):
                for r in range(g.ring):
                    lane = g.hshard * r + g.block * chip
                    g_in[mine, lane : lane + g.block] = ref[
                        0 : g.half, g.block * r : g.block * (r + 1)
                    ].astype(F32)


def last_kernel(g, sc, *refs):
    found = refs[: 2 * g.chips]
    gq, gk, gv, g_bq, g_bv, g_out, g_bin, *small = refs[2 * g.chips :]
    p, f = sc[0], sc[2]
    size, step = g.shard // g.chips, g.half - g.packed
    top = g.packed + 8
    for q, core, ref in sources(g, sc, found):

        @pl.when((q == f) & (core == 0))
        def _(ref=ref):
            row = ref[g.packed : top, :].astype(F32)[0:1]
            for dst, at in zip((g_bq, g_bv), (0, 2)):
                dst[...] = row[:, g.cols * at : g.cols * (at + 1)].reshape(g.shard)

        base = pl.multiple_of(g.half * core, 8)
        for chip in range(g.chips):

            @pl.when(q == chip)
            def _(chip=chip, ref=ref, base=base):
                lane = g.cols * chip
                for i, dst in enumerate((gq, gk, gv)):
                    dst[pl.ds(base, g.packed), lane : lane + g.cols] = ref[
                        0 : g.packed, g.cols * i : g.cols * (i + 1)
                    ].astype(F32)
                    dst[pl.ds(base + g.packed, step), lane : lane + g.cols] = ref[
                        step * i : step * (i + 1), g.qkv :
                    ].astype(F32)

    for j in range(g.chips):
        q = jnp.bitwise_xor(p, j)
        one, two = found[j], found[g.chips + j]
        both = one[top:, :].astype(F32) + two[top:, :].astype(F32)
        g_out[pl.ds(pl.multiple_of(size * q, 8), size), :] = both[0:size]
        back = pltpu.roll(both[size : size + VEC], lax.rem(g.width - g.shard * f, g.width), 1)
        for chip in range(g.chips):

            @pl.when(q == chip)
            def _(chip=chip, back=back):
                g_bin[g.block * chip : g.block * (chip + 1)] = back[3:4, : g.shard].reshape(g.shard)
                if chip == 0:
                    for i, dst in zip((0, 1, 2, 4, 5, 6), small):
                        dst[...] = back[i : i + 1, : g.shard].reshape(g.shard)


def to_core(x):
    n = lax.axis_size("ctx")
    return lax.ppermute(x, "ctx", [(i, i ^ 1) for i in range(n)])


def to_chip(x, j):
    n = lax.axis_size("ctx")
    return lax.ppermute(x, "ctx", [(i, i ^ (2 * j)) for i in range(n)])


def along(x, mask):
    n = lax.axis_size("fsdp")
    return lax.ppermute(x, "fsdp", [(i, i ^ mask) for i in range(n)])


def gather_ring(x, pause=None):
    n = lax.axis_size("fsdp")
    found, mask, first = {0: x}, n // 2, ()
    while mask:
        for s in sorted(found):
            first = [found[t] for t in sorted(found) if t]
            part = found[s] if s == 0 or pause is None else after(found[s], pause, *first)
            found[s | mask] = along(part, mask)
        mask //= 2
    return [found[s] for s in range(1, n)]


def spread(x, chips):
    far = {j: to_chip(x, j) for j in sorted(range(1, chips), key=lambda j: -bin(j).count("1"))}
    return [x] + [far[j] for j in range(1, chips)]


def pass_on(x, chips, pause):
    found = {0: x}
    mask = 1
    while mask < chips:
        for j in sorted(found):
            found[j | mask] = to_chip(found[j] if j == 0 else after(found[j], pause), mask)
        mask *= 2
    return [found[j] for j in range(chips)]


def swap(parts):
    far = {j: to_chip(parts[j], j) for j in sorted(range(1, len(parts)), key=lambda j: -bin(j).count("1"))}
    return [parts[0]] + [far[j] for j in range(1, len(parts))]


def ring_step(kept, away, mask):
    count, rows, width = kept.shape
    half = count // 2

    def step(mine, got):
        total = mine + got.astype(F32)
        if not half:
            return (total.astype(BF),)
        return total.reshape(half, 2, rows, width)[:, 0], total.reshape(
            half, 2, rows, width
        )[:, 1].astype(BF)

    outs = [shaped((half, rows, width), F32), shaped((half, rows, width), BF)]
    return mix(
        step,
        outs if half else [shaped((1, rows, width), BF)],
        kept,
        along(away, mask),
        name="ring_step",
    )


def kept_far(x):
    return pltpu.with_memory_space_constraint(x, pltpu.HBM)


def after(x, *first):
    return lax.optimization_barrier((x, *first))[0]


def ring_step(kept, away, mask):
    count, rows, width = kept.shape
    half = count // 2

    def step(mine, got):
        total = mine + got.astype(F32)
        if not half:
            return (total.astype(BF),)
        return total.reshape(half, 2, rows, width)[:, 0], total.reshape(
            half, 2, rows, width
        )[:, 1].astype(BF)

    outs = [shaped((half, rows, width), F32), shaped((half, rows, width), BF)]
    return mix(
        step,
        outs if half else [shaped((1, rows, width), BF)],
        kept,
        along(away, mask),
        name="ring_step",
    )


def kept_far(x):
    return pltpu.with_memory_space_constraint(x, pltpu.HBM)


def after(x, *first):
    return lax.optimization_barrier((x, *first))[0]


def plane_pieces(piece, chips):
    near = spread(piece, chips)
    return near + [to_core(part) for part in near]


def chip_body(
    hidden_in,
    out_grad,
    block_ids,
    clusters,
    w_query,
    w_key,
    w_value,
    w_out,
    b_query,
    b_value,
    b_out,
    ln1_gain,
    ln1_bias,
    w_in,
    b_in,
    w_down,
    b_down,
    ln2_gain,
    ln2_bias,
):
    n, ring = lax.axis_size("ctx"), lax.axis_size("fsdp")
    chips = n // 2
    rows, width = hidden_in.shape[1:]
    hidden = w_in.shape[1]
    g = Plan(chips, ring, width, hidden, rows)
    c, f = lax.axis_index("ctx"), lax.axis_index("fsdp")
    p, k = c // 2, c % 2
    sc = jnp.stack([p, k, f]).astype(jnp.int32)
    bind = functools.partial

    gate = pltpu.SemaphoreType.DMA((2 * ring - 1,))

    qall, qsend, vec = call(
        bind(pick_kernel, g),
        [
            shaped((g.shard, g.qkv), BF),
            shaped((g.half + VEC, g.qkv), BF),
            shaped((VEC, LANES), BF),
        ],
        [SMEM] + [FAR] * 12,
        [
            sc,
            *map(
                kept_far,
                (
                    w_query,
                    w_key,
                    w_value,
                    b_query,
                    b_value,
                    b_out,
                    ln1_gain,
                    ln1_bias,
                    b_down,
                    ln2_gain,
                    ln2_bias,
                    b_in,
                ),
            ),
        ],
        [
            pltpu.VMEM((3, g.shard, width), BF),
        ]
        + [pltpu.VMEM((g.shard,), BF)] * 8
        + [pltpu.VMEM((g.hshard,), BF), pltpu.SemaphoreType.DMA((12,))],
        name="pick_weights",
    )
    q_mine = gather_ring(qsend)
    x_own = after(hidden_in.reshape(rows, width), qsend)
    xs = spread(x_own, chips)
    iall, send = call(
        bind(prep_kernel, g),
        [
            shaped((g.shard, g.share), BF),
            shaped((2 * g.half + g.bhalf, width), BF),
        ],
        [SMEM, HBM, FAR, FAR, FAR],
        [sc, qsend, kept_far(w_in), kept_far(w_down), kept_far(w_out)],
        [pltpu.VMEM((g.shard, hidden), BF), pltpu.SemaphoreType.DMA((3,))],
        name="prepare_weights",
    )

    step = g.clusters * g.members
    pick, place, blk = call(
        bind(tables_kernel, g),
        [
            shaped((g.heads, 2 * chips * step, rows), BF),
            shaped((g.heads, 2 * g.tokens, step), BF),
            shaped((8, 2 * g.tokens), BF),
        ],
        [SMEM, HBM] + [VMEM] * 2,
        [sc, q_mine[-1], clusters[0], block_ids],
        name="cluster_tables",
    )
    (mask,) = call(
        bind(mask_kernel, g),
        [shaped((g.heads * g.clusters, CLUSTER, CLUSTER), F32)],
        [VMEM] * 2,
        [blk, place],
        name="cluster_mask",
    )
    x_other = [to_core(after(xs[0], xs[1]))] + [to_core(x) for x in xs[1:]]
    q_theirs = [to_core(after(part, *xs[1:])) for part in q_mine]
    qkv, w_qkv, full = call(
        bind(qkv_kernel, g),
        [
            shaped((2 * g.tokens, g.padded), BF),
            shaped((width, g.qkv), BF),
            shaped((VEC, width), F32),
        ],
        [SMEM] + [VMEM] * (2 * chips + 1) + [HBM] * (2 * ring - 1),
        [sc, *xs, *x_other, after(vec, pick), qall, *q_mine, *q_theirs],
        [
            pltpu.VMEM((ring - 1, VEC, LANES), BF),
            gate,
            pltpu.SemaphoreType.DMA((ring - 1,)),
        ],
        name="project",
    )
    ctx_own, ctx_other, kept, probs = call(
        bind(attend_kernel, g),
        [
            shaped((g.tokens, g.cols), BF),
            shaped((g.tokens, g.cols), BF),
            shaped((g.heads, g.entries, LANES), BF),
            shaped((g.heads * g.clusters, CLUSTER, CLUSTER), F32),
        ],
        [VMEM] * 4,
        [qkv, pick, place, mask],
        [pltpu.VMEM((g.heads, g.entries, DH), BF)],
        name="attend",
    )
    (ctx,) = mix(
        lambda a, b: (a + b,),
        [shaped((g.tokens, g.cols), BF)],
        ctx_own,
        to_core(ctx_other),
        name="join_context",
    )
    ctxs = spread(ctx, chips)
    w_mine = gather_ring(send, ctx)

    w_theirs = [to_core(after(part, *ctxs[1:])) for part in w_mine]
    *second, active, inner, low, z_own, s_own, wo_rows, wi, wd = call(
        bind(forward_kernel, g),
        [shaped((rows, width), F32)]
        + [shaped((rows, width), BF)] * (chips - 1)
        + [
            shaped((g.tokens, g.share), BF),
            shaped((g.tokens, g.share), F32),
            shaped((g.tokens, width), BF),
            shaped((rows, width), F32),
            shaped((rows, 128), F32),
            shaped((g.cols, width), BF),
            shaped((width, g.share), BF),
            shaped((g.share, width), BF),
        ],
        [SMEM] + [VMEM] * (2 * chips + 1) + [FAR, HBM, FAR] + [HBM] * (2 * ring - 2),
        [sc, *ctxs, *xs, full, kept_far(w_out), iall, kept_far(w_down), *w_mine, *w_theirs],
        [pltpu.VMEM((width, width), BF), pltpu.VMEM((g.tokens, width), F32), gate, gate, gate],
        name="mlp_forward",
    )
    (slope,) = mix(
        lambda u: (
            0.5 * (1.0 + lax.erf(u * (0.5**0.5)))
            + u * jnp.exp(-0.5 * u * u) * (1.0 / (2.0 * math.pi) ** 0.5),
        ),
        [shaped((g.tokens, g.share), F32)],
        inner,
        name="gelu_slope",
    )
    (turned_x,) = call(
        bind(turn_rows_kernel, g),
        [shaped((ring * g.half, 2 * g.tokens), BF)],
        [SMEM] + [VMEM] * (2 * chips),
        [sc, after(xs[0], inner), *xs[1:], *x_other],
        name="turn_rows",
    )
    second = swap(second)
    layer_out, d_second, branch = call(
        bind(turn_kernel, g),
        [
            shaped((rows, width), BF),
            shaped((rows, width), F32),
            shaped((rows + VEC, width), BF),
        ],
        [VMEM] * (chips + 2),
        [*second, after(full, turned_x), out_grad.reshape(rows, width)],
        name="norm_two",
    )
    branches = spread(branch, chips)
    *d_first, d_inner = call(
        bind(back_kernel, g),
        [shaped((rows, width), F32)]
        + [shaped((rows, width), BF)] * (chips - 1)
        + [shaped((g.tokens, g.share), BF)],
        [VMEM] * (chips + 3),
        [*branches, slope, wd, wi],
        name="mlp_back",
    )
    d_first = swap(d_first)
    m_own, m_other, sums = call(
        bind(mlp_grads_kernel, g),
        [
            shaped((ring, g.half + g.bhalf, width), F32),
            shaped((ring, g.half + g.bhalf, width), BF),
            shaped((8, width), F32),
        ],
        [SMEM] + [VMEM] * (chips + 3),
        [sc, *branches, active, low, d_inner],
        [pltpu.VMEM((width, g.share), F32)],
        name="mlp_grads",
    )
    m_got = to_core(m_other)
    m_rows = g.half + g.bhalf

    def joined(own, got):
        total = own + got.astype(F32)
        return (total[0], *(total[s].astype(BF) for s in range(1, ring)))

    m_kept, *m_away = mix(
        joined,
        [shaped((m_rows, width), F32)] + [shaped((m_rows, width), BF)] * (ring - 1),
        m_own,
        m_got,
        name="join_grads",
    )
    (m_piece,) = mix(
        lambda kept, *parts: (sum((part.astype(F32) for part in parts), kept).astype(BF),),
        [shaped((m_rows, width), BF)],
        m_kept,
        *(along(part, s) for s, part in enumerate(m_away, 1)),
        name="mlp_sum",
    )
    d_sum, attended = call(
        bind(first_kernel, g),
        [shaped((rows, width), F32), shaped((rows + VEC, width), BF)],
        [VMEM] * (chips + 4),
        [*d_first, after(d_second, *m_away), z_own, s_own, full],
        name="norm_one",
    )
    grads = spread(attended, chips)
    (d_ctx,) = call(
        bind(context_kernel, g),
        [shaped((g.tokens, g.cols), BF)],
        [VMEM] * (chips + 1),
        [*grads, after(wo_rows, m_piece)],
        name="context_back",
    )
    d_ctx_other = to_core(d_ctx)
    o_rows = g.shard // chips + VEC
    o_own, o_away = call(
        bind(out_grads_kernel, g),
        [shaped((ring // 2, o_rows, width), F32), shaped((ring // 2, o_rows, width), BF)],
        [SMEM] + [VMEM] * (2 * chips + 1),
        [sc, *grads, *ctxs, sums],
        [pltpu.VMEM((width, width), F32)],
        name="out_grads",
    )
    (dq_mine,) = call(
        bind(attend_back_kernel, g),
        [shaped((2 * g.tokens, g.wide), BF)],
        [VMEM] * 6,
        [d_ctx, d_ctx_other, pick, place, after(kept, o_own), probs],
        [
            pltpu.VMEM((g.heads, g.entries, DH), BF),
            pltpu.VMEM((g.heads, g.entries, 3 * DH), BF),
            pltpu.VMEM((g.heads * g.clusters, CLUSTER, CLUSTER), BF),
        ],
        name="attend_back",
    )
    dq_theirs = to_core(dq_mine)
    q_rows = g.packed + 8
    q_own, q_away = call(
        bind(qkv_grads_kernel, g),
        [shaped((ring // 2, q_rows, width), F32), shaped((ring // 2, q_rows, width), BF)],
        [SMEM] + [VMEM] * 3,
        [sc, dq_mine, dq_theirs, turned_x],
        [pltpu.VMEM((ring * g.half, g.qkv), F32)],
        name="project_grads",
    )
    d_in = call(
        bind(input_kernel, g),
        [shaped((rows, width), F32)] + [shaped((rows, width), BF)] * (chips - 1),
        [VMEM] * 3,
        [dq_mine, dq_theirs, w_qkv],
        name="project_back",
    )
    d_in = swap(d_in)
    mask_at = 2
    q_away0 = q_away
    o_away = after(o_away, dq_mine)
    while q_own.shape[0] > 1:
        q_own, q_away = ring_step(q_own, q_away, mask_at // 2)
        o_own, o_away = ring_step(o_own, o_away, mask_at // 2)
        mask_at *= 2
    near = spread(m_piece, chips)
    m_pieces = near + [to_core(after(part, q_away)) for part in near]
    (input_grad,) = mix(
        lambda kept, *parts: (sum((part.astype(F32) for part in parts), kept).astype(BF),),
        [shaped((rows, width), BF)],
        d_sum,
        *d_in,
        name="input_sum",
    )
    g_in, g_down = call(
        bind(mlp_final_kernel, g),
        [shaped((g.shard, hidden), F32), shaped((g.hshard, width), F32)],
        [SMEM] + [VMEM] * len(m_pieces),
        [sc, *m_pieces],
        name="mlp_lay",
    )
    vector = shaped((g.shard,), F32)
    (piece,) = mix(
        lambda a, b, c, d: (
            jnp.concatenate([a[0] + b[0].astype(F32), c[0] + d[0].astype(F32)], axis=0).astype(BF),
        ),
        [shaped((q_rows + o_rows, width), BF)],
        q_own,
        along(q_away, mask_at // 2),
        o_own,
        along(o_away, mask_at // 2),
        name="last_sum",
    )
    near = spread(piece, chips)
    pieces = near + [to_core(after(part, input_grad, g_down)) for part in near]
    found = call(
        bind(last_kernel, g),
        [shaped((g.shard, width), F32)] * 3
        + [vector] * 2
        + [shaped((g.shard, width), F32), shaped((g.hshard,), F32)]
        + [vector] * 6,
        [SMEM] + [VMEM] * (2 * chips),
        [sc, *pieces],
        name="last_lay",
    )
    gq, gk, gv, g_bq, g_bv, g_out, g_bin, g_gain2, g_bias2, g_bdown, g_gain1, g_bias1, g_bout = found
    return (
        layer_out.reshape(1, rows, width),
        input_grad.reshape(1, rows, width),
        gq,
        gk,
        gv,
        g_out,
        g_bq,
        g_bv,
        g_bout,
        g_gain1,
        g_bias1,
        g_in,
        g_bin,
        g_down,
        g_bdown,
        g_gain2,
        g_bias2,
    )


def fits(mesh):
    n, ring = mesh.shape["ctx"], mesh.shape["fsdp"]
    chips = n // 2
    return n % 2 == 0 and chips & (chips - 1) == 0 and chips > 1 and ring == chips and H % chips == 0 and ring * chips <= 16


def solution(mesh):
    in_specs = (
        P("fsdp", "ctx", None),
        P("fsdp", "ctx", None),
        P("fsdp", None),
        P("fsdp", None, None),
        P("fsdp", None),
        P("fsdp", None),
        P("fsdp", None),
        P("fsdp", None),
        P("fsdp"),
        P("fsdp"),
        P("fsdp"),
        P("fsdp"),
        P("fsdp"),
        P("fsdp", None),
        P("fsdp"),
        P("fsdp", None),
        P("fsdp"),
        P("fsdp"),
        P("fsdp"),
    )
    out_specs = (
        P("fsdp", "ctx", None),
        P("fsdp", "ctx", None),
        P("fsdp", None),
        P("fsdp", None),
        P("fsdp", None),
        P("fsdp", None),
        P("fsdp"),
        P("fsdp"),
        P("fsdp"),
        P("fsdp"),
        P("fsdp"),
        P("fsdp", None),
        P("fsdp"),
        P("fsdp", None),
        P("fsdp"),
        P("fsdp"),
        P("fsdp"),
    )
    body = chip_body if fits(mesh) else general_body
    return jax.shard_map(body, mesh=mesh, in_specs=in_specs, out_specs=out_specs, check_vma=False)
```

```python
import functools
import math

import jax
import jax.numpy as jnp
from jax import lax
from jax.experimental import pallas as pl
from jax.experimental.pallas import tpu as pltpu
from jax.sharding import PartitionSpec as P

H = 12
DH = 64
CLUSTER = 128


EPSILON = 1e-12
FLOOR = -1e30


def layer_norm(values, gain, shift):
    centre = values - jnp.mean(values, axis=-1, keepdims=True)
    spread = jnp.mean(centre * centre, axis=-1, keepdims=True)
    return centre * lax.rsqrt(spread + EPSILON) * gain + shift


def exact_gelu(values):
    return jax.nn.gelu(values, approximate=False)


def positions(length, per_device, parts):
    stored = jnp.arange(length, dtype=jnp.int32)
    device = stored // per_device
    within = stored % per_device
    half = per_device // 2
    return jnp.where(
        within < half, device * half + within, (2 * parts - 1 - device) * half + within - half
    )


def contract(left, right):
    return lax.dot_general(
        left, right, (((0,), (0,)), ((), ())), preferred_element_type=jnp.float32
    )


def back_product(grad, weight):
    return lax.dot_general(
        grad, weight, (((1,), (1,)), ((), ())), preferred_element_type=jnp.float32
    )


def column_sum(values):
    return jnp.sum(values.astype(jnp.float32), axis=0)


def per_head_rows(rows, index):
    split = rows.reshape(rows.shape[0], H, DH)
    return jnp.take_along_axis(split, index.T[:, :, None], axis=0)


def cluster_tables(order, device, per_device, parts):
    heads, length = order.shape
    groups = length // CLUSTER
    members = CLUSTER // parts
    mine = (order // per_device == device).astype(jnp.int32)
    rank = jnp.cumsum(mine.reshape(heads, groups, CLUSTER), axis=-1).reshape(heads, length) - 1
    entry = jnp.arange(length, dtype=jnp.int32)[None, :]
    slot = jnp.where(mine == 1, entry // CLUSTER * members + rank, per_device)
    head_index = jnp.arange(heads, dtype=jnp.int32)[:, None]
    picked = (
        jnp.zeros((heads, per_device), jnp.int32)
        .at[head_index, slot]
        .set(order - device * per_device, mode="drop")
    )
    counter = jnp.broadcast_to(
        jnp.arange(per_device, dtype=jnp.int32)[None, :], (heads, per_device)
    )
    placed = jnp.zeros((heads, per_device), jnp.int32).at[head_index, picked].set(counter)
    inverse = (
        jnp.zeros((heads, length), jnp.int32)
        .at[head_index, order]
        .set(jnp.broadcast_to(jnp.arange(length, dtype=jnp.int32)[None, :], (heads, length)))
    )
    return (picked, placed, inverse)


def score_blocks(query, key_rows, query_blocks, key_blocks, scale):
    scores = (
        jnp.einsum("cqhd,ckhd->hcqk", query, key_rows, preferred_element_type=jnp.float32) * scale
    )
    allowed = key_blocks[:, :, None, :] <= query_blocks[:, :, :, None]
    return (scores, allowed)


def attend(query, key_rows, value_rows, query_blocks, key_blocks, scale):
    scores, allowed = score_blocks(query, key_rows, query_blocks, key_blocks, scale)
    masked = jnp.where(allowed, scores, FLOOR)
    top = jnp.max(masked, axis=-1, keepdims=True)
    weights = jnp.where(allowed, jnp.exp(masked - top), 0.0)
    total = jnp.sum(weights, axis=-1, keepdims=True)
    probs = (weights / total).astype(jnp.bfloat16)
    mixed = jnp.einsum("hcqk,ckhd->cqhd", probs, value_rows, preferred_element_type=jnp.float32)
    return (mixed.astype(jnp.bfloat16), top + jnp.log(total))


def attend_back(query, key_rows, value_rows, query_blocks, key_blocks, logsum, d_mixed, scale):
    scores, allowed = score_blocks(query, key_rows, query_blocks, key_blocks, scale)
    probs = jnp.where(allowed, jnp.exp(jnp.where(allowed, scores, FLOOR) - logsum), 0.0)
    rounded = probs.astype(jnp.bfloat16)
    d_probs = jnp.einsum("cqhd,ckhd->hcqk", d_mixed, value_rows, preferred_element_type=jnp.float32)
    centred = jnp.sum(probs * d_probs, axis=-1, keepdims=True)
    d_scores = (probs * (d_probs - centred)).astype(jnp.bfloat16)
    d_query = (
        jnp.einsum("hcqk,ckhd->cqhd", d_scores, key_rows, preferred_element_type=jnp.float32)
        * scale
    )
    d_key = (
        jnp.einsum("hcqk,cqhd->ckhd", d_scores, query, preferred_element_type=jnp.float32) * scale
    )
    d_value = jnp.einsum("hcqk,cqhd->ckhd", rounded, d_mixed, preferred_element_type=jnp.float32)
    return (d_query, d_key, d_value)


def general_body(
    hidden_in,
    out_grad,
    block_ids,
    clusters,
    w_query,
    w_key,
    w_value,
    w_out,
    b_query,
    b_value,
    b_out,
    ln1_gain,
    ln1_bias,
    w_in,
    b_in,
    w_down,
    b_down,
    ln2_gain,
    ln2_bias,
):
    parts = lax.axis_size("ctx")
    device = lax.axis_index("ctx")
    sequences, per_device, width = hidden_in.shape
    length = per_device * parts
    members = CLUSTER // parts
    groups = length // CLUSTER
    scale = DH ** (-0.5)
    (
        full_query,
        full_key,
        full_value,
        full_out,
        bias_query,
        bias_value,
        bias_out,
        gain_one,
        shift_one,
    ) = (
        lax.all_gather(w_query, "fsdp", axis=0, tiled=True),
        lax.all_gather(w_key, "fsdp", axis=0, tiled=True),
        lax.all_gather(w_value, "fsdp", axis=0, tiled=True),
        lax.all_gather(w_out, "fsdp", axis=0, tiled=True),
        lax.all_gather(b_query, "fsdp", axis=0, tiled=True),
        lax.all_gather(b_value, "fsdp", axis=0, tiled=True),
        lax.all_gather(b_out, "fsdp", axis=0, tiled=True),
        lax.all_gather(ln1_gain, "fsdp", axis=0, tiled=True),
        lax.all_gather(ln1_bias, "fsdp", axis=0, tiled=True),
    )
    full_in, full_down, bias_in, bias_down, gain_two, shift_two = (
        lax.all_gather(w_in, "fsdp", axis=0, tiled=True),
        lax.all_gather(w_down, "fsdp", axis=0, tiled=True),
        lax.all_gather(b_in, "fsdp", axis=0, tiled=True),
        lax.all_gather(b_down, "fsdp", axis=0, tiled=True),
        lax.all_gather(ln2_gain, "fsdp", axis=0, tiled=True),
        lax.all_gather(ln2_bias, "fsdp", axis=0, tiled=True),
    )
    hidden = hidden_in.reshape(sequences * per_device, width)
    query_rows = (
        jnp.dot(hidden, full_query, preferred_element_type=jnp.float32) + bias_query
    ).astype(jnp.bfloat16)
    key_rows = jnp.dot(hidden, full_key, preferred_element_type=jnp.float32).astype(jnp.bfloat16)
    value_rows = (
        jnp.dot(hidden, full_value, preferred_element_type=jnp.float32) + bias_value
    ).astype(jnp.bfloat16)
    place = positions(length, per_device, parts)
    index = 0
    order = clusters[index]
    stored_blocks = block_ids[index][place]
    picked, placed, inverse = cluster_tables(order, device, per_device, parts)
    q_local = per_head_rows(query_rows, picked).reshape(groups, members, H, DH)
    query_blocks = stored_blocks[device * per_device + picked].reshape(H, groups, members)
    key_all = lax.all_gather(key_rows, "ctx", axis=0, tiled=True)
    value_all = lax.all_gather(value_rows, "ctx", axis=0, tiled=True)
    key_cluster = per_head_rows(key_all, order).reshape(groups, CLUSTER, H, DH)
    value_cluster = per_head_rows(value_all, order).reshape(groups, CLUSTER, H, DH)
    key_blocks = stored_blocks[order].reshape(H, groups, CLUSTER)
    mixed, logsum = attend(q_local, key_cluster, value_cluster, query_blocks, key_blocks, scale)
    contexts = per_head_rows(mixed.reshape(per_device, width), placed).reshape(per_device, width)
    kept = [
        (
            q_local,
            key_cluster,
            value_cluster,
            query_blocks,
            key_blocks,
            logsum,
            picked,
            placed,
            inverse,
        )
    ]
    attended = jnp.dot(contexts, full_out, preferred_element_type=jnp.float32) + bias_out
    first_sum = hidden.astype(jnp.float32) + attended
    first, first_pull = jax.vjp(
        layer_norm, first_sum, gain_one.astype(jnp.float32), shift_one.astype(jnp.float32)
    )
    first_low = first.astype(jnp.bfloat16)
    inner = jnp.dot(first_low, full_in, preferred_element_type=jnp.float32) + bias_in
    active_full, gelu_pull = jax.vjp(exact_gelu, inner)
    active = active_full.astype(jnp.bfloat16)
    second_sum = first + jnp.dot(active, full_down, preferred_element_type=jnp.float32) + bias_down
    second, second_pull = jax.vjp(
        layer_norm, second_sum, gain_two.astype(jnp.float32), shift_two.astype(jnp.float32)
    )
    layer_out = second.astype(jnp.bfloat16).reshape(sequences, per_device, width)
    d_out = out_grad.reshape(sequences * per_device, width).astype(jnp.float32)
    d_second, g_gain_two, g_shift_two = second_pull(d_out)
    d_branch = d_second.astype(jnp.bfloat16)
    g_w_down = contract(active, d_branch)
    g_b_down = column_sum(d_branch)
    d_active = back_product(d_branch, full_down)
    d_inner = gelu_pull(d_active)[0].astype(jnp.bfloat16)
    g_w_in = contract(first_low, d_inner)
    g_b_in = column_sum(d_inner)
    d_first = d_second + back_product(d_inner, full_in)
    d_sum, g_gain_one, g_shift_one = first_pull(d_first)
    d_attended = d_sum.astype(jnp.bfloat16)
    g_w_out = contract(contexts, d_attended)
    g_b_out = column_sum(d_attended)
    d_context = back_product(d_attended, full_out).astype(jnp.bfloat16)
    index = 0
    q_kept, k_kept, v_kept, blocks_q, blocks_k, logsum, picked, placed, inverse = kept[index]
    d_cluster = per_head_rows(d_context, picked).reshape(groups, members, H, DH)
    d_query, d_key, d_value = attend_back(
        q_kept, k_kept, v_kept, blocks_q, blocks_k, logsum, d_cluster, scale
    )
    key_full = per_head_rows(d_key.reshape(length, width), inverse).reshape(length, width)
    value_full = per_head_rows(d_value.reshape(length, width), inverse).reshape(length, width)
    key_part = lax.psum_scatter(
        key_full.astype(jnp.bfloat16), "ctx", scatter_dimension=0, tiled=True
    )
    value_part = lax.psum_scatter(
        value_full.astype(jnp.bfloat16), "ctx", scatter_dimension=0, tiled=True
    )
    query_local = d_query.astype(jnp.bfloat16).reshape(per_device, width)
    query_grads = per_head_rows(query_local, placed).reshape(per_device, width)
    g_w_query = contract(hidden, query_grads)
    g_b_query = column_sum(query_grads)
    g_w_key = contract(hidden, key_part)
    g_w_value = contract(hidden, value_part)
    g_b_value = column_sum(value_part)
    input_total = (
        d_sum
        + back_product(query_grads, full_query)
        + back_product(key_part, full_key)
        + back_product(value_part, full_value)
    )
    input_grad = input_total.astype(jnp.bfloat16).reshape(sequences, per_device, width)
    shares = (
        lax.psum_scatter(
            g_w_query.astype(jnp.bfloat16), "fsdp", scatter_dimension=0, tiled=True
        ).astype(jnp.float32),
        lax.psum_scatter(
            g_w_key.astype(jnp.bfloat16), "fsdp", scatter_dimension=0, tiled=True
        ).astype(jnp.float32),
        lax.psum_scatter(
            g_w_value.astype(jnp.bfloat16), "fsdp", scatter_dimension=0, tiled=True
        ).astype(jnp.float32),
        lax.psum_scatter(
            g_w_out.astype(jnp.bfloat16), "fsdp", scatter_dimension=0, tiled=True
        ).astype(jnp.float32),
        lax.psum_scatter(
            g_b_query.astype(jnp.bfloat16), "fsdp", scatter_dimension=0, tiled=True
        ).astype(jnp.float32),
        lax.psum_scatter(
            g_b_value.astype(jnp.bfloat16), "fsdp", scatter_dimension=0, tiled=True
        ).astype(jnp.float32),
        lax.psum_scatter(
            g_b_out.astype(jnp.bfloat16), "fsdp", scatter_dimension=0, tiled=True
        ).astype(jnp.float32),
        lax.psum_scatter(
            g_gain_one.astype(jnp.bfloat16), "fsdp", scatter_dimension=0, tiled=True
        ).astype(jnp.float32),
        lax.psum_scatter(
            g_shift_one.astype(jnp.bfloat16), "fsdp", scatter_dimension=0, tiled=True
        ).astype(jnp.float32),
        lax.psum_scatter(
            g_w_in.astype(jnp.bfloat16), "fsdp", scatter_dimension=0, tiled=True
        ).astype(jnp.float32),
        lax.psum_scatter(
            g_b_in.astype(jnp.bfloat16), "fsdp", scatter_dimension=0, tiled=True
        ).astype(jnp.float32),
        lax.psum_scatter(
            g_w_down.astype(jnp.bfloat16), "fsdp", scatter_dimension=0, tiled=True
        ).astype(jnp.float32),
        lax.psum_scatter(
            g_b_down.astype(jnp.bfloat16), "fsdp", scatter_dimension=0, tiled=True
        ).astype(jnp.float32),
        lax.psum_scatter(
            g_gain_two.astype(jnp.bfloat16), "fsdp", scatter_dimension=0, tiled=True
        ).astype(jnp.float32),
        lax.psum_scatter(
            g_shift_two.astype(jnp.bfloat16), "fsdp", scatter_dimension=0, tiled=True
        ).astype(jnp.float32),
    )
    totals = (
        lax.psum(shares[0].astype(jnp.bfloat16), "ctx").astype(jnp.float32),
        lax.psum(shares[1].astype(jnp.bfloat16), "ctx").astype(jnp.float32),
        lax.psum(shares[2].astype(jnp.bfloat16), "ctx").astype(jnp.float32),
        lax.psum(shares[3].astype(jnp.bfloat16), "ctx").astype(jnp.float32),
        lax.psum(shares[4].astype(jnp.bfloat16), "ctx").astype(jnp.float32),
        lax.psum(shares[5].astype(jnp.bfloat16), "ctx").astype(jnp.float32),
        lax.psum(shares[6].astype(jnp.bfloat16), "ctx").astype(jnp.float32),
        lax.psum(shares[7].astype(jnp.bfloat16), "ctx").astype(jnp.float32),
        lax.psum(shares[8].astype(jnp.bfloat16), "ctx").astype(jnp.float32),
        lax.psum(shares[9].astype(jnp.bfloat16), "ctx").astype(jnp.float32),
        lax.psum(shares[10].astype(jnp.bfloat16), "ctx").astype(jnp.float32),
        lax.psum(shares[11].astype(jnp.bfloat16), "ctx").astype(jnp.float32),
        lax.psum(shares[12].astype(jnp.bfloat16), "ctx").astype(jnp.float32),
        lax.psum(shares[13].astype(jnp.bfloat16), "ctx").astype(jnp.float32),
        lax.psum(shares[14].astype(jnp.bfloat16), "ctx").astype(jnp.float32),
    )
    return (
        layer_out,
        input_grad,
        totals[0],
        totals[1],
        totals[2],
        totals[3],
        totals[4],
        totals[5],
        totals[6],
        totals[7],
        totals[8],
        totals[9],
        totals[10],
        totals[11],
        totals[12],
        totals[13],
        totals[14],
    )


BF = jnp.bfloat16
F32 = jnp.float32
LANES = 256
VMEM = pl.BlockSpec(memory_space=pltpu.VMEM)
HBM = pl.BlockSpec(memory_space=pl.ANY)
FAR = pl.BlockSpec(memory_space=pltpu.HBM)
SMEM = pl.BlockSpec(memory_space=pltpu.SMEM)
VEC = 16
SLAB = 64


def shaped(shape, dtype):
    return jax.ShapeDtypeStruct(shape, dtype)


def call(kernel, outs, ins, args, scratch=(), name=None, weight=1):
    moved = sum(a.size * a.dtype.itemsize for a in args)
    moved += sum(o.size * o.dtype.itemsize for o in outs)
    held = sum(
        math.prod(r.shape) * jnp.dtype(r.dtype).itemsize
        for r in scratch
        if jnp.issubdtype(r.dtype, jnp.number)
    )
    return pl.pallas_call(
        kernel,
        out_shape=outs,
        in_specs=ins,
        out_specs=[VMEM] * len(outs),
        scratch_shapes=list(scratch),
        name=name,
        cost_estimate=pl.CostEstimate(flops=weight, transcendentals=0, bytes_accessed=weight),
        compiler_params=pltpu.CompilerParams(vmem_limit_bytes=moved + held + (4 << 20)),
    )(*args)


def mix(function, outs, *args, name=None):
    def kernel(*refs):
        found = function(*(ref[...] for ref in refs[: len(args)]))
        for ref, value in zip(refs[len(args) :], found):
            ref[...] = value

    return call(kernel, outs, [VMEM] * len(args), args, name=name)


def dot(left, right):
    return jnp.dot(left, right, preferred_element_type=F32)


def dot_nt(left, right):
    return lax.dot_general(left, right, (((1,), (1,)), ((), ())), preferred_element_type=F32)


def dot_tn(left, right):
    return lax.dot_general(left, right, (((0,), (0,)), ((), ())), preferred_element_type=F32)


class Plan:
    def __init__(self, chips, ring, width, hidden, per_device):
        self.chips, self.ring, self.width, self.hidden = chips, ring, width, hidden
        self.rows = per_device
        self.tokens = chips * per_device
        self.shard = width // ring
        self.half = self.shard // 2
        self.share = hidden // chips
        self.hshard = hidden // ring
        self.block = self.hshard // chips
        self.bhalf = self.block // 2
        self.heads = H // chips
        self.cols = self.heads * DH
        self.qkv = 3 * self.cols
        self.padded = self.heads * LANES
        self.wide = -(-self.qkv // 128) * 128
        self.packed = self.half * self.qkv // width
        self.clusters = chips
        self.members = CLUSTER // (2 * chips)
        self.entries = chips * CLUSTER


def pick_kernel(g, sc, *refs):
    weights, small = refs[:3], refs[3:12]
    qall, qsend, vec, here, *lines, sem = refs[12:]
    p, k = sc[0], sc[1]
    copies = [
        pltpu.make_async_copy(w, here.at[i], sem.at[i]) for i, w in enumerate(weights)
    ]
    copies += [
        pltpu.make_async_copy(ref, lines[i], sem.at[3 + i])
        for i, ref in enumerate(small)
    ]
    start(copies)
    finish(copies)
    for q in range(g.chips):

        @pl.when(p == q)
        def _(q=q):
            for i in range(3):
                qall[:, g.cols * i : g.cols * (i + 1)] = here[
                    i, :, g.cols * q : g.cols * (q + 1)
                ]

    vec[...] = jnp.zeros((VEC, LANES), BF)
    for i in range(8):
        vec[i : i + 1, 0 : g.shard] = lines[i][...].reshape(1, g.shard)
    for q in range(g.chips):
        vec[8 + q : 9 + q, 0 : g.block] = lines[8][g.block * q : g.block * (q + 1)].reshape(
            1, g.block
        )
    mine = pl.ds(pl.multiple_of(g.half * k, 16), g.half)
    qsend[0 : g.half] = qall[mine]
    qsend[g.half : g.half + VEC, 0:LANES] = vec[...]
    qsend[g.half : g.half + VEC, LANES:] = jnp.zeros((VEC, g.qkv - LANES), BF)


def prep_kernel(g, sc, _, wi, wd, wo, iall, oall, dall, send, here, sem):
    p, k = sc[0], sc[1]
    at = pl.multiple_of(g.block * p, 16)
    copies = [
        pltpu.make_async_copy(wi, here, sem.at[0]),
        pltpu.make_async_copy(wo, oall, sem.at[1]),
        pltpu.make_async_copy(wd.at[pl.ds(at, g.block)], dall, sem.at[2]),
    ]
    start(copies)
    finish(copies[:1])
    for q in range(g.chips):

        @pl.when(p == q)
        def _(q=q):
            for r in range(g.ring):
                src = g.hshard * r + g.block * q
                iall[:, g.block * r : g.block * (r + 1)] = here[:, src : src + g.block]

    mine = pl.ds(pl.multiple_of(g.half * k, 16), g.half)
    send[0 : g.half] = iall[mine]
    finish(copies[1:])
    send[g.half : 2 * g.half] = oall[mine]
    send[2 * g.half :] = dall[pl.ds(pl.multiple_of(g.bhalf * k, 16), g.bhalf)]


def lay(g, sc, own, mine, theirs, at, size, dst, turn=0):
    k, f = sc[1], jnp.bitwise_xor(sc[2], turn)
    dst[pl.ds(pl.multiple_of(2 * size * f, 16), 2 * size), :] = own[...]
    for s in range(1, g.ring):
        base = 2 * size * jnp.bitwise_xor(f, s)
        for src, core in ((mine[s - 1], k), (theirs[s - 1], 1 - k)):
            dst[pl.ds(pl.multiple_of(base + size * core, 16), size), :] = src[at : at + size, :]


def start(copies):
    for copy in copies:
        copy.start()


def finish(copies):
    for copy in copies:
        copy.wait()


def qkv_kernel(g, sc, *refs):
    n, c = g.ring - 1, 2 * g.chips
    xs = refs[:c]
    vec, own = refs[c : c + 2]
    mine = refs[c + 2 : c + 2 + n]
    theirs = refs[c + 2 + n : c + 2 + 2 * n]
    out, w, full = refs[c + 2 + 2 * n :]
    p, f = sc[0], sc[2]
    lay(g, sc, own, mine, theirs, 0, g.half, w)
    rest = jnp.zeros((VEC, g.width - LANES), F32)
    total = jnp.zeros((VEC, g.width), F32)
    for s in range(g.ring):
        piece = vec[...] if s == 0 else mine[s - 1][g.half : g.half + VEC, 0:LANES]
        piece = piece.astype(F32)
        wide = jnp.concatenate([piece, rest], axis=1)
        total = total + pltpu.roll(wide, g.shard * jnp.bitwise_xor(f, s), 1)
    full[...] = total
    back = pltpu.roll(total, lax.rem(g.width - g.cols * p, g.width), 1)
    bias = jnp.concatenate(
        [back[0:1, : g.cols], jnp.zeros((1, g.cols), F32), back[1:2, : g.cols]], axis=1
    )
    rows = jnp.concatenate([x[...] for x in xs], axis=0)
    found = (dot(rows, w[...]) + bias).astype(BF)
    for h in range(g.heads):
        for i in range(3):
            out[:, LANES * h + DH * i : LANES * h + DH * (i + 1)] = found[
                :, g.cols * i + DH * h : g.cols * i + DH * (h + 1)
            ]
        out[:, LANES * h + 3 * DH : LANES * (h + 1)] = jnp.zeros((2 * g.tokens, DH), BF)


def select(index, size, axis_size, lanes):
    if lanes:
        ids = lax.broadcasted_iota(jnp.int32, (size, axis_size), 1)
    else:
        ids = lax.broadcasted_iota(jnp.int32, (axis_size, size), 0)
    return jnp.where(ids == index, 1.0, 0.0).astype(BF)


def over(x, size):
    return lax.shift_right_logical(x, jnp.int32(size.bit_length() - 1))


def tables_kernel(g, sc, _, clusters, block_ids, pick, place, blocks):
    p, k = sc[0], sc[1]
    ranges, step = 2 * g.chips, g.clusters * g.members
    shape = (2 * ranges, 2 * ranges)
    piece, source = (lax.broadcasted_iota(jnp.int32, shape, axis) for axis in (0, 1))
    device = 2 * jnp.bitwise_xor(p, over(piece, 2) & (g.chips - 1)) + jnp.bitwise_xor(
        k, over(piece, 2 * g.chips)
    )
    found = jnp.where(piece & 1 == 0, device, 2 * ranges - 1 - device)
    hot = jnp.where(found == source, 1.0, 0.0).astype(BF)
    half = g.rows // 2
    line = block_ids[...].astype(F32)
    lines = [line[:, half * i : half * (i + 1)] for i in range(2 * ranges)]
    ids = dot(hot, jnp.concatenate(lines, axis=0).astype(BF))
    for d in range(ranges):
        line = jnp.concatenate([ids[2 * d : 2 * d + 1], ids[2 * d + 1 : 2 * d + 2]], axis=1)
        blocks[:, g.rows * d : g.rows * (d + 1)] = jnp.broadcast_to(line, (8, g.rows)).astype(BF)
    before = lax.broadcasted_iota(jnp.int32, (CLUSTER, CLUSTER), 1) < lax.broadcasted_iota(
        jnp.int32, (CLUSTER, CLUSTER), 0
    )
    rows, cols, tokens = [], [], []
    for h in range(g.heads):
        order = clusters[
            pl.ds(g.heads * p + h, 1), pl.ds(pl.multiple_of(g.entries * k, 128), g.entries)
        ]
        chip, core = over(order, 2 * g.rows), over(order, g.rows) & 1
        within = order & (g.rows - 1)
        rows.append(
            jnp.bitwise_xor(core, k) * g.tokens + jnp.bitwise_xor(chip, p) * g.rows + within
        )
    units = [(h, c) for h in range(g.heads) for c in range(g.clusters)]
    for h, c in units:
        row = rows[h][:, CLUSTER * c : CLUSTER * (c + 1)]
        tall = jnp.broadcast_to(row.astype(F32), (CLUSTER, CLUSTER))
        cols.append(over(jnp.transpose(tall)[:, 0:1].astype(jnp.int32), g.rows))
    spots = []
    for (h, c), col in zip(units, cols):
        row = rows[h][:, CLUSTER * c : CLUSTER * (c + 1)]
        same = (col == over(row, g.rows)) & before
        rank = jnp.sum(jnp.where(same, 1.0, 0.0), axis=1, keepdims=True).astype(jnp.int32)
        spots.append(select(col * g.members + rank, CLUSTER, CLUSTER, True))
    for (h, c), spot in zip(units, spots):
        row = rows[h][:, CLUSTER * c : CLUSTER * (c + 1)]
        within = jnp.broadcast_to((row & (g.rows - 1)).astype(F32), (8, CLUSTER)).astype(BF)
        tokens.append(dot(within, spot))
    for h in range(g.heads):
        for d in range(ranges):
            lanes = slice(g.members * d, g.members * (d + 1))
            mine = jnp.concatenate(
                [tokens[h * g.clusters + c][:, lanes] for c in range(g.clusters)], axis=1
            ).astype(jnp.int32)
            place[h, g.rows * d : g.rows * (d + 1)] = select(mine[0:1, :], step, g.rows, False)
            pick[h, step * d : step * (d + 1)] = select(
                jnp.transpose(mine)[:, 0:1], step, g.rows, True
            )


def mask_kernel(g, blocks, place, mask):
    ids = [
        [
            dot(blocks[:, g.rows * d : g.rows * (d + 1)], place[h, g.rows * d : g.rows * (d + 1)])
            for d in range(2 * g.chips)
        ]
        for h in range(g.heads)
    ]
    for h in range(g.heads):
        for c in range(g.clusters):
            lanes = slice(g.members * c, g.members * (c + 1))
            keys = jnp.concatenate([part[:, lanes] for part in ids[h]], axis=1)
            allowed = keys[0:1, :] <= jnp.transpose(keys)[:, 0:1]
            mask[h * g.clusters + c] = jnp.where(allowed, 0.0, FLOOR)


def cluster_rows(g, ref, c):
    step = g.clusters * g.members
    return jnp.concatenate(
        [
            ref[step * d + g.members * c : step * d + g.members * (c + 1)]
            for d in range(2 * g.chips)
        ],
        axis=0,
    )


def put_cluster(g, ref, c, values):
    step = g.clusters * g.members
    for d in range(2 * g.chips):
        ref[step * d + g.members * c : step * d + g.members * (c + 1)] = values[
            g.members * d : g.members * (d + 1)
        ]


def attend_kernel(g, qkv, pick, place, mask, ctx_own, ctx_other, kept, probs, mixed):
    step, ranges = g.clusters * g.members, 2 * g.chips
    units = [(h, c) for h in range(g.heads) for c in range(g.clusters)]
    for h in range(g.heads):
        for d in range(ranges):
            rows = qkv[g.rows * d : g.rows * (d + 1), LANES * h : LANES * (h + 1)]
            slots = slice(step * d, step * (d + 1))
            kept[h, slots] = dot(pick[h, slots], rows).astype(BF)
    for h, c in units:
        rows = cluster_rows(g, kept.at[h], c)
        q, key = rows[:, 0:DH], rows[:, DH : 2 * DH]
        at = h * g.clusters + c
        probs[at] = dot_nt(q, key) * (DH ** (-0.5)) + mask[at]
    for h, c in units:
        at = h * g.clusters + c
        masked = probs[at]
        weights = jnp.exp(masked - jnp.max(masked, axis=-1, keepdims=True))
        probs[at] = weights * (1.0 / jnp.sum(weights, axis=-1, keepdims=True))
    for h, c in units:
        v = cluster_rows(g, kept.at[h], c)[:, 2 * DH : 3 * DH]
        put_cluster(
            g, mixed.at[h], c, dot(probs[h * g.clusters + c].astype(BF), v).astype(BF)
        )
    for h in range(g.heads):
        for d in range(ranges):
            side, at = (ctx_own, d) if d < g.chips else (ctx_other, d - g.chips)
            rows = dot(
                place[h, g.rows * d : g.rows * (d + 1)], mixed[h, step * d : step * (d + 1)]
            )
            side[g.rows * at : g.rows * (at + 1), DH * h : DH * (h + 1)] = rows.astype(BF)


def attend_back_kernel(g, own, other, pick, place, kept, probs, grads, d_mixed, found, d_scores):
    step, ranges = g.clusters * g.members, 2 * g.chips
    scale = DH ** (-0.5)
    units = [(h, c) for h in range(g.heads) for c in range(g.clusters)]
    for h in range(g.heads):
        for d in range(ranges):
            side, at = (own, d) if d < g.chips else (other, d - g.chips)
            rows = side[g.rows * at : g.rows * (at + 1), DH * h : DH * (h + 1)]
            slots = slice(step * d, step * (d + 1))
            d_mixed[h, slots] = dot(pick[h, slots], rows).astype(BF)
    for h, c in units:
        v = cluster_rows(g, kept.at[h], c)[:, 2 * DH : 3 * DH]
        share = probs[h * g.clusters + c]
        d_share = dot_nt(cluster_rows(g, d_mixed.at[h], c), v)
        delta = jnp.sum(share * d_share, axis=-1, keepdims=True)
        d_scores[h * g.clusters + c] = (share * (d_share - delta)).astype(BF)
    for h, c in units:
        rows = cluster_rows(g, kept.at[h], c)
        d_s, share = d_scores[h * g.clusters + c], probs[h * g.clusters + c].astype(BF)
        d_q = dot(d_s, rows[:, DH : 2 * DH]) * scale
        d_k = dot_tn(d_s, rows[:, 0:DH]) * scale
        d_v = dot_tn(share, cluster_rows(g, d_mixed.at[h], c))
        put_cluster(g, found.at[h], c, jnp.concatenate([d_q, d_k, d_v], axis=1).astype(BF))
    for h in range(g.heads):
        for d in range(ranges):
            at = slice(g.rows * d, g.rows * (d + 1))
            rows = dot(place[h, at], found[h, step * d : step * (d + 1)]).astype(BF)
            for i in range(3):
                grads[at, g.cols * i + DH * h : g.cols * i + DH * (h + 1)] = rows[
                    :, DH * i : DH * (i + 1)
                ]
    grads[:, g.qkv :] = jnp.zeros((2 * g.tokens, g.wide - g.qkv), BF)


def norm_parts(values):
    centre = values - jnp.mean(values, axis=-1, keepdims=True)
    spread = jnp.mean(centre * centre, axis=-1, keepdims=True)
    scale = lax.rsqrt(spread + EPSILON)
    return centre * scale, scale


def norm_back(grad, z, scale):
    return scale * (
        grad
        - jnp.mean(grad, axis=-1, keepdims=True)
        - z * jnp.mean(grad * z, axis=-1, keepdims=True)
    )


def seen(g, ref, j):
    return jnp.concatenate(
        [ref[g.rows * (i ^ j) : g.rows * ((i ^ j) + 1)] for i in range(g.chips)], axis=0
    )


def forward_kernel(g, sc, *refs):
    c, n = g.chips, g.ring - 1
    ctxs, xs, full = refs[:c], refs[c : 2 * c], refs[2 * c]
    wo_own, wi_own, wd_own = refs[2 * c + 1 : 2 * c + 4]
    refs = refs[2 * c + 4 :]
    mine, theirs = refs[:n], refs[n : 2 * n]
    refs = refs[2 * n :]
    parts, (active, inner, low, z_own, s_own, wo_rows, wi, wd) = refs[:c], refs[c : c + 8]
    wo, work = refs[c + 8 :]
    p = sc[0]
    lay(g, sc, wo_own, mine, theirs, g.half, g.half, wo, p)
    rows = jnp.concatenate([seen(g, ctxs[j], j) for j in range(c)], axis=1)
    wo_rows[...] = wo[0 : g.cols]
    halves = [slice(i, i + g.tokens // 2) for i in range(0, g.tokens, g.tokens // 2)]
    bias = full[pl.ds(8 + p, 1), :]

    def first_norm(half):
        for i in range(half.start, half.stop, SLAB):
            at = slice(i, i + SLAB)
            x = xs[i // g.rows][i % g.rows : i % g.rows + SLAB].astype(F32)
            z, scale = norm_parts(work[at] + x + full[2:3, :])
            first = z * full[3:4, :] + full[4:5, :]
            low[at] = first.astype(BF)
            if i < g.rows:
                z_own[at] = z
                s_own[at] = jnp.broadcast_to(scale, (SLAB, 128))
                parts[0][at] = first + full[5:6, :]

    def activate(half):
        for i in range(half.start, half.stop, SLAB):
            at = slice(i, i + SLAB)
            u = inner[at] + bias
            inner[at] = u
            active[at] = (u * (1.0 + lax.erf(u * (0.5**0.5))) * 0.5).astype(BF)

    def descend(half):
        second = dot(active[half], wd[...])
        for i in range(half.start, half.stop, g.rows):
            block = second[i - half.start : i - half.start + g.rows]
            if i == 0:
                parts[0][...] += block
            else:
                parts[i // g.rows][...] = block.astype(BF)

    one, two = halves
    work[one] = dot(rows[one], wo[...])
    work[two] = dot(rows[two], wo[...])
    lay(g, sc, wi_own, mine, theirs, 0, g.half, wi)
    first_norm(one)
    inner[one] = dot(low[one], wi[...])
    first_norm(two)
    inner[two] = dot(low[two], wi[...])
    lay(g, sc, wd_own, mine, theirs, 2 * g.half, g.bhalf, wd)
    activate(one)
    descend(one)
    activate(two)
    descend(two)


def turn_kernel(g, *refs):
    c = g.chips
    parts, full, cotangent = refs[:c], refs[c], refs[c + 1]
    out, d_second, branch = refs[c + 2 :]
    second = parts[0][...]
    for j in range(1, c):
        second = second + parts[j][...].astype(F32)
    z, scale = norm_parts(second)
    gain = full[6:7, :]
    out[...] = (z * gain + full[7:8, :]).astype(BF)
    dy = cotangent[...].astype(F32)
    grad = norm_back(dy * gain, z, scale)
    d_second[...] = grad
    branch[0 : g.rows] = grad.astype(BF)
    one = jnp.sum(dy * z, axis=0, keepdims=True)
    two = jnp.sum(dy, axis=0, keepdims=True)
    rest = jnp.zeros((VEC - 2, g.width), F32)
    branch[g.rows : g.rows + VEC] = jnp.concatenate([one, two, rest], axis=0).astype(BF)


def back_kernel(g, *refs):
    c = g.chips
    branches, slope, wd, wi = refs[:c], refs[c], refs[c + 1], refs[c + 2]
    parts, d_inner = refs[c + 3 : 2 * c + 3], refs[2 * c + 3]
    rows = jnp.concatenate([b[0 : g.rows] for b in branches], axis=0)
    d_active = dot_nt(rows, wd[...])
    d_inner[...] = (d_active * slope[...]).astype(BF)
    total = dot_nt(d_inner[...], wi[...])
    parts[0][...] = total[: g.rows]
    for j in range(1, c):
        parts[j][...] = total[g.rows * j : g.rows * (j + 1)].astype(BF)


def split_rows(g, sc, total, size, own, other, at):
    k, f = sc[1], sc[2]
    for s in range(g.ring):
        base = 2 * size * jnp.bitwise_xor(f, s)
        own[s, at : at + size] = total[pl.ds(pl.multiple_of(base + size * k, 8), size), :]
        other[s, at : at + size] = total[
            pl.ds(pl.multiple_of(base + size * (1 - k), 8), size), :
        ].astype(BF)


def mlp_grads_kernel(g, sc, *refs):
    c = g.chips
    branches, active, low, d_inner = refs[:c], refs[c], refs[c + 1], refs[c + 2]
    own, other, sums, total = refs[c + 3 :]
    rows = jnp.concatenate([b[0 : g.rows] for b in branches], axis=0)
    total[...] = dot_tn(active[...], rows)
    split_rows(g, sc, total, g.bhalf, own, other, g.half)
    total[...] = dot_tn(low[...], d_inner[...])
    split_rows(g, sc, total, g.half, own, other, 0)
    stats = branches[0][g.rows : g.rows + VEC].astype(F32)
    for j in range(1, c):
        stats = stats + branches[j][g.rows : g.rows + VEC].astype(F32)
    down = jnp.sum(rows.astype(F32), axis=0, keepdims=True)
    up = jnp.sum(d_inner[...].astype(F32), axis=0, keepdims=True)
    sums[...] = jnp.concatenate([stats[0:2], down, up, jnp.zeros((4, g.width), F32)], axis=0)


def first_kernel(g, *refs):
    c = g.chips
    parts, d_second, z_own, s_own, full = refs[:c], *refs[c : c + 4]
    d_sum, attended = refs[c + 4 :]
    d_first = d_second[...] + parts[0][...]
    for j in range(1, c):
        d_first = d_first + parts[j][...].astype(F32)
    z = z_own[...]
    grad = norm_back(d_first * full[3:4, :], z, s_own[:, 0:1])
    d_sum[...] = grad
    attended[0 : g.rows] = grad.astype(BF)
    one = jnp.sum(d_first * z, axis=0, keepdims=True)
    two = jnp.sum(d_first, axis=0, keepdims=True)
    rest = jnp.zeros((VEC - 2, g.width), F32)
    attended[g.rows : g.rows + VEC] = jnp.concatenate([one, two, rest], axis=0).astype(BF)


def context_kernel(g, *refs):
    grads, wo_rows, out = refs[: g.chips], refs[g.chips], refs[g.chips + 1]
    rows = jnp.concatenate([b[0 : g.rows] for b in grads], axis=0)
    out[...] = dot_nt(rows, wo_rows[...]).astype(BF)


def out_grads_kernel(g, sc, *refs):
    c = g.chips
    grads, ctxs, sums = refs[:c], refs[c : 2 * c], refs[2 * c]
    own, away, total = refs[2 * c + 1 :]
    p, f = sc[0], sc[2]
    rows = jnp.concatenate([b[0 : g.rows] for b in grads], axis=0)
    for j in range(c):
        q = jnp.bitwise_xor(p, j)
        total[pl.ds(pl.multiple_of(g.cols * q, 64), g.cols), :] = dot_tn(seen(g, ctxs[j], j), rows)
    stats = grads[0][g.rows : g.rows + VEC].astype(F32)
    for j in range(1, c):
        stats = stats + grads[j][g.rows : g.rows + VEC].astype(F32)
    out = jnp.sum(rows.astype(F32), axis=0, keepdims=True)
    rest = jnp.zeros((VEC - 7, g.width), F32)
    block = jnp.concatenate([sums[0:4], stats[0:2], out, rest], axis=0)
    size = g.shard // c
    for s in range(g.ring):
        base = g.shard * jnp.bitwise_xor(f, s) + size * p
        part = total[pl.ds(pl.multiple_of(base, 8), size), :]
        if s % 2:
            away[s // 2, 0:size] = part.astype(BF)
            away[s // 2, size:] = block.astype(BF)
        else:
            own[s // 2, 0:size] = part
            own[s // 2, size:] = block


def summed(g, mine, theirs, at):
    one = mine[g.tokens * at : g.tokens * (at + 1), : g.qkv].astype(F32)
    two = theirs[g.tokens * (1 - at) : g.tokens * (2 - at), : g.qkv].astype(F32)
    return (one + two).astype(BF)


def input_kernel(g, mine, theirs, w, *parts):
    total = dot_nt(summed(g, mine, theirs, 0), w[...])
    parts[0][...] = total[: g.rows]
    for j in range(1, g.chips):
        parts[j][...] = total[g.rows * j : g.rows * (j + 1)].astype(BF)


def turn_rows_kernel(g, sc, *refs):
    xs, out = refs[: 2 * g.chips], refs[2 * g.chips]
    rows = jnp.concatenate([x[...] for x in xs], axis=0)
    for core in range(2):

        @pl.when(sc[1] == core)
        def _(core=core):
            for r in range(g.ring):
                lane = g.shard * r + g.half * core
                out[g.half * r : g.half * (r + 1), :] = jnp.transpose(rows[:, lane : lane + g.half])


def qkv_grads_kernel(g, sc, mine, theirs, turned_x, own, away, total):
    f = sc[2]
    rows = jnp.concatenate([summed(g, mine, theirs, 0), summed(g, mine, theirs, 1)], axis=0)
    total[...] = dot(turned_x[...], rows)
    sums = jnp.sum(rows.astype(F32), axis=0, keepdims=True)
    gap = jnp.zeros((8, g.width - g.qkv), F32)
    block = jnp.concatenate(
        [jnp.concatenate([sums, jnp.zeros((7, g.qkv), F32)], axis=0), gap], axis=1
    )
    for s in range(g.ring):
        part = total[pl.ds(pl.multiple_of(g.half * jnp.bitwise_xor(f, s), 8), g.half), :]
        packed = pack(g, part)
        if s % 2:
            away[s // 2, 0 : g.packed] = packed.astype(BF)
            away[s // 2, g.packed :] = block.astype(BF)
        else:
            own[s // 2, 0 : g.packed] = packed
            own[s // 2, g.packed :] = block


def pack(g, part):
    step = g.half - g.packed
    beside = [
        part[g.packed :, step_lanes : step_lanes + g.width - g.qkv]
        for step_lanes in range(0, g.qkv, g.width - g.qkv)
    ]
    return jnp.concatenate(
        [part[0 : g.packed], jnp.concatenate(beside, axis=0)], axis=1
    )


def sources(g, sc, refs):
    p, k = sc[0], sc[1]
    out = []
    for j, (mine, theirs) in enumerate(zip(refs, others(g, refs))):
        q = jnp.bitwise_xor(p, j)
        out.append((q, k, mine))
        out.append((q, 1 - k, theirs))
    return out


def others(g, refs):
    far = refs[g.chips :]
    return far if len(far) > 1 else [far[0].at[j] for j in range(g.chips)]


def mlp_final_kernel(g, sc, *refs):
    found, (g_in, g_down) = refs[:-2], refs[-2:]
    for q, core, ref in sources(g, sc, found):
        at = pl.multiple_of(g.block * q + g.bhalf * core, 8)
        g_down[pl.ds(at, g.bhalf), :] = ref[g.half :, :].astype(F32)
        mine = pl.ds(pl.multiple_of(g.half * core, 8), g.half)
        for chip in range(g.chips):

            @pl.when(q == chip)
            def _(chip=chip, ref=ref, mine=mine):
                for r in range(g.ring):
                    lane = g.hshard * r + g.block * chip
                    g_in[mine, lane : lane + g.block] = ref[
                        0 : g.half, g.block * r : g.block * (r + 1)
                    ].astype(F32)


def last_kernel(g, sc, *refs):
    found = refs[: 2 * g.chips]
    gq, gk, gv, g_bq, g_bv, g_out, g_bin, *small = refs[2 * g.chips :]
    p, f = sc[0], sc[2]
    size, step = g.shard // g.chips, g.half - g.packed
    top = g.packed + 8
    for q, core, ref in sources(g, sc, found):

        @pl.when((q == f) & (core == 0))
        def _(ref=ref):
            row = ref[g.packed : top, :].astype(F32)[0:1]
            for dst, at in zip((g_bq, g_bv), (0, 2)):
                dst[...] = row[:, g.cols * at : g.cols * (at + 1)].reshape(g.shard)

        base = pl.multiple_of(g.half * core, 8)
        for chip in range(g.chips):

            @pl.when(q == chip)
            def _(chip=chip, ref=ref, base=base):
                lane = g.cols * chip
                for i, dst in enumerate((gq, gk, gv)):
                    dst[pl.ds(base, g.packed), lane : lane + g.cols] = ref[
                        0 : g.packed, g.cols * i : g.cols * (i + 1)
                    ].astype(F32)
                    dst[pl.ds(base + g.packed, step), lane : lane + g.cols] = ref[
                        step * i : step * (i + 1), g.qkv :
                    ].astype(F32)

    for j in range(g.chips):
        q = jnp.bitwise_xor(p, j)
        one, two = found[j], found[g.chips + j]
        both = one[top:, :].astype(F32) + two[top:, :].astype(F32)
        g_out[pl.ds(pl.multiple_of(size * q, 8), size), :] = both[0:size]
        back = pltpu.roll(both[size : size + VEC], lax.rem(g.width - g.shard * f, g.width), 1)
        for chip in range(g.chips):

            @pl.when(q == chip)
            def _(chip=chip, back=back):
                g_bin[g.block * chip : g.block * (chip + 1)] = back[3:4, : g.shard].reshape(g.shard)
                if chip == 0:
                    for i, dst in zip((0, 1, 2, 4, 5, 6), small):
                        dst[...] = back[i : i + 1, : g.shard].reshape(g.shard)


def to_core(x):
    n = lax.axis_size("ctx")
    return lax.ppermute(x, "ctx", [(i, i ^ 1) for i in range(n)])


def to_chip(x, j):
    n = lax.axis_size("ctx")
    return lax.ppermute(x, "ctx", [(i, i ^ (2 * j)) for i in range(n)])


def along(x, mask):
    n = lax.axis_size("fsdp")
    return lax.ppermute(x, "fsdp", [(i, i ^ mask) for i in range(n)])


def gather_ring(x, pause=None):
    n = lax.axis_size("fsdp")
    found, mask, first = {0: x}, n // 2, ()
    while mask:
        for s in sorted(found):
            first = [found[t] for t in sorted(found) if t]
            part = found[s] if s == 0 or pause is None else after(found[s], pause, *first)
            found[s | mask] = along(part, mask)
        mask //= 2
    return [found[s] for s in range(1, n)]


def spread(x, chips):
    far = {j: to_chip(x, j) for j in sorted(range(1, chips), key=lambda j: -bin(j).count("1"))}
    return [x] + [far[j] for j in range(1, chips)]


def pass_on(x, chips, pause):
    found = {0: x}
    mask = 1
    while mask < chips:
        for j in sorted(found):
            found[j | mask] = to_chip(found[j] if j == 0 else after(found[j], pause), mask)
        mask *= 2
    return [found[j] for j in range(chips)]


def swap(parts):
    far = {j: to_chip(parts[j], j) for j in sorted(range(1, len(parts)), key=lambda j: -bin(j).count("1"))}
    return [parts[0]] + [far[j] for j in range(1, len(parts))]


def ring_step(kept, away, mask):
    count, rows, width = kept.shape
    half = count // 2

    def step(mine, got):
        total = mine + got.astype(F32)
        if not half:
            return (total.astype(BF),)
        return total.reshape(half, 2, rows, width)[:, 0], total.reshape(
            half, 2, rows, width
        )[:, 1].astype(BF)

    outs = [shaped((half, rows, width), F32), shaped((half, rows, width), BF)]
    return mix(
        step,
        outs if half else [shaped((1, rows, width), BF)],
        kept,
        along(away, mask),
        name="ring_step",
    )


def kept_far(x):
    return pltpu.with_memory_space_constraint(x, pltpu.HBM)


def after(x, *first):
    return lax.optimization_barrier((x, *first))[0]


def ring_step(kept, away, mask):
    count, rows, width = kept.shape
    half = count // 2

    def step(mine, got):
        total = mine + got.astype(F32)
        if not half:
            return (total.astype(BF),)
        return total.reshape(half, 2, rows, width)[:, 0], total.reshape(
            half, 2, rows, width
        )[:, 1].astype(BF)

    outs = [shaped((half, rows, width), F32), shaped((half, rows, width), BF)]
    return mix(
        step,
        outs if half else [shaped((1, rows, width), BF)],
        kept,
        along(away, mask),
        name="ring_step",
    )


def kept_far(x):
    return pltpu.with_memory_space_constraint(x, pltpu.HBM)


def after(x, *first):
    return lax.optimization_barrier((x, *first))[0]


def plane_pieces(piece, chips):
    near = spread(piece, chips)
    return near + [to_core(part) for part in near]


def chip_body(
    hidden_in,
    out_grad,
    block_ids,
    clusters,
    w_query,
    w_key,
    w_value,
    w_out,
    b_query,
    b_value,
    b_out,
    ln1_gain,
    ln1_bias,
    w_in,
    b_in,
    w_down,
    b_down,
    ln2_gain,
    ln2_bias,
):
    n, ring = lax.axis_size("ctx"), lax.axis_size("fsdp")
    chips = n // 2
    rows, width = hidden_in.shape[1:]
    hidden = w_in.shape[1]
    g = Plan(chips, ring, width, hidden, rows)
    c, f = lax.axis_index("ctx"), lax.axis_index("fsdp")
    p, k = c // 2, c % 2
    sc = jnp.stack([p, k, f]).astype(jnp.int32)
    bind = functools.partial


    qall, qsend, vec = call(
        bind(pick_kernel, g),
        [
            shaped((g.shard, g.qkv), BF),
            shaped((g.half + VEC, g.qkv), BF),
            shaped((VEC, LANES), BF),
        ],
        [SMEM] + [FAR] * 12,
        [
            sc,
            *map(
                kept_far,
                (
                    w_query,
                    w_key,
                    w_value,
                    b_query,
                    b_value,
                    b_out,
                    ln1_gain,
                    ln1_bias,
                    b_down,
                    ln2_gain,
                    ln2_bias,
                    b_in,
                ),
            ),
        ],
        [
            pltpu.VMEM((3, g.shard, width), BF),
        ]
        + [pltpu.VMEM((g.shard,), BF)] * 8
        + [pltpu.VMEM((g.hshard,), BF), pltpu.SemaphoreType.DMA((12,))],
        name="pick_weights",
    )
    x_own = after(hidden_in.reshape(rows, width), qsend)
    xs = spread(x_own, chips)
    iall, oall, dall, send = call(
        bind(prep_kernel, g),
        [
            shaped((g.shard, g.share), BF),
            shaped((g.shard, width), BF),
            shaped((g.block, width), BF),
            shaped((2 * g.half + g.bhalf, width), BF),
        ],
        [SMEM, HBM, FAR, FAR, FAR],
        [sc, qsend, kept_far(w_in), kept_far(w_down), kept_far(w_out)],
        [pltpu.VMEM((g.shard, hidden), BF), pltpu.SemaphoreType.DMA((3,))],
        name="prepare_weights",
    )
    q_mine = gather_ring(qsend, send)

    step = g.clusters * g.members
    pick, place, blk = call(
        bind(tables_kernel, g),
        [
            shaped((g.heads, 2 * chips * step, rows), BF),
            shaped((g.heads, 2 * g.tokens, step), BF),
            shaped((8, 2 * g.tokens), BF),
        ],
        [SMEM, HBM] + [VMEM] * 2,
        [sc, q_mine[0], clusters[0], block_ids],
        name="cluster_tables",
    )
    (mask,) = call(
        bind(mask_kernel, g),
        [shaped((g.heads * g.clusters, CLUSTER, CLUSTER), F32)],
        [VMEM] * 2,
        [blk, place],
        name="cluster_mask",
    )
    x_other = [to_core(after(xs[0], xs[1]))] + [to_core(x) for x in xs[1:]]
    q_theirs = [to_core(after(part, xs[1])) for part in q_mine]
    qkv, w_qkv, full = call(
        bind(qkv_kernel, g),
        [
            shaped((2 * g.tokens, g.padded), BF),
            shaped((width, g.qkv), BF),
            shaped((VEC, width), F32),
        ],
        [SMEM] + [VMEM] * (2 * chips + 2 * ring),
        [sc, *xs, *x_other, after(vec, send), qall, *q_mine, *q_theirs],
        name="project",
    )
    ctx_own, ctx_other, kept, probs = call(
        bind(attend_kernel, g),
        [
            shaped((g.tokens, g.cols), BF),
            shaped((g.tokens, g.cols), BF),
            shaped((g.heads, g.entries, LANES), BF),
            shaped((g.heads * g.clusters, CLUSTER, CLUSTER), F32),
        ],
        [VMEM] * 4,
        [qkv, pick, place, mask],
        [pltpu.VMEM((g.heads, g.entries, DH), BF)],
        name="attend",
    )
    (ctx,) = mix(
        lambda a, b: (a + b,),
        [shaped((g.tokens, g.cols), BF)],
        ctx_own,
        to_core(ctx_other),
        name="join_context",
    )
    ctxs = spread(ctx, chips)
    w_mine = gather_ring(send, ctx_own)

    w_theirs = [to_core(after(part, *ctxs[1:])) for part in w_mine]
    *second, active, inner, low, z_own, s_own, wo_rows, wi, wd = call(
        bind(forward_kernel, g),
        [shaped((rows, width), F32)]
        + [shaped((rows, width), BF)] * (chips - 1)
        + [
            shaped((g.tokens, g.share), BF),
            shaped((g.tokens, g.share), F32),
            shaped((g.tokens, width), BF),
            shaped((rows, width), F32),
            shaped((rows, 128), F32),
            shaped((g.cols, width), BF),
            shaped((width, g.share), BF),
            shaped((g.share, width), BF),
        ],
        [SMEM] + [VMEM] * (2 * chips + 2 * ring + 2),
        [sc, *ctxs, *xs, full, oall, iall, dall, *w_mine, *w_theirs],
        [pltpu.VMEM((width, width), BF), pltpu.VMEM((g.tokens, width), F32)],
        name="mlp_forward",
    )
    (slope,) = mix(
        lambda u: (
            0.5 * (1.0 + lax.erf(u * (0.5**0.5)))
            + u * jnp.exp(-0.5 * u * u) * (1.0 / (2.0 * math.pi) ** 0.5),
        ),
        [shaped((g.tokens, g.share), F32)],
        inner,
        name="gelu_slope",
    )
    (turned_x,) = call(
        bind(turn_rows_kernel, g),
        [shaped((ring * g.half, 2 * g.tokens), BF)],
        [SMEM] + [VMEM] * (2 * chips),
        [sc, after(xs[0], inner), *xs[1:], *x_other],
        name="turn_rows",
    )
    second = swap(second)
    layer_out, d_second, branch = call(
        bind(turn_kernel, g),
        [
            shaped((rows, width), BF),
            shaped((rows, width), F32),
            shaped((rows + VEC, width), BF),
        ],
        [VMEM] * (chips + 2),
        [*second, after(full, turned_x), out_grad.reshape(rows, width)],
        name="norm_two",
    )
    branches = spread(branch, chips)
    *d_first, d_inner = call(
        bind(back_kernel, g),
        [shaped((rows, width), F32)]
        + [shaped((rows, width), BF)] * (chips - 1)
        + [shaped((g.tokens, g.share), BF)],
        [VMEM] * (chips + 3),
        [*branches, slope, wd, wi],
        name="mlp_back",
    )
    d_first = swap(d_first)
    m_own, m_other, sums = call(
        bind(mlp_grads_kernel, g),
        [
            shaped((ring, g.half + g.bhalf, width), F32),
            shaped((ring, g.half + g.bhalf, width), BF),
            shaped((8, width), F32),
        ],
        [SMEM] + [VMEM] * (chips + 3),
        [sc, *branches, active, low, d_inner],
        [pltpu.VMEM((width, g.share), F32)],
        name="mlp_grads",
    )
    m_got = to_core(m_other)
    m_rows = g.half + g.bhalf

    def joined(own, got):
        total = own + got.astype(F32)
        return (total[0], *(total[s].astype(BF) for s in range(1, ring)))

    m_kept, *m_away = mix(
        joined,
        [shaped((m_rows, width), F32)] + [shaped((m_rows, width), BF)] * (ring - 1),
        m_own,
        m_got,
        name="join_grads",
    )
    (m_piece,) = mix(
        lambda kept, *parts: (sum((part.astype(F32) for part in parts), kept).astype(BF),),
        [shaped((m_rows, width), BF)],
        m_kept,
        *(along(part, s) for s, part in enumerate(m_away, 1)),
        name="mlp_sum",
    )
    d_sum, attended = call(
        bind(first_kernel, g),
        [shaped((rows, width), F32), shaped((rows + VEC, width), BF)],
        [VMEM] * (chips + 4),
        [*d_first, after(d_second, *m_away), z_own, s_own, full],
        name="norm_one",
    )
    grads = spread(attended, chips)
    (d_ctx,) = call(
        bind(context_kernel, g),
        [shaped((g.tokens, g.cols), BF)],
        [VMEM] * (chips + 1),
        [*grads, after(wo_rows, m_piece)],
        name="context_back",
    )
    d_ctx_other = to_core(d_ctx)
    o_rows = g.shard // chips + VEC
    o_own, o_away = call(
        bind(out_grads_kernel, g),
        [shaped((ring // 2, o_rows, width), F32), shaped((ring // 2, o_rows, width), BF)],
        [SMEM] + [VMEM] * (2 * chips + 1),
        [sc, *grads, *ctxs, sums],
        [pltpu.VMEM((width, width), F32)],
        name="out_grads",
    )
    (dq_mine,) = call(
        bind(attend_back_kernel, g),
        [shaped((2 * g.tokens, g.wide), BF)],
        [VMEM] * 6,
        [d_ctx, d_ctx_other, pick, place, after(kept, o_own), probs],
        [
            pltpu.VMEM((g.heads, g.entries, DH), BF),
            pltpu.VMEM((g.heads, g.entries, 3 * DH), BF),
            pltpu.VMEM((g.heads * g.clusters, CLUSTER, CLUSTER), BF),
        ],
        name="attend_back",
    )
    dq_theirs = to_core(dq_mine)
    q_rows = g.packed + 8
    q_own, q_away = call(
        bind(qkv_grads_kernel, g),
        [shaped((ring // 2, q_rows, width), F32), shaped((ring // 2, q_rows, width), BF)],
        [SMEM] + [VMEM] * 3,
        [sc, dq_mine, dq_theirs, turned_x],
        [pltpu.VMEM((ring * g.half, g.qkv), F32)],
        name="project_grads",
    )
    d_in = call(
        bind(input_kernel, g),
        [shaped((rows, width), F32)] + [shaped((rows, width), BF)] * (chips - 1),
        [VMEM] * 3,
        [dq_mine, dq_theirs, w_qkv],
        name="project_back",
    )
    d_in = swap(d_in)
    mask_at = 2
    q_away0 = q_away
    o_away = after(o_away, dq_mine)
    while q_own.shape[0] > 1:
        q_own, q_away = ring_step(q_own, q_away, mask_at // 2)
        o_own, o_away = ring_step(o_own, o_away, mask_at // 2)
        mask_at *= 2
    near = pass_on(m_piece, chips, dq_theirs)
    m_pieces = near + [to_core(part) for part in near]
    (input_grad,) = mix(
        lambda kept, *parts: (sum((part.astype(F32) for part in parts), kept).astype(BF),),
        [shaped((rows, width), BF)],
        d_sum,
        *d_in,
        name="input_sum",
    )
    g_in, g_down = call(
        bind(mlp_final_kernel, g),
        [shaped((g.shard, hidden), F32), shaped((g.hshard, width), F32)],
        [SMEM] + [VMEM] * len(m_pieces),
        [sc, *m_pieces],
        name="mlp_lay",
    )
    vector = shaped((g.shard,), F32)
    (piece,) = mix(
        lambda a, b, c, d: (
            jnp.concatenate([a[0] + b[0].astype(F32), c[0] + d[0].astype(F32)], axis=0).astype(BF),
        ),
        [shaped((q_rows + o_rows, width), BF)],
        q_own,
        along(q_away, mask_at // 2),
        o_own,
        along(o_away, mask_at // 2),
        name="last_sum",
    )
    near = spread(after(piece, input_grad), chips)
    pieces = near + [to_core(part) for part in near]
    found = call(
        bind(last_kernel, g),
        [shaped((g.shard, width), F32)] * 3
        + [vector] * 2
        + [shaped((g.shard, width), F32), shaped((g.hshard,), F32)]
        + [vector] * 6,
        [SMEM] + [VMEM] * (2 * chips),
        [after(sc, g_down), *pieces],
        name="last_lay",
    )
    gq, gk, gv, g_bq, g_bv, g_out, g_bin, g_gain2, g_bias2, g_bdown, g_gain1, g_bias1, g_bout = found
    return (
        layer_out.reshape(1, rows, width),
        input_grad.reshape(1, rows, width),
        gq,
        gk,
        gv,
        g_out,
        g_bq,
        g_bv,
        g_bout,
        g_gain1,
        g_bias1,
        g_in,
        g_bin,
        g_down,
        g_bdown,
        g_gain2,
        g_bias2,
    )


def fits(mesh):
    n, ring = mesh.shape["ctx"], mesh.shape["fsdp"]
    chips = n // 2
    return n % 2 == 0 and chips & (chips - 1) == 0 and chips > 1 and ring == chips and H % chips == 0 and ring * chips <= 16


def solution(mesh):
    in_specs = (
        P("fsdp", "ctx", None),
        P("fsdp", "ctx", None),
        P("fsdp", None),
        P("fsdp", None, None),
        P("fsdp", None),
        P("fsdp", None),
        P("fsdp", None),
        P("fsdp", None),
        P("fsdp"),
        P("fsdp"),
        P("fsdp"),
        P("fsdp"),
        P("fsdp"),
        P("fsdp", None),
        P("fsdp"),
        P("fsdp", None),
        P("fsdp"),
        P("fsdp"),
        P("fsdp"),
    )
    out_specs = (
        P("fsdp", "ctx", None),
        P("fsdp", "ctx", None),
        P("fsdp", None),
        P("fsdp", None),
        P("fsdp", None),
        P("fsdp", None),
        P("fsdp"),
        P("fsdp"),
        P("fsdp"),
        P("fsdp"),
        P("fsdp"),
        P("fsdp", None),
        P("fsdp"),
        P("fsdp", None),
        P("fsdp"),
        P("fsdp"),
        P("fsdp"),
    )
    body = chip_body if fits(mesh) else general_body
    return jax.shard_map(body, mesh=mesh, in_specs=in_specs, out_specs=out_specs, check_vma=False)
```

```python
import functools
import math

import jax
import jax.numpy as jnp
from jax import lax
from jax.experimental import pallas as pl
from jax.experimental.pallas import tpu as pltpu
from jax.sharding import PartitionSpec as P

H = 12
DH = 64
CLUSTER = 128


EPSILON = 1e-12
FLOOR = -1e30


def layer_norm(values, gain, shift):
    centre = values - jnp.mean(values, axis=-1, keepdims=True)
    spread = jnp.mean(centre * centre, axis=-1, keepdims=True)
    return centre * lax.rsqrt(spread + EPSILON) * gain + shift


def exact_gelu(values):
    return jax.nn.gelu(values, approximate=False)


def positions(length, per_device, parts):
    stored = jnp.arange(length, dtype=jnp.int32)
    device = stored // per_device
    within = stored % per_device
    half = per_device // 2
    return jnp.where(
        within < half, device * half + within, (2 * parts - 1 - device) * half + within - half
    )


def contract(left, right):
    return lax.dot_general(
        left, right, (((0,), (0,)), ((), ())), preferred_element_type=jnp.float32
    )


def back_product(grad, weight):
    return lax.dot_general(
        grad, weight, (((1,), (1,)), ((), ())), preferred_element_type=jnp.float32
    )


def column_sum(values):
    return jnp.sum(values.astype(jnp.float32), axis=0)


def per_head_rows(rows, index):
    split = rows.reshape(rows.shape[0], H, DH)
    return jnp.take_along_axis(split, index.T[:, :, None], axis=0)


def cluster_tables(order, device, per_device, parts):
    heads, length = order.shape
    groups = length // CLUSTER
    members = CLUSTER // parts
    mine = (order // per_device == device).astype(jnp.int32)
    rank = jnp.cumsum(mine.reshape(heads, groups, CLUSTER), axis=-1).reshape(heads, length) - 1
    entry = jnp.arange(length, dtype=jnp.int32)[None, :]
    slot = jnp.where(mine == 1, entry // CLUSTER * members + rank, per_device)
    head_index = jnp.arange(heads, dtype=jnp.int32)[:, None]
    picked = (
        jnp.zeros((heads, per_device), jnp.int32)
        .at[head_index, slot]
        .set(order - device * per_device, mode="drop")
    )
    counter = jnp.broadcast_to(
        jnp.arange(per_device, dtype=jnp.int32)[None, :], (heads, per_device)
    )
    placed = jnp.zeros((heads, per_device), jnp.int32).at[head_index, picked].set(counter)
    inverse = (
        jnp.zeros((heads, length), jnp.int32)
        .at[head_index, order]
        .set(jnp.broadcast_to(jnp.arange(length, dtype=jnp.int32)[None, :], (heads, length)))
    )
    return (picked, placed, inverse)


def score_blocks(query, key_rows, query_blocks, key_blocks, scale):
    scores = (
        jnp.einsum("cqhd,ckhd->hcqk", query, key_rows, preferred_element_type=jnp.float32) * scale
    )
    allowed = key_blocks[:, :, None, :] <= query_blocks[:, :, :, None]
    return (scores, allowed)


def attend(query, key_rows, value_rows, query_blocks, key_blocks, scale):
    scores, allowed = score_blocks(query, key_rows, query_blocks, key_blocks, scale)
    masked = jnp.where(allowed, scores, FLOOR)
    top = jnp.max(masked, axis=-1, keepdims=True)
    weights = jnp.where(allowed, jnp.exp(masked - top), 0.0)
    total = jnp.sum(weights, axis=-1, keepdims=True)
    probs = (weights / total).astype(jnp.bfloat16)
    mixed = jnp.einsum("hcqk,ckhd->cqhd", probs, value_rows, preferred_element_type=jnp.float32)
    return (mixed.astype(jnp.bfloat16), top + jnp.log(total))


def attend_back(query, key_rows, value_rows, query_blocks, key_blocks, logsum, d_mixed, scale):
    scores, allowed = score_blocks(query, key_rows, query_blocks, key_blocks, scale)
    probs = jnp.where(allowed, jnp.exp(jnp.where(allowed, scores, FLOOR) - logsum), 0.0)
    rounded = probs.astype(jnp.bfloat16)
    d_probs = jnp.einsum("cqhd,ckhd->hcqk", d_mixed, value_rows, preferred_element_type=jnp.float32)
    centred = jnp.sum(probs * d_probs, axis=-1, keepdims=True)
    d_scores = (probs * (d_probs - centred)).astype(jnp.bfloat16)
    d_query = (
        jnp.einsum("hcqk,ckhd->cqhd", d_scores, key_rows, preferred_element_type=jnp.float32)
        * scale
    )
    d_key = (
        jnp.einsum("hcqk,cqhd->ckhd", d_scores, query, preferred_element_type=jnp.float32) * scale
    )
    d_value = jnp.einsum("hcqk,cqhd->ckhd", rounded, d_mixed, preferred_element_type=jnp.float32)
    return (d_query, d_key, d_value)


def general_body(
    hidden_in,
    out_grad,
    block_ids,
    clusters,
    w_query,
    w_key,
    w_value,
    w_out,
    b_query,
    b_value,
    b_out,
    ln1_gain,
    ln1_bias,
    w_in,
    b_in,
    w_down,
    b_down,
    ln2_gain,
    ln2_bias,
):
    parts = lax.axis_size("ctx")
    device = lax.axis_index("ctx")
    sequences, per_device, width = hidden_in.shape
    length = per_device * parts
    members = CLUSTER // parts
    groups = length // CLUSTER
    scale = DH ** (-0.5)
    (
        full_query,
        full_key,
        full_value,
        full_out,
        bias_query,
        bias_value,
        bias_out,
        gain_one,
        shift_one,
    ) = (
        lax.all_gather(w_query, "fsdp", axis=0, tiled=True),
        lax.all_gather(w_key, "fsdp", axis=0, tiled=True),
        lax.all_gather(w_value, "fsdp", axis=0, tiled=True),
        lax.all_gather(w_out, "fsdp", axis=0, tiled=True),
        lax.all_gather(b_query, "fsdp", axis=0, tiled=True),
        lax.all_gather(b_value, "fsdp", axis=0, tiled=True),
        lax.all_gather(b_out, "fsdp", axis=0, tiled=True),
        lax.all_gather(ln1_gain, "fsdp", axis=0, tiled=True),
        lax.all_gather(ln1_bias, "fsdp", axis=0, tiled=True),
    )
    full_in, full_down, bias_in, bias_down, gain_two, shift_two = (
        lax.all_gather(w_in, "fsdp", axis=0, tiled=True),
        lax.all_gather(w_down, "fsdp", axis=0, tiled=True),
        lax.all_gather(b_in, "fsdp", axis=0, tiled=True),
        lax.all_gather(b_down, "fsdp", axis=0, tiled=True),
        lax.all_gather(ln2_gain, "fsdp", axis=0, tiled=True),
        lax.all_gather(ln2_bias, "fsdp", axis=0, tiled=True),
    )
    hidden = hidden_in.reshape(sequences * per_device, width)
    query_rows = (
        jnp.dot(hidden, full_query, preferred_element_type=jnp.float32) + bias_query
    ).astype(jnp.bfloat16)
    key_rows = jnp.dot(hidden, full_key, preferred_element_type=jnp.float32).astype(jnp.bfloat16)
    value_rows = (
        jnp.dot(hidden, full_value, preferred_element_type=jnp.float32) + bias_value
    ).astype(jnp.bfloat16)
    place = positions(length, per_device, parts)
    index = 0
    order = clusters[index]
    stored_blocks = block_ids[index][place]
    picked, placed, inverse = cluster_tables(order, device, per_device, parts)
    q_local = per_head_rows(query_rows, picked).reshape(groups, members, H, DH)
    query_blocks = stored_blocks[device * per_device + picked].reshape(H, groups, members)
    key_all = lax.all_gather(key_rows, "ctx", axis=0, tiled=True)
    value_all = lax.all_gather(value_rows, "ctx", axis=0, tiled=True)
    key_cluster = per_head_rows(key_all, order).reshape(groups, CLUSTER, H, DH)
    value_cluster = per_head_rows(value_all, order).reshape(groups, CLUSTER, H, DH)
    key_blocks = stored_blocks[order].reshape(H, groups, CLUSTER)
    mixed, logsum = attend(q_local, key_cluster, value_cluster, query_blocks, key_blocks, scale)
    contexts = per_head_rows(mixed.reshape(per_device, width), placed).reshape(per_device, width)
    kept = [
        (
            q_local,
            key_cluster,
            value_cluster,
            query_blocks,
            key_blocks,
            logsum,
            picked,
            placed,
            inverse,
        )
    ]
    attended = jnp.dot(contexts, full_out, preferred_element_type=jnp.float32) + bias_out
    first_sum = hidden.astype(jnp.float32) + attended
    first, first_pull = jax.vjp(
        layer_norm, first_sum, gain_one.astype(jnp.float32), shift_one.astype(jnp.float32)
    )
    first_low = first.astype(jnp.bfloat16)
    inner = jnp.dot(first_low, full_in, preferred_element_type=jnp.float32) + bias_in
    active_full, gelu_pull = jax.vjp(exact_gelu, inner)
    active = active_full.astype(jnp.bfloat16)
    second_sum = first + jnp.dot(active, full_down, preferred_element_type=jnp.float32) + bias_down
    second, second_pull = jax.vjp(
        layer_norm, second_sum, gain_two.astype(jnp.float32), shift_two.astype(jnp.float32)
    )
    layer_out = second.astype(jnp.bfloat16).reshape(sequences, per_device, width)
    d_out = out_grad.reshape(sequences * per_device, width).astype(jnp.float32)
    d_second, g_gain_two, g_shift_two = second_pull(d_out)
    d_branch = d_second.astype(jnp.bfloat16)
    g_w_down = contract(active, d_branch)
    g_b_down = column_sum(d_branch)
    d_active = back_product(d_branch, full_down)
    d_inner = gelu_pull(d_active)[0].astype(jnp.bfloat16)
    g_w_in = contract(first_low, d_inner)
    g_b_in = column_sum(d_inner)
    d_first = d_second + back_product(d_inner, full_in)
    d_sum, g_gain_one, g_shift_one = first_pull(d_first)
    d_attended = d_sum.astype(jnp.bfloat16)
    g_w_out = contract(contexts, d_attended)
    g_b_out = column_sum(d_attended)
    d_context = back_product(d_attended, full_out).astype(jnp.bfloat16)
    index = 0
    q_kept, k_kept, v_kept, blocks_q, blocks_k, logsum, picked, placed, inverse = kept[index]
    d_cluster = per_head_rows(d_context, picked).reshape(groups, members, H, DH)
    d_query, d_key, d_value = attend_back(
        q_kept, k_kept, v_kept, blocks_q, blocks_k, logsum, d_cluster, scale
    )
    key_full = per_head_rows(d_key.reshape(length, width), inverse).reshape(length, width)
    value_full = per_head_rows(d_value.reshape(length, width), inverse).reshape(length, width)
    key_part = lax.psum_scatter(
        key_full.astype(jnp.bfloat16), "ctx", scatter_dimension=0, tiled=True
    )
    value_part = lax.psum_scatter(
        value_full.astype(jnp.bfloat16), "ctx", scatter_dimension=0, tiled=True
    )
    query_local = d_query.astype(jnp.bfloat16).reshape(per_device, width)
    query_grads = per_head_rows(query_local, placed).reshape(per_device, width)
    g_w_query = contract(hidden, query_grads)
    g_b_query = column_sum(query_grads)
    g_w_key = contract(hidden, key_part)
    g_w_value = contract(hidden, value_part)
    g_b_value = column_sum(value_part)
    input_total = (
        d_sum
        + back_product(query_grads, full_query)
        + back_product(key_part, full_key)
        + back_product(value_part, full_value)
    )
    input_grad = input_total.astype(jnp.bfloat16).reshape(sequences, per_device, width)
    shares = (
        lax.psum_scatter(
            g_w_query.astype(jnp.bfloat16), "fsdp", scatter_dimension=0, tiled=True
        ).astype(jnp.float32),
        lax.psum_scatter(
            g_w_key.astype(jnp.bfloat16), "fsdp", scatter_dimension=0, tiled=True
        ).astype(jnp.float32),
        lax.psum_scatter(
            g_w_value.astype(jnp.bfloat16), "fsdp", scatter_dimension=0, tiled=True
        ).astype(jnp.float32),
        lax.psum_scatter(
            g_w_out.astype(jnp.bfloat16), "fsdp", scatter_dimension=0, tiled=True
        ).astype(jnp.float32),
        lax.psum_scatter(
            g_b_query.astype(jnp.bfloat16), "fsdp", scatter_dimension=0, tiled=True
        ).astype(jnp.float32),
        lax.psum_scatter(
            g_b_value.astype(jnp.bfloat16), "fsdp", scatter_dimension=0, tiled=True
        ).astype(jnp.float32),
        lax.psum_scatter(
            g_b_out.astype(jnp.bfloat16), "fsdp", scatter_dimension=0, tiled=True
        ).astype(jnp.float32),
        lax.psum_scatter(
            g_gain_one.astype(jnp.bfloat16), "fsdp", scatter_dimension=0, tiled=True
        ).astype(jnp.float32),
        lax.psum_scatter(
            g_shift_one.astype(jnp.bfloat16), "fsdp", scatter_dimension=0, tiled=True
        ).astype(jnp.float32),
        lax.psum_scatter(
            g_w_in.astype(jnp.bfloat16), "fsdp", scatter_dimension=0, tiled=True
        ).astype(jnp.float32),
        lax.psum_scatter(
            g_b_in.astype(jnp.bfloat16), "fsdp", scatter_dimension=0, tiled=True
        ).astype(jnp.float32),
        lax.psum_scatter(
            g_w_down.astype(jnp.bfloat16), "fsdp", scatter_dimension=0, tiled=True
        ).astype(jnp.float32),
        lax.psum_scatter(
            g_b_down.astype(jnp.bfloat16), "fsdp", scatter_dimension=0, tiled=True
        ).astype(jnp.float32),
        lax.psum_scatter(
            g_gain_two.astype(jnp.bfloat16), "fsdp", scatter_dimension=0, tiled=True
        ).astype(jnp.float32),
        lax.psum_scatter(
            g_shift_two.astype(jnp.bfloat16), "fsdp", scatter_dimension=0, tiled=True
        ).astype(jnp.float32),
    )
    totals = (
        lax.psum(shares[0].astype(jnp.bfloat16), "ctx").astype(jnp.float32),
        lax.psum(shares[1].astype(jnp.bfloat16), "ctx").astype(jnp.float32),
        lax.psum(shares[2].astype(jnp.bfloat16), "ctx").astype(jnp.float32),
        lax.psum(shares[3].astype(jnp.bfloat16), "ctx").astype(jnp.float32),
        lax.psum(shares[4].astype(jnp.bfloat16), "ctx").astype(jnp.float32),
        lax.psum(shares[5].astype(jnp.bfloat16), "ctx").astype(jnp.float32),
        lax.psum(shares[6].astype(jnp.bfloat16), "ctx").astype(jnp.float32),
        lax.psum(shares[7].astype(jnp.bfloat16), "ctx").astype(jnp.float32),
        lax.psum(shares[8].astype(jnp.bfloat16), "ctx").astype(jnp.float32),
        lax.psum(shares[9].astype(jnp.bfloat16), "ctx").astype(jnp.float32),
        lax.psum(shares[10].astype(jnp.bfloat16), "ctx").astype(jnp.float32),
        lax.psum(shares[11].astype(jnp.bfloat16), "ctx").astype(jnp.float32),
        lax.psum(shares[12].astype(jnp.bfloat16), "ctx").astype(jnp.float32),
        lax.psum(shares[13].astype(jnp.bfloat16), "ctx").astype(jnp.float32),
        lax.psum(shares[14].astype(jnp.bfloat16), "ctx").astype(jnp.float32),
    )
    return (
        layer_out,
        input_grad,
        totals[0],
        totals[1],
        totals[2],
        totals[3],
        totals[4],
        totals[5],
        totals[6],
        totals[7],
        totals[8],
        totals[9],
        totals[10],
        totals[11],
        totals[12],
        totals[13],
        totals[14],
    )


BF = jnp.bfloat16
F32 = jnp.float32
LANES = 256
VMEM = pl.BlockSpec(memory_space=pltpu.VMEM)
HBM = pl.BlockSpec(memory_space=pl.ANY)
FAR = pl.BlockSpec(memory_space=pltpu.HBM)
SMEM = pl.BlockSpec(memory_space=pltpu.SMEM)
VEC = 16
STATS = 8
SLAB = 64


def shaped(shape, dtype):
    return jax.ShapeDtypeStruct(shape, dtype)


def call(kernel, outs, ins, args, scratch=(), name=None, weight=1):
    moved = sum(a.size * a.dtype.itemsize for a in args)
    moved += sum(o.size * o.dtype.itemsize for o in outs)
    held = sum(
        math.prod(r.shape) * jnp.dtype(r.dtype).itemsize
        for r in scratch
        if jnp.issubdtype(r.dtype, jnp.number)
    )
    return pl.pallas_call(
        kernel,
        out_shape=outs,
        in_specs=ins,
        out_specs=[VMEM] * len(outs),
        scratch_shapes=list(scratch),
        name=name,
        cost_estimate=pl.CostEstimate(flops=weight, transcendentals=0, bytes_accessed=weight),
        compiler_params=pltpu.CompilerParams(vmem_limit_bytes=moved + held + (4 << 20)),
    )(*args)


def mix(function, outs, *args, name=None):
    def kernel(*refs):
        found = function(*(ref[...] for ref in refs[: len(args)]))
        for ref, value in zip(refs[len(args) :], found):
            ref[...] = value

    return call(kernel, outs, [VMEM] * len(args), args, name=name)


def dot(left, right):
    return jnp.dot(left, right, preferred_element_type=F32)


def dot_nt(left, right):
    return lax.dot_general(left, right, (((1,), (1,)), ((), ())), preferred_element_type=F32)


def dot_tn(left, right):
    return lax.dot_general(left, right, (((0,), (0,)), ((), ())), preferred_element_type=F32)


class Plan:
    def __init__(self, chips, ring, width, hidden, per_device):
        self.chips, self.ring, self.width, self.hidden = chips, ring, width, hidden
        self.rows = per_device
        self.tokens = chips * per_device
        self.shard = width // ring
        self.half = self.shard // 2
        self.share = hidden // chips
        self.hshard = hidden // ring
        self.block = self.hshard // chips
        self.bhalf = self.block // 2
        self.heads = H // chips
        self.cols = self.heads * DH
        self.qkv = 3 * self.cols
        self.padded = self.heads * LANES
        self.wide = -(-self.qkv // 128) * 128
        self.packed = self.half * self.qkv // width
        self.clusters = chips
        self.members = CLUSTER // (2 * chips)
        self.entries = chips * CLUSTER


def pick_kernel(g, sc, *refs):
    weights, small = refs[:3], refs[3:12]
    qall, qsend, vec, here, *lines, sem = refs[12:]
    p, k = sc[0], sc[1]
    copies = [
        pltpu.make_async_copy(w, here.at[i], sem.at[i]) for i, w in enumerate(weights)
    ]
    copies += [
        pltpu.make_async_copy(ref, lines[i], sem.at[3 + i])
        for i, ref in enumerate(small)
    ]
    start(copies)
    finish(copies)
    for q in range(g.chips):

        @pl.when(p == q)
        def _(q=q):
            for i in range(3):
                qall[:, g.cols * i : g.cols * (i + 1)] = here[
                    i, :, g.cols * q : g.cols * (q + 1)
                ]

    vec[...] = jnp.zeros((VEC, LANES), BF)
    for i in range(8):
        vec[i : i + 1, 0 : g.shard] = lines[i][...].reshape(1, g.shard)
    for q in range(g.chips):
        vec[8 + q : 9 + q, 0 : g.block] = lines[8][g.block * q : g.block * (q + 1)].reshape(
            1, g.block
        )
    mine = pl.ds(pl.multiple_of(g.half * k, 16), g.half)
    qsend[0 : g.half] = qall[mine]
    qsend[g.half : g.half + VEC, 0:LANES] = vec[...]
    qsend[g.half : g.half + VEC, LANES:] = jnp.zeros((VEC, g.qkv - LANES), BF)


def prep_kernel(g, sc, _, wi, wd, wo, iall, oall, dall, send, here, sem):
    p, k = sc[0], sc[1]
    at = pl.multiple_of(g.block * p, 16)
    copies = [
        pltpu.make_async_copy(wi, here, sem.at[0]),
        pltpu.make_async_copy(wo, oall, sem.at[1]),
        pltpu.make_async_copy(wd.at[pl.ds(at, g.block)], dall, sem.at[2]),
    ]
    start(copies)
    finish(copies[:1])
    for q in range(g.chips):

        @pl.when(p == q)
        def _(q=q):
            for r in range(g.ring):
                src = g.hshard * r + g.block * q
                iall[:, g.block * r : g.block * (r + 1)] = here[:, src : src + g.block]

    mine = pl.ds(pl.multiple_of(g.half * k, 16), g.half)
    send[0 : g.half] = iall[mine]
    finish(copies[1:])
    send[g.half : 2 * g.half] = oall[mine]
    send[2 * g.half :] = dall[pl.ds(pl.multiple_of(g.bhalf * k, 16), g.bhalf)]


def lay(g, sc, own, mine, theirs, at, size, dst, turn=0):
    k, f = sc[1], jnp.bitwise_xor(sc[2], turn)
    dst[pl.ds(pl.multiple_of(2 * size * f, 16), 2 * size), :] = own[...]
    for s in range(1, g.ring):
        base = 2 * size * jnp.bitwise_xor(f, s)
        for src, core in ((mine[s - 1], k), (theirs[s - 1], 1 - k)):
            dst[pl.ds(pl.multiple_of(base + size * core, 16), size), :] = src[at : at + size, :]


def start(copies):
    for copy in copies:
        copy.start()


def finish(copies):
    for copy in copies:
        copy.wait()


def qkv_kernel(g, sc, *refs):
    n, c = g.ring - 1, 2 * g.chips
    xs = refs[:c]
    vec, own = refs[c : c + 2]
    mine = refs[c + 2 : c + 2 + n]
    theirs = refs[c + 2 + n : c + 2 + 2 * n]
    out, w, full = refs[c + 2 + 2 * n :]
    p, f = sc[0], sc[2]
    lay(g, sc, own, mine, theirs, 0, g.half, w)
    rest = jnp.zeros((VEC, g.width - LANES), F32)
    total = jnp.zeros((VEC, g.width), F32)
    for s in range(g.ring):
        piece = vec[...] if s == 0 else mine[s - 1][g.half : g.half + VEC, 0:LANES]
        piece = piece.astype(F32)
        wide = jnp.concatenate([piece, rest], axis=1)
        total = total + pltpu.roll(wide, g.shard * jnp.bitwise_xor(f, s), 1)
    full[...] = total
    back = pltpu.roll(total, lax.rem(g.width - g.cols * p, g.width), 1)
    bias = jnp.concatenate(
        [back[0:1, : g.cols], jnp.zeros((1, g.cols), F32), back[1:2, : g.cols]], axis=1
    )
    rows = jnp.concatenate([x[...] for x in xs], axis=0)
    found = (dot(rows, w[...]) + bias).astype(BF)
    for h in range(g.heads):
        for i in range(3):
            out[:, LANES * h + DH * i : LANES * h + DH * (i + 1)] = found[
                :, g.cols * i + DH * h : g.cols * i + DH * (h + 1)
            ]
        out[:, LANES * h + 3 * DH : LANES * (h + 1)] = jnp.zeros((2 * g.tokens, DH), BF)


def select(index, size, axis_size, lanes):
    if lanes:
        ids = lax.broadcasted_iota(jnp.int32, (size, axis_size), 1)
    else:
        ids = lax.broadcasted_iota(jnp.int32, (axis_size, size), 0)
    return jnp.where(ids == index, 1.0, 0.0).astype(BF)


def over(x, size):
    return lax.shift_right_logical(x, jnp.int32(size.bit_length() - 1))


def tables_kernel(g, sc, _, clusters, block_ids, pick, place, blocks):
    p, k = sc[0], sc[1]
    ranges, step = 2 * g.chips, g.clusters * g.members
    shape = (2 * ranges, 2 * ranges)
    piece, source = (lax.broadcasted_iota(jnp.int32, shape, axis) for axis in (0, 1))
    device = 2 * jnp.bitwise_xor(p, over(piece, 2) & (g.chips - 1)) + jnp.bitwise_xor(
        k, over(piece, 2 * g.chips)
    )
    found = jnp.where(piece & 1 == 0, device, 2 * ranges - 1 - device)
    hot = jnp.where(found == source, 1.0, 0.0).astype(BF)
    half = g.rows // 2
    line = block_ids[...].astype(F32)
    lines = [line[:, half * i : half * (i + 1)] for i in range(2 * ranges)]
    ids = dot(hot, jnp.concatenate(lines, axis=0).astype(BF))
    for d in range(ranges):
        line = jnp.concatenate([ids[2 * d : 2 * d + 1], ids[2 * d + 1 : 2 * d + 2]], axis=1)
        blocks[:, g.rows * d : g.rows * (d + 1)] = jnp.broadcast_to(line, (8, g.rows)).astype(BF)
    before = lax.broadcasted_iota(jnp.int32, (CLUSTER, CLUSTER), 1) < lax.broadcasted_iota(
        jnp.int32, (CLUSTER, CLUSTER), 0
    )
    rows, cols, tokens = [], [], []
    for h in range(g.heads):
        order = clusters[
            pl.ds(g.heads * p + h, 1), pl.ds(pl.multiple_of(g.entries * k, 128), g.entries)
        ]
        chip, core = over(order, 2 * g.rows), over(order, g.rows) & 1
        within = order & (g.rows - 1)
        rows.append(
            jnp.bitwise_xor(core, k) * g.tokens + jnp.bitwise_xor(chip, p) * g.rows + within
        )
    units = [(h, c) for h in range(g.heads) for c in range(g.clusters)]
    for h, c in units:
        row = rows[h][:, CLUSTER * c : CLUSTER * (c + 1)]
        tall = jnp.broadcast_to(row.astype(F32), (CLUSTER, CLUSTER))
        cols.append(over(jnp.transpose(tall)[:, 0:1].astype(jnp.int32), g.rows))
    spots = []
    for (h, c), col in zip(units, cols):
        row = rows[h][:, CLUSTER * c : CLUSTER * (c + 1)]
        same = (col == over(row, g.rows)) & before
        rank = jnp.sum(jnp.where(same, 1.0, 0.0), axis=1, keepdims=True).astype(jnp.int32)
        spots.append(select(col * g.members + rank, CLUSTER, CLUSTER, True))
    for (h, c), spot in zip(units, spots):
        row = rows[h][:, CLUSTER * c : CLUSTER * (c + 1)]
        within = jnp.broadcast_to((row & (g.rows - 1)).astype(F32), (8, CLUSTER)).astype(BF)
        tokens.append(dot(within, spot))
    for h in range(g.heads):
        for d in range(ranges):
            lanes = slice(g.members * d, g.members * (d + 1))
            mine = jnp.concatenate(
                [tokens[h * g.clusters + c][:, lanes] for c in range(g.clusters)], axis=1
            ).astype(jnp.int32)
            place[h, g.rows * d : g.rows * (d + 1)] = select(mine[0:1, :], step, g.rows, False)
            pick[h, step * d : step * (d + 1)] = select(
                jnp.transpose(mine)[:, 0:1], step, g.rows, True
            )


def mask_kernel(g, blocks, place, mask):
    ids = [
        [
            dot(blocks[:, g.rows * d : g.rows * (d + 1)], place[h, g.rows * d : g.rows * (d + 1)])
            for d in range(2 * g.chips)
        ]
        for h in range(g.heads)
    ]
    for h in range(g.heads):
        for c in range(g.clusters):
            lanes = slice(g.members * c, g.members * (c + 1))
            keys = jnp.concatenate([part[:, lanes] for part in ids[h]], axis=1)
            allowed = keys[0:1, :] <= jnp.transpose(keys)[:, 0:1]
            mask[h * g.clusters + c] = jnp.where(allowed, 0.0, FLOOR)


def cluster_rows(g, ref, c):
    step = g.clusters * g.members
    return jnp.concatenate(
        [
            ref[step * d + g.members * c : step * d + g.members * (c + 1)]
            for d in range(2 * g.chips)
        ],
        axis=0,
    )


def put_cluster(g, ref, c, values):
    step = g.clusters * g.members
    for d in range(2 * g.chips):
        ref[step * d + g.members * c : step * d + g.members * (c + 1)] = values[
            g.members * d : g.members * (d + 1)
        ]


def attend_kernel(g, qkv, pick, place, mask, ctx_own, ctx_other, kept, probs, mixed):
    step, ranges = g.clusters * g.members, 2 * g.chips
    units = [(h, c) for h in range(g.heads) for c in range(g.clusters)]
    for h in range(g.heads):
        for d in range(ranges):
            rows = qkv[g.rows * d : g.rows * (d + 1), LANES * h : LANES * (h + 1)]
            slots = slice(step * d, step * (d + 1))
            kept[h, slots] = dot(pick[h, slots], rows).astype(BF)
    for h, c in units:
        rows = cluster_rows(g, kept.at[h], c)
        q, key = rows[:, 0:DH], rows[:, DH : 2 * DH]
        at = h * g.clusters + c
        probs[at] = dot_nt(q, key) * (DH ** (-0.5)) + mask[at]
    for h, c in units:
        at = h * g.clusters + c
        masked = probs[at]
        weights = jnp.exp(masked - jnp.max(masked, axis=-1, keepdims=True))
        probs[at] = weights * (1.0 / jnp.sum(weights, axis=-1, keepdims=True))
    for h, c in units:
        v = cluster_rows(g, kept.at[h], c)[:, 2 * DH : 3 * DH]
        put_cluster(
            g, mixed.at[h], c, dot(probs[h * g.clusters + c].astype(BF), v).astype(BF)
        )
    for h in range(g.heads):
        for d in range(ranges):
            side, at = (ctx_own, d) if d < g.chips else (ctx_other, d - g.chips)
            rows = dot(
                place[h, g.rows * d : g.rows * (d + 1)], mixed[h, step * d : step * (d + 1)]
            )
            side[g.rows * at : g.rows * (at + 1), DH * h : DH * (h + 1)] = rows.astype(BF)


def attend_back_kernel(g, own, other, pick, place, kept, probs, grads, d_mixed, found, d_scores):
    step, ranges = g.clusters * g.members, 2 * g.chips
    scale = DH ** (-0.5)
    units = [(h, c) for h in range(g.heads) for c in range(g.clusters)]
    for h in range(g.heads):
        for d in range(ranges):
            side, at = (own, d) if d < g.chips else (other, d - g.chips)
            rows = side[g.rows * at : g.rows * (at + 1), DH * h : DH * (h + 1)]
            slots = slice(step * d, step * (d + 1))
            d_mixed[h, slots] = dot(pick[h, slots], rows).astype(BF)
    for h, c in units:
        v = cluster_rows(g, kept.at[h], c)[:, 2 * DH : 3 * DH]
        share = probs[h * g.clusters + c]
        d_share = dot_nt(cluster_rows(g, d_mixed.at[h], c), v)
        delta = jnp.sum(share * d_share, axis=-1, keepdims=True)
        d_scores[h * g.clusters + c] = (share * (d_share - delta)).astype(BF)
    for h, c in units:
        rows = cluster_rows(g, kept.at[h], c)
        d_s, share = d_scores[h * g.clusters + c], probs[h * g.clusters + c].astype(BF)
        d_q = dot(d_s, rows[:, DH : 2 * DH]) * scale
        d_k = dot_tn(d_s, rows[:, 0:DH]) * scale
        d_v = dot_tn(share, cluster_rows(g, d_mixed.at[h], c))
        put_cluster(g, found.at[h], c, jnp.concatenate([d_q, d_k, d_v], axis=1).astype(BF))
    for h in range(g.heads):
        for d in range(ranges):
            at = slice(g.rows * d, g.rows * (d + 1))
            rows = dot(place[h, at], found[h, step * d : step * (d + 1)]).astype(BF)
            for i in range(3):
                grads[at, g.cols * i + DH * h : g.cols * i + DH * (h + 1)] = rows[
                    :, DH * i : DH * (i + 1)
                ]
    grads[:, g.qkv :] = jnp.zeros((2 * g.tokens, g.wide - g.qkv), BF)


def norm_parts(values):
    centre = values - jnp.mean(values, axis=-1, keepdims=True)
    spread = jnp.mean(centre * centre, axis=-1, keepdims=True)
    scale = lax.rsqrt(spread + EPSILON)
    return centre * scale, scale


def norm_back(grad, z, scale):
    return scale * (
        grad
        - jnp.mean(grad, axis=-1, keepdims=True)
        - z * jnp.mean(grad * z, axis=-1, keepdims=True)
    )


def seen(g, ref, j):
    half = g.chips // 2
    return jnp.concatenate(
        [
            ref[
                g.rows * ((i ^ j) % half) : g.rows * ((i ^ j) % half + 1),
                g.cols * ((i ^ j) // half) : g.cols * ((i ^ j) // half + 1),
            ]
            for i in range(g.chips)
        ],
        axis=0,
    )


def forward_kernel(g, sc, *refs):
    c, n = g.chips, g.ring - 1
    ctxs, xs, full = refs[:c], refs[c : 2 * c], refs[2 * c]
    wo_own, wi_own, wd_own = refs[2 * c + 1 : 2 * c + 4]
    refs = refs[2 * c + 4 :]
    mine, theirs = refs[:n], refs[n : 2 * n]
    refs = refs[2 * n :]
    parts, (active, inner, low, z_own, s_own, wo_rows, wi, wd) = refs[:c], refs[c : c + 8]
    wo, work = refs[c + 8 :]
    p = sc[0]
    lay(g, sc, wo_own, mine, theirs, g.half, g.half, wo, p)
    rows = jnp.concatenate([seen(g, ctxs[j], j) for j in range(c)], axis=1)
    wo_rows[...] = wo[0 : g.cols]
    halves = [slice(i, i + g.tokens // 2) for i in range(0, g.tokens, g.tokens // 2)]
    bias = full[pl.ds(8 + p, 1), :]

    def first_norm(half):
        for i in range(half.start, half.stop, SLAB):
            at = slice(i, i + SLAB)
            x = xs[i // g.rows][i % g.rows : i % g.rows + SLAB].astype(F32)
            z, scale = norm_parts(work[at] + x + full[2:3, :])
            first = z * full[3:4, :] + full[4:5, :]
            low[at] = first.astype(BF)
            if i < g.rows:
                z_own[at] = z
                s_own[at] = jnp.broadcast_to(scale, (SLAB, 128))
                parts[0][at] = first + full[5:6, :]

    def activate(half):
        for i in range(half.start, half.stop, SLAB):
            at = slice(i, i + SLAB)
            u = inner[at] + bias
            inner[at] = u
            active[at] = (u * (1.0 + lax.erf(u * (0.5**0.5))) * 0.5).astype(BF)

    def descend(half):
        second = dot(active[half], wd[...])
        for i in range(half.start, half.stop, g.rows):
            block = second[i - half.start : i - half.start + g.rows]
            if i == 0:
                parts[0][...] += block
            else:
                parts[i // g.rows][...] = block.astype(BF)

    one, two = halves
    work[one] = dot(rows[one], wo[...])
    work[two] = dot(rows[two], wo[...])
    lay(g, sc, wi_own, mine, theirs, 0, g.half, wi)
    first_norm(one)
    inner[one] = dot(low[one], wi[...])
    first_norm(two)
    inner[two] = dot(low[two], wi[...])
    lay(g, sc, wd_own, mine, theirs, 2 * g.half, g.bhalf, wd)
    activate(one)
    descend(one)
    activate(two)
    descend(two)


def turn_kernel(g, *refs):
    c = g.chips
    parts, full, cotangent = refs[:c], refs[c], refs[c + 1]
    out, d_second, branch = refs[c + 2 :]
    second = parts[0][...]
    for j in range(1, c):
        second = second + parts[j][...].astype(F32)
    z, scale = norm_parts(second)
    gain = full[6:7, :]
    out[...] = (z * gain + full[7:8, :]).astype(BF)
    dy = cotangent[...].astype(F32)
    grad = norm_back(dy * gain, z, scale)
    d_second[...] = grad
    branch[0 : g.rows] = grad.astype(BF)
    one = jnp.sum(dy * z, axis=0, keepdims=True)
    two = jnp.sum(dy, axis=0, keepdims=True)
    rest = jnp.zeros((STATS - 2, g.width), F32)
    branch[g.rows : g.rows + STATS] = jnp.concatenate([one, two, rest], axis=0).astype(BF)


def back_kernel(g, *refs):
    c = g.chips
    branches, slope, wd, wi = refs[:c], refs[c], refs[c + 1], refs[c + 2]
    parts, d_inner = refs[c + 3 : 2 * c + 3], refs[2 * c + 3]
    rows = jnp.concatenate([b[0 : g.rows] for b in branches], axis=0)
    d_active = dot_nt(rows, wd[...])
    d_inner[...] = (d_active * slope[...]).astype(BF)
    total = dot_nt(d_inner[...], wi[...])
    parts[0][...] = total[: g.rows]
    for j in range(1, c):
        parts[j][...] = total[g.rows * j : g.rows * (j + 1)].astype(BF)


def split_rows(g, sc, total, size, own, other, at):
    k, f = sc[1], sc[2]
    for s in range(g.ring):
        base = 2 * size * jnp.bitwise_xor(f, s)
        own[s, at : at + size] = total[pl.ds(pl.multiple_of(base + size * k, 8), size), :]
        other[s, at : at + size] = total[
            pl.ds(pl.multiple_of(base + size * (1 - k), 8), size), :
        ].astype(BF)


def mlp_grads_kernel(g, sc, *refs):
    c = g.chips
    branches, active, low, d_inner = refs[:c], refs[c], refs[c + 1], refs[c + 2]
    own, other, sums, total = refs[c + 3 :]
    rows = jnp.concatenate([b[0 : g.rows] for b in branches], axis=0)
    total[...] = dot_tn(active[...], rows)
    split_rows(g, sc, total, g.bhalf, own, other, g.half)
    total[...] = dot_tn(low[...], d_inner[...])
    split_rows(g, sc, total, g.half, own, other, 0)
    stats = branches[0][g.rows : g.rows + STATS].astype(F32)
    for j in range(1, c):
        stats = stats + branches[j][g.rows : g.rows + STATS].astype(F32)
    down = jnp.sum(rows.astype(F32), axis=0, keepdims=True)
    up = jnp.sum(d_inner[...].astype(F32), axis=0, keepdims=True)
    sums[...] = jnp.concatenate([stats[0:2], down, up, jnp.zeros((4, g.width), F32)], axis=0)


def first_kernel(g, *refs):
    c = g.chips
    parts, d_second, z_own, s_own, full = refs[:c], *refs[c : c + 4]
    d_sum, attended = refs[c + 4 :]
    d_first = d_second[...] + parts[0][...]
    for j in range(1, c):
        d_first = d_first + parts[j][...].astype(F32)
    z = z_own[...]
    grad = norm_back(d_first * full[3:4, :], z, s_own[:, 0:1])
    d_sum[...] = grad
    attended[0 : g.rows] = grad.astype(BF)
    one = jnp.sum(d_first * z, axis=0, keepdims=True)
    two = jnp.sum(d_first, axis=0, keepdims=True)
    rest = jnp.zeros((STATS - 2, g.width), F32)
    attended[g.rows : g.rows + STATS] = jnp.concatenate([one, two, rest], axis=0).astype(BF)


def context_kernel(g, *refs):
    grads, wo_rows, out = refs[: g.chips], refs[g.chips], refs[g.chips + 1]
    rows = jnp.concatenate([b[0 : g.rows] for b in grads], axis=0)
    out[...] = dot_nt(rows, wo_rows[...]).astype(BF)


def out_grads_kernel(g, sc, *refs):
    c = g.chips
    grads, ctxs, sums = refs[:c], refs[c : 2 * c], refs[2 * c]
    own, away, total = refs[2 * c + 1 :]
    p, f = sc[0], sc[2]
    rows = jnp.concatenate([b[0 : g.rows] for b in grads], axis=0)
    for j in range(c):
        q = jnp.bitwise_xor(p, j)
        total[pl.ds(pl.multiple_of(g.cols * q, 64), g.cols), :] = dot_tn(seen(g, ctxs[j], j), rows)
    stats = grads[0][g.rows : g.rows + STATS].astype(F32)
    for j in range(1, c):
        stats = stats + grads[j][g.rows : g.rows + STATS].astype(F32)
    out = jnp.sum(rows.astype(F32), axis=0, keepdims=True)
    rest = jnp.zeros((STATS - 7, g.width), F32)
    block = jnp.concatenate([sums[0:4], stats[0:2], out, rest], axis=0)
    size = g.shard // c
    for s in range(g.ring):
        base = g.shard * jnp.bitwise_xor(f, s) + size * p
        part = total[pl.ds(pl.multiple_of(base, 8), size), :]
        if s % 2:
            away[s // 2, 0:size] = part.astype(BF)
            away[s // 2, size:] = block.astype(BF)
        else:
            own[s // 2, 0:size] = part
            own[s // 2, size:] = block


def summed(g, mine, theirs, at):
    one = mine[g.tokens * at : g.tokens * (at + 1), : g.qkv].astype(F32)
    two = theirs[g.tokens * (1 - at) : g.tokens * (2 - at), : g.qkv].astype(F32)
    return (one + two).astype(BF)


def input_kernel(g, mine, theirs, w, *parts):
    total = dot_nt(summed(g, mine, theirs, 0), w[...])
    parts[0][...] = total[: g.rows]
    for j in range(1, g.chips):
        parts[j][...] = total[g.rows * j : g.rows * (j + 1)].astype(BF)


def turn_rows_kernel(g, sc, *refs):
    xs, out = refs[: 2 * g.chips], refs[2 * g.chips]
    rows = jnp.concatenate([x[...] for x in xs], axis=0)
    for core in range(2):

        @pl.when(sc[1] == core)
        def _(core=core):
            for r in range(g.ring):
                lane = g.shard * r + g.half * core
                out[g.half * r : g.half * (r + 1), :] = jnp.transpose(rows[:, lane : lane + g.half])


def qkv_grads_kernel(g, sc, mine, theirs, turned_x, own, away, total):
    f = sc[2]
    rows = jnp.concatenate([summed(g, mine, theirs, 0), summed(g, mine, theirs, 1)], axis=0)
    total[...] = dot(turned_x[...], rows)
    sums = jnp.sum(rows.astype(F32), axis=0, keepdims=True)
    gap = jnp.zeros((8, g.width - g.qkv), F32)
    block = jnp.concatenate(
        [jnp.concatenate([sums, jnp.zeros((7, g.qkv), F32)], axis=0), gap], axis=1
    )
    for s in range(g.ring):
        part = total[pl.ds(pl.multiple_of(g.half * jnp.bitwise_xor(f, s), 8), g.half), :]
        packed = pack(g, part)
        if s % 2:
            away[s // 2, 0 : g.packed] = packed.astype(BF)
            away[s // 2, g.packed :] = block.astype(BF)
        else:
            own[s // 2, 0 : g.packed] = packed
            own[s // 2, g.packed :] = block


def pack(g, part):
    step = g.half - g.packed
    beside = [
        part[g.packed :, step_lanes : step_lanes + g.width - g.qkv]
        for step_lanes in range(0, g.qkv, g.width - g.qkv)
    ]
    return jnp.concatenate(
        [part[0 : g.packed], jnp.concatenate(beside, axis=0)], axis=1
    )


def sources(g, sc, refs):
    p, k = sc[0], sc[1]
    out = []
    for j, (mine, theirs) in enumerate(zip(refs, others(g, refs))):
        q = jnp.bitwise_xor(p, j)
        out.append((q, k, mine))
        out.append((q, 1 - k, theirs))
    return out


def others(g, refs):
    far = refs[g.chips :]
    return far if len(far) > 1 else [far[0].at[j] for j in range(g.chips)]


def paired(g, sc, refs, body):
    p, k = sc[0], sc[1]
    mine, theirs = refs[: g.chips], others(g, refs)
    for odd in range(2):

        @pl.when(p & 1 == odd)
        def _(odd=odd):
            for j in range(0, g.chips, 2):
                pair = jnp.bitwise_xor(over(p, 2), j // 2)
                for found, core in ((mine, k), (theirs, 1 - k)):
                    body(pair, core, found[j ^ odd], found[j ^ odd ^ 1])


def mlp_final_kernel(g, sc, *refs):
    found, (g_in, g_down) = refs[:-2], refs[-2:]

    def place(pair, core, even, odd):
        mine = pl.ds(pl.multiple_of(g.half * core, 8), g.half)
        for i, ref in enumerate((even, odd)):
            at = pl.multiple_of(g.block * (2 * pair + i) + g.bhalf * core, 8)
            g_down[pl.ds(at, g.bhalf), :] = ref[g.half :, :].astype(F32)
        for r in range(g.ring):
            lane = pl.multiple_of(g.hshard * r + 2 * g.block * pair, 128)
            lanes = slice(g.block * r, g.block * (r + 1))
            g_in[mine, pl.ds(lane, 2 * g.block)] = jnp.concatenate(
                [even[0 : g.half, lanes], odd[0 : g.half, lanes]], axis=1
            ).astype(F32)

    paired(g, sc, found, place)


def last_kernel(g, sc, *refs):
    found = refs[: 2 * g.chips]
    gq, gk, gv, g_bq, g_bv, g_out, g_bin, *small = refs[2 * g.chips :]
    p, f = sc[0], sc[2]
    size, step = g.shard // g.chips, g.half - g.packed
    top = g.packed + 8
    for q, core, ref in sources(g, sc, found):

        @pl.when((q == f) & (core == 0))
        def _(ref=ref):
            row = ref[g.packed : top, :].astype(F32)[0:1]
            for dst, at in zip((g_bq, g_bv), (0, 2)):
                dst[...] = row[:, g.cols * at : g.cols * (at + 1)].reshape(g.shard)

    def place(pair, core, even, odd):
        base = pl.multiple_of(g.half * core, 8)
        lane = pl.ds(pl.multiple_of(2 * g.cols * pair, 128), 2 * g.cols)
        for i, dst in enumerate((gq, gk, gv)):
            for rows, at, lanes in (
                (pl.ds(base, g.packed), slice(0, g.packed), slice(g.cols * i, g.cols * (i + 1))),
                (
                    pl.ds(base + g.packed, step),
                    slice(step * i, step * (i + 1)),
                    slice(g.qkv, g.width),
                ),
            ):
                dst[rows, lane] = jnp.concatenate(
                    [even[at, lanes], odd[at, lanes]], axis=1
                ).astype(F32)

    paired(g, sc, found, place)
    far = others(g, found)
    for j in range(g.chips):
        q = jnp.bitwise_xor(p, j)
        one, two = found[j], far[j]
        both = one[top:, :].astype(F32) + two[top:, :].astype(F32)
        g_out[pl.ds(pl.multiple_of(size * q, 8), size), :] = both[0:size]
        back = pltpu.roll(both[size : size + STATS], lax.rem(g.width - g.shard * f, g.width), 1)
        for chip in range(g.chips):

            @pl.when(q == chip)
            def _(chip=chip, back=back):
                g_bin[g.block * chip : g.block * (chip + 1)] = back[3:4, : g.shard].reshape(g.shard)
                if chip == 0:
                    for i, dst in zip((0, 1, 2, 4, 5, 6), small):
                        dst[...] = back[i : i + 1, : g.shard].reshape(g.shard)


def to_core(x):
    n = lax.axis_size("ctx")
    return lax.ppermute(x, "ctx", [(i, i ^ 1) for i in range(n)])


def to_chip(x, j):
    n = lax.axis_size("ctx")
    return lax.ppermute(x, "ctx", [(i, i ^ (2 * j)) for i in range(n)])


def along(x, mask):
    n = lax.axis_size("fsdp")
    return lax.ppermute(x, "fsdp", [(i, i ^ mask) for i in range(n)])


def gather_ring(x, pause=None):
    n = lax.axis_size("fsdp")
    found, mask, first = {0: x}, n // 2, ()
    while mask:
        for s in sorted(found):
            first = [found[t] for t in sorted(found) if t]
            part = found[s] if s == 0 or pause is None else after(found[s], pause, *first)
            found[s | mask] = along(part, mask)
        mask //= 2
    return [found[s] for s in range(1, n)]


def spread(x, chips):
    far = {j: to_chip(x, j) for j in sorted(range(1, chips), key=lambda j: -bin(j).count("1"))}
    return [x] + [far[j] for j in range(1, chips)]


def pass_on(x, chips, pause):
    found = {0: x}
    mask = 1
    while mask < chips:
        for j in sorted(found):
            found[j | mask] = to_chip(found[j] if j == 0 else after(found[j], pause), mask)
        mask *= 2
    return [found[j] for j in range(chips)]


def swap(parts):
    far = {j: to_chip(parts[j], j) for j in sorted(range(1, len(parts)), key=lambda j: -bin(j).count("1"))}
    return [parts[0]] + [far[j] for j in range(1, len(parts))]


def ring_step(kept, away, mask):
    count, rows, width = kept.shape
    half = count // 2

    def step(mine, got):
        total = mine + got.astype(F32)
        if not half:
            return (total.astype(BF),)
        return total.reshape(half, 2, rows, width)[:, 0], total.reshape(
            half, 2, rows, width
        )[:, 1].astype(BF)

    outs = [shaped((half, rows, width), F32), shaped((half, rows, width), BF)]
    return mix(
        step,
        outs if half else [shaped((1, rows, width), BF)],
        kept,
        along(away, mask),
        name="ring_step",
    )


def kept_far(x):
    return pltpu.with_memory_space_constraint(x, pltpu.HBM)


def after(x, *first):
    return lax.optimization_barrier((x, *first))[0]


def ring_step(kept, away, mask):
    count, rows, width = kept.shape
    half = count // 2

    def step(mine, got):
        total = mine + got.astype(F32)
        if not half:
            return (total.astype(BF),)
        return total.reshape(half, 2, rows, width)[:, 0], total.reshape(
            half, 2, rows, width
        )[:, 1].astype(BF)

    outs = [shaped((half, rows, width), F32), shaped((half, rows, width), BF)]
    return mix(
        step,
        outs if half else [shaped((1, rows, width), BF)],
        kept,
        along(away, mask),
        name="ring_step",
    )


def kept_far(x):
    return pltpu.with_memory_space_constraint(x, pltpu.HBM)


def after(x, *first):
    return lax.optimization_barrier((x, *first))[0]


def plane_pieces(piece, chips):
    near = spread(piece, chips)
    return near + [to_core(part) for part in near]


def chip_body(
    hidden_in,
    out_grad,
    block_ids,
    clusters,
    w_query,
    w_key,
    w_value,
    w_out,
    b_query,
    b_value,
    b_out,
    ln1_gain,
    ln1_bias,
    w_in,
    b_in,
    w_down,
    b_down,
    ln2_gain,
    ln2_bias,
):
    n, ring = lax.axis_size("ctx"), lax.axis_size("fsdp")
    chips = n // 2
    rows, width = hidden_in.shape[1:]
    hidden = w_in.shape[1]
    g = Plan(chips, ring, width, hidden, rows)
    c, f = lax.axis_index("ctx"), lax.axis_index("fsdp")
    p, k = c // 2, c % 2
    sc = jnp.stack([p, k, f]).astype(jnp.int32)
    bind = functools.partial


    qall, qsend, vec = call(
        bind(pick_kernel, g),
        [
            shaped((g.shard, g.qkv), BF),
            shaped((g.half + VEC, g.qkv), BF),
            shaped((VEC, LANES), BF),
        ],
        [SMEM] + [FAR] * 12,
        [
            sc,
            *map(
                kept_far,
                (
                    w_query,
                    w_key,
                    w_value,
                    b_query,
                    b_value,
                    b_out,
                    ln1_gain,
                    ln1_bias,
                    b_down,
                    ln2_gain,
                    ln2_bias,
                    b_in,
                ),
            ),
        ],
        [
            pltpu.VMEM((3, g.shard, width), BF),
        ]
        + [pltpu.VMEM((g.shard,), BF)] * 8
        + [pltpu.VMEM((g.hshard,), BF), pltpu.SemaphoreType.DMA((12,))],
        name="pick_weights",
    )
    x_own = after(hidden_in.reshape(rows, width), qsend)
    xs = spread(x_own, chips)
    iall, oall, dall, send = call(
        bind(prep_kernel, g),
        [
            shaped((g.shard, g.share), BF),
            shaped((g.shard, width), BF),
            shaped((g.block, width), BF),
            shaped((2 * g.half + g.bhalf, width), BF),
        ],
        [SMEM, HBM, FAR, FAR, FAR],
        [sc, qsend, kept_far(w_in), kept_far(w_down), kept_far(w_out)],
        [pltpu.VMEM((g.shard, hidden), BF), pltpu.SemaphoreType.DMA((3,))],
        name="prepare_weights",
    )
    q_mine = gather_ring(qsend, send)

    step = g.clusters * g.members
    pick, place, blk = call(
        bind(tables_kernel, g),
        [
            shaped((g.heads, 2 * chips * step, rows), BF),
            shaped((g.heads, 2 * g.tokens, step), BF),
            shaped((8, 2 * g.tokens), BF),
        ],
        [SMEM, HBM] + [VMEM] * 2,
        [sc, q_mine[0], clusters[0], block_ids],
        name="cluster_tables",
    )
    (mask,) = call(
        bind(mask_kernel, g),
        [shaped((g.heads * g.clusters, CLUSTER, CLUSTER), F32)],
        [VMEM] * 2,
        [blk, place],
        name="cluster_mask",
    )
    x_other = [to_core(after(xs[0], xs[1]))] + [to_core(x) for x in xs[1:]]
    q_theirs = [to_core(after(part, xs[1])) for part in q_mine]
    qkv, w_qkv, full = call(
        bind(qkv_kernel, g),
        [
            shaped((2 * g.tokens, g.padded), BF),
            shaped((width, g.qkv), BF),
            shaped((VEC, width), F32),
        ],
        [SMEM] + [VMEM] * (2 * chips + 2 * ring),
        [sc, *xs, *x_other, after(vec, send), qall, *q_mine, *q_theirs],
        name="project",
    )
    ctx_own, ctx_other, kept, probs = call(
        bind(attend_kernel, g),
        [
            shaped((g.tokens, g.cols), BF),
            shaped((g.tokens, g.cols), BF),
            shaped((g.heads, g.entries, LANES), BF),
            shaped((g.heads * g.clusters, CLUSTER, CLUSTER), F32),
        ],
        [VMEM] * 4,
        [qkv, pick, place, mask],
        [pltpu.VMEM((g.heads, g.entries, DH), BF)],
        name="attend",
    )
    (ctx,) = mix(
        lambda a, b: (
            jnp.concatenate([a[: g.tokens // 2] + b[: g.tokens // 2], a[g.tokens // 2 :] + b[g.tokens // 2 :]], axis=1),
        ),
        [shaped((g.tokens // 2, 2 * g.cols), BF)],
        ctx_own,
        to_core(ctx_other),
        name="join_context",
    )
    ctxs = spread(ctx, chips)
    w_mine = gather_ring(send, ctx_own)

    w_theirs = [to_core(after(part, *ctxs[1:])) for part in w_mine]
    *second, active, inner, low, z_own, s_own, wo_rows, wi, wd = call(
        bind(forward_kernel, g),
        [shaped((rows, width), F32)]
        + [shaped((rows, width), BF)] * (chips - 1)
        + [
            shaped((g.tokens, g.share), BF),
            shaped((g.tokens, g.share), F32),
            shaped((g.tokens, width), BF),
            shaped((rows, width), F32),
            shaped((rows, 128), F32),
            shaped((g.cols, width), BF),
            shaped((width, g.share), BF),
            shaped((g.share, width), BF),
        ],
        [SMEM] + [VMEM] * (2 * chips + 2 * ring + 2),
        [sc, *ctxs, *xs, full, oall, iall, dall, *w_mine, *w_theirs],
        [pltpu.VMEM((width, width), BF), pltpu.VMEM((g.tokens, width), F32)],
        name="mlp_forward",
    )
    (slope,) = mix(
        lambda u: (
            0.5 * (1.0 + lax.erf(u * (0.5**0.5)))
            + u * jnp.exp(-0.5 * u * u) * (1.0 / (2.0 * math.pi) ** 0.5),
        ),
        [shaped((g.tokens, g.share), F32)],
        inner,
        name="gelu_slope",
    )
    (turned_x,) = call(
        bind(turn_rows_kernel, g),
        [shaped((ring * g.half, 2 * g.tokens), BF)],
        [SMEM] + [VMEM] * (2 * chips),
        [sc, after(xs[0], inner), *xs[1:], *x_other],
        name="turn_rows",
    )
    second = swap(second)
    layer_out, d_second, branch = call(
        bind(turn_kernel, g),
        [
            shaped((rows, width), BF),
            shaped((rows, width), F32),
            shaped((rows + STATS, width), BF),
        ],
        [VMEM] * (chips + 2),
        [*second, after(full, turned_x), out_grad.reshape(rows, width)],
        name="norm_two",
    )
    branches = spread(branch, chips)
    *d_first, d_inner = call(
        bind(back_kernel, g),
        [shaped((rows, width), F32)]
        + [shaped((rows, width), BF)] * (chips - 1)
        + [shaped((g.tokens, g.share), BF)],
        [VMEM] * (chips + 3),
        [*branches, slope, wd, wi],
        name="mlp_back",
    )
    d_first = swap(d_first)
    m_own, m_other, sums = call(
        bind(mlp_grads_kernel, g),
        [
            shaped((ring, g.half + g.bhalf, width), F32),
            shaped((ring, g.half + g.bhalf, width), BF),
            shaped((8, width), F32),
        ],
        [SMEM] + [VMEM] * (chips + 3),
        [sc, *branches, active, low, d_inner],
        [pltpu.VMEM((width, g.share), F32)],
        name="mlp_grads",
    )
    m_got = to_core(m_other)
    m_rows = g.half + g.bhalf

    def joined(own, got):
        total = own + got.astype(F32)
        return (total[0], *(total[s].astype(BF) for s in range(1, ring)))

    m_kept, *m_away = mix(
        joined,
        [shaped((m_rows, width), F32)] + [shaped((m_rows, width), BF)] * (ring - 1),
        m_own,
        m_got,
        name="join_grads",
    )
    (m_piece,) = mix(
        lambda kept, *parts: (sum((part.astype(F32) for part in parts), kept).astype(BF),),
        [shaped((m_rows, width), BF)],
        m_kept,
        *(along(part, s) for s, part in enumerate(m_away, 1)),
        name="mlp_sum",
    )
    d_sum, attended = call(
        bind(first_kernel, g),
        [shaped((rows, width), F32), shaped((rows + STATS, width), BF)],
        [VMEM] * (chips + 4),
        [*d_first, after(d_second, *m_away), z_own, s_own, full],
        name="norm_one",
    )
    grads = spread(attended, chips)
    (d_ctx,) = call(
        bind(context_kernel, g),
        [shaped((g.tokens, g.cols), BF)],
        [VMEM] * (chips + 1),
        [*grads, after(wo_rows, m_piece)],
        name="context_back",
    )
    d_ctx_other = to_core(d_ctx)
    o_rows = g.shard // chips + STATS
    o_own, o_away = call(
        bind(out_grads_kernel, g),
        [shaped((ring // 2, o_rows, width), F32), shaped((ring // 2, o_rows, width), BF)],
        [SMEM] + [VMEM] * (2 * chips + 1),
        [sc, *grads, *ctxs, sums],
        [pltpu.VMEM((width, width), F32)],
        name="out_grads",
    )
    (dq_mine,) = call(
        bind(attend_back_kernel, g),
        [shaped((2 * g.tokens, g.wide), BF)],
        [VMEM] * 6,
        [d_ctx, d_ctx_other, pick, place, after(kept, o_own), probs],
        [
            pltpu.VMEM((g.heads, g.entries, DH), BF),
            pltpu.VMEM((g.heads, g.entries, 3 * DH), BF),
            pltpu.VMEM((g.heads * g.clusters, CLUSTER, CLUSTER), BF),
        ],
        name="attend_back",
    )
    dq_theirs = to_core(dq_mine)
    q_rows = g.packed + 8
    q_own, q_away = call(
        bind(qkv_grads_kernel, g),
        [shaped((ring // 2, q_rows, width), F32), shaped((ring // 2, q_rows, width), BF)],
        [SMEM] + [VMEM] * 3,
        [sc, dq_mine, dq_theirs, turned_x],
        [pltpu.VMEM((ring * g.half, g.qkv), F32)],
        name="project_grads",
    )
    d_in = call(
        bind(input_kernel, g),
        [shaped((rows, width), F32)] + [shaped((rows, width), BF)] * (chips - 1),
        [VMEM] * 3,
        [dq_mine, dq_theirs, w_qkv],
        name="project_back",
    )
    d_in = swap(d_in)
    mask_at = 2
    q_away0 = q_away
    o_away = after(o_away, dq_mine)
    while q_own.shape[0] > 1:
        q_own, q_away = ring_step(q_own, q_away, mask_at // 2)
        o_own, o_away = ring_step(o_own, o_away, mask_at // 2)
        mask_at *= 2
    near = pass_on(m_piece, chips, dq_theirs)
    m_pieces = near + [to_core(part) for part in near]
    (input_grad,) = mix(
        lambda kept, *parts: (sum((part.astype(F32) for part in parts), kept).astype(BF),),
        [shaped((rows, width), BF)],
        d_sum,
        *d_in,
        name="input_sum",
    )
    g_in, g_down = call(
        bind(mlp_final_kernel, g),
        [shaped((g.shard, hidden), F32), shaped((g.hshard, width), F32)],
        [SMEM] + [VMEM] * len(m_pieces),
        [sc, *m_pieces],
        name="mlp_lay",
    )
    vector = shaped((g.shard,), F32)
    (piece,) = mix(
        lambda a, b, c, d: (
            jnp.concatenate([a[0] + b[0].astype(F32), c[0] + d[0].astype(F32)], axis=0).astype(BF),
        ),
        [shaped((q_rows + o_rows, width), BF)],
        q_own,
        along(q_away, mask_at // 2),
        o_own,
        along(o_away, mask_at // 2),
        name="last_sum",
    )
    near = spread(after(piece, input_grad), chips)
    pieces = near + [to_core(part) for part in near]
    found = call(
        bind(last_kernel, g),
        [shaped((g.shard, width), F32)] * 3
        + [vector] * 2
        + [shaped((g.shard, width), F32), shaped((g.hshard,), F32)]
        + [vector] * 6,
        [SMEM] + [VMEM] * (2 * chips),
        [after(sc, g_down), *pieces],
        name="last_lay",
    )
    gq, gk, gv, g_bq, g_bv, g_out, g_bin, g_gain2, g_bias2, g_bdown, g_gain1, g_bias1, g_bout = found
    return (
        layer_out.reshape(1, rows, width),
        input_grad.reshape(1, rows, width),
        gq,
        gk,
        gv,
        g_out,
        g_bq,
        g_bv,
        g_bout,
        g_gain1,
        g_bias1,
        g_in,
        g_bin,
        g_down,
        g_bdown,
        g_gain2,
        g_bias2,
    )


def fits(mesh):
    n, ring = mesh.shape["ctx"], mesh.shape["fsdp"]
    chips = n // 2
    return n % 2 == 0 and chips & (chips - 1) == 0 and chips > 1 and ring == chips and H % chips == 0 and ring * chips <= 16


def solution(mesh):
    in_specs = (
        P("fsdp", "ctx", None),
        P("fsdp", "ctx", None),
        P("fsdp", None),
        P("fsdp", None, None),
        P("fsdp", None),
        P("fsdp", None),
        P("fsdp", None),
        P("fsdp", None),
        P("fsdp"),
        P("fsdp"),
        P("fsdp"),
        P("fsdp"),
        P("fsdp"),
        P("fsdp", None),
        P("fsdp"),
        P("fsdp", None),
        P("fsdp"),
        P("fsdp"),
        P("fsdp"),
    )
    out_specs = (
        P("fsdp", "ctx", None),
        P("fsdp", "ctx", None),
        P("fsdp", None),
        P("fsdp", None),
        P("fsdp", None),
        P("fsdp", None),
        P("fsdp"),
        P("fsdp"),
        P("fsdp"),
        P("fsdp"),
        P("fsdp"),
        P("fsdp", None),
        P("fsdp"),
        P("fsdp", None),
        P("fsdp"),
        P("fsdp"),
        P("fsdp"),
    )
    body = chip_body if fits(mesh) else general_body
    return jax.shard_map(body, mesh=mesh, in_specs=in_specs, out_specs=out_specs, check_vma=False)
```

```python
import functools
import math

import jax
import jax.numpy as jnp
from jax import lax
from jax.experimental import pallas as pl
from jax.experimental.pallas import tpu as pltpu
from jax.sharding import PartitionSpec as P

H = 12
DH = 64
CLUSTER = 128


EPSILON = 1e-12
FLOOR = -1e30


def layer_norm(values, gain, shift):
    centre = values - jnp.mean(values, axis=-1, keepdims=True)
    spread = jnp.mean(centre * centre, axis=-1, keepdims=True)
    return centre * lax.rsqrt(spread + EPSILON) * gain + shift


def exact_gelu(values):
    return jax.nn.gelu(values, approximate=False)


def positions(length, per_device, parts):
    stored = jnp.arange(length, dtype=jnp.int32)
    device = stored // per_device
    within = stored % per_device
    half = per_device // 2
    return jnp.where(
        within < half, device * half + within, (2 * parts - 1 - device) * half + within - half
    )


def contract(left, right):
    return lax.dot_general(
        left, right, (((0,), (0,)), ((), ())), preferred_element_type=jnp.float32
    )


def back_product(grad, weight):
    return lax.dot_general(
        grad, weight, (((1,), (1,)), ((), ())), preferred_element_type=jnp.float32
    )


def column_sum(values):
    return jnp.sum(values.astype(jnp.float32), axis=0)


def per_head_rows(rows, index):
    split = rows.reshape(rows.shape[0], H, DH)
    return jnp.take_along_axis(split, index.T[:, :, None], axis=0)


def cluster_tables(order, device, per_device, parts):
    heads, length = order.shape
    groups = length // CLUSTER
    members = CLUSTER // parts
    mine = (order // per_device == device).astype(jnp.int32)
    rank = jnp.cumsum(mine.reshape(heads, groups, CLUSTER), axis=-1).reshape(heads, length) - 1
    entry = jnp.arange(length, dtype=jnp.int32)[None, :]
    slot = jnp.where(mine == 1, entry // CLUSTER * members + rank, per_device)
    head_index = jnp.arange(heads, dtype=jnp.int32)[:, None]
    picked = (
        jnp.zeros((heads, per_device), jnp.int32)
        .at[head_index, slot]
        .set(order - device * per_device, mode="drop")
    )
    counter = jnp.broadcast_to(
        jnp.arange(per_device, dtype=jnp.int32)[None, :], (heads, per_device)
    )
    placed = jnp.zeros((heads, per_device), jnp.int32).at[head_index, picked].set(counter)
    inverse = (
        jnp.zeros((heads, length), jnp.int32)
        .at[head_index, order]
        .set(jnp.broadcast_to(jnp.arange(length, dtype=jnp.int32)[None, :], (heads, length)))
    )
    return (picked, placed, inverse)


def score_blocks(query, key_rows, query_blocks, key_blocks, scale):
    scores = (
        jnp.einsum("cqhd,ckhd->hcqk", query, key_rows, preferred_element_type=jnp.float32) * scale
    )
    allowed = key_blocks[:, :, None, :] <= query_blocks[:, :, :, None]
    return (scores, allowed)


def attend(query, key_rows, value_rows, query_blocks, key_blocks, scale):
    scores, allowed = score_blocks(query, key_rows, query_blocks, key_blocks, scale)
    masked = jnp.where(allowed, scores, FLOOR)
    top = jnp.max(masked, axis=-1, keepdims=True)
    weights = jnp.where(allowed, jnp.exp(masked - top), 0.0)
    total = jnp.sum(weights, axis=-1, keepdims=True)
    probs = (weights / total).astype(jnp.bfloat16)
    mixed = jnp.einsum("hcqk,ckhd->cqhd", probs, value_rows, preferred_element_type=jnp.float32)
    return (mixed.astype(jnp.bfloat16), top + jnp.log(total))


def attend_back(query, key_rows, value_rows, query_blocks, key_blocks, logsum, d_mixed, scale):
    scores, allowed = score_blocks(query, key_rows, query_blocks, key_blocks, scale)
    probs = jnp.where(allowed, jnp.exp(jnp.where(allowed, scores, FLOOR) - logsum), 0.0)
    rounded = probs.astype(jnp.bfloat16)
    d_probs = jnp.einsum("cqhd,ckhd->hcqk", d_mixed, value_rows, preferred_element_type=jnp.float32)
    centred = jnp.sum(probs * d_probs, axis=-1, keepdims=True)
    d_scores = (probs * (d_probs - centred)).astype(jnp.bfloat16)
    d_query = (
        jnp.einsum("hcqk,ckhd->cqhd", d_scores, key_rows, preferred_element_type=jnp.float32)
        * scale
    )
    d_key = (
        jnp.einsum("hcqk,cqhd->ckhd", d_scores, query, preferred_element_type=jnp.float32) * scale
    )
    d_value = jnp.einsum("hcqk,cqhd->ckhd", rounded, d_mixed, preferred_element_type=jnp.float32)
    return (d_query, d_key, d_value)


def general_body(
    hidden_in,
    out_grad,
    block_ids,
    clusters,
    w_query,
    w_key,
    w_value,
    w_out,
    b_query,
    b_value,
    b_out,
    ln1_gain,
    ln1_bias,
    w_in,
    b_in,
    w_down,
    b_down,
    ln2_gain,
    ln2_bias,
):
    parts = lax.axis_size("ctx")
    device = lax.axis_index("ctx")
    sequences, per_device, width = hidden_in.shape
    length = per_device * parts
    members = CLUSTER // parts
    groups = length // CLUSTER
    scale = DH ** (-0.5)
    (
        full_query,
        full_key,
        full_value,
        full_out,
        bias_query,
        bias_value,
        bias_out,
        gain_one,
        shift_one,
    ) = (
        lax.all_gather(w_query, "fsdp", axis=0, tiled=True),
        lax.all_gather(w_key, "fsdp", axis=0, tiled=True),
        lax.all_gather(w_value, "fsdp", axis=0, tiled=True),
        lax.all_gather(w_out, "fsdp", axis=0, tiled=True),
        lax.all_gather(b_query, "fsdp", axis=0, tiled=True),
        lax.all_gather(b_value, "fsdp", axis=0, tiled=True),
        lax.all_gather(b_out, "fsdp", axis=0, tiled=True),
        lax.all_gather(ln1_gain, "fsdp", axis=0, tiled=True),
        lax.all_gather(ln1_bias, "fsdp", axis=0, tiled=True),
    )
    full_in, full_down, bias_in, bias_down, gain_two, shift_two = (
        lax.all_gather(w_in, "fsdp", axis=0, tiled=True),
        lax.all_gather(w_down, "fsdp", axis=0, tiled=True),
        lax.all_gather(b_in, "fsdp", axis=0, tiled=True),
        lax.all_gather(b_down, "fsdp", axis=0, tiled=True),
        lax.all_gather(ln2_gain, "fsdp", axis=0, tiled=True),
        lax.all_gather(ln2_bias, "fsdp", axis=0, tiled=True),
    )
    hidden = hidden_in.reshape(sequences * per_device, width)
    query_rows = (
        jnp.dot(hidden, full_query, preferred_element_type=jnp.float32) + bias_query
    ).astype(jnp.bfloat16)
    key_rows = jnp.dot(hidden, full_key, preferred_element_type=jnp.float32).astype(jnp.bfloat16)
    value_rows = (
        jnp.dot(hidden, full_value, preferred_element_type=jnp.float32) + bias_value
    ).astype(jnp.bfloat16)
    place = positions(length, per_device, parts)
    index = 0
    order = clusters[index]
    stored_blocks = block_ids[index][place]
    picked, placed, inverse = cluster_tables(order, device, per_device, parts)
    q_local = per_head_rows(query_rows, picked).reshape(groups, members, H, DH)
    query_blocks = stored_blocks[device * per_device + picked].reshape(H, groups, members)
    key_all = lax.all_gather(key_rows, "ctx", axis=0, tiled=True)
    value_all = lax.all_gather(value_rows, "ctx", axis=0, tiled=True)
    key_cluster = per_head_rows(key_all, order).reshape(groups, CLUSTER, H, DH)
    value_cluster = per_head_rows(value_all, order).reshape(groups, CLUSTER, H, DH)
    key_blocks = stored_blocks[order].reshape(H, groups, CLUSTER)
    mixed, logsum = attend(q_local, key_cluster, value_cluster, query_blocks, key_blocks, scale)
    contexts = per_head_rows(mixed.reshape(per_device, width), placed).reshape(per_device, width)
    kept = [
        (
            q_local,
            key_cluster,
            value_cluster,
            query_blocks,
            key_blocks,
            logsum,
            picked,
            placed,
            inverse,
        )
    ]
    attended = jnp.dot(contexts, full_out, preferred_element_type=jnp.float32) + bias_out
    first_sum = hidden.astype(jnp.float32) + attended
    first, first_pull = jax.vjp(
        layer_norm, first_sum, gain_one.astype(jnp.float32), shift_one.astype(jnp.float32)
    )
    first_low = first.astype(jnp.bfloat16)
    inner = jnp.dot(first_low, full_in, preferred_element_type=jnp.float32) + bias_in
    active_full, gelu_pull = jax.vjp(exact_gelu, inner)
    active = active_full.astype(jnp.bfloat16)
    second_sum = first + jnp.dot(active, full_down, preferred_element_type=jnp.float32) + bias_down
    second, second_pull = jax.vjp(
        layer_norm, second_sum, gain_two.astype(jnp.float32), shift_two.astype(jnp.float32)
    )
    layer_out = second.astype(jnp.bfloat16).reshape(sequences, per_device, width)
    d_out = out_grad.reshape(sequences * per_device, width).astype(jnp.float32)
    d_second, g_gain_two, g_shift_two = second_pull(d_out)
    d_branch = d_second.astype(jnp.bfloat16)
    g_w_down = contract(active, d_branch)
    g_b_down = column_sum(d_branch)
    d_active = back_product(d_branch, full_down)
    d_inner = gelu_pull(d_active)[0].astype(jnp.bfloat16)
    g_w_in = contract(first_low, d_inner)
    g_b_in = column_sum(d_inner)
    d_first = d_second + back_product(d_inner, full_in)
    d_sum, g_gain_one, g_shift_one = first_pull(d_first)
    d_attended = d_sum.astype(jnp.bfloat16)
    g_w_out = contract(contexts, d_attended)
    g_b_out = column_sum(d_attended)
    d_context = back_product(d_attended, full_out).astype(jnp.bfloat16)
    index = 0
    q_kept, k_kept, v_kept, blocks_q, blocks_k, logsum, picked, placed, inverse = kept[index]
    d_cluster = per_head_rows(d_context, picked).reshape(groups, members, H, DH)
    d_query, d_key, d_value = attend_back(
        q_kept, k_kept, v_kept, blocks_q, blocks_k, logsum, d_cluster, scale
    )
    key_full = per_head_rows(d_key.reshape(length, width), inverse).reshape(length, width)
    value_full = per_head_rows(d_value.reshape(length, width), inverse).reshape(length, width)
    key_part = lax.psum_scatter(
        key_full.astype(jnp.bfloat16), "ctx", scatter_dimension=0, tiled=True
    )
    value_part = lax.psum_scatter(
        value_full.astype(jnp.bfloat16), "ctx", scatter_dimension=0, tiled=True
    )
    query_local = d_query.astype(jnp.bfloat16).reshape(per_device, width)
    query_grads = per_head_rows(query_local, placed).reshape(per_device, width)
    g_w_query = contract(hidden, query_grads)
    g_b_query = column_sum(query_grads)
    g_w_key = contract(hidden, key_part)
    g_w_value = contract(hidden, value_part)
    g_b_value = column_sum(value_part)
    input_total = (
        d_sum
        + back_product(query_grads, full_query)
        + back_product(key_part, full_key)
        + back_product(value_part, full_value)
    )
    input_grad = input_total.astype(jnp.bfloat16).reshape(sequences, per_device, width)
    shares = (
        lax.psum_scatter(
            g_w_query.astype(jnp.bfloat16), "fsdp", scatter_dimension=0, tiled=True
        ).astype(jnp.float32),
        lax.psum_scatter(
            g_w_key.astype(jnp.bfloat16), "fsdp", scatter_dimension=0, tiled=True
        ).astype(jnp.float32),
        lax.psum_scatter(
            g_w_value.astype(jnp.bfloat16), "fsdp", scatter_dimension=0, tiled=True
        ).astype(jnp.float32),
        lax.psum_scatter(
            g_w_out.astype(jnp.bfloat16), "fsdp", scatter_dimension=0, tiled=True
        ).astype(jnp.float32),
        lax.psum_scatter(
            g_b_query.astype(jnp.bfloat16), "fsdp", scatter_dimension=0, tiled=True
        ).astype(jnp.float32),
        lax.psum_scatter(
            g_b_value.astype(jnp.bfloat16), "fsdp", scatter_dimension=0, tiled=True
        ).astype(jnp.float32),
        lax.psum_scatter(
            g_b_out.astype(jnp.bfloat16), "fsdp", scatter_dimension=0, tiled=True
        ).astype(jnp.float32),
        lax.psum_scatter(
            g_gain_one.astype(jnp.bfloat16), "fsdp", scatter_dimension=0, tiled=True
        ).astype(jnp.float32),
        lax.psum_scatter(
            g_shift_one.astype(jnp.bfloat16), "fsdp", scatter_dimension=0, tiled=True
        ).astype(jnp.float32),
        lax.psum_scatter(
            g_w_in.astype(jnp.bfloat16), "fsdp", scatter_dimension=0, tiled=True
        ).astype(jnp.float32),
        lax.psum_scatter(
            g_b_in.astype(jnp.bfloat16), "fsdp", scatter_dimension=0, tiled=True
        ).astype(jnp.float32),
        lax.psum_scatter(
            g_w_down.astype(jnp.bfloat16), "fsdp", scatter_dimension=0, tiled=True
        ).astype(jnp.float32),
        lax.psum_scatter(
            g_b_down.astype(jnp.bfloat16), "fsdp", scatter_dimension=0, tiled=True
        ).astype(jnp.float32),
        lax.psum_scatter(
            g_gain_two.astype(jnp.bfloat16), "fsdp", scatter_dimension=0, tiled=True
        ).astype(jnp.float32),
        lax.psum_scatter(
            g_shift_two.astype(jnp.bfloat16), "fsdp", scatter_dimension=0, tiled=True
        ).astype(jnp.float32),
    )
    totals = (
        lax.psum(shares[0].astype(jnp.bfloat16), "ctx").astype(jnp.float32),
        lax.psum(shares[1].astype(jnp.bfloat16), "ctx").astype(jnp.float32),
        lax.psum(shares[2].astype(jnp.bfloat16), "ctx").astype(jnp.float32),
        lax.psum(shares[3].astype(jnp.bfloat16), "ctx").astype(jnp.float32),
        lax.psum(shares[4].astype(jnp.bfloat16), "ctx").astype(jnp.float32),
        lax.psum(shares[5].astype(jnp.bfloat16), "ctx").astype(jnp.float32),
        lax.psum(shares[6].astype(jnp.bfloat16), "ctx").astype(jnp.float32),
        lax.psum(shares[7].astype(jnp.bfloat16), "ctx").astype(jnp.float32),
        lax.psum(shares[8].astype(jnp.bfloat16), "ctx").astype(jnp.float32),
        lax.psum(shares[9].astype(jnp.bfloat16), "ctx").astype(jnp.float32),
        lax.psum(shares[10].astype(jnp.bfloat16), "ctx").astype(jnp.float32),
        lax.psum(shares[11].astype(jnp.bfloat16), "ctx").astype(jnp.float32),
        lax.psum(shares[12].astype(jnp.bfloat16), "ctx").astype(jnp.float32),
        lax.psum(shares[13].astype(jnp.bfloat16), "ctx").astype(jnp.float32),
        lax.psum(shares[14].astype(jnp.bfloat16), "ctx").astype(jnp.float32),
    )
    return (
        layer_out,
        input_grad,
        totals[0],
        totals[1],
        totals[2],
        totals[3],
        totals[4],
        totals[5],
        totals[6],
        totals[7],
        totals[8],
        totals[9],
        totals[10],
        totals[11],
        totals[12],
        totals[13],
        totals[14],
    )


BF = jnp.bfloat16
F32 = jnp.float32
LANES = 256
VMEM = pl.BlockSpec(memory_space=pltpu.VMEM)
HBM = pl.BlockSpec(memory_space=pl.ANY)
FAR = pl.BlockSpec(memory_space=pltpu.HBM)
SMEM = pl.BlockSpec(memory_space=pltpu.SMEM)
VEC = 16
STATS = 8
SLAB = 64


def shaped(shape, dtype):
    return jax.ShapeDtypeStruct(shape, dtype)


def call(kernel, outs, ins, args, scratch=(), name=None, weight=1):
    moved = sum(a.size * a.dtype.itemsize for a in args)
    moved += sum(o.size * o.dtype.itemsize for o in outs)
    held = sum(
        math.prod(r.shape) * jnp.dtype(r.dtype).itemsize
        for r in scratch
        if jnp.issubdtype(r.dtype, jnp.number)
    )
    return pl.pallas_call(
        kernel,
        out_shape=outs,
        in_specs=ins,
        out_specs=[VMEM] * len(outs),
        scratch_shapes=list(scratch),
        name=name,
        cost_estimate=pl.CostEstimate(flops=weight, transcendentals=0, bytes_accessed=weight),
        compiler_params=pltpu.CompilerParams(vmem_limit_bytes=moved + held + (4 << 20)),
    )(*args)


def mix(function, outs, *args, name=None):
    def kernel(*refs):
        found = function(*(ref[...] for ref in refs[: len(args)]))
        for ref, value in zip(refs[len(args) :], found):
            ref[...] = value

    return call(kernel, outs, [VMEM] * len(args), args, name=name)


def dot(left, right):
    return jnp.dot(left, right, preferred_element_type=F32)


def dot_nt(left, right):
    return lax.dot_general(left, right, (((1,), (1,)), ((), ())), preferred_element_type=F32)


def dot_tn(left, right):
    return lax.dot_general(left, right, (((0,), (0,)), ((), ())), preferred_element_type=F32)


class Plan:
    def __init__(self, chips, ring, width, hidden, per_device):
        self.chips, self.ring, self.width, self.hidden = chips, ring, width, hidden
        self.rows = per_device
        self.tokens = chips * per_device
        self.shard = width // ring
        self.half = self.shard // 2
        self.share = hidden // chips
        self.hshard = hidden // ring
        self.block = self.hshard // chips
        self.bhalf = self.block // 2
        self.heads = H // chips
        self.cols = self.heads * DH
        self.qkv = 3 * self.cols
        self.padded = self.heads * LANES
        self.wide = -(-self.qkv // 128) * 128
        self.packed = self.half * self.qkv // width
        self.clusters = chips
        self.members = CLUSTER // (2 * chips)
        self.entries = chips * CLUSTER


def pick_kernel(g, sc, *refs):
    weights, small = refs[:3], refs[3:12]
    qall, qsend, vec, here, *lines, sem = refs[12:]
    p, k = sc[0], sc[1]
    copies = [
        pltpu.make_async_copy(w, here.at[i], sem.at[i]) for i, w in enumerate(weights)
    ]
    copies += [
        pltpu.make_async_copy(ref, lines[i], sem.at[3 + i])
        for i, ref in enumerate(small)
    ]
    start(copies)
    finish(copies)
    for q in range(g.chips):

        @pl.when(p == q)
        def _(q=q):
            for i in range(3):
                qall[:, g.cols * i : g.cols * (i + 1)] = here[
                    i, :, g.cols * q : g.cols * (q + 1)
                ]

    vec[...] = jnp.zeros((VEC, LANES), BF)
    for i in range(8):
        vec[i : i + 1, 0 : g.shard] = lines[i][...].reshape(1, g.shard)
    for q in range(g.chips):
        vec[8 + q : 9 + q, 0 : g.block] = lines[8][g.block * q : g.block * (q + 1)].reshape(
            1, g.block
        )
    mine = pl.ds(pl.multiple_of(g.half * k, 16), g.half)
    qsend[0 : g.half] = qall[mine]
    qsend[g.half : g.half + VEC, 0:LANES] = vec[...]
    qsend[g.half : g.half + VEC, LANES:] = jnp.zeros((VEC, g.qkv - LANES), BF)


def prep_kernel(g, sc, _, wi, wd, wo, iall, oall, dall, send, here, sem):
    p, k = sc[0], sc[1]
    at = pl.multiple_of(g.block * p, 16)
    copies = [
        pltpu.make_async_copy(wi, here, sem.at[0]),
        pltpu.make_async_copy(wo, oall, sem.at[1]),
        pltpu.make_async_copy(wd.at[pl.ds(at, g.block)], dall, sem.at[2]),
    ]
    start(copies)
    finish(copies[:1])
    for q in range(g.chips):

        @pl.when(p == q)
        def _(q=q):
            for r in range(g.ring):
                src = g.hshard * r + g.block * q
                iall[:, g.block * r : g.block * (r + 1)] = here[:, src : src + g.block]

    mine = pl.ds(pl.multiple_of(g.half * k, 16), g.half)
    send[0 : g.half] = iall[mine]
    finish(copies[1:])
    send[g.half : 2 * g.half] = oall[mine]
    send[2 * g.half :] = dall[pl.ds(pl.multiple_of(g.bhalf * k, 16), g.bhalf)]


def lay(g, sc, own, mine, theirs, at, size, dst, turn=0):
    k, f = sc[1], jnp.bitwise_xor(sc[2], turn)
    dst[pl.ds(pl.multiple_of(2 * size * f, 16), 2 * size), :] = own[...]
    for s in range(1, g.ring):
        base = 2 * size * jnp.bitwise_xor(f, s)
        for src, core in ((mine[s - 1], k), (theirs[s - 1], 1 - k)):
            dst[pl.ds(pl.multiple_of(base + size * core, 16), size), :] = src[at : at + size, :]


def start(copies):
    for copy in copies:
        copy.start()


def finish(copies):
    for copy in copies:
        copy.wait()


def qkv_kernel(g, sc, *refs):
    n, c = g.ring - 1, 2 * g.chips
    xs = refs[:c]
    vec, own = refs[c : c + 2]
    mine = refs[c + 2 : c + 2 + n]
    theirs = refs[c + 2 + n : c + 2 + 2 * n]
    out, w, full = refs[c + 2 + 2 * n :]
    p, f = sc[0], sc[2]
    lay(g, sc, own, mine, theirs, 0, g.half, w)
    rest = jnp.zeros((VEC, g.width - LANES), F32)
    total = jnp.zeros((VEC, g.width), F32)
    for s in range(g.ring):
        piece = vec[...] if s == 0 else mine[s - 1][g.half : g.half + VEC, 0:LANES]
        piece = piece.astype(F32)
        wide = jnp.concatenate([piece, rest], axis=1)
        total = total + pltpu.roll(wide, g.shard * jnp.bitwise_xor(f, s), 1)
    full[...] = total
    back = pltpu.roll(total, lax.rem(g.width - g.cols * p, g.width), 1)
    bias = jnp.concatenate(
        [back[0:1, : g.cols], jnp.zeros((1, g.cols), F32), back[1:2, : g.cols]], axis=1
    )
    rows = jnp.concatenate([x[...] for x in xs], axis=0)
    found = (dot(rows, w[...]) + bias).astype(BF)
    for h in range(g.heads):
        for i in range(3):
            out[:, LANES * h + DH * i : LANES * h + DH * (i + 1)] = found[
                :, g.cols * i + DH * h : g.cols * i + DH * (h + 1)
            ]
        out[:, LANES * h + 3 * DH : LANES * (h + 1)] = jnp.zeros((2 * g.tokens, DH), BF)


def select(index, size, axis_size, lanes):
    if lanes:
        ids = lax.broadcasted_iota(jnp.int32, (size, axis_size), 1)
    else:
        ids = lax.broadcasted_iota(jnp.int32, (axis_size, size), 0)
    return jnp.where(ids == index, 1.0, 0.0).astype(BF)


def over(x, size):
    return lax.shift_right_logical(x, jnp.int32(size.bit_length() - 1))


def tables_kernel(g, sc, _, clusters, block_ids, pick, place, blocks):
    p, k = sc[0], sc[1]
    ranges, step = 2 * g.chips, g.clusters * g.members
    shape = (2 * ranges, 2 * ranges)
    piece, source = (lax.broadcasted_iota(jnp.int32, shape, axis) for axis in (0, 1))
    device = 2 * jnp.bitwise_xor(p, over(piece, 2) & (g.chips - 1)) + jnp.bitwise_xor(
        k, over(piece, 2 * g.chips)
    )
    found = jnp.where(piece & 1 == 0, device, 2 * ranges - 1 - device)
    hot = jnp.where(found == source, 1.0, 0.0).astype(BF)
    half = g.rows // 2
    line = block_ids[...].astype(F32)
    lines = [line[:, half * i : half * (i + 1)] for i in range(2 * ranges)]
    ids = dot(hot, jnp.concatenate(lines, axis=0).astype(BF))
    for d in range(ranges):
        line = jnp.concatenate([ids[2 * d : 2 * d + 1], ids[2 * d + 1 : 2 * d + 2]], axis=1)
        blocks[:, g.rows * d : g.rows * (d + 1)] = jnp.broadcast_to(line, (8, g.rows)).astype(BF)
    before = lax.broadcasted_iota(jnp.int32, (CLUSTER, CLUSTER), 1) < lax.broadcasted_iota(
        jnp.int32, (CLUSTER, CLUSTER), 0
    )
    rows, cols, tokens = [], [], []
    for h in range(g.heads):
        order = clusters[
            pl.ds(g.heads * p + h, 1), pl.ds(pl.multiple_of(g.entries * k, 128), g.entries)
        ]
        chip, core = over(order, 2 * g.rows), over(order, g.rows) & 1
        within = order & (g.rows - 1)
        rows.append(
            jnp.bitwise_xor(core, k) * g.tokens + jnp.bitwise_xor(chip, p) * g.rows + within
        )
    units = [(h, c) for h in range(g.heads) for c in range(g.clusters)]
    for h, c in units:
        row = rows[h][:, CLUSTER * c : CLUSTER * (c + 1)]
        tall = jnp.broadcast_to(row.astype(F32), (CLUSTER, CLUSTER))
        cols.append(over(jnp.transpose(tall)[:, 0:1].astype(jnp.int32), g.rows))
    spots = []
    for (h, c), col in zip(units, cols):
        row = rows[h][:, CLUSTER * c : CLUSTER * (c + 1)]
        same = (col == over(row, g.rows)) & before
        rank = jnp.sum(jnp.where(same, 1.0, 0.0), axis=1, keepdims=True).astype(jnp.int32)
        spots.append(select(col * g.members + rank, CLUSTER, CLUSTER, True))
    for (h, c), spot in zip(units, spots):
        row = rows[h][:, CLUSTER * c : CLUSTER * (c + 1)]
        within = jnp.broadcast_to((row & (g.rows - 1)).astype(F32), (8, CLUSTER)).astype(BF)
        tokens.append(dot(within, spot))
    for h in range(g.heads):
        for d in range(ranges):
            lanes = slice(g.members * d, g.members * (d + 1))
            mine = jnp.concatenate(
                [tokens[h * g.clusters + c][:, lanes] for c in range(g.clusters)], axis=1
            ).astype(jnp.int32)
            place[h, g.rows * d : g.rows * (d + 1)] = select(mine[0:1, :], step, g.rows, False)
            pick[h, step * d : step * (d + 1)] = select(
                jnp.transpose(mine)[:, 0:1], step, g.rows, True
            )


def mask_kernel(g, blocks, place, mask):
    ids = [
        [
            dot(blocks[:, g.rows * d : g.rows * (d + 1)], place[h, g.rows * d : g.rows * (d + 1)])
            for d in range(2 * g.chips)
        ]
        for h in range(g.heads)
    ]
    for h in range(g.heads):
        for c in range(g.clusters):
            lanes = slice(g.members * c, g.members * (c + 1))
            keys = jnp.concatenate([part[:, lanes] for part in ids[h]], axis=1)
            allowed = keys[0:1, :] <= jnp.transpose(keys)[:, 0:1]
            mask[h * g.clusters + c] = jnp.where(allowed, 0.0, FLOOR)


def cluster_rows(g, ref, c):
    step = g.clusters * g.members
    return jnp.concatenate(
        [
            ref[step * d + g.members * c : step * d + g.members * (c + 1)]
            for d in range(2 * g.chips)
        ],
        axis=0,
    )


def put_cluster(g, ref, c, values):
    step = g.clusters * g.members
    for d in range(2 * g.chips):
        ref[step * d + g.members * c : step * d + g.members * (c + 1)] = values[
            g.members * d : g.members * (d + 1)
        ]


def attend_kernel(g, qkv, pick, place, mask, ctx_own, ctx_other, kept, probs, mixed):
    step, ranges = g.clusters * g.members, 2 * g.chips
    units = [(h, c) for h in range(g.heads) for c in range(g.clusters)]
    for h in range(g.heads):
        for d in range(ranges):
            rows = qkv[g.rows * d : g.rows * (d + 1), LANES * h : LANES * (h + 1)]
            slots = slice(step * d, step * (d + 1))
            kept[h, slots] = dot(pick[h, slots], rows).astype(BF)
    for h, c in units:
        rows = cluster_rows(g, kept.at[h], c)
        q, key = rows[:, 0:DH], rows[:, DH : 2 * DH]
        at = h * g.clusters + c
        probs[at] = dot_nt(q, key) * (DH ** (-0.5)) + mask[at]
    for h, c in units:
        at = h * g.clusters + c
        masked = probs[at]
        weights = jnp.exp(masked - jnp.max(masked, axis=-1, keepdims=True))
        probs[at] = weights * (1.0 / jnp.sum(weights, axis=-1, keepdims=True))
    for h, c in units:
        v = cluster_rows(g, kept.at[h], c)[:, 2 * DH : 3 * DH]
        put_cluster(
            g, mixed.at[h], c, dot(probs[h * g.clusters + c].astype(BF), v).astype(BF)
        )
    for h in range(g.heads):
        for d in range(ranges):
            side, at = (ctx_own, d) if d < g.chips else (ctx_other, d - g.chips)
            rows = dot(
                place[h, g.rows * d : g.rows * (d + 1)], mixed[h, step * d : step * (d + 1)]
            )
            side[g.rows * at : g.rows * (at + 1), DH * h : DH * (h + 1)] = rows.astype(BF)


def attend_back_kernel(g, own, other, pick, place, kept, probs, grads, d_mixed, found, d_scores):
    step, ranges = g.clusters * g.members, 2 * g.chips
    scale = DH ** (-0.5)
    units = [(h, c) for h in range(g.heads) for c in range(g.clusters)]
    for h in range(g.heads):
        for d in range(ranges):
            side, at = (own, d) if d < g.chips else (other, d - g.chips)
            rows = side[g.rows * at : g.rows * (at + 1), DH * h : DH * (h + 1)]
            slots = slice(step * d, step * (d + 1))
            d_mixed[h, slots] = dot(pick[h, slots], rows).astype(BF)
    for h, c in units:
        v = cluster_rows(g, kept.at[h], c)[:, 2 * DH : 3 * DH]
        share = probs[h * g.clusters + c]
        d_share = dot_nt(cluster_rows(g, d_mixed.at[h], c), v)
        delta = jnp.sum(share * d_share, axis=-1, keepdims=True)
        d_scores[h * g.clusters + c] = (share * (d_share - delta)).astype(BF)
    for h, c in units:
        rows = cluster_rows(g, kept.at[h], c)
        d_s, share = d_scores[h * g.clusters + c], probs[h * g.clusters + c].astype(BF)
        d_q = dot(d_s, rows[:, DH : 2 * DH]) * scale
        d_k = dot_tn(d_s, rows[:, 0:DH]) * scale
        d_v = dot_tn(share, cluster_rows(g, d_mixed.at[h], c))
        put_cluster(g, found.at[h], c, jnp.concatenate([d_q, d_k, d_v], axis=1).astype(BF))
    for h in range(g.heads):
        for d in range(ranges):
            at = slice(g.rows * d, g.rows * (d + 1))
            rows = dot(place[h, at], found[h, step * d : step * (d + 1)]).astype(BF)
            for i in range(3):
                grads[at, g.cols * i + DH * h : g.cols * i + DH * (h + 1)] = rows[
                    :, DH * i : DH * (i + 1)
                ]
    grads[:, g.qkv :] = jnp.zeros((2 * g.tokens, g.wide - g.qkv), BF)


def norm_parts(values):
    centre = values - jnp.mean(values, axis=-1, keepdims=True)
    spread = jnp.mean(centre * centre, axis=-1, keepdims=True)
    scale = lax.rsqrt(spread + EPSILON)
    return centre * scale, scale


def norm_back(grad, z, scale):
    return scale * (
        grad
        - jnp.mean(grad, axis=-1, keepdims=True)
        - z * jnp.mean(grad * z, axis=-1, keepdims=True)
    )


def seen(g, ref, j):
    half = g.chips // 2
    return jnp.concatenate(
        [
            ref[
                g.rows * ((i ^ j) % half) : g.rows * ((i ^ j) % half + 1),
                g.cols * ((i ^ j) // half) : g.cols * ((i ^ j) // half + 1),
            ]
            for i in range(g.chips)
        ],
        axis=0,
    )


def forward_kernel(g, sc, *refs):
    c, n = g.chips, g.ring - 1
    ctxs, xs, full = refs[:c], refs[c : 2 * c], refs[2 * c]
    wo_own, wi_own, wd_own = refs[2 * c + 1 : 2 * c + 4]
    refs = refs[2 * c + 4 :]
    mine, theirs = refs[:n], refs[n : 2 * n]
    refs = refs[2 * n :]
    parts, (active, inner, low, z_own, s_own, wo_rows, wi, wd) = refs[:c], refs[c : c + 8]
    wo, work = refs[c + 8 :]
    p = sc[0]
    lay(g, sc, wo_own, mine, theirs, g.half, g.half, wo, p)
    rows = jnp.concatenate([seen(g, ctxs[j], j) for j in range(c)], axis=1)
    wo_rows[...] = wo[0 : g.cols]
    halves = [slice(i, i + g.tokens // 2) for i in range(0, g.tokens, g.tokens // 2)]
    bias = full[pl.ds(8 + p, 1), :]

    def first_norm(half):
        for i in range(half.start, half.stop, SLAB):
            at = slice(i, i + SLAB)
            x = xs[i // g.rows][i % g.rows : i % g.rows + SLAB].astype(F32)
            z, scale = norm_parts(work[at] + x + full[2:3, :])
            first = z * full[3:4, :] + full[4:5, :]
            low[at] = first.astype(BF)
            if i < g.rows:
                z_own[at] = z
                s_own[at] = jnp.broadcast_to(scale, (SLAB, 128))
                parts[0][at] = first + full[5:6, :]

    def activate(half):
        for i in range(half.start, half.stop, SLAB):
            at = slice(i, i + SLAB)
            u = inner[at] + bias
            inner[at] = u
            active[at] = (u * (1.0 + lax.erf(u * (0.5**0.5))) * 0.5).astype(BF)

    def descend(half):
        second = dot(active[half], wd[...])
        for i in range(half.start, half.stop, g.rows):
            block = second[i - half.start : i - half.start + g.rows]
            if i == 0:
                parts[0][...] += block
            else:
                parts[i // g.rows][...] = block.astype(BF)

    one, two = halves
    work[one] = dot(rows[one], wo[...])
    work[two] = dot(rows[two], wo[...])
    lay(g, sc, wi_own, mine, theirs, 0, g.half, wi)
    first_norm(one)
    inner[one] = dot(low[one], wi[...])
    first_norm(two)
    inner[two] = dot(low[two], wi[...])
    lay(g, sc, wd_own, mine, theirs, 2 * g.half, g.bhalf, wd)
    activate(one)
    descend(one)
    activate(two)
    descend(two)


def turn_kernel(g, *refs):
    c = g.chips
    parts, full, cotangent = refs[:c], refs[c], refs[c + 1]
    out, d_second, branch = refs[c + 2 :]
    second = parts[0][...]
    for j in range(1, c):
        second = second + parts[j][...].astype(F32)
    z, scale = norm_parts(second)
    gain = full[6:7, :]
    out[...] = (z * gain + full[7:8, :]).astype(BF)
    dy = cotangent[...].astype(F32)
    grad = norm_back(dy * gain, z, scale)
    d_second[...] = grad
    branch[0 : g.rows] = grad.astype(BF)
    one = jnp.sum(dy * z, axis=0, keepdims=True)
    two = jnp.sum(dy, axis=0, keepdims=True)
    rest = jnp.zeros((STATS - 2, g.width), F32)
    branch[g.rows : g.rows + STATS] = jnp.concatenate([one, two, rest], axis=0).astype(BF)


def back_kernel(g, *refs):
    c = g.chips
    branches, slope, wd, wi = refs[:c], refs[c], refs[c + 1], refs[c + 2]
    parts, d_inner = refs[c + 3 : 2 * c + 3], refs[2 * c + 3]
    rows = jnp.concatenate([b[0 : g.rows] for b in branches], axis=0)
    d_active = dot_nt(rows, wd[...])
    d_inner[...] = (d_active * slope[...]).astype(BF)
    total = dot_nt(d_inner[...], wi[...])
    parts[0][...] = total[: g.rows]
    for j in range(1, c):
        parts[j][...] = total[g.rows * j : g.rows * (j + 1)].astype(BF)


def split_rows(g, sc, total, size, own, other, at):
    k, f = sc[1], sc[2]
    for s in range(g.ring):
        base = 2 * size * jnp.bitwise_xor(f, s)
        own[s, at : at + size] = total[pl.ds(pl.multiple_of(base + size * k, 8), size), :]
        other[s, at : at + size] = total[
            pl.ds(pl.multiple_of(base + size * (1 - k), 8), size), :
        ].astype(BF)


def mlp_grads_kernel(g, sc, *refs):
    c = g.chips
    branches, active, low, d_inner = refs[:c], refs[c], refs[c + 1], refs[c + 2]
    own, other, sums, total = refs[c + 3 :]
    rows = jnp.concatenate([b[0 : g.rows] for b in branches], axis=0)
    total[...] = dot_tn(active[...], rows)
    split_rows(g, sc, total, g.bhalf, own, other, g.half)
    total[...] = dot_tn(low[...], d_inner[...])
    split_rows(g, sc, total, g.half, own, other, 0)
    stats = branches[0][g.rows : g.rows + STATS].astype(F32)
    for j in range(1, c):
        stats = stats + branches[j][g.rows : g.rows + STATS].astype(F32)
    down = jnp.sum(rows.astype(F32), axis=0, keepdims=True)
    up = jnp.sum(d_inner[...].astype(F32), axis=0, keepdims=True)
    sums[...] = jnp.concatenate([stats[0:2], down, up, jnp.zeros((4, g.width), F32)], axis=0)


def first_kernel(g, *refs):
    c = g.chips
    parts, d_second, z_own, s_own, full = refs[:c], *refs[c : c + 4]
    d_sum, attended = refs[c + 4 :]
    d_first = d_second[...] + parts[0][...]
    for j in range(1, c):
        d_first = d_first + parts[j][...].astype(F32)
    z = z_own[...]
    grad = norm_back(d_first * full[3:4, :], z, s_own[:, 0:1])
    d_sum[...] = grad
    attended[0 : g.rows] = grad.astype(BF)
    one = jnp.sum(d_first * z, axis=0, keepdims=True)
    two = jnp.sum(d_first, axis=0, keepdims=True)
    rest = jnp.zeros((STATS - 2, g.width), F32)
    attended[g.rows : g.rows + STATS] = jnp.concatenate([one, two, rest], axis=0).astype(BF)


def context_kernel(g, *refs):
    grads, wo_rows, out = refs[: g.chips], refs[g.chips], refs[g.chips + 1]
    rows = jnp.concatenate([b[0 : g.rows] for b in grads], axis=0)
    out[...] = dot_nt(rows, wo_rows[...]).astype(BF)


def out_grads_kernel(g, sc, *refs):
    c = g.chips
    grads, ctxs, sums = refs[:c], refs[c : 2 * c], refs[2 * c]
    own, away, total = refs[2 * c + 1 :]
    p, f = sc[0], sc[2]
    rows = jnp.concatenate([b[0 : g.rows] for b in grads], axis=0)
    for j in range(c):
        q = jnp.bitwise_xor(p, j)
        total[pl.ds(pl.multiple_of(g.cols * q, 64), g.cols), :] = dot_tn(seen(g, ctxs[j], j), rows)
    stats = grads[0][g.rows : g.rows + STATS].astype(F32)
    for j in range(1, c):
        stats = stats + grads[j][g.rows : g.rows + STATS].astype(F32)
    out = jnp.sum(rows.astype(F32), axis=0, keepdims=True)
    rest = jnp.zeros((STATS - 7, g.width), F32)
    block = jnp.concatenate([sums[0:4], stats[0:2], out, rest], axis=0)
    size = g.shard // c
    for s in range(g.ring):
        base = g.shard * jnp.bitwise_xor(f, s) + size * p
        part = total[pl.ds(pl.multiple_of(base, 8), size), :]
        if s % 2:
            away[s // 2, 0:size] = part.astype(BF)
            away[s // 2, size:] = block.astype(BF)
        else:
            own[s // 2, 0:size] = part
            own[s // 2, size:] = block


def summed(g, mine, theirs, at):
    one = mine[g.tokens * at : g.tokens * (at + 1), : g.qkv].astype(F32)
    two = theirs[g.tokens * (1 - at) : g.tokens * (2 - at), : g.qkv].astype(F32)
    return (one + two).astype(BF)


def input_kernel(g, mine, theirs, w, *parts):
    total = dot_nt(summed(g, mine, theirs, 0), w[...])
    parts[0][...] = total[: g.rows]
    for j in range(1, g.chips):
        parts[j][...] = total[g.rows * j : g.rows * (j + 1)].astype(BF)


def turn_rows_kernel(g, sc, *refs):
    xs, out = refs[: 2 * g.chips], refs[2 * g.chips]
    rows = jnp.concatenate([x[...] for x in xs], axis=0)
    for core in range(2):

        @pl.when(sc[1] == core)
        def _(core=core):
            for r in range(g.ring):
                lane = g.shard * r + g.half * core
                out[g.half * r : g.half * (r + 1), :] = jnp.transpose(rows[:, lane : lane + g.half])


def qkv_grads_kernel(g, sc, mine, theirs, turned_x, own, away, total):
    f = sc[2]
    rows = jnp.concatenate([summed(g, mine, theirs, 0), summed(g, mine, theirs, 1)], axis=0)
    total[...] = dot(turned_x[...], rows)
    sums = jnp.sum(rows.astype(F32), axis=0, keepdims=True)
    gap = jnp.zeros((8, g.width - g.qkv), F32)
    block = jnp.concatenate(
        [jnp.concatenate([sums, jnp.zeros((7, g.qkv), F32)], axis=0), gap], axis=1
    )
    for s in range(g.ring):
        part = total[pl.ds(pl.multiple_of(g.half * jnp.bitwise_xor(f, s), 8), g.half), :]
        packed = pack(g, part)
        if s % 2:
            away[s // 2, 0 : g.packed] = packed.astype(BF)
            away[s // 2, g.packed :] = block.astype(BF)
        else:
            own[s // 2, 0 : g.packed] = packed
            own[s // 2, g.packed :] = block


def pack(g, part):
    step = g.half - g.packed
    beside = [
        part[g.packed :, step_lanes : step_lanes + g.width - g.qkv]
        for step_lanes in range(0, g.qkv, g.width - g.qkv)
    ]
    return jnp.concatenate(
        [part[0 : g.packed], jnp.concatenate(beside, axis=0)], axis=1
    )


def sources(g, sc, refs):
    p, k = sc[0], sc[1]
    out = []
    for j, (mine, theirs) in enumerate(zip(refs, others(g, refs))):
        q = jnp.bitwise_xor(p, j)
        out.append((q, k, mine))
        out.append((q, 1 - k, theirs))
    return out


def others(g, refs):
    far = refs[g.chips :]
    return far if len(far) > 1 else [far[0].at[j] for j in range(g.chips)]


def paired(g, sc, refs, body):
    p, k = sc[0], sc[1]
    mine, theirs = refs[: g.chips], others(g, refs)
    for odd in range(2):

        @pl.when(p & 1 == odd)
        def _(odd=odd):
            for j in range(0, g.chips, 2):
                pair = jnp.bitwise_xor(over(p, 2), j // 2)
                for found, core in ((mine, k), (theirs, 1 - k)):
                    body(pair, core, found[j ^ odd], found[j ^ odd ^ 1])


def mlp_final_kernel(g, sc, *refs):
    found, (g_in, g_down) = refs[:-2], refs[-2:]

    def place(pair, core, even, odd):
        mine = pl.ds(pl.multiple_of(g.half * core, 8), g.half)
        for i, ref in enumerate((even, odd)):
            at = pl.multiple_of(g.block * (2 * pair + i) + g.bhalf * core, 8)
            g_down[pl.ds(at, g.bhalf), :] = ref[g.half :, :].astype(F32)
        for r in range(g.ring):
            lane = pl.multiple_of(g.hshard * r + 2 * g.block * pair, 128)
            lanes = slice(g.block * r, g.block * (r + 1))
            g_in[mine, pl.ds(lane, 2 * g.block)] = jnp.concatenate(
                [even[0 : g.half, lanes], odd[0 : g.half, lanes]], axis=1
            ).astype(F32)

    paired(g, sc, found, place)


def last_kernel(g, sc, *refs):
    found = refs[: 2 * g.chips]
    gq, gk, gv, g_bq, g_bv, g_out, g_bin, *small = refs[2 * g.chips :]
    p, f = sc[0], sc[2]
    size, step = g.shard // g.chips, g.half - g.packed
    top = g.packed + 8
    for q, core, ref in sources(g, sc, found):

        @pl.when((q == f) & (core == 0))
        def _(ref=ref):
            row = ref[g.packed : top, :].astype(F32)[0:1]
            for dst, at in zip((g_bq, g_bv), (0, 2)):
                dst[...] = row[:, g.cols * at : g.cols * (at + 1)].reshape(g.shard)

    def place(pair, core, even, odd):
        base = pl.multiple_of(g.half * core, 8)
        lane = pl.ds(pl.multiple_of(2 * g.cols * pair, 128), 2 * g.cols)
        for i, dst in enumerate((gq, gk, gv)):
            for rows, at, lanes in (
                (pl.ds(base, g.packed), slice(0, g.packed), slice(g.cols * i, g.cols * (i + 1))),
                (
                    pl.ds(base + g.packed, step),
                    slice(step * i, step * (i + 1)),
                    slice(g.qkv, g.width),
                ),
            ):
                dst[rows, lane] = jnp.concatenate(
                    [even[at, lanes], odd[at, lanes]], axis=1
                ).astype(F32)

    paired(g, sc, found, place)
    far = others(g, found)
    for j in range(g.chips):
        q = jnp.bitwise_xor(p, j)
        one, two = found[j], far[j]
        both = one[top:, :].astype(F32) + two[top:, :].astype(F32)
        g_out[pl.ds(pl.multiple_of(size * q, 8), size), :] = both[0:size]
        back = pltpu.roll(both[size : size + STATS], lax.rem(g.width - g.shard * f, g.width), 1)
        for chip in range(g.chips):

            @pl.when(q == chip)
            def _(chip=chip, back=back):
                g_bin[g.block * chip : g.block * (chip + 1)] = back[3:4, : g.shard].reshape(g.shard)
                if chip == 0:
                    for i, dst in zip((0, 1, 2, 4, 5, 6), small):
                        dst[...] = back[i : i + 1, : g.shard].reshape(g.shard)


def to_core(x):
    n = lax.axis_size("ctx")
    return lax.ppermute(x, "ctx", [(i, i ^ 1) for i in range(n)])


def to_chip(x, j):
    n = lax.axis_size("ctx")
    return lax.ppermute(x, "ctx", [(i, i ^ (2 * j)) for i in range(n)])


def along(x, mask):
    n = lax.axis_size("fsdp")
    return lax.ppermute(x, "fsdp", [(i, i ^ mask) for i in range(n)])


def gather_ring(x, pause=None):
    n = lax.axis_size("fsdp")
    found, mask, first = {0: x}, n // 2, ()
    while mask:
        for s in sorted(found):
            first = [found[t] for t in sorted(found) if t]
            part = found[s] if s == 0 or pause is None else after(found[s], pause, *first)
            found[s | mask] = along(part, mask)
        mask //= 2
    return [found[s] for s in range(1, n)]


def spread(x, chips):
    far = {j: to_chip(x, j) for j in sorted(range(1, chips), key=lambda j: -bin(j).count("1"))}
    return [x] + [far[j] for j in range(1, chips)]


def pass_on(x, chips, pause):
    found = {0: x}
    mask = 1
    while mask < chips:
        for j in sorted(found):
            found[j | mask] = to_chip(found[j] if j == 0 else after(found[j], pause), mask)
        mask *= 2
    return [found[j] for j in range(chips)]


def swap(parts):
    far = {j: to_chip(parts[j], j) for j in sorted(range(1, len(parts)), key=lambda j: -bin(j).count("1"))}
    return [parts[0]] + [far[j] for j in range(1, len(parts))]


def ring_step(kept, away, mask):
    count, rows, width = kept.shape
    half = count // 2

    def step(mine, got):
        total = mine + got.astype(F32)
        if not half:
            return (total.astype(BF),)
        return total.reshape(half, 2, rows, width)[:, 0], total.reshape(
            half, 2, rows, width
        )[:, 1].astype(BF)

    outs = [shaped((half, rows, width), F32), shaped((half, rows, width), BF)]
    return mix(
        step,
        outs if half else [shaped((1, rows, width), BF)],
        kept,
        along(away, mask),
        name="ring_step",
    )


def kept_far(x):
    return pltpu.with_memory_space_constraint(x, pltpu.HBM)


def after(x, *first):
    return lax.optimization_barrier((x, *first))[0]


def ring_step(kept, away, mask):
    count, rows, width = kept.shape
    half = count // 2

    def step(mine, got):
        total = mine + got.astype(F32)
        if not half:
            return (total.astype(BF),)
        return total.reshape(half, 2, rows, width)[:, 0], total.reshape(
            half, 2, rows, width
        )[:, 1].astype(BF)

    outs = [shaped((half, rows, width), F32), shaped((half, rows, width), BF)]
    return mix(
        step,
        outs if half else [shaped((1, rows, width), BF)],
        kept,
        along(away, mask),
        name="ring_step",
    )


def kept_far(x):
    return pltpu.with_memory_space_constraint(x, pltpu.HBM)


def after(x, *first):
    return lax.optimization_barrier((x, *first))[0]


def plane_pieces(piece, chips):
    near = spread(piece, chips)
    return near + [to_core(part) for part in near]


def chip_body(
    hidden_in,
    out_grad,
    block_ids,
    clusters,
    w_query,
    w_key,
    w_value,
    w_out,
    b_query,
    b_value,
    b_out,
    ln1_gain,
    ln1_bias,
    w_in,
    b_in,
    w_down,
    b_down,
    ln2_gain,
    ln2_bias,
):
    n, ring = lax.axis_size("ctx"), lax.axis_size("fsdp")
    chips = n // 2
    rows, width = hidden_in.shape[1:]
    hidden = w_in.shape[1]
    g = Plan(chips, ring, width, hidden, rows)
    c, f = lax.axis_index("ctx"), lax.axis_index("fsdp")
    p, k = c // 2, c % 2
    sc = jnp.stack([p, k, f]).astype(jnp.int32)
    bind = functools.partial


    qall, qsend, vec = call(
        bind(pick_kernel, g),
        [
            shaped((g.shard, g.qkv), BF),
            shaped((g.half + VEC, g.qkv), BF),
            shaped((VEC, LANES), BF),
        ],
        [SMEM] + [FAR] * 12,
        [
            sc,
            *map(
                kept_far,
                (
                    w_query,
                    w_key,
                    w_value,
                    b_query,
                    b_value,
                    b_out,
                    ln1_gain,
                    ln1_bias,
                    b_down,
                    ln2_gain,
                    ln2_bias,
                    b_in,
                ),
            ),
        ],
        [
            pltpu.VMEM((3, g.shard, width), BF),
        ]
        + [pltpu.VMEM((g.shard,), BF)] * 8
        + [pltpu.VMEM((g.hshard,), BF), pltpu.SemaphoreType.DMA((12,))],
        name="pick_weights",
    )
    x_own = after(hidden_in.reshape(rows, width), qsend)
    xs = spread(x_own, chips)
    iall, oall, dall, send = call(
        bind(prep_kernel, g),
        [
            shaped((g.shard, g.share), BF),
            shaped((g.shard, width), BF),
            shaped((g.block, width), BF),
            shaped((2 * g.half + g.bhalf, width), BF),
        ],
        [SMEM, HBM, FAR, FAR, FAR],
        [sc, qsend, kept_far(w_in), kept_far(w_down), kept_far(w_out)],
        [pltpu.VMEM((g.shard, hidden), BF), pltpu.SemaphoreType.DMA((3,))],
        name="prepare_weights",
    )
    q_mine = gather_ring(qsend, send)

    step = g.clusters * g.members
    pick, place, blk = call(
        bind(tables_kernel, g),
        [
            shaped((g.heads, 2 * chips * step, rows), BF),
            shaped((g.heads, 2 * g.tokens, step), BF),
            shaped((8, 2 * g.tokens), BF),
        ],
        [SMEM, HBM] + [VMEM] * 2,
        [sc, q_mine[0], clusters[0], block_ids],
        name="cluster_tables",
    )
    (mask,) = call(
        bind(mask_kernel, g),
        [shaped((g.heads * g.clusters, CLUSTER, CLUSTER), F32)],
        [VMEM] * 2,
        [blk, place],
        name="cluster_mask",
    )
    x_other = [to_core(after(xs[0], xs[1]))] + [to_core(x) for x in xs[1:]]
    q_theirs = [to_core(after(part, xs[1])) for part in q_mine]
    qkv, w_qkv, full = call(
        bind(qkv_kernel, g),
        [
            shaped((2 * g.tokens, g.padded), BF),
            shaped((width, g.qkv), BF),
            shaped((VEC, width), F32),
        ],
        [SMEM] + [VMEM] * (2 * chips + 2 * ring),
        [sc, *xs, *x_other, after(vec, send), qall, *q_mine, *q_theirs],
        name="project",
    )
    ctx_own, ctx_other, kept, probs = call(
        bind(attend_kernel, g),
        [
            shaped((g.tokens, g.cols), BF),
            shaped((g.tokens, g.cols), BF),
            shaped((g.heads, g.entries, LANES), BF),
            shaped((g.heads * g.clusters, CLUSTER, CLUSTER), F32),
        ],
        [VMEM] * 4,
        [qkv, pick, place, mask],
        [pltpu.VMEM((g.heads, g.entries, DH), BF)],
        name="attend",
    )
    (ctx,) = mix(
        lambda a, b: (
            jnp.concatenate([a[: g.tokens // 2] + b[: g.tokens // 2], a[g.tokens // 2 :] + b[g.tokens // 2 :]], axis=1),
        ),
        [shaped((g.tokens // 2, 2 * g.cols), BF)],
        ctx_own,
        to_core(ctx_other),
        name="join_context",
    )
    ctxs = spread(ctx, chips)
    w_mine = gather_ring(send, ctx_own)

    w_theirs = [to_core(after(part, *ctxs[1:])) for part in w_mine]
    *second, active, inner, low, z_own, s_own, wo_rows, wi, wd = call(
        bind(forward_kernel, g),
        [shaped((rows, width), F32)]
        + [shaped((rows, width), BF)] * (chips - 1)
        + [
            shaped((g.tokens, g.share), BF),
            shaped((g.tokens, g.share), F32),
            shaped((g.tokens, width), BF),
            shaped((rows, width), F32),
            shaped((rows, 128), F32),
            shaped((g.cols, width), BF),
            shaped((width, g.share), BF),
            shaped((g.share, width), BF),
        ],
        [SMEM] + [VMEM] * (2 * chips + 2 * ring + 2),
        [sc, *ctxs, *xs, full, oall, iall, dall, *w_mine, *w_theirs],
        [pltpu.VMEM((width, width), BF), pltpu.VMEM((g.tokens, width), F32)],
        name="mlp_forward",
    )
    (slope,) = mix(
        lambda u: (
            0.5 * (1.0 + lax.erf(u * (0.5**0.5)))
            + u * jnp.exp(-0.5 * u * u) * (1.0 / (2.0 * math.pi) ** 0.5),
        ),
        [shaped((g.tokens, g.share), F32)],
        inner,
        name="gelu_slope",
    )
    (turned_x,) = call(
        bind(turn_rows_kernel, g),
        [shaped((ring * g.half, 2 * g.tokens), BF)],
        [SMEM] + [VMEM] * (2 * chips),
        [sc, after(xs[0], inner), *xs[1:], *x_other],
        name="turn_rows",
    )
    second = swap(second)
    layer_out, d_second, branch = call(
        bind(turn_kernel, g),
        [
            shaped((rows, width), BF),
            shaped((rows, width), F32),
            shaped((rows + STATS, width), BF),
        ],
        [VMEM] * (chips + 2),
        [*second, after(full, turned_x), out_grad.reshape(rows, width)],
        name="norm_two",
    )
    branches = spread(branch, chips)
    *d_first, d_inner = call(
        bind(back_kernel, g),
        [shaped((rows, width), F32)]
        + [shaped((rows, width), BF)] * (chips - 1)
        + [shaped((g.tokens, g.share), BF)],
        [VMEM] * (chips + 3),
        [*branches, slope, wd, wi],
        name="mlp_back",
    )
    d_first = swap(d_first)
    m_own, m_other, sums = call(
        bind(mlp_grads_kernel, g),
        [
            shaped((ring, g.half + g.bhalf, width), F32),
            shaped((ring, g.half + g.bhalf, width), BF),
            shaped((8, width), F32),
        ],
        [SMEM] + [VMEM] * (chips + 3),
        [sc, *branches, active, low, d_inner],
        [pltpu.VMEM((width, g.share), F32)],
        name="mlp_grads",
    )
    m_got = to_core(m_other)
    m_rows = g.half + g.bhalf

    def joined(own, got):
        total = own + got.astype(F32)
        return (total[0], *(total[s].astype(BF) for s in range(1, ring)))

    m_kept, *m_away = mix(
        joined,
        [shaped((m_rows, width), F32)] + [shaped((m_rows, width), BF)] * (ring - 1),
        m_own,
        m_got,
        name="join_grads",
    )
    (m_piece,) = mix(
        lambda kept, *parts: (sum((part.astype(F32) for part in parts), kept).astype(BF),),
        [shaped((m_rows, width), BF)],
        m_kept,
        *(along(part, s) for s, part in enumerate(m_away, 1)),
        name="mlp_sum",
    )
    d_sum, attended = call(
        bind(first_kernel, g),
        [shaped((rows, width), F32), shaped((rows + STATS, width), BF)],
        [VMEM] * (chips + 4),
        [*d_first, after(d_second, *m_away), z_own, s_own, full],
        name="norm_one",
    )
    grads = spread(attended, chips)
    (d_ctx,) = call(
        bind(context_kernel, g),
        [shaped((g.tokens, g.cols), BF)],
        [VMEM] * (chips + 1),
        [*grads, after(wo_rows, m_piece)],
        name="context_back",
    )
    d_ctx_other = to_core(d_ctx)
    o_rows = g.shard // chips + STATS
    o_own, o_away = call(
        bind(out_grads_kernel, g),
        [shaped((ring // 2, o_rows, width), F32), shaped((ring // 2, o_rows, width), BF)],
        [SMEM] + [VMEM] * (2 * chips + 1),
        [sc, *grads, *ctxs, sums],
        [pltpu.VMEM((width, width), F32)],
        name="out_grads",
    )
    (dq_mine,) = call(
        bind(attend_back_kernel, g),
        [shaped((2 * g.tokens, g.wide), BF)],
        [VMEM] * 6,
        [d_ctx, d_ctx_other, pick, place, after(kept, o_own), probs],
        [
            pltpu.VMEM((g.heads, g.entries, DH), BF),
            pltpu.VMEM((g.heads, g.entries, 3 * DH), BF),
            pltpu.VMEM((g.heads * g.clusters, CLUSTER, CLUSTER), BF),
        ],
        name="attend_back",
    )
    dq_theirs = to_core(dq_mine)
    q_rows = g.packed + 8
    q_own, q_away = call(
        bind(qkv_grads_kernel, g),
        [shaped((ring // 2, q_rows, width), F32), shaped((ring // 2, q_rows, width), BF)],
        [SMEM] + [VMEM] * 3,
        [sc, dq_mine, dq_theirs, turned_x],
        [pltpu.VMEM((ring * g.half, g.qkv), F32)],
        name="project_grads",
    )
    d_in = call(
        bind(input_kernel, g),
        [shaped((rows, width), F32)] + [shaped((rows, width), BF)] * (chips - 1),
        [VMEM] * 3,
        [after(dq_mine, q_away), dq_theirs, w_qkv],
        name="project_back",
    )
    d_in = swap(d_in)
    mask_at = 2
    q_away0 = q_away
    o_away = after(o_away, dq_mine)
    while q_own.shape[0] > 1:
        q_own, q_away = ring_step(q_own, q_away, mask_at // 2)
        o_own, o_away = ring_step(o_own, o_away, mask_at // 2)
        mask_at *= 2
    near = pass_on(m_piece, chips, dq_theirs)
    m_pieces = near + [to_core(after(part, q_away)) for part in near]
    (input_grad,) = mix(
        lambda kept, *parts: (sum((part.astype(F32) for part in parts), kept).astype(BF),),
        [shaped((rows, width), BF)],
        d_sum,
        *d_in,
        name="input_sum",
    )
    g_in, g_down = call(
        bind(mlp_final_kernel, g),
        [shaped((g.shard, hidden), F32), shaped((g.hshard, width), F32)],
        [SMEM] + [VMEM] * len(m_pieces),
        [sc, *m_pieces],
        name="mlp_lay",
    )
    vector = shaped((g.shard,), F32)
    (piece,) = mix(
        lambda a, b, c, d: (
            jnp.concatenate([a[0] + b[0].astype(F32), c[0] + d[0].astype(F32)], axis=0).astype(BF),
        ),
        [shaped((q_rows + o_rows, width), BF)],
        q_own,
        along(q_away, mask_at // 2),
        o_own,
        along(o_away, mask_at // 2),
        name="last_sum",
    )
    near = spread(after(piece, input_grad), chips)
    pieces = near + [to_core(after(part, g_down)) for part in near]
    found = call(
        bind(last_kernel, g),
        [shaped((g.shard, width), F32)] * 3
        + [vector] * 2
        + [shaped((g.shard, width), F32), shaped((g.hshard,), F32)]
        + [vector] * 6,
        [SMEM] + [VMEM] * (2 * chips),
        [sc, *pieces],
        name="last_lay",
    )
    gq, gk, gv, g_bq, g_bv, g_out, g_bin, g_gain2, g_bias2, g_bdown, g_gain1, g_bias1, g_bout = found
    return (
        layer_out.reshape(1, rows, width),
        input_grad.reshape(1, rows, width),
        gq,
        gk,
        gv,
        g_out,
        g_bq,
        g_bv,
        g_bout,
        g_gain1,
        g_bias1,
        g_in,
        g_bin,
        g_down,
        g_bdown,
        g_gain2,
        g_bias2,
    )


def fits(mesh):
    n, ring = mesh.shape["ctx"], mesh.shape["fsdp"]
    chips = n // 2
    return n % 2 == 0 and chips & (chips - 1) == 0 and chips > 1 and ring == chips and H % chips == 0 and ring * chips <= 16


def solution(mesh):
    in_specs = (
        P("fsdp", "ctx", None),
        P("fsdp", "ctx", None),
        P("fsdp", None),
        P("fsdp", None, None),
        P("fsdp", None),
        P("fsdp", None),
        P("fsdp", None),
        P("fsdp", None),
        P("fsdp"),
        P("fsdp"),
        P("fsdp"),
        P("fsdp"),
        P("fsdp"),
        P("fsdp", None),
        P("fsdp"),
        P("fsdp", None),
        P("fsdp"),
        P("fsdp"),
        P("fsdp"),
    )
    out_specs = (
        P("fsdp", "ctx", None),
        P("fsdp", "ctx", None),
        P("fsdp", None),
        P("fsdp", None),
        P("fsdp", None),
        P("fsdp", None),
        P("fsdp"),
        P("fsdp"),
        P("fsdp"),
        P("fsdp"),
        P("fsdp"),
        P("fsdp", None),
        P("fsdp"),
        P("fsdp", None),
        P("fsdp"),
        P("fsdp"),
        P("fsdp"),
    )
    body = chip_body if fits(mesh) else general_body
    return jax.shard_map(body, mesh=mesh, in_specs=in_specs, out_specs=out_specs, check_vma=False)
```

```python
import functools
import math

import jax
import jax.numpy as jnp
from jax import lax
from jax.experimental import pallas as pl
from jax.experimental.pallas import tpu as pltpu
from jax.sharding import PartitionSpec as P

H = 12
DH = 64
CLUSTER = 128


EPSILON = 1e-12
FLOOR = -1e30


def layer_norm(values, gain, shift):
    centre = values - jnp.mean(values, axis=-1, keepdims=True)
    spread = jnp.mean(centre * centre, axis=-1, keepdims=True)
    return centre * lax.rsqrt(spread + EPSILON) * gain + shift


def exact_gelu(values):
    return jax.nn.gelu(values, approximate=False)


def positions(length, per_device, parts):
    stored = jnp.arange(length, dtype=jnp.int32)
    device = stored // per_device
    within = stored % per_device
    half = per_device // 2
    return jnp.where(
        within < half, device * half + within, (2 * parts - 1 - device) * half + within - half
    )


def contract(left, right):
    return lax.dot_general(
        left, right, (((0,), (0,)), ((), ())), preferred_element_type=jnp.float32
    )


def back_product(grad, weight):
    return lax.dot_general(
        grad, weight, (((1,), (1,)), ((), ())), preferred_element_type=jnp.float32
    )


def column_sum(values):
    return jnp.sum(values.astype(jnp.float32), axis=0)


def per_head_rows(rows, index):
    split = rows.reshape(rows.shape[0], H, DH)
    return jnp.take_along_axis(split, index.T[:, :, None], axis=0)


def cluster_tables(order, device, per_device, parts):
    heads, length = order.shape
    groups = length // CLUSTER
    members = CLUSTER // parts
    mine = (order // per_device == device).astype(jnp.int32)
    rank = jnp.cumsum(mine.reshape(heads, groups, CLUSTER), axis=-1).reshape(heads, length) - 1
    entry = jnp.arange(length, dtype=jnp.int32)[None, :]
    slot = jnp.where(mine == 1, entry // CLUSTER * members + rank, per_device)
    head_index = jnp.arange(heads, dtype=jnp.int32)[:, None]
    picked = (
        jnp.zeros((heads, per_device), jnp.int32)
        .at[head_index, slot]
        .set(order - device * per_device, mode="drop")
    )
    counter = jnp.broadcast_to(
        jnp.arange(per_device, dtype=jnp.int32)[None, :], (heads, per_device)
    )
    placed = jnp.zeros((heads, per_device), jnp.int32).at[head_index, picked].set(counter)
    inverse = (
        jnp.zeros((heads, length), jnp.int32)
        .at[head_index, order]
        .set(jnp.broadcast_to(jnp.arange(length, dtype=jnp.int32)[None, :], (heads, length)))
    )
    return (picked, placed, inverse)


def score_blocks(query, key_rows, query_blocks, key_blocks, scale):
    scores = (
        jnp.einsum("cqhd,ckhd->hcqk", query, key_rows, preferred_element_type=jnp.float32) * scale
    )
    allowed = key_blocks[:, :, None, :] <= query_blocks[:, :, :, None]
    return (scores, allowed)


def attend(query, key_rows, value_rows, query_blocks, key_blocks, scale):
    scores, allowed = score_blocks(query, key_rows, query_blocks, key_blocks, scale)
    masked = jnp.where(allowed, scores, FLOOR)
    top = jnp.max(masked, axis=-1, keepdims=True)
    weights = jnp.where(allowed, jnp.exp(masked - top), 0.0)
    total = jnp.sum(weights, axis=-1, keepdims=True)
    probs = (weights / total).astype(jnp.bfloat16)
    mixed = jnp.einsum("hcqk,ckhd->cqhd", probs, value_rows, preferred_element_type=jnp.float32)
    return (mixed.astype(jnp.bfloat16), top + jnp.log(total))


def attend_back(query, key_rows, value_rows, query_blocks, key_blocks, logsum, d_mixed, scale):
    scores, allowed = score_blocks(query, key_rows, query_blocks, key_blocks, scale)
    probs = jnp.where(allowed, jnp.exp(jnp.where(allowed, scores, FLOOR) - logsum), 0.0)
    rounded = probs.astype(jnp.bfloat16)
    d_probs = jnp.einsum("cqhd,ckhd->hcqk", d_mixed, value_rows, preferred_element_type=jnp.float32)
    centred = jnp.sum(probs * d_probs, axis=-1, keepdims=True)
    d_scores = (probs * (d_probs - centred)).astype(jnp.bfloat16)
    d_query = (
        jnp.einsum("hcqk,ckhd->cqhd", d_scores, key_rows, preferred_element_type=jnp.float32)
        * scale
    )
    d_key = (
        jnp.einsum("hcqk,cqhd->ckhd", d_scores, query, preferred_element_type=jnp.float32) * scale
    )
    d_value = jnp.einsum("hcqk,cqhd->ckhd", rounded, d_mixed, preferred_element_type=jnp.float32)
    return (d_query, d_key, d_value)


def general_body(
    hidden_in,
    out_grad,
    block_ids,
    clusters,
    w_query,
    w_key,
    w_value,
    w_out,
    b_query,
    b_value,
    b_out,
    ln1_gain,
    ln1_bias,
    w_in,
    b_in,
    w_down,
    b_down,
    ln2_gain,
    ln2_bias,
):
    parts = lax.axis_size("ctx")
    device = lax.axis_index("ctx")
    sequences, per_device, width = hidden_in.shape
    length = per_device * parts
    members = CLUSTER // parts
    groups = length // CLUSTER
    scale = DH ** (-0.5)
    (
        full_query,
        full_key,
        full_value,
        full_out,
        bias_query,
        bias_value,
        bias_out,
        gain_one,
        shift_one,
    ) = (
        lax.all_gather(w_query, "fsdp", axis=0, tiled=True),
        lax.all_gather(w_key, "fsdp", axis=0, tiled=True),
        lax.all_gather(w_value, "fsdp", axis=0, tiled=True),
        lax.all_gather(w_out, "fsdp", axis=0, tiled=True),
        lax.all_gather(b_query, "fsdp", axis=0, tiled=True),
        lax.all_gather(b_value, "fsdp", axis=0, tiled=True),
        lax.all_gather(b_out, "fsdp", axis=0, tiled=True),
        lax.all_gather(ln1_gain, "fsdp", axis=0, tiled=True),
        lax.all_gather(ln1_bias, "fsdp", axis=0, tiled=True),
    )
    full_in, full_down, bias_in, bias_down, gain_two, shift_two = (
        lax.all_gather(w_in, "fsdp", axis=0, tiled=True),
        lax.all_gather(w_down, "fsdp", axis=0, tiled=True),
        lax.all_gather(b_in, "fsdp", axis=0, tiled=True),
        lax.all_gather(b_down, "fsdp", axis=0, tiled=True),
        lax.all_gather(ln2_gain, "fsdp", axis=0, tiled=True),
        lax.all_gather(ln2_bias, "fsdp", axis=0, tiled=True),
    )
    hidden = hidden_in.reshape(sequences * per_device, width)
    query_rows = (
        jnp.dot(hidden, full_query, preferred_element_type=jnp.float32) + bias_query
    ).astype(jnp.bfloat16)
    key_rows = jnp.dot(hidden, full_key, preferred_element_type=jnp.float32).astype(jnp.bfloat16)
    value_rows = (
        jnp.dot(hidden, full_value, preferred_element_type=jnp.float32) + bias_value
    ).astype(jnp.bfloat16)
    place = positions(length, per_device, parts)
    index = 0
    order = clusters[index]
    stored_blocks = block_ids[index][place]
    picked, placed, inverse = cluster_tables(order, device, per_device, parts)
    q_local = per_head_rows(query_rows, picked).reshape(groups, members, H, DH)
    query_blocks = stored_blocks[device * per_device + picked].reshape(H, groups, members)
    key_all = lax.all_gather(key_rows, "ctx", axis=0, tiled=True)
    value_all = lax.all_gather(value_rows, "ctx", axis=0, tiled=True)
    key_cluster = per_head_rows(key_all, order).reshape(groups, CLUSTER, H, DH)
    value_cluster = per_head_rows(value_all, order).reshape(groups, CLUSTER, H, DH)
    key_blocks = stored_blocks[order].reshape(H, groups, CLUSTER)
    mixed, logsum = attend(q_local, key_cluster, value_cluster, query_blocks, key_blocks, scale)
    contexts = per_head_rows(mixed.reshape(per_device, width), placed).reshape(per_device, width)
    kept = [
        (
            q_local,
            key_cluster,
            value_cluster,
            query_blocks,
            key_blocks,
            logsum,
            picked,
            placed,
            inverse,
        )
    ]
    attended = jnp.dot(contexts, full_out, preferred_element_type=jnp.float32) + bias_out
    first_sum = hidden.astype(jnp.float32) + attended
    first, first_pull = jax.vjp(
        layer_norm, first_sum, gain_one.astype(jnp.float32), shift_one.astype(jnp.float32)
    )
    first_low = first.astype(jnp.bfloat16)
    inner = jnp.dot(first_low, full_in, preferred_element_type=jnp.float32) + bias_in
    active_full, gelu_pull = jax.vjp(exact_gelu, inner)
    active = active_full.astype(jnp.bfloat16)
    second_sum = first + jnp.dot(active, full_down, preferred_element_type=jnp.float32) + bias_down
    second, second_pull = jax.vjp(
        layer_norm, second_sum, gain_two.astype(jnp.float32), shift_two.astype(jnp.float32)
    )
    layer_out = second.astype(jnp.bfloat16).reshape(sequences, per_device, width)
    d_out = out_grad.reshape(sequences * per_device, width).astype(jnp.float32)
    d_second, g_gain_two, g_shift_two = second_pull(d_out)
    d_branch = d_second.astype(jnp.bfloat16)
    g_w_down = contract(active, d_branch)
    g_b_down = column_sum(d_branch)
    d_active = back_product(d_branch, full_down)
    d_inner = gelu_pull(d_active)[0].astype(jnp.bfloat16)
    g_w_in = contract(first_low, d_inner)
    g_b_in = column_sum(d_inner)
    d_first = d_second + back_product(d_inner, full_in)
    d_sum, g_gain_one, g_shift_one = first_pull(d_first)
    d_attended = d_sum.astype(jnp.bfloat16)
    g_w_out = contract(contexts, d_attended)
    g_b_out = column_sum(d_attended)
    d_context = back_product(d_attended, full_out).astype(jnp.bfloat16)
    index = 0
    q_kept, k_kept, v_kept, blocks_q, blocks_k, logsum, picked, placed, inverse = kept[index]
    d_cluster = per_head_rows(d_context, picked).reshape(groups, members, H, DH)
    d_query, d_key, d_value = attend_back(
        q_kept, k_kept, v_kept, blocks_q, blocks_k, logsum, d_cluster, scale
    )
    key_full = per_head_rows(d_key.reshape(length, width), inverse).reshape(length, width)
    value_full = per_head_rows(d_value.reshape(length, width), inverse).reshape(length, width)
    key_part = lax.psum_scatter(
        key_full.astype(jnp.bfloat16), "ctx", scatter_dimension=0, tiled=True
    )
    value_part = lax.psum_scatter(
        value_full.astype(jnp.bfloat16), "ctx", scatter_dimension=0, tiled=True
    )
    query_local = d_query.astype(jnp.bfloat16).reshape(per_device, width)
    query_grads = per_head_rows(query_local, placed).reshape(per_device, width)
    g_w_query = contract(hidden, query_grads)
    g_b_query = column_sum(query_grads)
    g_w_key = contract(hidden, key_part)
    g_w_value = contract(hidden, value_part)
    g_b_value = column_sum(value_part)
    input_total = (
        d_sum
        + back_product(query_grads, full_query)
        + back_product(key_part, full_key)
        + back_product(value_part, full_value)
    )
    input_grad = input_total.astype(jnp.bfloat16).reshape(sequences, per_device, width)
    shares = (
        lax.psum_scatter(
            g_w_query.astype(jnp.bfloat16), "fsdp", scatter_dimension=0, tiled=True
        ).astype(jnp.float32),
        lax.psum_scatter(
            g_w_key.astype(jnp.bfloat16), "fsdp", scatter_dimension=0, tiled=True
        ).astype(jnp.float32),
        lax.psum_scatter(
            g_w_value.astype(jnp.bfloat16), "fsdp", scatter_dimension=0, tiled=True
        ).astype(jnp.float32),
        lax.psum_scatter(
            g_w_out.astype(jnp.bfloat16), "fsdp", scatter_dimension=0, tiled=True
        ).astype(jnp.float32),
        lax.psum_scatter(
            g_b_query.astype(jnp.bfloat16), "fsdp", scatter_dimension=0, tiled=True
        ).astype(jnp.float32),
        lax.psum_scatter(
            g_b_value.astype(jnp.bfloat16), "fsdp", scatter_dimension=0, tiled=True
        ).astype(jnp.float32),
        lax.psum_scatter(
            g_b_out.astype(jnp.bfloat16), "fsdp", scatter_dimension=0, tiled=True
        ).astype(jnp.float32),
        lax.psum_scatter(
            g_gain_one.astype(jnp.bfloat16), "fsdp", scatter_dimension=0, tiled=True
        ).astype(jnp.float32),
        lax.psum_scatter(
            g_shift_one.astype(jnp.bfloat16), "fsdp", scatter_dimension=0, tiled=True
        ).astype(jnp.float32),
        lax.psum_scatter(
            g_w_in.astype(jnp.bfloat16), "fsdp", scatter_dimension=0, tiled=True
        ).astype(jnp.float32),
        lax.psum_scatter(
            g_b_in.astype(jnp.bfloat16), "fsdp", scatter_dimension=0, tiled=True
        ).astype(jnp.float32),
        lax.psum_scatter(
            g_w_down.astype(jnp.bfloat16), "fsdp", scatter_dimension=0, tiled=True
        ).astype(jnp.float32),
        lax.psum_scatter(
            g_b_down.astype(jnp.bfloat16), "fsdp", scatter_dimension=0, tiled=True
        ).astype(jnp.float32),
        lax.psum_scatter(
            g_gain_two.astype(jnp.bfloat16), "fsdp", scatter_dimension=0, tiled=True
        ).astype(jnp.float32),
        lax.psum_scatter(
            g_shift_two.astype(jnp.bfloat16), "fsdp", scatter_dimension=0, tiled=True
        ).astype(jnp.float32),
    )
    totals = (
        lax.psum(shares[0].astype(jnp.bfloat16), "ctx").astype(jnp.float32),
        lax.psum(shares[1].astype(jnp.bfloat16), "ctx").astype(jnp.float32),
        lax.psum(shares[2].astype(jnp.bfloat16), "ctx").astype(jnp.float32),
        lax.psum(shares[3].astype(jnp.bfloat16), "ctx").astype(jnp.float32),
        lax.psum(shares[4].astype(jnp.bfloat16), "ctx").astype(jnp.float32),
        lax.psum(shares[5].astype(jnp.bfloat16), "ctx").astype(jnp.float32),
        lax.psum(shares[6].astype(jnp.bfloat16), "ctx").astype(jnp.float32),
        lax.psum(shares[7].astype(jnp.bfloat16), "ctx").astype(jnp.float32),
        lax.psum(shares[8].astype(jnp.bfloat16), "ctx").astype(jnp.float32),
        lax.psum(shares[9].astype(jnp.bfloat16), "ctx").astype(jnp.float32),
        lax.psum(shares[10].astype(jnp.bfloat16), "ctx").astype(jnp.float32),
        lax.psum(shares[11].astype(jnp.bfloat16), "ctx").astype(jnp.float32),
        lax.psum(shares[12].astype(jnp.bfloat16), "ctx").astype(jnp.float32),
        lax.psum(shares[13].astype(jnp.bfloat16), "ctx").astype(jnp.float32),
        lax.psum(shares[14].astype(jnp.bfloat16), "ctx").astype(jnp.float32),
    )
    return (
        layer_out,
        input_grad,
        totals[0],
        totals[1],
        totals[2],
        totals[3],
        totals[4],
        totals[5],
        totals[6],
        totals[7],
        totals[8],
        totals[9],
        totals[10],
        totals[11],
        totals[12],
        totals[13],
        totals[14],
    )


BF = jnp.bfloat16
F32 = jnp.float32
LANES = 256
VMEM = pl.BlockSpec(memory_space=pltpu.VMEM)
HBM = pl.BlockSpec(memory_space=pl.ANY)
FAR = pl.BlockSpec(memory_space=pltpu.HBM)
SMEM = pl.BlockSpec(memory_space=pltpu.SMEM)
VEC = 16
STATS = 8
SLAB = 64


def shaped(shape, dtype):
    return jax.ShapeDtypeStruct(shape, dtype)


def call(kernel, outs, ins, args, scratch=(), name=None, weight=1):
    moved = sum(a.size * a.dtype.itemsize for a in args)
    moved += sum(o.size * o.dtype.itemsize for o in outs)
    held = sum(
        math.prod(r.shape) * jnp.dtype(r.dtype).itemsize
        for r in scratch
        if jnp.issubdtype(r.dtype, jnp.number)
    )
    return pl.pallas_call(
        kernel,
        out_shape=outs,
        in_specs=ins,
        out_specs=[VMEM] * len(outs),
        scratch_shapes=list(scratch),
        name=name,
        cost_estimate=pl.CostEstimate(flops=weight, transcendentals=0, bytes_accessed=weight),
        compiler_params=pltpu.CompilerParams(vmem_limit_bytes=moved + held + (4 << 20)),
    )(*args)


def mix(function, outs, *args, name=None):
    def kernel(*refs):
        found = function(*(ref[...] for ref in refs[: len(args)]))
        for ref, value in zip(refs[len(args) :], found):
            ref[...] = value

    return call(kernel, outs, [VMEM] * len(args), args, name=name)


def dot(left, right):
    return jnp.dot(left, right, preferred_element_type=F32)


def dot_nt(left, right):
    return lax.dot_general(left, right, (((1,), (1,)), ((), ())), preferred_element_type=F32)


def dot_tn(left, right):
    return lax.dot_general(left, right, (((0,), (0,)), ((), ())), preferred_element_type=F32)


class Plan:
    def __init__(self, chips, ring, width, hidden, per_device):
        self.chips, self.ring, self.width, self.hidden = chips, ring, width, hidden
        self.rows = per_device
        self.tokens = chips * per_device
        self.shard = width // ring
        self.half = self.shard // 2
        self.share = hidden // chips
        self.hshard = hidden // ring
        self.block = self.hshard // chips
        self.bhalf = self.block // 2
        self.heads = H // chips
        self.cols = self.heads * DH
        self.qkv = 3 * self.cols
        self.padded = self.heads * LANES
        self.wide = -(-self.qkv // 128) * 128
        self.packed = self.half * self.qkv // width
        self.clusters = chips
        self.members = CLUSTER // (2 * chips)
        self.entries = chips * CLUSTER


def pick_kernel(g, sc, *refs):
    weights, small = refs[:3], refs[3:12]
    qall, qsend, vec, here, *lines, sem = refs[12:]
    p, k = sc[0], sc[1]
    copies = [
        pltpu.make_async_copy(w, here.at[i], sem.at[i]) for i, w in enumerate(weights)
    ]
    copies += [
        pltpu.make_async_copy(ref, lines[i], sem.at[3 + i])
        for i, ref in enumerate(small)
    ]
    start(copies)
    finish(copies)
    for q in range(g.chips):

        @pl.when(p == q)
        def _(q=q):
            for i in range(3):
                qall[:, g.cols * i : g.cols * (i + 1)] = here[
                    i, :, g.cols * q : g.cols * (q + 1)
                ]

    vec[...] = jnp.zeros((VEC, LANES), BF)
    for i in range(8):
        vec[i : i + 1, 0 : g.shard] = lines[i][...].reshape(1, g.shard)
    for q in range(g.chips):
        vec[8 + q : 9 + q, 0 : g.block] = lines[8][g.block * q : g.block * (q + 1)].reshape(
            1, g.block
        )
    mine = pl.ds(pl.multiple_of(g.half * k, 16), g.half)
    qsend[0 : g.half] = qall[mine]
    qsend[g.half : g.half + VEC, 0:LANES] = vec[...]
    qsend[g.half : g.half + VEC, LANES:] = jnp.zeros((VEC, g.qkv - LANES), BF)


def prep_kernel(g, sc, _, wi, wd, wo, iall, oall, dall, send, here, sem):
    p, k = sc[0], sc[1]
    at = pl.multiple_of(g.block * p, 16)
    copies = [
        pltpu.make_async_copy(wi, here, sem.at[0]),
        pltpu.make_async_copy(wo, oall, sem.at[1]),
        pltpu.make_async_copy(wd.at[pl.ds(at, g.block)], dall, sem.at[2]),
    ]
    start(copies)
    finish(copies[:1])
    for q in range(g.chips):

        @pl.when(p == q)
        def _(q=q):
            for r in range(g.ring):
                src = g.hshard * r + g.block * q
                iall[:, g.block * r : g.block * (r + 1)] = here[:, src : src + g.block]

    mine = pl.ds(pl.multiple_of(g.half * k, 16), g.half)
    send[0 : g.half] = iall[mine]
    finish(copies[1:])
    send[g.half : 2 * g.half] = oall[mine]
    send[2 * g.half :] = dall[pl.ds(pl.multiple_of(g.bhalf * k, 16), g.bhalf)]


def lay(g, sc, own, mine, theirs, at, size, dst, turn=0):
    k, f = sc[1], jnp.bitwise_xor(sc[2], turn)
    dst[pl.ds(pl.multiple_of(2 * size * f, 16), 2 * size), :] = own[...]
    for s in range(1, g.ring):
        base = 2 * size * jnp.bitwise_xor(f, s)
        for src, core in ((mine[s - 1], k), (theirs[s - 1], 1 - k)):
            dst[pl.ds(pl.multiple_of(base + size * core, 16), size), :] = src[at : at + size, :]


def start(copies):
    for copy in copies:
        copy.start()


def finish(copies):
    for copy in copies:
        copy.wait()


def qkv_kernel(g, sc, *refs):
    n, c = g.ring - 1, 2 * g.chips
    xs = refs[:c]
    vec, own = refs[c : c + 2]
    mine = refs[c + 2 : c + 2 + n]
    theirs = refs[c + 2 + n : c + 2 + 2 * n]
    out, w, full = refs[c + 2 + 2 * n :]
    p, f = sc[0], sc[2]
    lay(g, sc, own, mine, theirs, 0, g.half, w)
    rest = jnp.zeros((VEC, g.width - LANES), F32)
    total = jnp.zeros((VEC, g.width), F32)
    for s in range(g.ring):
        piece = vec[...] if s == 0 else mine[s - 1][g.half : g.half + VEC, 0:LANES]
        piece = piece.astype(F32)
        wide = jnp.concatenate([piece, rest], axis=1)
        total = total + pltpu.roll(wide, g.shard * jnp.bitwise_xor(f, s), 1)
    full[...] = total
    back = pltpu.roll(total, lax.rem(g.width - g.cols * p, g.width), 1)
    bias = jnp.concatenate(
        [back[0:1, : g.cols], jnp.zeros((1, g.cols), F32), back[1:2, : g.cols]], axis=1
    )
    rows = jnp.concatenate([x[...] for x in xs], axis=0)
    found = (dot(rows, w[...]) + bias).astype(BF)
    for h in range(g.heads):
        for i in range(3):
            out[:, LANES * h + DH * i : LANES * h + DH * (i + 1)] = found[
                :, g.cols * i + DH * h : g.cols * i + DH * (h + 1)
            ]
        out[:, LANES * h + 3 * DH : LANES * (h + 1)] = jnp.zeros((2 * g.tokens, DH), BF)


def select(index, size, axis_size, lanes):
    if lanes:
        ids = lax.broadcasted_iota(jnp.int32, (size, axis_size), 1)
    else:
        ids = lax.broadcasted_iota(jnp.int32, (axis_size, size), 0)
    return jnp.where(ids == index, 1.0, 0.0).astype(BF)


def over(x, size):
    return lax.shift_right_logical(x, jnp.int32(size.bit_length() - 1))


def tables_kernel(g, sc, _, clusters, block_ids, pick, place, blocks):
    p, k = sc[0], sc[1]
    ranges, step = 2 * g.chips, g.clusters * g.members
    shape = (2 * ranges, 2 * ranges)
    piece, source = (lax.broadcasted_iota(jnp.int32, shape, axis) for axis in (0, 1))
    device = 2 * jnp.bitwise_xor(p, over(piece, 2) & (g.chips - 1)) + jnp.bitwise_xor(
        k, over(piece, 2 * g.chips)
    )
    found = jnp.where(piece & 1 == 0, device, 2 * ranges - 1 - device)
    hot = jnp.where(found == source, 1.0, 0.0).astype(BF)
    half = g.rows // 2
    line = block_ids[...].astype(F32)
    lines = [line[:, half * i : half * (i + 1)] for i in range(2 * ranges)]
    ids = dot(hot, jnp.concatenate(lines, axis=0).astype(BF))
    for d in range(ranges):
        line = jnp.concatenate([ids[2 * d : 2 * d + 1], ids[2 * d + 1 : 2 * d + 2]], axis=1)
        blocks[:, g.rows * d : g.rows * (d + 1)] = jnp.broadcast_to(line, (8, g.rows)).astype(BF)
    before = lax.broadcasted_iota(jnp.int32, (CLUSTER, CLUSTER), 1) < lax.broadcasted_iota(
        jnp.int32, (CLUSTER, CLUSTER), 0
    )
    rows, cols, tokens = [], [], []
    for h in range(g.heads):
        order = clusters[
            pl.ds(g.heads * p + h, 1), pl.ds(pl.multiple_of(g.entries * k, 128), g.entries)
        ]
        chip, core = over(order, 2 * g.rows), over(order, g.rows) & 1
        within = order & (g.rows - 1)
        rows.append(
            jnp.bitwise_xor(core, k) * g.tokens + jnp.bitwise_xor(chip, p) * g.rows + within
        )
    units = [(h, c) for h in range(g.heads) for c in range(g.clusters)]
    for h, c in units:
        row = rows[h][:, CLUSTER * c : CLUSTER * (c + 1)]
        tall = jnp.broadcast_to(row.astype(F32), (CLUSTER, CLUSTER))
        cols.append(over(jnp.transpose(tall)[:, 0:1].astype(jnp.int32), g.rows))
    spots = []
    for (h, c), col in zip(units, cols):
        row = rows[h][:, CLUSTER * c : CLUSTER * (c + 1)]
        same = (col == over(row, g.rows)) & before
        rank = jnp.sum(jnp.where(same, 1.0, 0.0), axis=1, keepdims=True).astype(jnp.int32)
        spots.append(select(col * g.members + rank, CLUSTER, CLUSTER, True))
    for (h, c), spot in zip(units, spots):
        row = rows[h][:, CLUSTER * c : CLUSTER * (c + 1)]
        within = jnp.broadcast_to((row & (g.rows - 1)).astype(F32), (8, CLUSTER)).astype(BF)
        tokens.append(dot(within, spot))
    for h in range(g.heads):
        for d in range(ranges):
            lanes = slice(g.members * d, g.members * (d + 1))
            mine = jnp.concatenate(
                [tokens[h * g.clusters + c][:, lanes] for c in range(g.clusters)], axis=1
            ).astype(jnp.int32)
            place[h, g.rows * d : g.rows * (d + 1)] = select(mine[0:1, :], step, g.rows, False)
            pick[h, step * d : step * (d + 1)] = select(
                jnp.transpose(mine)[:, 0:1], step, g.rows, True
            )


def mask_kernel(g, blocks, place, mask):
    ids = [
        [
            dot(blocks[:, g.rows * d : g.rows * (d + 1)], place[h, g.rows * d : g.rows * (d + 1)])
            for d in range(2 * g.chips)
        ]
        for h in range(g.heads)
    ]
    for h in range(g.heads):
        for c in range(g.clusters):
            lanes = slice(g.members * c, g.members * (c + 1))
            keys = jnp.concatenate([part[:, lanes] for part in ids[h]], axis=1)
            allowed = keys[0:1, :] <= jnp.transpose(keys)[:, 0:1]
            mask[h * g.clusters + c] = jnp.where(allowed, 0.0, FLOOR)


def cluster_rows(g, ref, c):
    step = g.clusters * g.members
    return jnp.concatenate(
        [
            ref[step * d + g.members * c : step * d + g.members * (c + 1)]
            for d in range(2 * g.chips)
        ],
        axis=0,
    )


def put_cluster(g, ref, c, values):
    step = g.clusters * g.members
    for d in range(2 * g.chips):
        ref[step * d + g.members * c : step * d + g.members * (c + 1)] = values[
            g.members * d : g.members * (d + 1)
        ]


def attend_kernel(g, qkv, pick, place, mask, ctx_own, ctx_other, kept, probs, mixed):
    step, ranges = g.clusters * g.members, 2 * g.chips
    units = [(h, c) for h in range(g.heads) for c in range(g.clusters)]
    for h in range(g.heads):
        for d in range(ranges):
            rows = qkv[g.rows * d : g.rows * (d + 1), LANES * h : LANES * (h + 1)]
            slots = slice(step * d, step * (d + 1))
            kept[h, slots] = dot(pick[h, slots], rows).astype(BF)
    for h, c in units:
        rows = cluster_rows(g, kept.at[h], c)
        q, key = rows[:, 0:DH], rows[:, DH : 2 * DH]
        at = h * g.clusters + c
        probs[at] = dot_nt(q, key) * (DH ** (-0.5)) + mask[at]
    for h, c in units:
        at = h * g.clusters + c
        masked = probs[at]
        weights = jnp.exp(masked - jnp.max(masked, axis=-1, keepdims=True))
        probs[at] = weights * (1.0 / jnp.sum(weights, axis=-1, keepdims=True))
    for h, c in units:
        v = cluster_rows(g, kept.at[h], c)[:, 2 * DH : 3 * DH]
        put_cluster(
            g, mixed.at[h], c, dot(probs[h * g.clusters + c].astype(BF), v).astype(BF)
        )
    for h in range(g.heads):
        for d in range(ranges):
            side, at = (ctx_own, d) if d < g.chips else (ctx_other, d - g.chips)
            rows = dot(
                place[h, g.rows * d : g.rows * (d + 1)], mixed[h, step * d : step * (d + 1)]
            )
            side[g.rows * at : g.rows * (at + 1), DH * h : DH * (h + 1)] = rows.astype(BF)


def attend_back_kernel(g, own, other, pick, place, kept, probs, grads, d_mixed, found, d_scores):
    step, ranges = g.clusters * g.members, 2 * g.chips
    scale = DH ** (-0.5)
    units = [(h, c) for h in range(g.heads) for c in range(g.clusters)]
    for h in range(g.heads):
        for d in range(ranges):
            side, at = (own, d) if d < g.chips else (other, d - g.chips)
            rows = side[g.rows * at : g.rows * (at + 1), DH * h : DH * (h + 1)]
            slots = slice(step * d, step * (d + 1))
            d_mixed[h, slots] = dot(pick[h, slots], rows).astype(BF)
    for h, c in units:
        v = cluster_rows(g, kept.at[h], c)[:, 2 * DH : 3 * DH]
        share = probs[h * g.clusters + c]
        d_share = dot_nt(cluster_rows(g, d_mixed.at[h], c), v)
        delta = jnp.sum(share * d_share, axis=-1, keepdims=True)
        d_scores[h * g.clusters + c] = (share * (d_share - delta)).astype(BF)
    for h, c in units:
        rows = cluster_rows(g, kept.at[h], c)
        d_s, share = d_scores[h * g.clusters + c], probs[h * g.clusters + c].astype(BF)
        d_q = dot(d_s, rows[:, DH : 2 * DH]) * scale
        d_k = dot_tn(d_s, rows[:, 0:DH]) * scale
        d_v = dot_tn(share, cluster_rows(g, d_mixed.at[h], c))
        put_cluster(g, found.at[h], c, jnp.concatenate([d_q, d_k, d_v], axis=1).astype(BF))
    for h in range(g.heads):
        for d in range(ranges):
            at = slice(g.rows * d, g.rows * (d + 1))
            rows = dot(place[h, at], found[h, step * d : step * (d + 1)]).astype(BF)
            for i in range(3):
                grads[at, g.cols * i + DH * h : g.cols * i + DH * (h + 1)] = rows[
                    :, DH * i : DH * (i + 1)
                ]
    grads[:, g.qkv :] = jnp.zeros((2 * g.tokens, g.wide - g.qkv), BF)


def norm_parts(values):
    centre = values - jnp.mean(values, axis=-1, keepdims=True)
    spread = jnp.mean(centre * centre, axis=-1, keepdims=True)
    scale = lax.rsqrt(spread + EPSILON)
    return centre * scale, scale


def norm_back(grad, z, scale):
    return scale * (
        grad
        - jnp.mean(grad, axis=-1, keepdims=True)
        - z * jnp.mean(grad * z, axis=-1, keepdims=True)
    )


def seen(g, ref, j):
    half = g.chips // 2
    return jnp.concatenate(
        [
            ref[
                g.rows * ((i ^ j) % half) : g.rows * ((i ^ j) % half + 1),
                g.cols * ((i ^ j) // half) : g.cols * ((i ^ j) // half + 1),
            ]
            for i in range(g.chips)
        ],
        axis=0,
    )


def forward_kernel(g, sc, *refs):
    c, n = g.chips, g.ring - 1
    ctxs, xs, full = refs[:c], refs[c : 2 * c], refs[2 * c]
    wo_own, wi_own, wd_own = refs[2 * c + 1 : 2 * c + 4]
    refs = refs[2 * c + 4 :]
    mine, theirs = refs[:n], refs[n : 2 * n]
    refs = refs[2 * n :]
    parts, (active, inner, low, z_own, s_own, wo_rows, wi, wd) = refs[:c], refs[c : c + 8]
    wo, work = refs[c + 8 :]
    p = sc[0]
    lay(g, sc, wo_own, mine, theirs, g.half, g.half, wo, p)
    rows = jnp.concatenate([seen(g, ctxs[j], j) for j in range(c)], axis=1)
    wo_rows[...] = wo[0 : g.cols]
    halves = [slice(i, i + g.tokens // 2) for i in range(0, g.tokens, g.tokens // 2)]
    bias = full[pl.ds(8 + p, 1), :]

    def first_norm(half):
        for i in range(half.start, half.stop, SLAB):
            at = slice(i, i + SLAB)
            x = xs[i // g.rows][i % g.rows : i % g.rows + SLAB].astype(F32)
            z, scale = norm_parts(work[at] + x + full[2:3, :])
            first = z * full[3:4, :] + full[4:5, :]
            low[at] = first.astype(BF)
            if i < g.rows:
                z_own[at] = z
                s_own[at] = jnp.broadcast_to(scale, (SLAB, 128))
                parts[0][at] = first + full[5:6, :]

    def activate(half):
        for i in range(half.start, half.stop, SLAB):
            at = slice(i, i + SLAB)
            u = inner[at] + bias
            inner[at] = u
            active[at] = (u * (1.0 + lax.erf(u * (0.5**0.5))) * 0.5).astype(BF)

    def descend(half):
        second = dot(active[half], wd[...])
        for i in range(half.start, half.stop, g.rows):
            block = second[i - half.start : i - half.start + g.rows]
            if i == 0:
                parts[0][...] += block
            else:
                parts[i // g.rows][...] = block.astype(BF)

    one, two = halves
    work[one] = dot(rows[one], wo[...])
    work[two] = dot(rows[two], wo[...])
    lay(g, sc, wi_own, mine, theirs, 0, g.half, wi)
    first_norm(one)
    inner[one] = dot(low[one], wi[...])
    first_norm(two)
    inner[two] = dot(low[two], wi[...])
    lay(g, sc, wd_own, mine, theirs, 2 * g.half, g.bhalf, wd)
    activate(one)
    descend(one)
    activate(two)
    descend(two)


def turn_kernel(g, *refs):
    c = g.chips
    parts, full, cotangent = refs[:c], refs[c], refs[c + 1]
    out, d_second, branch = refs[c + 2 :]
    second = parts[0][...]
    for j in range(1, c):
        second = second + parts[j][...].astype(F32)
    z, scale = norm_parts(second)
    gain = full[6:7, :]
    out[...] = (z * gain + full[7:8, :]).astype(BF)
    dy = cotangent[...].astype(F32)
    grad = norm_back(dy * gain, z, scale)
    d_second[...] = grad
    branch[0 : g.rows] = grad.astype(BF)
    one = jnp.sum(dy * z, axis=0, keepdims=True)
    two = jnp.sum(dy, axis=0, keepdims=True)
    rest = jnp.zeros((STATS - 2, g.width), F32)
    branch[g.rows : g.rows + STATS] = jnp.concatenate([one, two, rest], axis=0).astype(BF)


def back_kernel(g, *refs):
    c = g.chips
    branches, slope, wd, wi = refs[:c], refs[c], refs[c + 1], refs[c + 2]
    parts, d_inner = refs[c + 3 : 2 * c + 3], refs[2 * c + 3]
    rows = jnp.concatenate([b[0 : g.rows] for b in branches], axis=0)
    halves = [slice(i, i + g.tokens // 2) for i in range(0, g.tokens, g.tokens // 2)]
    for half in halves:
        d_inner[half] = (dot_nt(rows[half], wd[...]) * slope[half]).astype(BF)
    for half in halves:
        total = dot_nt(d_inner[half], wi[...])
        for i in range(half.start, half.stop, g.rows):
            block = total[i - half.start : i - half.start + g.rows]
            parts[i // g.rows][...] = block if i == 0 else block.astype(BF)


def split_rows(g, sc, total, size, own, other, at):
    k, f = sc[1], sc[2]
    for s in range(g.ring):
        base = 2 * size * jnp.bitwise_xor(f, s)
        own[s, at : at + size] = total[pl.ds(pl.multiple_of(base + size * k, 8), size), :]
        other[s, at : at + size] = total[
            pl.ds(pl.multiple_of(base + size * (1 - k), 8), size), :
        ].astype(BF)


def mlp_grads_kernel(g, sc, *refs):
    c = g.chips
    branches, active, low, d_inner = refs[:c], refs[c], refs[c + 1], refs[c + 2]
    own, other, sums, total = refs[c + 3 :]
    rows = jnp.concatenate([b[0 : g.rows] for b in branches], axis=0)
    total[...] = dot_tn(active[...], rows)
    split_rows(g, sc, total, g.bhalf, own, other, g.half)
    total[...] = dot_tn(low[...], d_inner[...])
    split_rows(g, sc, total, g.half, own, other, 0)
    stats = branches[0][g.rows : g.rows + STATS].astype(F32)
    for j in range(1, c):
        stats = stats + branches[j][g.rows : g.rows + STATS].astype(F32)
    down = jnp.sum(rows.astype(F32), axis=0, keepdims=True)
    up = jnp.sum(d_inner[...].astype(F32), axis=0, keepdims=True)
    sums[...] = jnp.concatenate([stats[0:2], down, up, jnp.zeros((4, g.width), F32)], axis=0)


def first_kernel(g, *refs):
    c = g.chips
    parts, d_second, z_own, s_own, full = refs[:c], *refs[c : c + 4]
    d_sum, attended = refs[c + 4 :]
    d_first = d_second[...] + parts[0][...]
    for j in range(1, c):
        d_first = d_first + parts[j][...].astype(F32)
    z = z_own[...]
    grad = norm_back(d_first * full[3:4, :], z, s_own[:, 0:1])
    d_sum[...] = grad
    attended[0 : g.rows] = grad.astype(BF)
    one = jnp.sum(d_first * z, axis=0, keepdims=True)
    two = jnp.sum(d_first, axis=0, keepdims=True)
    rest = jnp.zeros((STATS - 2, g.width), F32)
    attended[g.rows : g.rows + STATS] = jnp.concatenate([one, two, rest], axis=0).astype(BF)


def context_kernel(g, *refs):
    grads, wo_rows, out = refs[: g.chips], refs[g.chips], refs[g.chips + 1]
    rows = jnp.concatenate([b[0 : g.rows] for b in grads], axis=0)
    out[...] = dot_nt(rows, wo_rows[...]).astype(BF)


def out_grads_kernel(g, sc, *refs):
    c = g.chips
    grads, ctxs, sums = refs[:c], refs[c : 2 * c], refs[2 * c]
    own, away, total = refs[2 * c + 1 :]
    p, f = sc[0], sc[2]
    rows = jnp.concatenate([b[0 : g.rows] for b in grads], axis=0)
    for j in range(c):
        q = jnp.bitwise_xor(p, j)
        total[pl.ds(pl.multiple_of(g.cols * q, 64), g.cols), :] = dot_tn(seen(g, ctxs[j], j), rows)
    stats = grads[0][g.rows : g.rows + STATS].astype(F32)
    for j in range(1, c):
        stats = stats + grads[j][g.rows : g.rows + STATS].astype(F32)
    out = jnp.sum(rows.astype(F32), axis=0, keepdims=True)
    rest = jnp.zeros((STATS - 7, g.width), F32)
    block = jnp.concatenate([sums[0:4], stats[0:2], out, rest], axis=0)
    size = g.shard // c
    for s in range(g.ring):
        base = g.shard * jnp.bitwise_xor(f, s) + size * p
        part = total[pl.ds(pl.multiple_of(base, 8), size), :]
        if s % 2:
            away[s // 2, 0:size] = part.astype(BF)
            away[s // 2, size:] = block.astype(BF)
        else:
            own[s // 2, 0:size] = part
            own[s // 2, size:] = block


def summed(g, mine, theirs, at):
    one = mine[g.tokens * at : g.tokens * (at + 1), : g.qkv].astype(F32)
    two = theirs[g.tokens * (1 - at) : g.tokens * (2 - at), : g.qkv].astype(F32)
    return (one + two).astype(BF)


def input_kernel(g, mine, theirs, w, *parts):
    total = dot_nt(summed(g, mine, theirs, 0), w[...])
    parts[0][...] = total[: g.rows]
    for j in range(1, g.chips):
        parts[j][...] = total[g.rows * j : g.rows * (j + 1)].astype(BF)


def turn_rows_kernel(g, sc, *refs):
    xs, out = refs[: 2 * g.chips], refs[2 * g.chips]
    rows = jnp.concatenate([x[...] for x in xs], axis=0)
    for core in range(2):

        @pl.when(sc[1] == core)
        def _(core=core):
            for r in range(g.ring):
                lane = g.shard * r + g.half * core
                out[g.half * r : g.half * (r + 1), :] = jnp.transpose(rows[:, lane : lane + g.half])


def qkv_grads_kernel(g, sc, mine, theirs, turned_x, own, away, total):
    f = sc[2]
    rows = jnp.concatenate([summed(g, mine, theirs, 0), summed(g, mine, theirs, 1)], axis=0)
    total[...] = dot(turned_x[...], rows)
    sums = jnp.sum(rows.astype(F32), axis=0, keepdims=True)
    gap = jnp.zeros((8, g.width - g.qkv), F32)
    block = jnp.concatenate(
        [jnp.concatenate([sums, jnp.zeros((7, g.qkv), F32)], axis=0), gap], axis=1
    )
    for s in range(g.ring):
        part = total[pl.ds(pl.multiple_of(g.half * jnp.bitwise_xor(f, s), 8), g.half), :]
        packed = pack(g, part)
        if s % 2:
            away[s // 2, 0 : g.packed] = packed.astype(BF)
            away[s // 2, g.packed :] = block.astype(BF)
        else:
            own[s // 2, 0 : g.packed] = packed
            own[s // 2, g.packed :] = block


def pack(g, part):
    step = g.half - g.packed
    beside = [
        part[g.packed :, step_lanes : step_lanes + g.width - g.qkv]
        for step_lanes in range(0, g.qkv, g.width - g.qkv)
    ]
    return jnp.concatenate(
        [part[0 : g.packed], jnp.concatenate(beside, axis=0)], axis=1
    )


def sources(g, sc, refs):
    p, k = sc[0], sc[1]
    out = []
    for j, (mine, theirs) in enumerate(zip(refs, others(g, refs))):
        q = jnp.bitwise_xor(p, j)
        out.append((q, k, mine))
        out.append((q, 1 - k, theirs))
    return out


def others(g, refs):
    far = refs[g.chips :]
    return far if len(far) > 1 else [far[0].at[j] for j in range(g.chips)]


def paired(g, sc, refs, body):
    p, k = sc[0], sc[1]
    mine, theirs = refs[: g.chips], others(g, refs)
    for odd in range(2):

        @pl.when(p & 1 == odd)
        def _(odd=odd):
            for j in range(0, g.chips, 2):
                pair = jnp.bitwise_xor(over(p, 2), j // 2)
                for found, core in ((mine, k), (theirs, 1 - k)):
                    body(pair, core, found[j ^ odd], found[j ^ odd ^ 1])


def mlp_final_kernel(g, sc, *refs):
    found, (g_in, g_down) = refs[:-2], refs[-2:]

    def place(pair, core, even, odd):
        mine = pl.ds(pl.multiple_of(g.half * core, 8), g.half)
        for i, ref in enumerate((even, odd)):
            at = pl.multiple_of(g.block * (2 * pair + i) + g.bhalf * core, 8)
            g_down[pl.ds(at, g.bhalf), :] = ref[g.half :, :].astype(F32)
        for r in range(g.ring):
            lane = pl.multiple_of(g.hshard * r + 2 * g.block * pair, 128)
            lanes = slice(g.block * r, g.block * (r + 1))
            g_in[mine, pl.ds(lane, 2 * g.block)] = jnp.concatenate(
                [even[0 : g.half, lanes], odd[0 : g.half, lanes]], axis=1
            ).astype(F32)

    paired(g, sc, found, place)


def last_kernel(g, sc, *refs):
    found = refs[: 2 * g.chips]
    gq, gk, gv, g_bq, g_bv, g_out, g_bin, *small = refs[2 * g.chips :]
    p, f = sc[0], sc[2]
    size, step = g.shard // g.chips, g.half - g.packed
    top = g.packed + 8
    for q, core, ref in sources(g, sc, found):

        @pl.when((q == f) & (core == 0))
        def _(ref=ref):
            row = ref[g.packed : top, :].astype(F32)[0:1]
            for dst, at in zip((g_bq, g_bv), (0, 2)):
                dst[...] = row[:, g.cols * at : g.cols * (at + 1)].reshape(g.shard)

    def place(pair, core, even, odd):
        base = pl.multiple_of(g.half * core, 8)
        lane = pl.ds(pl.multiple_of(2 * g.cols * pair, 128), 2 * g.cols)
        for i, dst in enumerate((gq, gk, gv)):
            for rows, at, lanes in (
                (pl.ds(base, g.packed), slice(0, g.packed), slice(g.cols * i, g.cols * (i + 1))),
                (
                    pl.ds(base + g.packed, step),
                    slice(step * i, step * (i + 1)),
                    slice(g.qkv, g.width),
                ),
            ):
                dst[rows, lane] = jnp.concatenate(
                    [even[at, lanes], odd[at, lanes]], axis=1
                ).astype(F32)

    paired(g, sc, found, place)
    far = others(g, found)
    for j in range(g.chips):
        q = jnp.bitwise_xor(p, j)
        one, two = found[j], far[j]
        both = one[top:, :].astype(F32) + two[top:, :].astype(F32)
        g_out[pl.ds(pl.multiple_of(size * q, 8), size), :] = both[0:size]
        back = pltpu.roll(both[size : size + STATS], lax.rem(g.width - g.shard * f, g.width), 1)
        for chip in range(g.chips):

            @pl.when(q == chip)
            def _(chip=chip, back=back):
                g_bin[g.block * chip : g.block * (chip + 1)] = back[3:4, : g.shard].reshape(g.shard)
                if chip == 0:
                    for i, dst in zip((0, 1, 2, 4, 5, 6), small):
                        dst[...] = back[i : i + 1, : g.shard].reshape(g.shard)


def to_core(x):
    n = lax.axis_size("ctx")
    return lax.ppermute(x, "ctx", [(i, i ^ 1) for i in range(n)])


def to_chip(x, j):
    n = lax.axis_size("ctx")
    return lax.ppermute(x, "ctx", [(i, i ^ (2 * j)) for i in range(n)])


def along(x, mask):
    n = lax.axis_size("fsdp")
    return lax.ppermute(x, "fsdp", [(i, i ^ mask) for i in range(n)])


def gather_ring(x, pause=None):
    n = lax.axis_size("fsdp")
    found, mask, first = {0: x}, n // 2, ()
    while mask:
        for s in sorted(found):
            first = [found[t] for t in sorted(found) if t]
            part = found[s] if s == 0 or pause is None else after(found[s], pause, *first)
            found[s | mask] = along(part, mask)
        mask //= 2
    return [found[s] for s in range(1, n)]


def spread(x, chips):
    far = {j: to_chip(x, j) for j in sorted(range(1, chips), key=lambda j: -bin(j).count("1"))}
    return [x] + [far[j] for j in range(1, chips)]


def pass_on(x, chips, pause):
    found = {0: x}
    mask = 1
    while mask < chips:
        for j in sorted(found):
            found[j | mask] = to_chip(found[j] if j == 0 else after(found[j], pause), mask)
        mask *= 2
    return [found[j] for j in range(chips)]


def swap(parts):
    far = {j: to_chip(parts[j], j) for j in sorted(range(1, len(parts)), key=lambda j: -bin(j).count("1"))}
    return [parts[0]] + [far[j] for j in range(1, len(parts))]


def ring_step(kept, away, mask):
    count, rows, width = kept.shape
    half = count // 2

    def step(mine, got):
        total = mine + got.astype(F32)
        if not half:
            return (total.astype(BF),)
        return total.reshape(half, 2, rows, width)[:, 0], total.reshape(
            half, 2, rows, width
        )[:, 1].astype(BF)

    outs = [shaped((half, rows, width), F32), shaped((half, rows, width), BF)]
    return mix(
        step,
        outs if half else [shaped((1, rows, width), BF)],
        kept,
        along(away, mask),
        name="ring_step",
    )


def kept_far(x):
    return pltpu.with_memory_space_constraint(x, pltpu.HBM)


def after(x, *first):
    return lax.optimization_barrier((x, *first))[0]


def ring_step(kept, away, mask):
    count, rows, width = kept.shape
    half = count // 2

    def step(mine, got):
        total = mine + got.astype(F32)
        if not half:
            return (total.astype(BF),)
        return total.reshape(half, 2, rows, width)[:, 0], total.reshape(
            half, 2, rows, width
        )[:, 1].astype(BF)

    outs = [shaped((half, rows, width), F32), shaped((half, rows, width), BF)]
    return mix(
        step,
        outs if half else [shaped((1, rows, width), BF)],
        kept,
        along(away, mask),
        name="ring_step",
    )


def kept_far(x):
    return pltpu.with_memory_space_constraint(x, pltpu.HBM)


def after(x, *first):
    return lax.optimization_barrier((x, *first))[0]


def plane_pieces(piece, chips):
    near = spread(piece, chips)
    return near + [to_core(part) for part in near]


def chip_body(
    hidden_in,
    out_grad,
    block_ids,
    clusters,
    w_query,
    w_key,
    w_value,
    w_out,
    b_query,
    b_value,
    b_out,
    ln1_gain,
    ln1_bias,
    w_in,
    b_in,
    w_down,
    b_down,
    ln2_gain,
    ln2_bias,
):
    n, ring = lax.axis_size("ctx"), lax.axis_size("fsdp")
    chips = n // 2
    rows, width = hidden_in.shape[1:]
    hidden = w_in.shape[1]
    g = Plan(chips, ring, width, hidden, rows)
    c, f = lax.axis_index("ctx"), lax.axis_index("fsdp")
    p, k = c // 2, c % 2
    sc = jnp.stack([p, k, f]).astype(jnp.int32)
    bind = functools.partial


    qall, qsend, vec = call(
        bind(pick_kernel, g),
        [
            shaped((g.shard, g.qkv), BF),
            shaped((g.half + VEC, g.qkv), BF),
            shaped((VEC, LANES), BF),
        ],
        [SMEM] + [FAR] * 12,
        [
            sc,
            *map(
                kept_far,
                (
                    w_query,
                    w_key,
                    w_value,
                    b_query,
                    b_value,
                    b_out,
                    ln1_gain,
                    ln1_bias,
                    b_down,
                    ln2_gain,
                    ln2_bias,
                    b_in,
                ),
            ),
        ],
        [
            pltpu.VMEM((3, g.shard, width), BF),
        ]
        + [pltpu.VMEM((g.shard,), BF)] * 8
        + [pltpu.VMEM((g.hshard,), BF), pltpu.SemaphoreType.DMA((12,))],
        name="pick_weights",
    )
    x_own = after(hidden_in.reshape(rows, width), qsend)
    xs = spread(x_own, chips)
    iall, oall, dall, send = call(
        bind(prep_kernel, g),
        [
            shaped((g.shard, g.share), BF),
            shaped((g.shard, width), BF),
            shaped((g.block, width), BF),
            shaped((2 * g.half + g.bhalf, width), BF),
        ],
        [SMEM, HBM, FAR, FAR, FAR],
        [sc, qsend, kept_far(w_in), kept_far(w_down), kept_far(w_out)],
        [pltpu.VMEM((g.shard, hidden), BF), pltpu.SemaphoreType.DMA((3,))],
        name="prepare_weights",
    )
    q_mine = gather_ring(qsend, send)

    step = g.clusters * g.members
    pick, place, blk = call(
        bind(tables_kernel, g),
        [
            shaped((g.heads, 2 * chips * step, rows), BF),
            shaped((g.heads, 2 * g.tokens, step), BF),
            shaped((8, 2 * g.tokens), BF),
        ],
        [SMEM, HBM] + [VMEM] * 2,
        [sc, q_mine[0], clusters[0], block_ids],
        name="cluster_tables",
    )
    (mask,) = call(
        bind(mask_kernel, g),
        [shaped((g.heads * g.clusters, CLUSTER, CLUSTER), F32)],
        [VMEM] * 2,
        [blk, place],
        name="cluster_mask",
    )
    x_other = [to_core(after(xs[0], xs[1]))] + [to_core(x) for x in xs[1:]]
    q_theirs = [to_core(after(part, xs[1])) for part in q_mine]
    qkv, w_qkv, full = call(
        bind(qkv_kernel, g),
        [
            shaped((2 * g.tokens, g.padded), BF),
            shaped((width, g.qkv), BF),
            shaped((VEC, width), F32),
        ],
        [SMEM] + [VMEM] * (2 * chips + 2 * ring),
        [sc, *xs, *x_other, after(vec, send), qall, *q_mine, *q_theirs],
        name="project",
    )
    ctx_own, ctx_other, kept, probs = call(
        bind(attend_kernel, g),
        [
            shaped((g.tokens, g.cols), BF),
            shaped((g.tokens, g.cols), BF),
            shaped((g.heads, g.entries, LANES), BF),
            shaped((g.heads * g.clusters, CLUSTER, CLUSTER), F32),
        ],
        [VMEM] * 4,
        [qkv, pick, place, mask],
        [pltpu.VMEM((g.heads, g.entries, DH), BF)],
        name="attend",
    )
    (ctx,) = mix(
        lambda a, b: (
            jnp.concatenate([a[: g.tokens // 2] + b[: g.tokens // 2], a[g.tokens // 2 :] + b[g.tokens // 2 :]], axis=1),
        ),
        [shaped((g.tokens // 2, 2 * g.cols), BF)],
        ctx_own,
        to_core(ctx_other),
        name="join_context",
    )
    ctxs = spread(ctx, chips)
    w_mine = gather_ring(send, ctx_own)

    w_theirs = [to_core(after(part, *ctxs[1:])) for part in w_mine]
    *second, active, inner, low, z_own, s_own, wo_rows, wi, wd = call(
        bind(forward_kernel, g),
        [shaped((rows, width), F32)]
        + [shaped((rows, width), BF)] * (chips - 1)
        + [
            shaped((g.tokens, g.share), BF),
            shaped((g.tokens, g.share), F32),
            shaped((g.tokens, width), BF),
            shaped((rows, width), F32),
            shaped((rows, 128), F32),
            shaped((g.cols, width), BF),
            shaped((width, g.share), BF),
            shaped((g.share, width), BF),
        ],
        [SMEM] + [VMEM] * (2 * chips + 2 * ring + 2),
        [sc, *ctxs, *xs, full, oall, iall, dall, *w_mine, *w_theirs],
        [pltpu.VMEM((width, width), BF), pltpu.VMEM((g.tokens, width), F32)],
        name="mlp_forward",
    )
    (slope,) = mix(
        lambda u: (
            0.5 * (1.0 + lax.erf(u * (0.5**0.5)))
            + u * jnp.exp(-0.5 * u * u) * (1.0 / (2.0 * math.pi) ** 0.5),
        ),
        [shaped((g.tokens, g.share), F32)],
        inner,
        name="gelu_slope",
    )
    (turned_x,) = call(
        bind(turn_rows_kernel, g),
        [shaped((ring * g.half, 2 * g.tokens), BF)],
        [SMEM] + [VMEM] * (2 * chips),
        [sc, after(xs[0], inner), *xs[1:], *x_other],
        name="turn_rows",
    )
    second = swap(second)
    layer_out, d_second, branch = call(
        bind(turn_kernel, g),
        [
            shaped((rows, width), BF),
            shaped((rows, width), F32),
            shaped((rows + STATS, width), BF),
        ],
        [VMEM] * (chips + 2),
        [*second, after(full, turned_x), out_grad.reshape(rows, width)],
        name="norm_two",
    )
    branches = spread(branch, chips)
    *d_first, d_inner = call(
        bind(back_kernel, g),
        [shaped((rows, width), F32)]
        + [shaped((rows, width), BF)] * (chips - 1)
        + [shaped((g.tokens, g.share), BF)],
        [VMEM] * (chips + 3),
        [*branches, slope, wd, wi],
        name="mlp_back",
    )
    d_first = swap(d_first)
    m_own, m_other, sums = call(
        bind(mlp_grads_kernel, g),
        [
            shaped((ring, g.half + g.bhalf, width), F32),
            shaped((ring, g.half + g.bhalf, width), BF),
            shaped((8, width), F32),
        ],
        [SMEM] + [VMEM] * (chips + 3),
        [sc, *branches, active, low, d_inner],
        [pltpu.VMEM((width, g.share), F32)],
        name="mlp_grads",
    )
    m_got = to_core(m_other)
    m_rows = g.half + g.bhalf

    def joined(own, got):
        total = own + got.astype(F32)
        return (total[0], *(total[s].astype(BF) for s in range(1, ring)))

    m_kept, *m_away = mix(
        joined,
        [shaped((m_rows, width), F32)] + [shaped((m_rows, width), BF)] * (ring - 1),
        m_own,
        m_got,
        name="join_grads",
    )
    (m_piece,) = mix(
        lambda kept, *parts: (sum((part.astype(F32) for part in parts), kept).astype(BF),),
        [shaped((m_rows, width), BF)],
        m_kept,
        *(along(part, s) for s, part in enumerate(m_away, 1)),
        name="mlp_sum",
    )
    d_sum, attended = call(
        bind(first_kernel, g),
        [shaped((rows, width), F32), shaped((rows + STATS, width), BF)],
        [VMEM] * (chips + 4),
        [*d_first, after(d_second, *m_away), z_own, s_own, full],
        name="norm_one",
    )
    grads = spread(attended, chips)
    (d_ctx,) = call(
        bind(context_kernel, g),
        [shaped((g.tokens, g.cols), BF)],
        [VMEM] * (chips + 1),
        [*grads, after(wo_rows, m_piece)],
        name="context_back",
    )
    d_ctx_other = to_core(d_ctx)
    o_rows = g.shard // chips + STATS
    o_own, o_away = call(
        bind(out_grads_kernel, g),
        [shaped((ring // 2, o_rows, width), F32), shaped((ring // 2, o_rows, width), BF)],
        [SMEM] + [VMEM] * (2 * chips + 1),
        [sc, *grads, *ctxs, sums],
        [pltpu.VMEM((width, width), F32)],
        name="out_grads",
    )
    (dq_mine,) = call(
        bind(attend_back_kernel, g),
        [shaped((2 * g.tokens, g.wide), BF)],
        [VMEM] * 6,
        [d_ctx, d_ctx_other, pick, place, after(kept, o_own), probs],
        [
            pltpu.VMEM((g.heads, g.entries, DH), BF),
            pltpu.VMEM((g.heads, g.entries, 3 * DH), BF),
            pltpu.VMEM((g.heads * g.clusters, CLUSTER, CLUSTER), BF),
        ],
        name="attend_back",
    )
    dq_theirs = to_core(dq_mine)
    q_rows = g.packed + 8
    q_own, q_away = call(
        bind(qkv_grads_kernel, g),
        [shaped((ring // 2, q_rows, width), F32), shaped((ring // 2, q_rows, width), BF)],
        [SMEM] + [VMEM] * 3,
        [sc, dq_mine, dq_theirs, turned_x],
        [pltpu.VMEM((ring * g.half, g.qkv), F32)],
        name="project_grads",
    )
    d_in = call(
        bind(input_kernel, g),
        [shaped((rows, width), F32)] + [shaped((rows, width), BF)] * (chips - 1),
        [VMEM] * 3,
        [after(dq_mine, q_away), dq_theirs, w_qkv],
        name="project_back",
    )
    d_in = swap(d_in)
    mask_at = 2
    q_away0 = q_away
    o_away = after(o_away, dq_mine)
    while q_own.shape[0] > 1:
        q_own, q_away = ring_step(q_own, q_away, mask_at // 2)
        o_own, o_away = ring_step(o_own, o_away, mask_at // 2)
        mask_at *= 2
    near = pass_on(m_piece, chips, dq_theirs)
    m_pieces = near + [to_core(after(part, q_away)) for part in near]
    (input_grad,) = mix(
        lambda kept, *parts: (sum((part.astype(F32) for part in parts), kept).astype(BF),),
        [shaped((rows, width), BF)],
        d_sum,
        *d_in,
        name="input_sum",
    )
    g_in, g_down = call(
        bind(mlp_final_kernel, g),
        [shaped((g.shard, hidden), F32), shaped((g.hshard, width), F32)],
        [SMEM] + [VMEM] * len(m_pieces),
        [sc, *m_pieces],
        name="mlp_lay",
    )
    vector = shaped((g.shard,), F32)
    (piece,) = mix(
        lambda a, b, c, d: (
            jnp.concatenate([a[0] + b[0].astype(F32), c[0] + d[0].astype(F32)], axis=0).astype(BF),
        ),
        [shaped((q_rows + o_rows, width), BF)],
        q_own,
        along(q_away, mask_at // 2),
        o_own,
        along(o_away, mask_at // 2),
        name="last_sum",
    )
    near = spread(after(piece, input_grad), chips)
    pieces = near + [to_core(after(part, g_down)) for part in near]
    found = call(
        bind(last_kernel, g),
        [shaped((g.shard, width), F32)] * 3
        + [vector] * 2
        + [shaped((g.shard, width), F32), shaped((g.hshard,), F32)]
        + [vector] * 6,
        [SMEM] + [VMEM] * (2 * chips),
        [sc, *pieces],
        name="last_lay",
    )
    gq, gk, gv, g_bq, g_bv, g_out, g_bin, g_gain2, g_bias2, g_bdown, g_gain1, g_bias1, g_bout = found
    return (
        layer_out.reshape(1, rows, width),
        input_grad.reshape(1, rows, width),
        gq,
        gk,
        gv,
        g_out,
        g_bq,
        g_bv,
        g_bout,
        g_gain1,
        g_bias1,
        g_in,
        g_bin,
        g_down,
        g_bdown,
        g_gain2,
        g_bias2,
    )


def fits(mesh):
    n, ring = mesh.shape["ctx"], mesh.shape["fsdp"]
    chips = n // 2
    return n % 2 == 0 and chips & (chips - 1) == 0 and chips > 1 and ring == chips and H % chips == 0 and ring * chips <= 16


def solution(mesh):
    in_specs = (
        P("fsdp", "ctx", None),
        P("fsdp", "ctx", None),
        P("fsdp", None),
        P("fsdp", None, None),
        P("fsdp", None),
        P("fsdp", None),
        P("fsdp", None),
        P("fsdp", None),
        P("fsdp"),
        P("fsdp"),
        P("fsdp"),
        P("fsdp"),
        P("fsdp"),
        P("fsdp", None),
        P("fsdp"),
        P("fsdp", None),
        P("fsdp"),
        P("fsdp"),
        P("fsdp"),
    )
    out_specs = (
        P("fsdp", "ctx", None),
        P("fsdp", "ctx", None),
        P("fsdp", None),
        P("fsdp", None),
        P("fsdp", None),
        P("fsdp", None),
        P("fsdp"),
        P("fsdp"),
        P("fsdp"),
        P("fsdp"),
        P("fsdp"),
        P("fsdp", None),
        P("fsdp"),
        P("fsdp", None),
        P("fsdp"),
        P("fsdp"),
        P("fsdp"),
    )
    body = chip_body if fits(mesh) else general_body
    return jax.shard_map(body, mesh=mesh, in_specs=in_specs, out_specs=out_specs, check_vma=False)
```
